32 devices in a mesh: grp: 2 (over x), seq: 16 (over z, y, core).
Axes of the slice: x: 2, y: 2, z: 4, core: 2. Of those that a mesh axis runs over, the one named last changes fastest.
Arguments:
- hidden_in: bfloat16 [2, 3, 2, 2048, 512], P('grp', None, None, 'seq'), may hold values from -6 to 6
- cotangent: bfloat16 [2, 3, 2, 2048, 512], P('grp', None, None, 'seq'), may hold values from -6 to 6
- cont_prompt: int32 [2, 12], P('grp'), may hold values from 0 to 2
- value_proj: bfloat16 [512, 1024], P('seq'), may hold values from -0.25 to 0.25
- shared_proj: bfloat16 [512, 128], P('seq'), may hold values from -0.25 to 0.25
- reset_proj: bfloat16 [512, 1024], P('seq'), may hold values from -0.25 to 0.25
- hidden_proj: bfloat16 [1024, 512], P('seq'), may hold values from -2 to 2
- inner_proj: bfloat16 [512, 1024], P('seq'), may hold values from -0.25 to 0.25
- outer_proj: bfloat16 [1024, 512], P('seq'), may hold values from -0.1875 to 0.1875
- ema_alpha: bfloat16 [512, 16], P('seq'), may hold values from 5e-05 to 0.3
- ema_delta: bfloat16 [512, 16], P('seq'), may hold values from 0.5 to 1
- ema_beta: bfloat16 [512, 16], P('seq'), may hold values from -600 to 600
- ema_eta: bfloat16 [512, 16], P('seq'), may hold values from -1.5 to 1.5
- ema_omega: bfloat16 [512], P('seq'), may hold values from -4 to 4
- norm_gain: bfloat16 [512], P('seq'), may hold values from 0.5 to 1.5
- ffn_gain: bfloat16 [512], P('seq'), may hold values from 0.5 to 1.5
- query_scale: bfloat16 [128], P('seq'), may hold values from -8 to 8
- query_shift: bfloat16 [128], P('seq'), may hold values from -2 to 2
- key_scale: bfloat16 [128], P('seq'), may hold values from -8 to 8
Outputs:
- layer_out: bfloat16 [2, 3, 2, 2048, 512], P('grp', None, None, 'seq')
- input_grad: bfloat16 [2, 3, 2, 2048, 512], P('grp', None, None, 'seq')
- value_grad: float32 [512, 1024], P('seq')
- shared_grad: float32 [512, 128], P('seq')
- reset_grad: float32 [512, 1024], P('seq')
- hidden_grad: float32 [1024, 512], P('seq')
- inner_grad: float32 [512, 1024], P('seq')
- outer_grad: float32 [1024, 512], P('seq')
- alpha_grad: float32 [512, 16], P('seq')
- delta_grad: float32 [512, 16], P('seq')
- beta_grad: float32 [512, 16], P('seq')
- eta_grad: float32 [512, 16], P('seq')
- omega_grad: float32 [512], P('seq')
- norm_gain_grad: float32 [512], P('seq')
- ffn_gain_grad: float32 [512], P('seq')
- query_scale_grad: float32 [128], P('seq')
- query_shift_grad: float32 [128], P('seq')
- key_scale_grad: float32 [128], P('seq')
The draws below stay inside these ranges and needn't reach their ends.
All inputs are finite; a program needn't handle non-finite values.
Results may differ from the reference program's by a relative error of at most 0.04.
Values may be sent and summed in bfloat16 or wider, within the bound.
A program may use at most 320 MiB of HBM per device.

```python
import math
import jax
import jax.numpy as jnp
from jax import lax

D = 512
ZD = 128
HV = 1024
NDIM = 16
FF = 1024
BLOCK = 128
CLEN = 512
PSETS = 3
GROUPS = 2
PLEN = 2048
CONTS = 4


def ema_rates(key):
    inner_key = jax.random.fold_in(key, 7301)
    key_alpha, key_delta, key_beta = jax.random.split(inner_key, 3)
    low_end = 0.0002
    high_end = 0.3
    rate_alpha = jnp.exp(jax.random.uniform(key_alpha, (D, NDIM), jnp.float32, math.log(low_end), math.log(high_end)))
    rate_delta = jax.random.uniform(key_delta, (D, NDIM), jnp.float32, 0.5, 1.0)
    input_beta = jnp.clip(jax.random.normal(key_beta, (D, NDIM), jnp.float32), -4.0, 4.0) * jnp.sqrt(rate_delta / rate_alpha)
    return (rate_alpha, rate_delta, input_beta)


def draw_ema_alpha(key, part):
    return ema_rates(key)[0].astype(jnp.bfloat16)


def draw_ema_delta(key, part):
    return ema_rates(key)[1].astype(jnp.bfloat16)


def draw_ema_beta(key, part):
    return ema_rates(key)[2].astype(jnp.bfloat16)


def touch_ends(drawn, key, low, largest):
    dims = drawn.shape
    place = [jax.random.randint(jax.random.fold_in(key, axis), (), 0, dims[axis]) for axis in range(len(dims))]
    drawn = drawn.at[tuple(place)].set(low)
    longest = dims.index(max(dims))
    place[longest] = (place[longest] + 1) % dims[longest]
    return drawn.at[tuple(place)].set(largest)


def spiked(drawn, key, source, target, parts, factor):
    def block_of(axis_at):
        return (jnp.arange(drawn.shape[axis_at]) // (drawn.shape[axis_at] // parts)).reshape((-1,) + (1,) * (drawn.ndim - 1 - axis_at))

    one_side = jax.random.permutation(key, parts)[block_of(target)]
    other_side = (block_of(target) + parts // 2) % parts
    return jnp.where((block_of(source) == one_side) | (block_of(source) == other_side), factor * drawn, drawn)


def level_of(key, shape, shards, low, largest):
    def one(dim, parts):
        draws = jax.random.uniform(jax.random.fold_in(jax.random.fold_in(key, 6), dim), (parts,), jnp.float32, low / len(shards), largest / len(shards))
        return jnp.repeat(jnp.exp(draws), shape[dim] // parts).reshape((-1,) + (1,) * (len(shape) - dim - 1))

    factor_of = one(*shards[0])
    for cut in shards[1:]:
        factor_of = factor_of * one(*cut)
    return factor_of


def scatter_about(key, extent, width, most, cuts=(), held_as=jnp.bfloat16):
    array = width * jax.random.normal(key, extent, jnp.float32)
    if cuts:
        array = array * level_of(key, extent, cuts, -0.22, 0.18)
    return jnp.clip(array, -most, most).astype(held_as)


def bell_draw_with(rng, extent, deviation, limit, cuts, heavy, kind=jnp.bfloat16):
    drawn = deviation * jax.random.normal(rng, extent, jnp.float32)
    if cuts:
        drawn = drawn * level_of(rng, extent, cuts, -0.22, 0.18)
    return jnp.clip(spiked(drawn, jax.random.fold_in(rng, 3), *heavy), -limit, limit).astype(kind)


def setup_inputs(seed: int = 0) -> dict:
    streams_of = jax.random.split(jax.random.key(seed), 20)
    return {
        "hidden_in": scatter_about(streams_of[0], (GROUPS, PSETS, 2, PLEN, D), 1.0, 6.0, ((0, 2), (3, 16))),
        "cotangent": bell_draw_with(streams_of[1], (GROUPS, PSETS, 2, PLEN, D), 1.0, 6.0, ((0, 2), (3, 16)), (3, 4, 16, 2.0)),
        "cont_prompt": touch_ends(jax.random.randint(streams_of[2], (GROUPS, PSETS * CONTS), 0, PSETS), jax.random.fold_in(streams_of[2], 1), 0, PSETS - 1).astype(jnp.int32),
        "value_proj": scatter_about(streams_of[3], (D, HV), D ** -0.5, 0.25, ((0, 16),)),
        "shared_proj": scatter_about(streams_of[4], (D, ZD), D ** -0.5, 0.25, ((0, 16),)),
        "reset_proj": scatter_about(streams_of[5], (D, HV), D ** -0.5, 0.25, ((0, 16),)),
        "hidden_proj": scatter_about(streams_of[6], (HV, D), (max(HV // 128, 1)) ** -0.5, 2.0, ((0, 16),)),
        "inner_proj": scatter_about(streams_of[7], (D, FF), D ** -0.5, 0.25, ((0, 16),)),
        "outer_proj": scatter_about(streams_of[8], (FF, D), FF ** -0.5, 0.1875, ((0, 16),)),
        "ema_alpha": draw_ema_alpha(jax.random.fold_in(streams_of[19], 71), 0),
        "ema_delta": draw_ema_delta(jax.random.fold_in(streams_of[19], 71), 0),
        "ema_beta": draw_ema_beta(jax.random.fold_in(streams_of[19], 71), 0),
        "ema_eta": scatter_about(streams_of[12], (D, NDIM), 0.25, 1.5, ((0, 16),)),
        "ema_omega": scatter_about(streams_of[13], (D,), 1.0, 4.0, ((0, 16),)),
        "norm_gain": jnp.clip(1.0 + 0.1 * jax.random.normal(streams_of[14], (D,), jnp.float32), 0.5, 1.5).astype(jnp.bfloat16),
        "ffn_gain": jnp.clip(1.0 + 0.1 * jax.random.normal(streams_of[15], (D,), jnp.float32), 0.5, 1.5).astype(jnp.bfloat16),
        "query_scale": scatter_about(streams_of[16], (ZD,), 2.0, 8.0, ((0, 16),)),
        "query_shift": scatter_about(streams_of[17], (ZD,), 0.5, 2.0, ((0, 16),)),
        "key_scale": scatter_about(streams_of[18], (ZD,), 2.0, 8.0, ((0, 16),)),
    }


PRECISE = lax.Precision.HIGHEST
NORM_EPS = 1e-05
MASKED_SCORE = -1e+30

@jax.custom_vjp
def low(v):
    return lax.optimization_barrier(v.astype(jnp.bfloat16)).astype(jnp.float32)

@jax.custom_vjp
def low_back(v):
    return v

def low_keep(v):
    return (low(v), None)

def low_pass(kept, grad):
    return (grad,)

def back_keep(v):
    return (v, None)

def back_low(kept, grad):
    return (low(grad),)
low.defvjp(low_keep, low_pass)
low_back.defvjp(back_keep, back_low)

def layer_norm(row_data, gain_vec):
    centered = row_data - lax.optimization_barrier(jnp.mean(row_data, axis=-1, keepdims=True))
    return centered * lax.rsqrt(lax.optimization_barrier(jnp.mean(centered * centered, axis=-1, keepdims=True)) + NORM_EPS) * gain_vec

def project(row_data, matrix):
    return jnp.einsum('...i,ij->...j', row_data, matrix, precision=PRECISE)

def ema_tables(rate_alpha, rate_delta, input_beta, mix_eta, sub_len):
    decay_rate = 1.0 - rate_alpha * rate_delta
    offsets = jnp.arange(sub_len, dtype=jnp.float32)
    powers = jnp.power(decay_rate[None, :, :], offsets[:, None, None])
    kernel = jnp.einsum('tcj,cj->ct', powers, mix_eta * rate_alpha * input_beta, precision=PRECISE)
    lag_index = jnp.arange(sub_len, dtype=jnp.int32)[:, None] - jnp.arange(sub_len, dtype=jnp.int32)[None, :]
    toeplitz = jnp.where(lag_index[None, :, :] >= 0, jnp.take(kernel, jnp.maximum(lag_index, 0), axis=1), 0.0)
    state_pow = powers[::-1] * (rate_alpha * input_beta)[None, :, :]
    carry_pow = jnp.power(decay_rate[None, :, :], (offsets + 1.0)[:, None, None]) * mix_eta[None, :, :]
    step_decay = jnp.power(decay_rate, 1.0 * sub_len)
    return (toeplitz, state_pow, carry_pow, step_decay)

def ema_block(sources, carry_in, tables, skip_omega):
    toeplitz, state_pow, carry_pow, step_decay = tables
    row_count, block_len, feat_width = sources.shape
    sub_len = toeplitz.shape[-1]
    sub_count = block_len // sub_len
    pieces = sources.reshape(row_count, sub_count, sub_len, feat_width)
    inner_part = jnp.einsum('cti,rsic->rstc', toeplitz, pieces, precision=PRECISE) + skip_omega * pieces
    states = jnp.einsum('rsic,icj->rscj', pieces, state_pow, precision=PRECISE)
    carries = []
    running = carry_in
    for sub_index in range(sub_count):
        carries.append(running)
        running = step_decay * running + states[:, sub_index]
    stacked = jnp.stack(carries, axis=1)
    outputs = inner_part + jnp.einsum('rscj,tcj->rstc', stacked, carry_pow, precision=PRECISE)
    return (outputs.reshape(row_count, block_len, feat_width), running)

def ema_run(sources, carry_start, tables, skip_omega):

    def advance(carry_in, block_in):
        block_out, carry_out = ema_block(block_in, carry_in, tables, skip_omega)
        return (carry_out, block_out)
    carry_end, outputs = lax.scan(jax.checkpoint(advance), carry_start, jnp.moveaxis(sources, 1, 0))
    return (carry_end, jnp.moveaxis(outputs, 0, 1))

def group_forward(tokens, prompt_of, value_proj, shared_proj, reset_proj, hidden_proj, inner_proj, outer_proj, ema_alpha, ema_delta, ema_beta, ema_eta, ema_omega, norm_gain, ffn_gain, query_scale, query_shift, key_scale):
    prompt_sets = tokens.shape[0]
    seq_len = tokens.shape[2]
    blocks = seq_len // BLOCK
    span_blocks = CLEN // BLOCK
    cont_count = seq_len // CLEN
    targets = prompt_of.reshape(prompt_sets, cont_count)
    normed = layer_norm(tokens, norm_gain)
    units_low = low(normed)
    value_pre = low_back(project(units_low, value_proj))
    values = low(jax.nn.silu(value_pre))
    tables = ema_tables(ema_alpha, ema_delta, ema_beta, ema_eta, math.gcd(16, BLOCK))
    prompt_src = normed[:, 0].reshape(prompt_sets, blocks, BLOCK, D)
    carry_zero = jnp.zeros((prompt_sets, D, NDIM), jnp.float32)
    final_state, prompt_ema = ema_run(prompt_src, carry_zero, tables, ema_omega)
    final_low = low(final_state)
    cont_start = jnp.take(final_low, targets.reshape(prompt_sets * cont_count), axis=0)
    cont_src = normed[:, 1].reshape(prompt_sets * cont_count, span_blocks, BLOCK, D)
    unused_end, cont_ema = ema_run(cont_src, cont_start, tables, ema_omega)
    ema_out = jnp.stack([prompt_ema.reshape(prompt_sets, seq_len, D), cont_ema.reshape(prompt_sets, seq_len, D)], axis=1)
    activ = low(jax.nn.silu(ema_out))
    shared_pre = low_back(project(activ, shared_proj))
    shared = jax.nn.silu(shared_pre)
    queries = low(shared * query_scale + query_shift)
    keys = low(shared * key_scale)
    reset_gate = jax.nn.silu(low_back(project(activ, reset_proj)))
    query_blocks = queries.reshape(prompt_sets, 2, blocks, BLOCK, ZD)
    key_blocks = keys.reshape(prompt_sets, 2, blocks, BLOCK, ZD)
    value_blocks = values.reshape(prompt_sets, 2, blocks, BLOCK, HV)
    extra_keys = jnp.repeat(jnp.take(key_blocks[:, 0, blocks - 1], targets, axis=0), span_blocks, axis=1)
    extra_values = jnp.repeat(jnp.take(value_blocks[:, 0, blocks - 1], targets, axis=0), span_blocks, axis=1)
    keys_all = jnp.concatenate([jnp.stack([jnp.zeros_like(extra_keys), extra_keys], axis=1), key_blocks], axis=-2)
    values_all = jnp.concatenate([jnp.stack([jnp.zeros_like(extra_values), extra_values], axis=1), value_blocks], axis=-2)
    extra_seen = jnp.broadcast_to(jnp.arange(2)[:, None] > 0, (2, blocks))
    causal = jnp.arange(BLOCK)[:, None] >= jnp.arange(BLOCK)[None, :]
    score_mask = jnp.concatenate([jnp.broadcast_to(extra_seen[:, :, None, None], (2, blocks, BLOCK, BLOCK)), jnp.broadcast_to(causal, (2, blocks, BLOCK, BLOCK))], axis=-1)
    scores = low_back(jnp.einsum('pknti,pknsi->pknts', query_blocks, keys_all, precision=PRECISE) / math.sqrt(ZD))
    scores = jnp.where(score_mask, scores, MASKED_SCORE)
    attn_probs = jax.nn.softmax(scores, axis=-1)
    mixed = low_back(jnp.einsum('pknts,pknsh->pknth', low(attn_probs), values_all, precision=PRECISE))
    gated = low(reset_gate * mixed.reshape(prompt_sets, 2, seq_len, HV))
    middle = tokens + low_back(project(gated, hidden_proj))
    mid_low = low(layer_norm(middle, ffn_gain))
    inner_low = low(jax.nn.silu(low_back(project(mid_low, inner_proj))))
    return middle + low_back(project(inner_low, outer_proj))

def reference(hidden_in, cotangent, cont_prompt, value_proj, shared_proj, reset_proj, hidden_proj, inner_proj, outer_proj, ema_alpha, ema_delta, ema_beta, ema_eta, ema_omega, norm_gain, ffn_gain, query_scale, query_shift, key_scale):
    weights = tuple((member.astype(jnp.float32) for member in (value_proj, shared_proj, reset_proj, hidden_proj, inner_proj, outer_proj, ema_alpha, ema_delta, ema_beta, ema_eta, ema_omega, norm_gain, ffn_gain, query_scale, query_shift, key_scale)))

    def one_group(running, inputs_group):
        tokens_group, cotangent_group, prompt_of = inputs_group

        def forward(layer_in, *params):
            return group_forward(layer_in, prompt_of, *params)
        out_group, pullback = jax.vjp(forward, tokens_group.astype(jnp.float32), *weights)
        grad_list = pullback(cotangent_group.astype(jnp.float32))
        running = tuple((total + part for total, part in zip(running, grad_list[1:])))
        return (running, (out_group.astype(jnp.bfloat16), grad_list[0].astype(jnp.bfloat16)))
    initial = tuple((jnp.zeros_like(member) for member in weights))
    totals, (outs, input_grads) = lax.scan(one_group, initial, (hidden_in, cotangent, cont_prompt))
    return (outs, input_grads, totals[0], totals[1], totals[2], totals[3], totals[4], totals[5], totals[6], totals[7], totals[8], totals[9], totals[10], totals[11], totals[12], totals[13], totals[14], totals[15])
```

```python
import functools
import math

import jax
import jax.numpy as jnp
from jax import lax
from jax.experimental import pallas as pl
from jax.experimental.pallas import tpu as pltpu
from jax.sharding import PartitionSpec as P

CLEN = 512
NORM_EPS = 1e-05
MASKED_SCORE = -1e30
MESH = pl.DeviceIdType.MESH
SUB = 16
NJ = 16
TINY = 1e-20
F32 = jnp.float32
BF16 = jnp.bfloat16
VMEM = pl.BlockSpec(memory_space=pltpu.VMEM)
ANY = pl.BlockSpec(memory_space=pl.ANY)
SMEM = pl.BlockSpec(memory_space=pltpu.SMEM)


def shift_down(value, count):
    rows = lax.broadcasted_iota(jnp.int32, value.shape, 0)
    return jnp.where(rows >= count, pltpu.roll(value, count, 0), 0.0)


def shift_up(value, count):
    rows = lax.broadcasted_iota(jnp.int32, value.shape, 0)
    return jnp.where(rows < 8 - count, pltpu.roll(value, 8 - count, 0), 0.0)


def row_of(ref, row):
    return jnp.broadcast_to(ref[pl.ds(row, 1), :], (8, 128))


def ema_local_pass(rows, x_ref, decay, decay16, decay32, decay64, inner_ref, final_ref, backward):
    shift = shift_up if backward else shift_down

    def body(item, carry):
        row, lane = item // 4, item % 4
        base = lane * (rows * 128) + row * 128
        dec = [row_of(decay, lane * 16 + j) for j in range(NJ)]
        state = [jnp.zeros((8, 128), F32)] * NJ
        for step in range(SUB - 1, -1, -1) if backward else range(SUB):
            x = x_ref[pl.ds(base + step, 8, stride=SUB), :]
            if backward:
                state = [dec[j] * (state[j] + x) for j in range(NJ)]
            else:
                state = [dec[j] * state[j] + x for j in range(NJ)]
        for j in range(NJ):
            total = state[j]
            total = total + row_of(decay16, lane * 16 + j) * shift(total, 1)
            total = total + row_of(decay32, lane * 16 + j) * shift(total, 2)
            total = total + row_of(decay64, lane * 16 + j) * shift(total, 4)
            inner_ref[pl.ds((item * 16 + j) * 8, 8), :] = shift(total, 1)
            final_ref[pl.ds(row * 64 + lane * 16 + j, 1), :] = total[0:1] if backward else total[7:8]
        return carry

    lax.fori_loop(0, rows * 4, body, 0)


def ema_apply_pass(rows, x_ref, decay, mix, omega, power, inner_ref, start_ref, y_ref):
    def body(item, carry):
        row, lane = item // 4, item % 4
        base = lane * (rows * 128) + row * 128
        state = [
            inner_ref[pl.ds((item * 16 + j) * 8, 8), :]
            + power[pl.ds((lane * 16 + j) * 8, 8), :] * row_of(start_ref, row * 64 + lane * 16 + j)
            for j in range(NJ)
        ]
        skip = row_of(omega, lane)
        for step in range(SUB):
            x = x_ref[pl.ds(base + step, 8, stride=SUB), :]
            sums = [skip * x, None]
            for j in range(NJ):
                state[j] = row_of(decay, lane * 16 + j) * state[j] + x
                term = row_of(mix, lane * 16 + j) * state[j]
                sums[j % 2] = term if sums[j % 2] is None else sums[j % 2] + term
            y_ref[pl.ds(base + step, 8, stride=SUB), :] = sums[0] + sums[1]
        return carry

    lax.fori_loop(0, rows * 4, body, 0)


def ema_back_pass(
    rows, x_rows, x_ref, g_ref, decay, mix, omega, power, inner_ref, start_ref, power_rev,
    back_inner_ref, back_start_ref, dx_ref, sum_in, sum_decay, sum_out, kept,
):
    half = 8

    def body(item, carry):
        row, lane = item // 4, item % 4
        base = lane * (rows * 128) + row * 128
        x_base = lane * (x_rows * 128) + row * 128
        skip = row_of(omega, lane)
        for part in range(NJ // half):
            js = range(part * half, part * half + half)
            dec = [row_of(decay, lane * 16 + j) for j in js]
            state = [
                inner_ref[pl.ds((item * 16 + j) * 8, 8), :]
                + power[pl.ds((lane * 16 + j) * 8, 8), :] * row_of(start_ref, row * 64 + lane * 16 + j)
                for j in js
            ]
            for step in range(SUB):
                x = x_ref[pl.ds(x_base + step, 8, stride=SUB), :]
                for i in range(half):
                    kept[step * half + i] = state[i]
                    state[i] = dec[i] * state[i] + x
            adj = [
                back_inner_ref[pl.ds((item * 16 + j) * 8, 8), :]
                + power_rev[pl.ds((lane * 16 + j) * 8, 8), :]
                * row_of(back_start_ref, row * 64 + lane * 16 + j)
                for j in js
            ]
            weight = [row_of(mix, lane * 16 + j) for j in js]
            edge = [-(adj[i] * state[i]) for i in range(half)]
            first, second = [None] * half, [None] * half
            for step in range(SUB - 1, -1, -1):
                x = x_ref[pl.ds(x_base + step, 8, stride=SUB), :]
                g = g_ref[pl.ds(base + step, 8, stride=SUB), :]
                sums = [skip * g if part == 0 else dx_ref[pl.ds(base + step, 8, stride=SUB), :], None]
                for i in range(half):
                    full = adj[i] + g
                    term = weight[i] * full
                    sums[i % 2] = term if sums[i % 2] is None else sums[i % 2] + term
                    with_x, with_s = full * x, full * kept[step * half + i]
                    first[i] = with_x if first[i] is None else first[i] + with_x
                    second[i] = with_s if second[i] is None else second[i] + with_s
                    adj[i] = dec[i] * full
                dx_ref[pl.ds(base + step, 8, stride=SUB), :] = sums[0] + sums[1]
            for i, j in enumerate(js):
                at = pl.ds(lane * 16 + j, 1)
                flow = edge[i] + adj[i] * kept[i]
                total = jnp.sum(first[i], axis=0, keepdims=True)
                sum_in[at, :] += total
                sum_decay[at, :] += jnp.sum(second[i], axis=0, keepdims=True)
                sum_out[at, :] += total + jnp.sum(flow, axis=0, keepdims=True)
        return carry

    lax.fori_loop(0, rows * 4, body, 0)


class Place:
    def __init__(self, n, groups):
        self.n, self.nq, self.groups = n, n // 4, groups
        self.g, self.s = lax.axis_index("grp"), lax.axis_index("seq")
        self.c, self.y, self.q, self.x = self.s % 2, (self.s // 2) % 2, self.s // 4, self.g % 2
        self.pos = self.s % 4
        self.core = (self.g, self.s + 1 - 2 * self.c)
        self.side = (self.g, self.s + 2 - 4 * self.y)
        self.cross = (self.g + 1 - 2 * self.x, self.s)
        self.is_last = self.s == n - 1

    def quad(self, k):
        return (self.q + k) % self.nq

    def at_quad(self, q):
        return (self.g, q * 4 + self.pos)

    def group_peers(self):
        return [(self.g, (self.s + k) % self.n) for k in range(1, self.n)]

    def cross_bit(self, bit):
        return (self.g + bit - 2 * bit * ((self.g // bit) % 2), self.s)

    def cross_bits(self):
        return [1 << b for b in range(self.groups.bit_length() - 1)]


def meet(peers):
    barrier = pltpu.get_barrier_semaphore()
    for peer in peers:
        pl.semaphore_signal(barrier, inc=1, device_id=peer, device_id_type=MESH)
    pl.semaphore_wait(barrier, len(peers))


def remote(src, dst, send, recv, device):
    return pltpu.make_async_remote_copy(
        src_ref=src, dst_ref=dst, send_sem=send, recv_sem=recv, device_id=device, device_id_type=MESH
    )


def gather_kernel(n, groups, s_in, a_in, b_in, x_in, s_out, a_out, b_out, x_out, ss, sr, zs, zr, ys, yr, xs, xr, cs, cr, ts, tr, ls):
    me = Place(n, groups)
    nq = me.nq
    meet(me.group_peers() + [me.cross])
    mats = ((a_in, a_out, a_in.shape[-1] // 2), (b_in, b_out, b_in.shape[-1] // 2))
    sent = []

    def send(*args):
        copy = remote(*args)
        copy.start()
        sent.append(copy)

    def got(ref, recv):
        remote(ref, ref, ls.at[0], recv, me.core).wait_recv()

    own = [pltpu.make_async_copy(s_in, s_out.at[me.s], ls.at[0])]
    own += [pltpu.make_async_copy(w_in, w_out.at[me.s], ls.at[1 + i]) for i, (w_in, w_out, _) in enumerate(mats)]
    for copy in own:
        copy.start()
    for k in range(1, n):
        send(s_in, s_out.at[me.s], ss.at[k - 1], sr.at[k - 1], (me.g, (me.s + k) % n))

    @pl.when(me.is_last)
    def _():
        for j in range(3):
            remote(x_in.at[j], x_out.at[j], ts.at[j], tr.at[0], (me.g, 4 * (nq - 1) + j)).start()
        pltpu.make_async_copy(x_in.at[3], x_out.at[3], ls.at[3]).start()

    def half(ref, width, which):
        return ref.at[:, pl.ds(pl.multiple_of(which * width, 128), width)]

    for k in range(1, nq):
        for i, (w_in, w_out, width) in enumerate(mats):
            send(half(w_in, width, me.x), half(w_out.at[me.s], width, me.x), zs.at[k - 1, i], zr.at[k - 1, i], me.at_quad(me.quad(k)))
    for i, (w_in, w_out, width) in enumerate(mats):
        send(w_in, w_out.at[me.s], ys.at[0, i], yr.at[0, i], me.side)
        send(w_in, w_out.at[me.s], cs.at[0, i], cr.at[0, i], me.core)

    @pl.when(me.q == nq - 1)
    def _():
        @pl.when(me.is_last)
        def _():
            pltpu.make_async_copy(x_in.at[3], x_out.at[3], ls.at[3]).wait()

        @pl.when(jnp.logical_not(me.is_last))
        def _():
            got(x_out.at[me.pos], tr.at[0])

        for k in range(1, nq):
            remote(x_out.at[me.pos], x_out.at[me.pos], ts.at[2 + k], tr.at[1], me.at_quad(me.quad(k))).start()

    other = 1 - me.x
    for k in range(1, nq):
        shard = me.quad(nq - k) * 4 + me.pos
        for i, (w_in, w_out, width) in enumerate(mats):
            piece = half(w_out.at[shard], width, me.x)
            got(piece, zr.at[k - 1, i])
            send(piece, piece, ys.at[k, i], yr.at[k, i], me.side)
            send(piece, piece, xs.at[k - 1, i], xr.at[k - 1, i], me.cross)
            send(piece, piece, cs.at[k, i], cr.at[k, i], me.core)

    @pl.when(me.q != nq - 1)
    def _():
        got(x_out.at[me.pos], tr.at[1])

    mine = x_out.at[me.pos]
    send(mine, mine, ts.at[nq + 2], tr.at[2], me.side)
    send(mine, mine, ts.at[nq + 3], tr.at[3], me.core)

    side_pos = me.pos + 2 - 4 * me.y
    for k in range(nq):
        shard = me.quad(nq - k) * 4 + side_pos
        for i, (w_in, w_out, width) in enumerate(mats):
            piece = w_out.at[shard] if k == 0 else half(w_out.at[shard], width, me.x)
            got(piece, yr.at[k, i])
            if k:
                send(piece, piece, xs.at[nq - 2 + k, i], xr.at[nq - 2 + k, i], me.cross)
            send(piece, piece, cs.at[nq + k, i], cr.at[nq + k, i], me.core)
    theirs = x_out.at[side_pos]
    got(theirs, tr.at[2])
    send(theirs, theirs, ts.at[nq + 4], tr.at[4], me.core)
    for group, pos in ((0, me.pos), (1, side_pos)):
        for k in range(1, nq):
            shard = me.quad(nq - k) * 4 + pos
            at = group * (nq - 1) + k - 1
            for i, (w_in, w_out, width) in enumerate(mats):
                piece = half(w_out.at[shard], width, other)
                got(piece, xr.at[at, i])
                send(piece, piece, cs.at[2 * nq + at, i], cr.at[2 * nq + at, i], me.core)
    flip = 1 - 2 * me.c
    for group, pos in ((0, me.pos + flip), (1, side_pos + flip)):
        for k in range(nq):
            shard = me.quad(nq - k) * 4 + pos
            for i, (w_in, w_out, width) in enumerate(mats):
                if k == 0:
                    got(w_out.at[shard], cr.at[group * nq, i])
                else:
                    got(half(w_out.at[shard], width, me.x), cr.at[group * nq + k, i])
                    at = 2 * nq + group * (nq - 1) + k - 1
                    got(half(w_out.at[shard], width, other), cr.at[at, i])
    got(x_out.at[me.pos + flip], tr.at[3])
    got(x_out.at[side_pos + flip], tr.at[4])
    for k in range(1, n):
        got(s_out.at[(me.s + n - k) % n], sr.at[k - 1])
    for copy in own:
        copy.wait()
    for copy in sent:
        copy.wait_send()

    @pl.when(me.is_last)
    def _():
        for j in range(3):
            remote(x_in.at[j], x_out.at[j], ts.at[j], tr.at[0], (me.g, 4 * (nq - 1) + j)).wait_send()

    @pl.when(me.q == nq - 1)
    def _():
        for k in range(1, nq):
            remote(x_out.at[me.pos], x_out.at[me.pos], ts.at[2 + k], tr.at[1], me.at_quad(me.quad(k))).wait_send()


def gather_call(n, groups, small, mat_a, mat_b, tail):
    nq = n // 4
    sems = [(n - 1,), (n - 1,), (nq - 1, 2), (nq - 1, 2), (nq, 2), (nq, 2), (2 * nq - 2, 2), (2 * nq - 2, 2), (4 * nq - 2, 2), (4 * nq - 2, 2), (nq + 5,), (5,), (4,)]
    return pl.pallas_call(
        functools.partial(gather_kernel, n, groups),
        out_shape=[
            jax.ShapeDtypeStruct((n,) + small.shape, BF16),
            jax.ShapeDtypeStruct((n,) + mat_a.shape, BF16),
            jax.ShapeDtypeStruct((n,) + mat_b.shape, BF16),
            jax.ShapeDtypeStruct(tail.shape, BF16),
        ],
        in_specs=[ANY] * 4,
        out_specs=[ANY] * 4,
        scratch_shapes=[pltpu.SemaphoreType.DMA(shape) for shape in sems],
        compiler_params=pltpu.CompilerParams(collective_id=0, has_side_effects=True),
        name="gather_weights",
    )(small, mat_a, mat_b, tail)


def pick(index, values):
    out = values[0]
    for k in range(1, len(values)):
        out = jnp.where(index == k, values[k], out)
    return out


def forward_exchange(n, groups, f_ref, ab_ref, d_ref, sel_ref, s_ref, m0, r0, m1, r1, m2, r2, ss, rs, zs, zr, ps, pr):
    me = Place(n, groups)
    nq = me.nq
    meet(me.group_peers())
    one, two, three, four = d_ref[0], d_ref[1], d_ref[2], d_ref[3]
    m0[...] = f_ref[0:3].astype(BF16)
    copy = remote(m0, r0, ss.at[0], rs.at[0], me.core)
    copy.start()
    copy.wait()
    upper_core, upper_side = me.c == 1, me.y == 1
    mine = f_ref[0:3]
    other = r0[...].astype(F32)
    lower = jnp.where(upper_core, other, mine)
    upper = jnp.where(upper_core, mine, other)
    pair = one * lower + upper
    before = jnp.where(upper_core, other, 0.0)
    m1[0] = pair.astype(BF16)
    m1[1, :, 0] = lower[:, 0].astype(BF16)
    copy = remote(m1, r1, ss.at[1], rs.at[1], me.side)
    m1[1, :, 1] = jnp.zeros_like(m1[1, :, 1])
    copy.start()
    copy.wait()
    far = r1[0].astype(F32)
    low_pair = jnp.where(upper_side, far, pair)
    high_pair = jnp.where(upper_side, pair, far)
    total = two * low_pair + high_pair
    before = jnp.where(upper_side, jnp.where(upper_core, one * far, far), 0.0) + before
    third = jnp.where(upper_side, lower[:, 0], r1[1, :, 0].astype(F32))
    last_in = one * low_pair[:, 0] + third
    m2[0] = total[:, 0].astype(BF16)
    m2[1] = last_in.astype(BF16)
    sends = []
    for k in range(1, nq):
        copy = remote(m2.at[0], r2.at[me.q], zs.at[k - 1], zr.at[k - 1], me.at_quad(me.quad(k)))
        copy.start()
        sends.append(copy)

    @pl.when(me.q == nq - 1)
    def _():
        for k in range(1, nq):
            remote(m2.at[1], r2.at[nq], ps.at[k - 1], pr.at[0], me.at_quad(me.quad(k))).start()
        r2[nq] = m2[1]

    r2[me.q] = m2[0]
    for k in range(1, nq):
        src = r2.at[me.quad(nq - k)]
        remote(src, src, zs.at[k - 1], zr.at[k - 1], me.core).wait_recv()

    @pl.when(me.q != nq - 1)
    def _():
        remote(r2.at[nq], r2.at[nq], ps.at[0], pr.at[0], me.core).wait_recv()

    run = jnp.zeros((3, 64, 128), F32)
    carry, tail_in = run, run
    for k in range(nq):
        carry = jnp.where(me.q == k, run, carry)
        if k == nq - 1:
            tail_in = three * run + r2[nq].astype(F32)
        run = four * run + r2[k].astype(F32)
    low = (ab_ref[...] * run).astype(BF16).astype(F32)
    safe = jnp.abs(ab_ref[...]) >= TINY
    begin = jnp.where(safe, low / jnp.where(safe, ab_ref[...], 1.0), run)
    lead = pick(me.pos, [jnp.ones_like(one), one, two, three])
    for p in range(3):
        start = sel_ref[p * 3] * begin[0] + sel_ref[p * 3 + 1] * begin[1] + sel_ref[p * 3 + 2] * begin[2]
        s_ref[2 * p] = lead * carry[p] + before[p, 0]
        s_ref[2 * p + 1] = lead * start + before[p, 1]
        s_ref[6 + p] = tail_in[p]
    for copy in sends:
        copy.wait_send()

    @pl.when(me.q == nq - 1)
    def _():
        for k in range(1, nq):
            remote(m2.at[1], r2.at[nq], ps.at[k - 1], pr.at[0], me.at_quad(me.quad(k))).wait_send()


def forward_exchange_call(n, groups, finals, ab, decays, sel):
    nq = n // 4
    dma = pltpu.SemaphoreType.DMA
    return pl.pallas_call(
        functools.partial(forward_exchange, n, groups),
        out_shape=jax.ShapeDtypeStruct((9, 64, 128), F32),
        in_specs=[VMEM, VMEM, VMEM, SMEM],
        out_specs=VMEM,
        scratch_shapes=[
            pltpu.VMEM((3, 2, 64, 128), BF16), pltpu.VMEM((3, 2, 64, 128), BF16),
            pltpu.VMEM((2, 3, 2, 64, 128), BF16), pltpu.VMEM((2, 3, 2, 64, 128), BF16),
            pltpu.VMEM((2, 3, 64, 128), BF16), pltpu.VMEM((nq + 1, 3, 64, 128), BF16),
            dma((2,)), dma((2,)), dma((nq - 1,)), dma((nq - 1,)), dma((nq - 1,)), dma((1,)),
        ],
        compiler_params=pltpu.CompilerParams(collective_id=1, has_side_effects=True, vmem_limit_bytes=40 << 20),
        name="forward_exchange",
    )(finals, ab, decays, sel)


def backward_exchange(n, groups, f_ref, d_ref, sel_ref, s_ref, m0, r0, m1, r1, m2, r2, ss, rs, zs, zr):
    me = Place(n, groups)
    nq = me.nq
    meet(me.group_peers())
    one, two, three, four = d_ref[0], d_ref[1], d_ref[2], d_ref[3]
    m0[...] = f_ref[...].astype(BF16)
    copy = remote(m0, r0, ss.at[0], rs.at[0], me.core)
    copy.start()
    copy.wait()
    upper_core, upper_side = me.c == 1, me.y == 1
    mine = f_ref[...]
    other = r0[...].astype(F32)
    lower = jnp.where(upper_core, other, mine)
    upper = jnp.where(upper_core, mine, other)
    pair = lower + one * upper
    after = jnp.where(upper_core, 0.0, other)
    m1[...] = pair.astype(BF16)
    copy = remote(m1, r1, ss.at[1], rs.at[1], me.side)
    copy.start()
    copy.wait()
    far = r1[...].astype(F32)
    low_pair = jnp.where(upper_side, far, pair)
    high_pair = jnp.where(upper_side, pair, far)
    total = low_pair + two * high_pair
    after = jnp.where(upper_side, 0.0, jnp.where(upper_core, far, one * far)) + after
    m2[0] = total[:, 0].astype(BF16)
    for m in range(3):
        m2[1, m] = (sel_ref[m] * total[0, 1] + sel_ref[3 + m] * total[1, 1] + sel_ref[6 + m] * total[2, 1]).astype(BF16)
    sends = []
    for k in range(1, nq):
        copy = remote(m2, r2.at[me.q], zs.at[k - 1], zr.at[k - 1], me.at_quad(me.quad(k)))
        copy.start()
        sends.append(copy)
    r2[me.q] = m2[...]
    for k in range(1, nq):
        src = r2.at[me.quad(nq - k)]
        remote(src, src, zs.at[k - 1], zr.at[k - 1], me.core).wait_recv()
    run = r2[0, 1].astype(F32)
    for k in range(1, nq):
        run = run + r2[k, 1].astype(F32)
    carry = run
    for k in range(nq - 1, -1, -1):
        carry = jnp.where(me.q == k, run, carry)
        run = four * run + r2[k, 0].astype(F32)
    lead = pick(me.pos, [three, two, one, jnp.ones_like(one)])
    for p in range(3):
        s_ref[2 * p] = lead * carry[p] + after[p, 0]
        s_ref[2 * p + 1] = after[p, 1]
    for copy in sends:
        copy.wait_send()


def backward_exchange_call(n, groups, flows, decays, sel):
    nq = n // 4
    dma = pltpu.SemaphoreType.DMA
    return pl.pallas_call(
        functools.partial(backward_exchange, n, groups),
        out_shape=jax.ShapeDtypeStruct((6, 64, 128), F32),
        in_specs=[VMEM, VMEM, SMEM],
        out_specs=VMEM,
        scratch_shapes=[
            pltpu.VMEM((3, 2, 64, 128), BF16), pltpu.VMEM((3, 2, 64, 128), BF16),
            pltpu.VMEM((3, 2, 64, 128), BF16), pltpu.VMEM((3, 2, 64, 128), BF16),
            pltpu.VMEM((2, 3, 64, 128), BF16), pltpu.VMEM((nq, 2, 3, 64, 128), BF16),
            dma((2,)), dma((2,)), dma((nq - 1,)), dma((nq - 1,)),
        ],
        compiler_params=pltpu.CompilerParams(collective_id=2, has_side_effects=True, vmem_limit_bytes=40 << 20),
        name="backward_exchange",
    )(flows, decays, sel)


def tail_flow(me, t, r1, w1, r2, w2, r3, out, send, recv):
    nq = me.nq
    last = me.q == nq - 1
    out[...] = jnp.zeros_like(out)
    copy1 = remote(t.at[:, 1 - me.c], r1, send.at[0], recv.at[0], me.core)
    copy1.start()
    yield
    copy1.wait()
    for i in range(2):
        w1[i] = (t[i, me.c].astype(F32) + r1[i].astype(F32)).astype(BF16)
    copy2 = remote(w1.at[1 - me.y], r2, send.at[1], recv.at[1], me.side)
    copy2.start()
    yield
    copy2.wait()
    w2[...] = (w1[me.y].astype(F32) + r2[...].astype(F32)).astype(BF16)
    top = (me.g, (nq - 1) * 4 + me.pos)
    end = (me.g, nq * 4 - 1)
    for k in range(nq - 1):
        @pl.when(me.q == k)
        def _():
            remote(w2, r3.at[k], send.at[2], recv.at[2 + k], top).start()
    yield

    @pl.when(last)
    def _():
        total = w2[...].astype(F32)
        for k in range(nq - 1):
            remote(r3.at[k], r3.at[k], send.at[2], recv.at[2 + k], me.core).wait_recv()
            total = total + r3[k].astype(F32)
        w2[...] = total.astype(BF16)

        @pl.when(jnp.logical_not(me.is_last))
        def _():
            for j in range(3):
                @pl.when(me.pos == j)
                def _():
                    remote(w2, out.at[j // 2, j % 2], send.at[2], recv.at[nq + 1 + j], end).start()

        @pl.when(me.is_last)
        def _():
            out[1, 1] = w2[...]
    yield

    @pl.when(me.is_last)
    def _():
        for j in range(3):
            dst = out.at[j // 2, j % 2]
            remote(dst, dst, send.at[2], recv.at[nq + 1 + j], me.core).wait_recv()

    @pl.when(jnp.logical_not(me.is_last))
    def _():
        remote(w2, w2, send.at[2], recv.at[2], me.core).wait_send()


def tail_scratch(nq, rows, width):
    return [
        pltpu.VMEM((2, rows, width), BF16), pltpu.VMEM((2, rows, width), BF16),
        pltpu.VMEM((rows, width), BF16), pltpu.VMEM((rows, width), BF16),
        pltpu.VMEM((nq - 1, rows, width), BF16),
    ]


def keys_kernel(n, groups, t, out, r1, w1, r2, w2, r3, send, recv):
    me = Place(n, groups)
    meet(me.group_peers())
    for _ in tail_flow(me, t, r1, w1, r2, w2, r3, out, send, recv):
        pass


def keys_call(n, groups, t):
    nq = n // 4
    dma = pltpu.SemaphoreType.DMA
    return pl.pallas_call(
        functools.partial(keys_kernel, n, groups),
        out_shape=jax.ShapeDtypeStruct(t.shape, BF16),
        in_specs=[VMEM],
        out_specs=VMEM,
        scratch_shapes=tail_scratch(nq, t.shape[2], t.shape[3]) + [dma((3,)), dma((nq + 4,))],
        compiler_params=pltpu.CompilerParams(collective_id=3, has_side_effects=True),
        name="tail_keys",
    )(t)


def sum_flow(me, cross_first, grads, r1, w1, r2, w2, r3, w3, r4, rx, out, send, recv):
    nq = me.nq
    rows, width = out.shape
    wide = width // 2
    ours = pl.ds(pl.multiple_of(me.x * wide, 128), wide)
    others = pl.ds(pl.multiple_of((1 - me.x) * wide, 128), wide)
    copy1 = remote(grads.at[:, :, 1 - me.c], r1, send.at[0], recv.at[0], me.core)
    copy1.start()
    yield
    copy1.wait()

    def add1(i, carry):
        w1[i // 2, i % 2] = (grads[i // 2, i % 2, me.c].astype(F32) + r1[i // 2, i % 2].astype(F32)).astype(BF16)
        return carry

    lax.fori_loop(0, 2 * nq, add1, 0)
    if cross_first:
        copy2 = remote(w1.at[:, :, :, others], r2, send.at[1], recv.at[1], me.cross)
    else:
        copy2 = remote(w1.at[:, 1 - me.y], r2, send.at[1], recv.at[1], me.side)
    copy2.start()
    yield
    copy2.wait()
    if cross_first:
        def add2(i, carry):
            w2[i // 2, i % 2] = (w1[i // 2, i % 2, :, ours].astype(F32) + r2[i // 2, i % 2].astype(F32)).astype(BF16)
            return carry

        lax.fori_loop(0, 2 * nq, add2, 0)
        copy3 = remote(w2.at[:, 1 - me.y], r3, send.at[2], recv.at[2], me.side)
    else:
        def add2(i, carry):
            w2[i] = (w1[i, me.y].astype(F32) + r2[i].astype(F32)).astype(BF16)
            return carry

        lax.fori_loop(0, nq, add2, 0)
        copy3 = remote(w2.at[:, :, others], r3, send.at[2], recv.at[2], me.cross)
    copy3.start()
    yield
    copy3.wait()

    def add3(i, carry):
        kept = w2[i, me.y] if cross_first else w2[i, :, ours]
        w3[i] = (kept.astype(F32) + r3[i].astype(F32)).astype(BF16)
        return carry

    lax.fori_loop(0, nq, add3, 0)
    copies = []
    for k in range(1, nq):
        copy = remote(w3.at[me.quad(k)], r4.at[k - 1], send.at[2 + k], recv.at[2 + k], me.at_quad(me.quad(k)))
        copy.start()
        copies.append(copy)
    yield
    total = w3[me.q].astype(F32)
    for k in range(1, nq):
        copies[k - 1].wait()
        total = total + r4[k - 1].astype(F32)
    out[:, ours] = total.astype(BF16)
    copy5 = remote(out.at[:, ours], out.at[:, ours], send.at[nq + 2], recv.at[nq + 2], me.cross)
    copy5.start()
    yield
    remote(out.at[:, others], out.at[:, others], send.at[nq + 2], recv.at[nq + 2], me.cross).wait_recv()
    copy5.wait_send()
    for at, bit in enumerate(me.cross_bits()[1:]):
        copy = remote(out, rx.at[at], send.at[nq + 3 + at], recv.at[nq + 3 + at], me.cross_bit(bit))
        copy.start()
        copy.wait()
        out[...] = (out[...].astype(F32) + rx[at].astype(F32)).astype(BF16)


def sum_scratch(nq, groups, cross_first, rows, width):
    extra = max(groups.bit_length() - 2, 1)
    half = width // 2
    full = [pltpu.VMEM((nq, 2, rows, width), BF16)] * 2
    if cross_first:
        mid = [pltpu.VMEM((nq, 2, rows, half), BF16)] * 2
    else:
        mid = [pltpu.VMEM((nq, rows, width), BF16)] * 2
    return full + mid + [
        pltpu.VMEM((nq, rows, half), BF16), pltpu.VMEM((nq, rows, half), BF16),
        pltpu.VMEM((nq - 1, rows, half), BF16), pltpu.VMEM((extra, rows, width), BF16),
    ]


def drive(flows):
    live, waiting = [], list(flows)
    while live or waiting:
        if waiting:
            live.append(waiting.pop(0))
        for flow in list(live):
            try:
                next(flow)
            except StopIteration:
                live.remove(flow)


def sums_kernel(n, groups, orders, *refs):
    me = Place(n, groups)
    count = len(orders)
    grads, t = refs[:count], refs[count]
    outs, t_out = refs[count + 1 : 2 * count + 1], refs[2 * count + 1]
    rest = list(refs[2 * count + 2 :])
    send, recv, tsend, trecv = rest[-4:]
    meet(me.group_peers() + [me.cross_bit(bit) for bit in me.cross_bits()])
    flows = []
    for i, order in enumerate(orders):
        scratch = rest[8 * i : 8 * i + 8]
        flows.append(sum_flow(me, order, grads[i], *scratch, outs[i], send.at[i], recv.at[i]))
    flows.append(tail_flow(me, t, *rest[8 * count : 8 * count + 5], t_out, tsend, trecv))
    drive(flows)


def sums_call(n, groups, grads, tail):
    nq = n // 4
    dma = pltpu.SemaphoreType.DMA
    orders = tuple(i % 2 == 0 for i in range(len(grads)))
    scratch = []
    for order, grad in zip(orders, grads):
        scratch += sum_scratch(nq, groups, order, grad.shape[-2], grad.shape[-1])
    scratch += tail_scratch(nq, tail.shape[2], tail.shape[3])
    sems = nq + 3 + max(groups.bit_length() - 2, 1)
    scratch += [dma((len(grads), sems)), dma((len(grads), sems)), dma((3,)), dma((nq + 4,))]
    return pl.pallas_call(
        functools.partial(sums_kernel, n, groups, orders),
        out_shape=[jax.ShapeDtypeStruct(grad.shape[-2:], BF16) for grad in grads] + [jax.ShapeDtypeStruct(tail.shape, BF16)],
        in_specs=[VMEM] * (len(grads) + 1),
        out_specs=[VMEM] * (len(grads) + 1),
        scratch_shapes=scratch,
        compiler_params=pltpu.CompilerParams(collective_id=4, has_side_effects=True, vmem_limit_bytes=56 << 20),
        name="sum_weights",
    )(*grads, tail)


def ema_call(kernel, name, outs, ins, scratch=()):
    return pl.pallas_call(
        kernel,
        out_shape=[jax.ShapeDtypeStruct(shape, F32) for shape in outs],
        in_specs=[VMEM] * len(ins),
        out_specs=[VMEM] * len(outs),
        scratch_shapes=scratch,
        compiler_params=pltpu.CompilerParams(vmem_limit_bytes=56 << 20),
        name=name,
    )(*ins)


def local_pass_call(rows, backward, x, dec):
    def kernel(x_ref, d_ref, inner_ref, final_ref):
        ema_local_pass(rows, x_ref, d_ref.at[0], d_ref.at[1], d_ref.at[2], d_ref.at[3], inner_ref, final_ref, backward)

    return ema_call(kernel, "ema_local", [(rows * 512, 128), (rows * 64, 128)], (x, dec))


def apply_pass_call(rows, x, dec, mix, omega, power, inner, start):
    def kernel(x_ref, d_ref, mix_ref, omega_ref, power_ref, inner_ref, start_ref, y_ref):
        ema_apply_pass(rows, x_ref, d_ref.at[0], mix_ref, omega_ref, power_ref, inner_ref, start_ref, y_ref)

    return ema_call(kernel, "ema_apply", [(rows * 512, 128)], (x, dec, mix, omega, power, inner, start))[0]


def back_pass_call(rows, x_rows, x, g, dec, mix, omega, power, inner, start, power_rev, back_inner, back_start):
    def kernel(x_ref, g_ref, d_ref, mix_ref, omega_ref, power_ref, inner_ref, start_ref, rev_ref, bi_ref, bs_ref, dx_ref, a_ref, b_ref, c_ref, kept):
        for ref in (a_ref, b_ref, c_ref):
            ref[...] = jnp.zeros_like(ref)
        ema_back_pass(
            rows, x_rows, x_ref, g_ref, d_ref.at[0], mix_ref, omega_ref, power_ref, inner_ref, start_ref,
            rev_ref, bi_ref, bs_ref, dx_ref, a_ref, b_ref, c_ref, kept,
        )

    return ema_call(
        kernel, "ema_back", [(rows * 512, 128), (64, 128), (64, 128), (64, 128)],
        (x, g, dec, mix, omega, power, inner, start, power_rev, back_inner, back_start),
        [pltpu.VMEM((128, 8, 128), F32)],
    )


def silu_grad(pre_act):
    sigmoid_val = jax.nn.sigmoid(pre_act)
    return sigmoid_val * (1.0 + pre_act * (1.0 - sigmoid_val))


def norm_rows(row_data):
    centered = row_data - jnp.mean(row_data, axis=-1, keepdims=True)
    scale_inv = lax.rsqrt(jnp.mean(centered * centered, axis=-1, keepdims=True) + NORM_EPS)
    return (centered * scale_inv, scale_inv)


def norm_back(grad_rows, plain, scale_inv, gain_vec):
    grad_norm = grad_rows * gain_vec
    inner_term = (
        grad_norm
        - jnp.mean(grad_norm, axis=-1, keepdims=True)
        - plain * jnp.mean(grad_norm * plain, axis=-1, keepdims=True)
    )
    return inner_term * scale_inv


def lanes_first(rows):
    return rows.reshape(-1, 4, 128).transpose(1, 0, 2).reshape(-1, 128)


def rows_first(lanes):
    return lanes.reshape(4, -1, 128).transpose(1, 0, 2).reshape(-1, 512)


def dot(lhs, rhs, dims):
    return lax.dot_general(lhs, rhs, ((dims[:1], dims[1:]), ((), ())), preferred_element_type=F32)


def local(
    hidden_in, cotangent, cont_prompt, value_proj, shared_proj, reset_proj, hidden_proj, inner_proj,
    outer_proj, ema_alpha, ema_delta, ema_beta, ema_eta, ema_omega, norm_gain, ffn_gain, query_scale,
    query_shift, key_scale,
):
    n, groups = lax.axis_size("seq"), lax.axis_size("grp")
    nq = n // 4
    seq_index = lax.axis_index("seq")
    sets, kinds, length, width = hidden_in.shape[1:]
    chan = width // n
    heads = query_scale.shape[0]
    tokens_low = hidden_in[0]
    vectors = jnp.stack((query_scale, query_shift, key_scale), axis=1)
    small = jnp.concatenate(
        (
            ema_alpha, ema_delta, ema_beta, ema_eta, ema_omega[:, None], norm_gain[:, None], ffn_gain[:, None],
            jnp.pad(vectors, ((0, chan - heads), (0, 0))), jnp.zeros((chan, 58), BF16),
        ),
        axis=1,
    )
    small = jnp.concatenate((small, shared_proj), axis=0)
    mat_a = jnp.concatenate((value_proj, reset_proj, inner_proj), axis=0)
    mat_b = jnp.concatenate((hidden_proj, outer_proj), axis=0)
    rows_b = hidden_proj.shape[0]
    all_small, all_a, all_b, tail_low = gather_call(
        n, groups, small, mat_a, mat_b, tokens_low[:, 0].reshape(4, sets * length // 4, width)
    )
    mat_shared = all_small[:, chan:].reshape(width, 128)
    mat_value = all_a[:, :chan].reshape(width, -1)
    mat_reset = all_a[:, chan : 2 * chan].reshape(width, -1)
    mat_inner = all_a[:, 2 * chan :].reshape(width, -1)
    mat_hidden = all_b[:, :rows_b].reshape(-1, width)
    mat_outer = all_b[:, rows_b:].reshape(-1, width)
    flat = all_small[:, :chan].astype(F32)
    table = flat.reshape(width, 128).T
    vecs = flat[:, :heads, 67:70].reshape(-1, 3)
    query_mul, query_add, key_mul = vecs[:, 0], vecs[:, 1], vecs[:, 2]

    def by_lane(part):
        return part.reshape(16, 4, 128).transpose(1, 0, 2).reshape(64, 128)

    alpha, delta, beta, eta = (by_lane(table[16 * i : 16 * i + 16]) for i in range(4))
    omega, gain_one, gain_two = table[64], table[65], table[66]
    omega_lanes = omega.reshape(4, 128)
    decay = 1.0 - alpha * delta
    decay2 = decay * decay
    decay4 = decay2 * decay2
    decay8 = decay4 * decay4
    decay16 = decay8 * decay8
    decay32 = decay16 * decay16
    decay64 = decay32 * decay32
    decay128 = decay64 * decay64
    decay256 = decay128 * decay128
    dec = jnp.stack((decay, decay16, decay32, decay64))
    far = jnp.stack((decay128, decay256, decay256 * decay128, decay256 * decay256))
    steps = [jnp.ones_like(decay), decay16, decay32, decay32 * decay16, decay64, decay64 * decay16, decay64 * decay32, decay64 * decay32 * decay16]
    power = jnp.stack(steps, axis=1).reshape(512, 128)
    power_rev = jnp.stack(steps[::-1], axis=1).reshape(512, 128)
    ab = alpha * beta
    mix = ab * eta
    targets = lax.dynamic_slice_in_dim(
        cont_prompt[0].reshape(sets, nq), seq_index // 4, 1, 1
    )[:, 0]
    select = (targets[:, None] == jnp.arange(sets, dtype=jnp.int32)[None, :]).astype(F32)
    sel = select.reshape(-1)
    own_rows = sets * kinds * length
    rows_low = jnp.concatenate((tokens_low.reshape(own_rows, width), tail_low.reshape(-1, width)), axis=0)
    tokens = rows_low.astype(F32)
    plain_in, inv_in = norm_rows(tokens)
    normed = plain_in * gain_one
    units_low = normed.astype(BF16)
    x_lanes = lanes_first(normed)
    inner, finals = local_pass_call(9, False, x_lanes, dec)
    starts = forward_exchange_call(n, groups, finals[: 6 * 64].reshape(3, 2, 64, 128), ab, far, sel)
    starts = starts.reshape(9 * 64, 128)
    ema_all = rows_first(apply_pass_call(9, x_lanes, dec, mix, omega_lanes, power, inner, starts))
    value_pre = dot(units_low, mat_value, (1, 0))
    values = jax.nn.silu(value_pre).astype(BF16)
    activ_all = jax.nn.silu(ema_all).astype(BF16)
    shared_pre_all = dot(activ_all, mat_shared, (1, 0))
    shared_all = jax.nn.silu(shared_pre_all)
    keys_all_rows = (shared_all * key_mul).astype(BF16)
    activ, shared, shared_pre = activ_all[:own_rows], shared_all[:own_rows], shared_pre_all[:own_rows]
    queries = (shared * query_mul + query_add).astype(BF16).reshape(sets, 2, length, 128)
    keys = keys_all_rows[:own_rows].reshape(sets, 2, length, 128)
    own_values = values[:own_rows].reshape(sets, 2, length, -1)
    pick_low = select.astype(BF16)
    extra_keys = jnp.einsum(
        "pm,mtz->ptz", pick_low, keys_all_rows[own_rows:].reshape(sets, length, 128), preferred_element_type=F32
    ).astype(BF16)
    extra_values = jnp.einsum(
        "pm,mth->pth", pick_low, values[own_rows:].reshape(sets, length, -1), preferred_element_type=F32
    ).astype(BF16)
    reset_pre = dot(activ, mat_reset, (1, 0))
    reset_gate = jax.nn.silu(reset_pre)
    causal = jnp.arange(length)[:, None] >= jnp.arange(length)[None, :]
    score_scale = math.sqrt(queries.shape[-1])
    cont_q, cont_k, cont_v = queries[:, 1], keys[:, 1], own_values[:, 1]

    def scores_of(lhs, rhs):
        return jnp.einsum("ptz,psz->pts", lhs, rhs, preferred_element_type=F32) / score_scale

    p_scores = jnp.where(causal, scores_of(queries[:, 0], keys[:, 0]), MASKED_SCORE)
    c_scores = jnp.concatenate(
        (scores_of(cont_q, extra_keys), jnp.where(causal, scores_of(cont_q, cont_k), MASKED_SCORE)), axis=2
    )
    p_probs, c_probs = jax.nn.softmax(p_scores, axis=-1), jax.nn.softmax(c_scores, axis=-1)
    p_low, c_low = p_probs.astype(BF16), c_probs.astype(BF16)
    cont_keys = jnp.concatenate((extra_keys, cont_k), axis=1)
    cont_values = jnp.concatenate((extra_values, cont_v), axis=1)
    p_mixed = jnp.einsum("pts,psh->pth", p_low, own_values[:, 0], preferred_element_type=F32)
    c_mixed = jnp.einsum("pts,psh->pth", c_low, cont_values, preferred_element_type=F32)
    mixed = jnp.stack((p_mixed, c_mixed), axis=1).reshape(own_rows, -1)
    gated = (reset_gate * mixed).astype(BF16)
    own_tokens = tokens[:own_rows]
    middle = own_tokens + dot(gated, mat_hidden, (1, 0))
    plain_mid, inv_mid = norm_rows(middle)
    mid_low = (plain_mid * gain_two).astype(BF16)
    inner_pre = dot(mid_low, mat_inner, (1, 0))
    inner_low = jax.nn.silu(inner_pre).astype(BF16)
    result = (middle + dot(inner_low, mat_outer, (1, 0))).astype(BF16)
    grad_outer = cotangent[0].reshape(own_rows, width)
    grad_top = grad_outer.astype(F32)
    sum_outer = dot(inner_low, grad_outer, (0, 0))
    grad_inner_pre = (dot(grad_outer, mat_outer, (1, 1)) * silu_grad(inner_pre)).astype(BF16)
    sum_inner = dot(mid_low, grad_inner_pre, (0, 0))
    grad_mid = dot(grad_inner_pre, mat_inner, (1, 1))
    sum_gain_two = jnp.sum(grad_mid * plain_mid, axis=0)
    grad_middle = grad_top + norm_back(grad_mid, plain_mid, inv_mid, gain_two)
    grad_branch = grad_middle.astype(BF16)
    sum_hidden = dot(gated, grad_branch, (0, 0))
    grad_gated = dot(grad_branch, mat_hidden, (1, 1))
    grad_mixed = (grad_gated * reset_gate).astype(BF16)
    grad_reset_pre = (grad_gated * mixed * silu_grad(reset_pre)).astype(BF16)
    sum_reset = dot(activ, grad_reset_pre, (0, 0))
    grad_act = dot(grad_reset_pre, mat_reset, (1, 1))
    grad_mixed = grad_mixed.reshape(sets, 2, length, -1)

    def score_grads(probs, grads, vals):
        back = jnp.einsum("pth,psh->pts", grads, vals, preferred_element_type=F32)
        return (probs * (back - jnp.sum(back * probs, axis=-1, keepdims=True))).astype(BF16)

    p_ds = score_grads(p_probs, grad_mixed[:, 0], own_values[:, 0])
    c_ds = score_grads(c_probs, grad_mixed[:, 1], cont_values)

    def pair(spec, p_args, c_args):
        return (
            jnp.einsum(spec, *p_args, preferred_element_type=F32),
            jnp.einsum(spec, *c_args, preferred_element_type=F32),
        )

    p_dq, c_dq = pair("pts,psz->ptz", (p_ds, keys[:, 0]), (c_ds, cont_keys))
    p_dk, c_dk = pair("pts,ptz->psz", (p_ds, queries[:, 0]), (c_ds, cont_q))
    p_dv, c_dv = pair("pts,pth->psh", (p_low, grad_mixed[:, 0]), (c_low, grad_mixed[:, 1]))
    sent_keys = jnp.einsum("pm,ptz->mtz", select, c_dk[:, :length], precision=lax.Precision.HIGHEST) / score_scale
    sent_values = jnp.einsum("pm,pth->mth", select, c_dv[:, :length], precision=lax.Precision.HIGHEST)
    tail_keys = keys_call(n, groups, sent_keys.astype(BF16).reshape(2, 2, sets * length // 4, 128))
    tail_keys = tail_keys.reshape(sets, length, 128).astype(F32)
    grad_queries = jnp.stack((p_dq, c_dq), axis=1).reshape(own_rows, 128) / score_scale
    grad_keys = jnp.stack((p_dk / score_scale + tail_keys, c_dk[:, length:] / score_scale), axis=1).reshape(own_rows, 128)
    own_dv = jnp.stack((p_dv, c_dv[:, length:]), axis=1).reshape(own_rows, -1)
    sum_query_mul = jnp.sum(grad_queries * shared, axis=0)
    sum_query_add = jnp.sum(grad_queries, axis=0)
    sum_key_mul = jnp.sum(grad_keys * shared, axis=0)
    grad_shared_pre = ((grad_queries * query_mul + grad_keys * key_mul) * silu_grad(shared_pre)).astype(BF16)
    sum_shared = dot(activ, grad_shared_pre, (0, 0))
    grad_act = grad_act + dot(grad_shared_pre, mat_shared, (1, 1))
    grad_ema = grad_act * silu_grad(ema_all[:own_rows])
    g_lanes = lanes_first(grad_ema)
    back_inner, back_flow = local_pass_call(6, True, g_lanes, dec)
    back_start = backward_exchange_call(n, groups, back_flow.reshape(3, 2, 64, 128), far, sel)
    dx_lanes, acc_in, acc_decay, acc_out = back_pass_call(
        6, 9, x_lanes, g_lanes, dec, mix, omega_lanes, power, inner, starts, power_rev, back_inner,
        back_start.reshape(6 * 64, 128),
    )
    all_dv = jnp.concatenate((own_dv, sent_values.reshape(sets * length, -1)), axis=0)
    grad_value_pre = (all_dv * silu_grad(value_pre)).astype(BF16)
    sum_value = dot(units_low, grad_value_pre, (0, 0))
    grad_units = dot(grad_value_pre, mat_value, (1, 1))
    grad_units = jnp.concatenate((grad_units[:own_rows] + rows_first(dx_lanes), grad_units[own_rows:]), axis=0)
    sum_gain_one = jnp.sum(grad_units * plain_in, axis=0)
    grad_in = norm_back(grad_units, plain_in, inv_in, gain_one)
    m_sum, q_sum = eta * acc_in, eta * ab * acc_decay
    sum_alpha = beta * m_sum - delta * q_sum
    sum_delta = -alpha * q_sum
    sum_beta = alpha * m_sum
    sum_eta = ab * acc_out
    sum_omega = jnp.sum(grad_ema * normed[:own_rows], axis=0)

    def by_channel(part):
        return part.reshape(4, 16, 128).transpose(1, 0, 2).reshape(16, 512)

    top = jnp.concatenate(
        [by_channel(part) for part in (sum_alpha, sum_delta, sum_beta, sum_eta)]
        + [sum_omega[None], sum_gain_one[None], sum_gain_two[None], jnp.zeros((61, width), F32)],
        axis=0,
    ).T.reshape(n, chan, 128)
    triple = jnp.stack((sum_query_mul, sum_query_add, sum_key_mul), axis=1).reshape(n, heads, 3)
    top = top + jnp.pad(triple, ((0, 0), (0, chan - heads), (67, 58)))
    small_grad = jnp.concatenate((top, sum_shared.reshape(n, chan, 128)), axis=1)
    small_grad = jnp.concatenate((small_grad, jnp.zeros_like(small_grad)), axis=2)

    def shards(grad):
        return grad.astype(BF16).reshape(nq, 2, 2, -1, grad.shape[-1])

    grads = [shards(part) for part in (sum_outer, sum_inner, sum_hidden, sum_reset, sum_value)]
    grads.append(small_grad.astype(BF16).reshape(nq, 2, 2, 2 * chan, 256))
    tail_grad = grad_in[own_rows:].astype(BF16).reshape(2, 2, sets * length // 4, width)
    *sums, tail_sum = sums_call(n, groups, grads, tail_grad)
    d_outer, d_inner, d_hidden, d_reset, d_value, d_small = [part.astype(F32) for part in sums]
    add_tail = tail_sum.reshape(sets, length, width).astype(F32)
    input_grad = (grad_middle + grad_in[:own_rows]).reshape(sets, 2, length, width)
    input_grad = jnp.stack((input_grad[:, 0] + add_tail, input_grad[:, 1]), axis=1).astype(BF16)
    return (
        result.reshape(hidden_in.shape), input_grad[None], d_value, d_small[chan:, :128], d_reset, d_hidden, d_inner, d_outer,
        d_small[:chan, 0:16], d_small[:chan, 16:32], d_small[:chan, 32:48], d_small[:chan, 48:64],
        d_small[:chan, 64], d_small[:chan, 65], d_small[:chan, 66],
        d_small[:heads, 67], d_small[:heads, 68], d_small[:heads, 69],
    )


def solution(mesh):
    mat, vec = P("seq", None), P("seq")
    tok = P("grp", None, None, "seq", None)
    in_specs = (tok, tok, P("grp", None)) + (mat,) * 10 + (vec,) * 6
    out_specs = (tok, tok) + (mat,) * 10 + (vec,) * 6
    return jax.shard_map(local, mesh=mesh, in_specs=in_specs, out_specs=out_specs, check_vma=False)
```

```python
import functools
import math

import jax
import jax.numpy as jnp
from jax import lax
from jax.experimental import pallas as pl
from jax.experimental.pallas import tpu as pltpu
from jax.sharding import PartitionSpec as P

CLEN = 512
NORM_EPS = 1e-05
MASKED_SCORE = -1e30
MESH = pl.DeviceIdType.MESH
SUB = 16
NJ = 16
TINY = 1e-20
F32 = jnp.float32
BF16 = jnp.bfloat16
VMEM = pl.BlockSpec(memory_space=pltpu.VMEM)
ANY = pl.BlockSpec(memory_space=pl.ANY)
SMEM = pl.BlockSpec(memory_space=pltpu.SMEM)


def shift_down(value, count):
    rows = lax.broadcasted_iota(jnp.int32, value.shape, 0)
    return jnp.where(rows >= count, pltpu.roll(value, count, 0), 0.0)


def shift_up(value, count):
    rows = lax.broadcasted_iota(jnp.int32, value.shape, 0)
    return jnp.where(rows < 8 - count, pltpu.roll(value, 8 - count, 0), 0.0)


def row_of(ref, row):
    return jnp.broadcast_to(ref[pl.ds(row, 1), :], (8, 128))


def ema_local_pass(rows, x_ref, decay, decay16, decay32, decay64, inner_ref, final_ref, backward):
    shift = shift_up if backward else shift_down

    def body(item, carry):
        row, lane = item // 4, item % 4
        base = lane * (rows * 128) + row * 128
        dec = [row_of(decay, lane * 16 + j) for j in range(NJ)]
        state = [jnp.zeros((8, 128), F32)] * NJ
        for step in range(SUB - 1, -1, -1) if backward else range(SUB):
            x = x_ref[pl.ds(base + step, 8, stride=SUB), :]
            if backward:
                state = [dec[j] * (state[j] + x) for j in range(NJ)]
            else:
                state = [dec[j] * state[j] + x for j in range(NJ)]
        for j in range(NJ):
            total = state[j]
            total = total + row_of(decay16, lane * 16 + j) * shift(total, 1)
            total = total + row_of(decay32, lane * 16 + j) * shift(total, 2)
            total = total + row_of(decay64, lane * 16 + j) * shift(total, 4)
            inner_ref[pl.ds((item * 16 + j) * 8, 8), :] = shift(total, 1)
            final_ref[pl.ds(row * 64 + lane * 16 + j, 1), :] = total[0:1] if backward else total[7:8]
        return carry

    lax.fori_loop(0, rows * 4, body, 0)


def ema_apply_pass(rows, x_ref, decay, mix, omega, power, inner_ref, start_ref, y_ref):
    def body(item, carry):
        row, lane = item // 4, item % 4
        base = lane * (rows * 128) + row * 128
        state = [
            inner_ref[pl.ds((item * 16 + j) * 8, 8), :]
            + power[pl.ds((lane * 16 + j) * 8, 8), :] * row_of(start_ref, row * 64 + lane * 16 + j)
            for j in range(NJ)
        ]
        skip = row_of(omega, lane)
        for step in range(SUB):
            x = x_ref[pl.ds(base + step, 8, stride=SUB), :]
            sums = [skip * x, None]
            for j in range(NJ):
                state[j] = row_of(decay, lane * 16 + j) * state[j] + x
                term = row_of(mix, lane * 16 + j) * state[j]
                sums[j % 2] = term if sums[j % 2] is None else sums[j % 2] + term
            y_ref[pl.ds(base + step, 8, stride=SUB), :] = sums[0] + sums[1]
        return carry

    lax.fori_loop(0, rows * 4, body, 0)


def ema_back_pass(
    rows, x_rows, x_ref, g_ref, decay, mix, omega, power, inner_ref, start_ref, power_rev,
    back_inner_ref, back_start_ref, dx_ref, sum_in, sum_decay, sum_out, kept,
):
    half = 8

    def body(item, carry):
        row, lane = item // 4, item % 4
        base = lane * (rows * 128) + row * 128
        x_base = lane * (x_rows * 128) + row * 128
        skip = row_of(omega, lane)
        for part in range(NJ // half):
            js = range(part * half, part * half + half)
            dec = [row_of(decay, lane * 16 + j) for j in js]
            state = [
                inner_ref[pl.ds((item * 16 + j) * 8, 8), :]
                + power[pl.ds((lane * 16 + j) * 8, 8), :] * row_of(start_ref, row * 64 + lane * 16 + j)
                for j in js
            ]
            for step in range(SUB):
                x = x_ref[pl.ds(x_base + step, 8, stride=SUB), :]
                for i in range(half):
                    kept[step * half + i] = state[i]
                    state[i] = dec[i] * state[i] + x
            adj = [
                back_inner_ref[pl.ds((item * 16 + j) * 8, 8), :]
                + power_rev[pl.ds((lane * 16 + j) * 8, 8), :]
                * row_of(back_start_ref, row * 64 + lane * 16 + j)
                for j in js
            ]
            weight = [row_of(mix, lane * 16 + j) for j in js]
            edge = [-(adj[i] * state[i]) for i in range(half)]
            first, second = [None] * half, [None] * half
            for step in range(SUB - 1, -1, -1):
                x = x_ref[pl.ds(x_base + step, 8, stride=SUB), :]
                g = g_ref[pl.ds(base + step, 8, stride=SUB), :]
                sums = [skip * g if part == 0 else dx_ref[pl.ds(base + step, 8, stride=SUB), :], None]
                for i in range(half):
                    full = adj[i] + g
                    term = weight[i] * full
                    sums[i % 2] = term if sums[i % 2] is None else sums[i % 2] + term
                    with_x, with_s = full * x, full * kept[step * half + i]
                    first[i] = with_x if first[i] is None else first[i] + with_x
                    second[i] = with_s if second[i] is None else second[i] + with_s
                    adj[i] = dec[i] * full
                dx_ref[pl.ds(base + step, 8, stride=SUB), :] = sums[0] + sums[1]
            for i, j in enumerate(js):
                at = pl.ds(lane * 16 + j, 1)
                flow = edge[i] + adj[i] * kept[i]
                total = jnp.sum(first[i], axis=0, keepdims=True)
                sum_in[at, :] += total
                sum_decay[at, :] += jnp.sum(second[i], axis=0, keepdims=True)
                sum_out[at, :] += total + jnp.sum(flow, axis=0, keepdims=True)
        return carry

    lax.fori_loop(0, rows * 4, body, 0)


class Place:
    def __init__(self, n, groups):
        self.n, self.nq, self.groups = n, n // 4, groups
        self.g, self.s = lax.axis_index("grp"), lax.axis_index("seq")
        self.c, self.y, self.q, self.x = self.s % 2, (self.s // 2) % 2, self.s // 4, self.g % 2
        self.pos = self.s % 4
        self.core = (self.g, self.s + 1 - 2 * self.c)
        self.side = (self.g, self.s + 2 - 4 * self.y)
        self.cross = (self.g + 1 - 2 * self.x, self.s)
        self.is_last = self.s == n - 1

    def quad(self, k):
        return (self.q + k) % self.nq

    def at_quad(self, q):
        return (self.g, q * 4 + self.pos)

    def group_peers(self):
        return [(self.g, (self.s + k) % self.n) for k in range(1, self.n)]

    def cross_bit(self, bit):
        return (self.g + bit - 2 * bit * ((self.g // bit) % 2), self.s)

    def cross_bits(self):
        return [1 << b for b in range(self.groups.bit_length() - 1)]


def meet(peers):
    barrier = pltpu.get_barrier_semaphore()
    for peer in peers:
        pl.semaphore_signal(barrier, inc=1, device_id=peer, device_id_type=MESH)
    pl.semaphore_wait(barrier, len(peers))


def remote(src, dst, send, recv, device):
    return pltpu.make_async_remote_copy(
        src_ref=src, dst_ref=dst, send_sem=send, recv_sem=recv, device_id=device, device_id_type=MESH
    )


def gather_kernel(n, groups, s_in, a_in, b_in, x_in, s_out, a_out, b_out, x_out, ss, sr, zs, zr, ys, yr, xs, xr, cs, cr, ts, tr, ls):
    me = Place(n, groups)
    nq = me.nq
    meet(me.group_peers() + [me.cross])
    mats = ((a_in, a_out, a_in.shape[-1] // 2), (b_in, b_out, b_in.shape[-1] // 2))
    sent = []

    def send(*args):
        copy = remote(*args)
        copy.start()
        sent.append(copy)

    def got(ref, recv):
        remote(ref, ref, ls.at[0], recv, me.core).wait_recv()

    own = [pltpu.make_async_copy(s_in, s_out.at[me.s], ls.at[0])]
    own += [pltpu.make_async_copy(w_in, w_out.at[me.s], ls.at[1 + i]) for i, (w_in, w_out, _) in enumerate(mats)]
    for copy in own:
        copy.start()
    for k in range(1, n):
        send(s_in, s_out.at[me.s], ss.at[k - 1], sr.at[k - 1], (me.g, (me.s + k) % n))

    @pl.when(me.is_last)
    def _():
        for j in range(3):
            remote(x_in.at[j], x_out.at[j], ts.at[j], tr.at[0], (me.g, 4 * (nq - 1) + j)).start()
        pltpu.make_async_copy(x_in.at[3], x_out.at[3], ls.at[3]).start()

    def half(ref, width, which):
        return ref.at[:, pl.ds(pl.multiple_of(which * width, 128), width)]

    for k in range(1, nq):
        for i, (w_in, w_out, width) in enumerate(mats):
            send(half(w_in, width, me.x), half(w_out.at[me.s], width, me.x), zs.at[k - 1, i], zr.at[k - 1, i], me.at_quad(me.quad(k)))
    for i, (w_in, w_out, width) in enumerate(mats):
        send(w_in, w_out.at[me.s], ys.at[0, i], yr.at[0, i], me.side)
        send(w_in, w_out.at[me.s], cs.at[0, i], cr.at[0, i], me.core)

    @pl.when(me.q == nq - 1)
    def _():
        @pl.when(me.is_last)
        def _():
            pltpu.make_async_copy(x_in.at[3], x_out.at[3], ls.at[3]).wait()

        @pl.when(jnp.logical_not(me.is_last))
        def _():
            got(x_out.at[me.pos], tr.at[0])

        for k in range(1, nq):
            remote(x_out.at[me.pos], x_out.at[me.pos], ts.at[2 + k], tr.at[1], me.at_quad(me.quad(k))).start()

    other = 1 - me.x
    for k in range(1, nq):
        shard = me.quad(nq - k) * 4 + me.pos
        for i, (w_in, w_out, width) in enumerate(mats):
            piece = half(w_out.at[shard], width, me.x)
            got(piece, zr.at[k - 1, i])
            send(piece, piece, ys.at[k, i], yr.at[k, i], me.side)
            send(piece, piece, xs.at[k - 1, i], xr.at[k - 1, i], me.cross)
            send(piece, piece, cs.at[k, i], cr.at[k, i], me.core)

    @pl.when(me.q != nq - 1)
    def _():
        got(x_out.at[me.pos], tr.at[1])

    mine = x_out.at[me.pos]
    send(mine, mine, ts.at[nq + 2], tr.at[2], me.side)
    send(mine, mine, ts.at[nq + 3], tr.at[3], me.core)

    side_pos = me.pos + 2 - 4 * me.y
    for k in range(nq):
        shard = me.quad(nq - k) * 4 + side_pos
        for i, (w_in, w_out, width) in enumerate(mats):
            piece = w_out.at[shard] if k == 0 else half(w_out.at[shard], width, me.x)
            got(piece, yr.at[k, i])
            if k:
                send(piece, piece, xs.at[nq - 2 + k, i], xr.at[nq - 2 + k, i], me.cross)
            send(piece, piece, cs.at[nq + k, i], cr.at[nq + k, i], me.core)
    theirs = x_out.at[side_pos]
    got(theirs, tr.at[2])
    send(theirs, theirs, ts.at[nq + 4], tr.at[4], me.core)
    for group, pos in ((0, me.pos), (1, side_pos)):
        for k in range(1, nq):
            shard = me.quad(nq - k) * 4 + pos
            at = group * (nq - 1) + k - 1
            for i, (w_in, w_out, width) in enumerate(mats):
                piece = half(w_out.at[shard], width, other)
                got(piece, xr.at[at, i])
                send(piece, piece, cs.at[2 * nq + at, i], cr.at[2 * nq + at, i], me.core)
    flip = 1 - 2 * me.c
    for group, pos in ((0, me.pos + flip), (1, side_pos + flip)):
        for k in range(nq):
            shard = me.quad(nq - k) * 4 + pos
            for i, (w_in, w_out, width) in enumerate(mats):
                if k == 0:
                    got(w_out.at[shard], cr.at[group * nq, i])
                else:
                    got(half(w_out.at[shard], width, me.x), cr.at[group * nq + k, i])
                    at = 2 * nq + group * (nq - 1) + k - 1
                    got(half(w_out.at[shard], width, other), cr.at[at, i])
    got(x_out.at[me.pos + flip], tr.at[3])
    got(x_out.at[side_pos + flip], tr.at[4])
    for k in range(1, n):
        got(s_out.at[(me.s + n - k) % n], sr.at[k - 1])
    for copy in own:
        copy.wait()
    for copy in sent:
        copy.wait_send()

    @pl.when(me.is_last)
    def _():
        for j in range(3):
            remote(x_in.at[j], x_out.at[j], ts.at[j], tr.at[0], (me.g, 4 * (nq - 1) + j)).wait_send()

    @pl.when(me.q == nq - 1)
    def _():
        for k in range(1, nq):
            remote(x_out.at[me.pos], x_out.at[me.pos], ts.at[2 + k], tr.at[1], me.at_quad(me.quad(k))).wait_send()


def gather_call(n, groups, small, mat_a, mat_b, tail):
    nq = n // 4
    sems = [(n - 1,), (n - 1,), (nq - 1, 2), (nq - 1, 2), (nq, 2), (nq, 2), (2 * nq - 2, 2), (2 * nq - 2, 2), (4 * nq - 2, 2), (4 * nq - 2, 2), (nq + 5,), (5,), (4,)]
    return pl.pallas_call(
        functools.partial(gather_kernel, n, groups),
        out_shape=[
            jax.ShapeDtypeStruct((n,) + small.shape, BF16),
            jax.ShapeDtypeStruct((n,) + mat_a.shape, BF16),
            jax.ShapeDtypeStruct((n,) + mat_b.shape, BF16),
            jax.ShapeDtypeStruct(tail.shape, BF16),
        ],
        in_specs=[ANY] * 4,
        out_specs=[ANY] * 4,
        scratch_shapes=[pltpu.SemaphoreType.DMA(shape) for shape in sems],
        compiler_params=pltpu.CompilerParams(collective_id=0, has_side_effects=True),
        name="gather_weights",
    )(small, mat_a, mat_b, tail)


def pick(index, values):
    out = values[0]
    for k in range(1, len(values)):
        out = jnp.where(index == k, values[k], out)
    return out


def forward_exchange(n, groups, f_ref, ab_ref, d_ref, sel_ref, s_ref, m0, r0, m1, r1, m2, r2, ss, rs, zs, zr, ps, pr):
    me = Place(n, groups)
    nq = me.nq
    meet(me.group_peers())
    one, two, three, four = d_ref[0], d_ref[1], d_ref[2], d_ref[3]
    m0[...] = f_ref[0:3].astype(BF16)
    copy = remote(m0, r0, ss.at[0], rs.at[0], me.core)
    copy.start()
    copy.wait()
    upper_core, upper_side = me.c == 1, me.y == 1
    mine = f_ref[0:3]
    other = r0[...].astype(F32)
    lower = jnp.where(upper_core, other, mine)
    upper = jnp.where(upper_core, mine, other)
    pair = one * lower + upper
    before = jnp.where(upper_core, other, 0.0)
    m1[0] = pair.astype(BF16)
    m1[1, :, 0] = lower[:, 0].astype(BF16)
    copy = remote(m1, r1, ss.at[1], rs.at[1], me.side)
    m1[1, :, 1] = jnp.zeros_like(m1[1, :, 1])
    copy.start()
    copy.wait()
    far = r1[0].astype(F32)
    low_pair = jnp.where(upper_side, far, pair)
    high_pair = jnp.where(upper_side, pair, far)
    total = two * low_pair + high_pair
    before = jnp.where(upper_side, jnp.where(upper_core, one * far, far), 0.0) + before
    third = jnp.where(upper_side, lower[:, 0], r1[1, :, 0].astype(F32))
    last_in = one * low_pair[:, 0] + third
    m2[0] = total[:, 0].astype(BF16)
    m2[1] = last_in.astype(BF16)
    sends = []
    for k in range(1, nq):
        copy = remote(m2.at[0], r2.at[me.q], zs.at[k - 1], zr.at[k - 1], me.at_quad(me.quad(k)))
        copy.start()
        sends.append(copy)

    @pl.when(me.q == nq - 1)
    def _():
        for k in range(1, nq):
            remote(m2.at[1], r2.at[nq], ps.at[k - 1], pr.at[0], me.at_quad(me.quad(k))).start()
        r2[nq] = m2[1]

    r2[me.q] = m2[0]
    for k in range(1, nq):
        src = r2.at[me.quad(nq - k)]
        remote(src, src, zs.at[k - 1], zr.at[k - 1], me.core).wait_recv()

    @pl.when(me.q != nq - 1)
    def _():
        remote(r2.at[nq], r2.at[nq], ps.at[0], pr.at[0], me.core).wait_recv()

    run = jnp.zeros((3, 64, 128), F32)
    carry, tail_in = run, run
    for k in range(nq):
        carry = jnp.where(me.q == k, run, carry)
        if k == nq - 1:
            tail_in = three * run + r2[nq].astype(F32)
        run = four * run + r2[k].astype(F32)
    low = (ab_ref[...] * run).astype(BF16).astype(F32)
    safe = jnp.abs(ab_ref[...]) >= TINY
    begin = jnp.where(safe, low / jnp.where(safe, ab_ref[...], 1.0), run)
    lead = pick(me.pos, [jnp.ones_like(one), one, two, three])
    for p in range(3):
        start = sel_ref[p * 3] * begin[0] + sel_ref[p * 3 + 1] * begin[1] + sel_ref[p * 3 + 2] * begin[2]
        s_ref[2 * p] = lead * carry[p] + before[p, 0]
        s_ref[2 * p + 1] = lead * start + before[p, 1]
        s_ref[6 + p] = tail_in[p]
    for copy in sends:
        copy.wait_send()

    @pl.when(me.q == nq - 1)
    def _():
        for k in range(1, nq):
            remote(m2.at[1], r2.at[nq], ps.at[k - 1], pr.at[0], me.at_quad(me.quad(k))).wait_send()


def forward_exchange_call(n, groups, finals, ab, decays, sel):
    nq = n // 4
    dma = pltpu.SemaphoreType.DMA
    return pl.pallas_call(
        functools.partial(forward_exchange, n, groups),
        out_shape=jax.ShapeDtypeStruct((9, 64, 128), F32),
        in_specs=[VMEM, VMEM, VMEM, SMEM],
        out_specs=VMEM,
        scratch_shapes=[
            pltpu.VMEM((3, 2, 64, 128), BF16), pltpu.VMEM((3, 2, 64, 128), BF16),
            pltpu.VMEM((2, 3, 2, 64, 128), BF16), pltpu.VMEM((2, 3, 2, 64, 128), BF16),
            pltpu.VMEM((2, 3, 64, 128), BF16), pltpu.VMEM((nq + 1, 3, 64, 128), BF16),
            dma((2,)), dma((2,)), dma((nq - 1,)), dma((nq - 1,)), dma((nq - 1,)), dma((1,)),
        ],
        compiler_params=pltpu.CompilerParams(collective_id=1, has_side_effects=True, vmem_limit_bytes=40 << 20),
        name="forward_exchange",
    )(finals, ab, decays, sel)


def backward_exchange(n, groups, f_ref, d_ref, sel_ref, s_ref, m0, r0, m1, r1, m2, r2, ss, rs, zs, zr):
    me = Place(n, groups)
    nq = me.nq
    meet(me.group_peers())
    one, two, three, four = d_ref[0], d_ref[1], d_ref[2], d_ref[3]
    m0[...] = f_ref[...].astype(BF16)
    copy = remote(m0, r0, ss.at[0], rs.at[0], me.core)
    copy.start()
    copy.wait()
    upper_core, upper_side = me.c == 1, me.y == 1
    mine = f_ref[...]
    other = r0[...].astype(F32)
    lower = jnp.where(upper_core, other, mine)
    upper = jnp.where(upper_core, mine, other)
    pair = lower + one * upper
    after = jnp.where(upper_core, 0.0, other)
    m1[...] = pair.astype(BF16)
    copy = remote(m1, r1, ss.at[1], rs.at[1], me.side)
    copy.start()
    copy.wait()
    far = r1[...].astype(F32)
    low_pair = jnp.where(upper_side, far, pair)
    high_pair = jnp.where(upper_side, pair, far)
    total = low_pair + two * high_pair
    after = jnp.where(upper_side, 0.0, jnp.where(upper_core, far, one * far)) + after
    m2[0] = total[:, 0].astype(BF16)
    for m in range(3):
        m2[1, m] = (sel_ref[m] * total[0, 1] + sel_ref[3 + m] * total[1, 1] + sel_ref[6 + m] * total[2, 1]).astype(BF16)
    sends = []
    for k in range(1, nq):
        copy = remote(m2, r2.at[me.q], zs.at[k - 1], zr.at[k - 1], me.at_quad(me.quad(k)))
        copy.start()
        sends.append(copy)
    r2[me.q] = m2[...]
    for k in range(1, nq):
        src = r2.at[me.quad(nq - k)]
        remote(src, src, zs.at[k - 1], zr.at[k - 1], me.core).wait_recv()
    run = r2[0, 1].astype(F32)
    for k in range(1, nq):
        run = run + r2[k, 1].astype(F32)
    carry = run
    for k in range(nq - 1, -1, -1):
        carry = jnp.where(me.q == k, run, carry)
        run = four * run + r2[k, 0].astype(F32)
    lead = pick(me.pos, [three, two, one, jnp.ones_like(one)])
    for p in range(3):
        s_ref[2 * p] = lead * carry[p] + after[p, 0]
        s_ref[2 * p + 1] = after[p, 1]
    for copy in sends:
        copy.wait_send()


def backward_exchange_call(n, groups, flows, decays, sel):
    nq = n // 4
    dma = pltpu.SemaphoreType.DMA
    return pl.pallas_call(
        functools.partial(backward_exchange, n, groups),
        out_shape=jax.ShapeDtypeStruct((6, 64, 128), F32),
        in_specs=[VMEM, VMEM, SMEM],
        out_specs=VMEM,
        scratch_shapes=[
            pltpu.VMEM((3, 2, 64, 128), BF16), pltpu.VMEM((3, 2, 64, 128), BF16),
            pltpu.VMEM((3, 2, 64, 128), BF16), pltpu.VMEM((3, 2, 64, 128), BF16),
            pltpu.VMEM((2, 3, 64, 128), BF16), pltpu.VMEM((nq, 2, 3, 64, 128), BF16),
            dma((2,)), dma((2,)), dma((nq - 1,)), dma((nq - 1,)),
        ],
        compiler_params=pltpu.CompilerParams(collective_id=2, has_side_effects=True, vmem_limit_bytes=40 << 20),
        name="backward_exchange",
    )(flows, decays, sel)


def tail_flow(me, t, r1, w1, r2, w2, r3, out, send, recv):
    nq = me.nq
    last = me.q == nq - 1
    out[...] = jnp.zeros_like(out)
    copy1 = remote(t.at[:, 1 - me.c], r1, send.at[0], recv.at[0], me.core)
    copy1.start()
    yield
    copy1.wait()
    for i in range(2):
        w1[i] = (t[i, me.c].astype(F32) + r1[i].astype(F32)).astype(BF16)
    copy2 = remote(w1.at[1 - me.y], r2, send.at[1], recv.at[1], me.side)
    copy2.start()
    yield
    copy2.wait()
    w2[...] = (w1[me.y].astype(F32) + r2[...].astype(F32)).astype(BF16)
    top = (me.g, (nq - 1) * 4 + me.pos)
    end = (me.g, nq * 4 - 1)
    for k in range(nq - 1):
        @pl.when(me.q == k)
        def _():
            remote(w2, r3.at[k], send.at[2], recv.at[2 + k], top).start()
    yield

    @pl.when(last)
    def _():
        total = w2[...].astype(F32)
        for k in range(nq - 1):
            remote(r3.at[k], r3.at[k], send.at[2], recv.at[2 + k], me.core).wait_recv()
            total = total + r3[k].astype(F32)
        w2[...] = total.astype(BF16)

        @pl.when(jnp.logical_not(me.is_last))
        def _():
            for j in range(3):
                @pl.when(me.pos == j)
                def _():
                    remote(w2, out.at[j // 2, j % 2], send.at[2], recv.at[nq + 1 + j], end).start()

        @pl.when(me.is_last)
        def _():
            out[1, 1] = w2[...]
    yield

    @pl.when(me.is_last)
    def _():
        for j in range(3):
            dst = out.at[j // 2, j % 2]
            remote(dst, dst, send.at[2], recv.at[nq + 1 + j], me.core).wait_recv()

    @pl.when(jnp.logical_not(me.is_last))
    def _():
        remote(w2, w2, send.at[2], recv.at[2], me.core).wait_send()


def tail_scratch(nq, rows, width):
    return [
        pltpu.VMEM((2, rows, width), BF16), pltpu.VMEM((2, rows, width), BF16),
        pltpu.VMEM((rows, width), BF16), pltpu.VMEM((rows, width), BF16),
        pltpu.VMEM((nq - 1, rows, width), BF16),
    ]


def keys_kernel(n, groups, t, out, r1, w1, r2, w2, r3, send, recv):
    me = Place(n, groups)
    meet(me.group_peers())
    for _ in tail_flow(me, t, r1, w1, r2, w2, r3, out, send, recv):
        pass


def keys_call(n, groups, t):
    nq = n // 4
    dma = pltpu.SemaphoreType.DMA
    return pl.pallas_call(
        functools.partial(keys_kernel, n, groups),
        out_shape=jax.ShapeDtypeStruct(t.shape, BF16),
        in_specs=[VMEM],
        out_specs=VMEM,
        scratch_shapes=tail_scratch(nq, t.shape[2], t.shape[3]) + [dma((3,)), dma((nq + 4,))],
        compiler_params=pltpu.CompilerParams(collective_id=3, has_side_effects=True),
        name="tail_keys",
    )(t)


def sum_flow(me, cross_first, grads, r1, w1, r2, w2, r3, w3, r4, rx, out, send, recv):
    nq = me.nq
    rows, width = out.shape
    wide = width // 2
    ours = pl.ds(pl.multiple_of(me.x * wide, 128), wide)
    others = pl.ds(pl.multiple_of((1 - me.x) * wide, 128), wide)
    copy1 = remote(grads.at[:, :, 1 - me.c], r1, send.at[0], recv.at[0], me.core)
    copy1.start()
    yield
    copy1.wait()

    def add1(i, carry):
        w1[i // 2, i % 2] = (grads[i // 2, i % 2, me.c].astype(F32) + r1[i // 2, i % 2].astype(F32)).astype(BF16)
        return carry

    lax.fori_loop(0, 2 * nq, add1, 0)
    if cross_first:
        copy2 = remote(w1.at[:, :, :, others], r2, send.at[1], recv.at[1], me.cross)
    else:
        copy2 = remote(w1.at[:, 1 - me.y], r2, send.at[1], recv.at[1], me.side)
    copy2.start()
    yield
    copy2.wait()
    if cross_first:
        def add2(i, carry):
            w2[i // 2, i % 2] = (w1[i // 2, i % 2, :, ours].astype(F32) + r2[i // 2, i % 2].astype(F32)).astype(BF16)
            return carry

        lax.fori_loop(0, 2 * nq, add2, 0)
        copy3 = remote(w2.at[:, 1 - me.y], r3, send.at[2], recv.at[2], me.side)
    else:
        def add2(i, carry):
            w2[i] = (w1[i, me.y].astype(F32) + r2[i].astype(F32)).astype(BF16)
            return carry

        lax.fori_loop(0, nq, add2, 0)
        copy3 = remote(w2.at[:, :, others], r3, send.at[2], recv.at[2], me.cross)
    copy3.start()
    yield
    copy3.wait()

    def add3(i, carry):
        kept = w2[i, me.y] if cross_first else w2[i, :, ours]
        w3[i] = (kept.astype(F32) + r3[i].astype(F32)).astype(BF16)
        return carry

    lax.fori_loop(0, nq, add3, 0)
    copies = []
    for k in range(1, nq):
        copy = remote(w3.at[me.quad(k)], r4.at[k - 1], send.at[2 + k], recv.at[2 + k], me.at_quad(me.quad(k)))
        copy.start()
        copies.append(copy)
    yield
    total = w3[me.q].astype(F32)
    for k in range(1, nq):
        copies[k - 1].wait()
        total = total + r4[k - 1].astype(F32)
    out[:, ours] = total.astype(BF16)
    copy5 = remote(out.at[:, ours], out.at[:, ours], send.at[nq + 2], recv.at[nq + 2], me.cross)
    copy5.start()
    yield
    remote(out.at[:, others], out.at[:, others], send.at[nq + 2], recv.at[nq + 2], me.cross).wait_recv()
    copy5.wait_send()
    for at, bit in enumerate(me.cross_bits()[1:]):
        copy = remote(out, rx.at[at], send.at[nq + 3 + at], recv.at[nq + 3 + at], me.cross_bit(bit))
        copy.start()
        copy.wait()
        out[...] = (out[...].astype(F32) + rx[at].astype(F32)).astype(BF16)


def sum_scratch(nq, groups, cross_first, rows, width):
    extra = max(groups.bit_length() - 2, 1)
    half = width // 2
    full = [pltpu.VMEM((nq, 2, rows, width), BF16)] * 2
    if cross_first:
        mid = [pltpu.VMEM((nq, 2, rows, half), BF16)] * 2
    else:
        mid = [pltpu.VMEM((nq, rows, width), BF16)] * 2
    return full + mid + [
        pltpu.VMEM((nq, rows, half), BF16), pltpu.VMEM((nq, rows, half), BF16),
        pltpu.VMEM((nq - 1, rows, half), BF16), pltpu.VMEM((extra, rows, width), BF16),
    ]


def drive(flows):
    live, waiting = [], list(flows)
    while live or waiting:
        if waiting:
            live.append(waiting.pop(0))
        for flow in list(live):
            try:
                next(flow)
            except StopIteration:
                live.remove(flow)


def sums_kernel(n, groups, orders, *refs):
    me = Place(n, groups)
    count = len(orders)
    grads, t = refs[:count], refs[count]
    outs, t_out = refs[count + 1 : 2 * count + 1], refs[2 * count + 1]
    rest = list(refs[2 * count + 2 :])
    send, recv, tsend, trecv = rest[-4:]
    meet(me.group_peers() + [me.cross_bit(bit) for bit in me.cross_bits()])
    flows = []
    for i, order in enumerate(orders):
        scratch = rest[8 * i : 8 * i + 8]
        flows.append(sum_flow(me, order, grads[i], *scratch, outs[i], send.at[i], recv.at[i]))
    flows.append(tail_flow(me, t, *rest[8 * count : 8 * count + 5], t_out, tsend, trecv))
    drive(flows)


def sums_call(n, groups, grads, tail):
    nq = n // 4
    dma = pltpu.SemaphoreType.DMA
    orders = tuple(i % 2 == 0 for i in range(len(grads)))
    scratch = []
    for order, grad in zip(orders, grads):
        scratch += sum_scratch(nq, groups, order, grad.shape[-2], grad.shape[-1])
    scratch += tail_scratch(nq, tail.shape[2], tail.shape[3])
    sems = nq + 3 + max(groups.bit_length() - 2, 1)
    scratch += [dma((len(grads), sems)), dma((len(grads), sems)), dma((3,)), dma((nq + 4,))]
    return pl.pallas_call(
        functools.partial(sums_kernel, n, groups, orders),
        out_shape=[jax.ShapeDtypeStruct(grad.shape[-2:], BF16) for grad in grads] + [jax.ShapeDtypeStruct(tail.shape, BF16)],
        in_specs=[VMEM] * (len(grads) + 1),
        out_specs=[VMEM] * (len(grads) + 1),
        scratch_shapes=scratch,
        compiler_params=pltpu.CompilerParams(collective_id=4, has_side_effects=True, vmem_limit_bytes=56 << 20),
        name="sum_weights",
    )(*grads, tail)


def ema_call(kernel, name, outs, ins, scratch=()):
    return pl.pallas_call(
        kernel,
        out_shape=[jax.ShapeDtypeStruct(shape, F32) for shape in outs],
        in_specs=[VMEM] * len(ins),
        out_specs=[VMEM] * len(outs),
        scratch_shapes=scratch,
        compiler_params=pltpu.CompilerParams(vmem_limit_bytes=56 << 20),
        name=name,
    )(*ins)


def local_pass_call(rows, backward, x, dec):
    def kernel(x_ref, d_ref, inner_ref, final_ref):
        ema_local_pass(rows, x_ref, d_ref.at[0], d_ref.at[1], d_ref.at[2], d_ref.at[3], inner_ref, final_ref, backward)

    return ema_call(kernel, "ema_local", [(rows * 512, 128), (rows * 64, 128)], (x, dec))


def apply_pass_call(rows, x, dec, mix, omega, power, inner, start):
    def kernel(x_ref, d_ref, mix_ref, omega_ref, power_ref, inner_ref, start_ref, y_ref):
        ema_apply_pass(rows, x_ref, d_ref.at[0], mix_ref, omega_ref, power_ref, inner_ref, start_ref, y_ref)

    return ema_call(kernel, "ema_apply", [(rows * 512, 128)], (x, dec, mix, omega, power, inner, start))[0]


def back_pass_call(rows, x_rows, x, g, dec, mix, omega, power, inner, start, power_rev, back_inner, back_start):
    def kernel(x_ref, g_ref, d_ref, mix_ref, omega_ref, power_ref, inner_ref, start_ref, rev_ref, bi_ref, bs_ref, dx_ref, a_ref, b_ref, c_ref, kept):
        for ref in (a_ref, b_ref, c_ref):
            ref[...] = jnp.zeros_like(ref)
        ema_back_pass(
            rows, x_rows, x_ref, g_ref, d_ref.at[0], mix_ref, omega_ref, power_ref, inner_ref, start_ref,
            rev_ref, bi_ref, bs_ref, dx_ref, a_ref, b_ref, c_ref, kept,
        )

    return ema_call(
        kernel, "ema_back", [(rows * 512, 128), (64, 128), (64, 128), (64, 128)],
        (x, g, dec, mix, omega, power, inner, start, power_rev, back_inner, back_start),
        [pltpu.VMEM((128, 8, 128), F32)],
    )


def silu_grad(pre_act):
    sigmoid_val = jax.nn.sigmoid(pre_act)
    return sigmoid_val * (1.0 + pre_act * (1.0 - sigmoid_val))


def norm_rows(row_data):
    centered = row_data - jnp.mean(row_data, axis=-1, keepdims=True)
    scale_inv = lax.rsqrt(jnp.mean(centered * centered, axis=-1, keepdims=True) + NORM_EPS)
    return (centered * scale_inv, scale_inv)


def norm_back(grad_rows, plain, scale_inv, gain_vec):
    grad_norm = grad_rows * gain_vec
    inner_term = (
        grad_norm
        - jnp.mean(grad_norm, axis=-1, keepdims=True)
        - plain * jnp.mean(grad_norm * plain, axis=-1, keepdims=True)
    )
    return inner_term * scale_inv


def nt(lhs, rhs):
    return lax.dot_general(lhs, rhs, (((1,), (1,)), ((), ())), preferred_element_type=F32)


def tn(lhs, rhs):
    return lax.dot_general(lhs, rhs, (((0,), (0,)), ((), ())), preferred_element_type=F32)


def nn(lhs, rhs):
    return lax.dot_general(lhs, rhs, (((1,), (0,)), ((), ())), preferred_element_type=F32)


def silu_pair(pre):
    sig = jax.nn.sigmoid(pre)
    return pre * sig, sig * (1.0 + pre * (1.0 - sig))


CHUNK = 256


def dense_kernel(
    n, tok, tail, ema, cot, mats_a, mats_b, w_shared, vec_wide, vec_head, target,
    result, g_middle, g_act, g_base, slope_s, shared_out, g_units, o_outer, o_inner, o_hidden, o_reset, o_value,
    tail_keys, sum_wide, sum_head,
    w_value, w_reset, w_inner, w_hidden, w_outer, values, slope_v, t_values, t_slope, t_keys, t_dv, t_dk,
    k_units, k_activ, k_gated, k_mid, k_inner, k_branch, k_gin, k_greset, k_gvalue, reset_pre, mixed, slope_i, sem,
):
    sets = t_keys.shape[0]
    length = t_keys.shape[1]
    own = tok.shape[0]
    total = own + tail.shape[0]
    width = tok.shape[1]
    chan = w_value.shape[1]
    rows_b = w_hidden.shape[1]
    hv = w_value.shape[2]
    parts = hv // CHUNK
    scale = 1.0 / math.sqrt(128.0)
    copies = [
        pltpu.make_async_copy(mats_a.at[:, 0:chan], w_value, sem.at[0]),
        pltpu.make_async_copy(mats_a.at[:, chan : 2 * chan], w_reset, sem.at[1]),
        pltpu.make_async_copy(mats_b.at[:, 0:rows_b], w_hidden, sem.at[2]),
        pltpu.make_async_copy(mats_a.at[:, 2 * chan : 3 * chan], w_inner, sem.at[3]),
        pltpu.make_async_copy(mats_b.at[:, rows_b : 2 * rows_b], w_outer, sem.at[4]),
    ]
    for copy in copies:
        copy.start()
    gain_one, gain_two = vec_wide[0:1], vec_wide[1:2]
    q_mul, q_add, k_mul = vec_head[0:1], vec_head[1:2], vec_head[2:3]
    t_dv[...] = jnp.zeros_like(t_dv)
    t_dk[...] = jnp.zeros_like(t_dk)
    sum_wide[...] = jnp.zeros_like(sum_wide)
    sum_head[...] = jnp.zeros_like(sum_head)

    def columns(ref, at):
        block = ref[:, :, at * CHUNK : (at + 1) * CHUNK]
        return block.reshape(block.shape[0] * block.shape[1], CHUNK)

    def rows(ref, at):
        per = CHUNK // rows_b
        return ref[at * per : (at + 1) * per].reshape(CHUNK, ref.shape[2])

    def ema_rows(start, count):
        return jnp.concatenate([ema[pl.ds(lane * total + start, count), :] for lane in range(4)], axis=1)

    copies[0].wait()

    def tail_step(m, carry):
        at = pl.multiple_of(m * length, length)
        here = pl.ds(at, length)
        plain, _ = norm_rows(tail[here, :].astype(F32))
        units = (plain * gain_one).astype(BF16)
        k_units[pl.ds(own + at, length), :] = units
        for part in range(parts):
            value, slope = silu_pair(nn(units, columns(w_value, part)))
            t_values[m, :, part * CHUNK : (part + 1) * CHUNK] = value.astype(BF16)
            t_slope[m, :, part * CHUNK : (part + 1) * CHUNK] = slope.astype(BF16)
        pre = ema_rows(own + at, length)
        activ = (pre * jax.nn.sigmoid(pre)).astype(BF16)
        shared = nn(activ, w_shared[...])
        t_keys[m] = (shared * jax.nn.sigmoid(shared) * k_mul).astype(BF16)
        return carry

    lax.fori_loop(0, sets, tail_step, 0)
    for copy in copies[1:]:
        copy.wait()
    causal = lax.broadcasted_iota(jnp.int32, (length, length), 0) >= lax.broadcasted_iota(jnp.int32, (length, length), 1)

    def set_step(p, carry):
        here = pl.ds(pl.multiple_of(p * 2 * length, 2 * length), 2 * length)
        m = target[p]
        x = tok[here, :].astype(F32)
        plain, _ = norm_rows(x)
        units = (plain * gain_one).astype(BF16)
        k_units[here, :] = units
        for part in range(parts):
            cut = slice(part * CHUNK, (part + 1) * CHUNK)
            value, slope = silu_pair(nn(units, columns(w_value, part)))
            values[:, cut] = value.astype(BF16)
            slope_v[:, cut] = slope.astype(BF16)
        pre = ema_rows(p * 2 * length, 2 * length)
        activ = (pre * jax.nn.sigmoid(pre)).astype(BF16)
        k_activ[here, :] = activ
        shared, slope = silu_pair(nn(activ, w_shared[...]))
        slope_s[here, :] = slope
        shared_out[here, :] = shared
        queries = (shared * q_mul + q_add).astype(BF16)
        keys = (shared * k_mul).astype(BF16)
        for part in range(parts):
            reset_pre[:, part * CHUNK : (part + 1) * CHUNK] = nn(activ, columns(w_reset, part))
        p_q, c_q, p_k, c_k = queries[:length], queries[length:], keys[:length], keys[length:]
        e_k = t_keys[m]

        def weights(scores):
            expo = jnp.exp(scores - jnp.max(scores, axis=-1, keepdims=True))
            return expo * (1.0 / jnp.sum(expo, axis=-1, keepdims=True))

        p_probs = weights(jnp.where(causal, nt(p_q, p_k) * scale, MASKED_SCORE))
        c_probs = weights(
            jnp.concatenate((nt(c_q, e_k) * scale, jnp.where(causal, nt(c_q, c_k) * scale, MASKED_SCORE)), axis=1)
        )
        p_low, c_low = p_probs.astype(BF16), c_probs.astype(BF16)
        for part in range(parts):
            cut = slice(part * CHUNK, (part + 1) * CHUNK)
            mix_p = nn(p_low, values[:length, cut])
            mix_c = nn(c_low, jnp.concatenate((t_values[m, :, cut], values[length:, cut]), axis=0))
            mix = jnp.concatenate((mix_p, mix_c), axis=0)
            mixed[:, cut] = mix
            gate = reset_pre[:, cut]
            k_gated[here, cut] = (gate * jax.nn.sigmoid(gate) * mix).astype(BF16)
        middle = x + nn(k_gated[here, :], w_hidden[...].reshape(-1, width))
        plain_mid, inv_mid = norm_rows(middle)
        mid_low = (plain_mid * gain_two).astype(BF16)
        k_mid[here, :] = mid_low
        for part in range(parts):
            cut = slice(part * CHUNK, (part + 1) * CHUNK)
            inner, slope = silu_pair(nn(mid_low, columns(w_inner, part)))
            k_inner[here, cut] = inner.astype(BF16)
            slope_i[:, cut] = slope
        result[here, :] = (middle + nn(k_inner[here, :], w_outer[...].reshape(-1, width))).astype(BF16)
        top = cot[here, :]
        for part in range(parts):
            cut = slice(part * CHUNK, (part + 1) * CHUNK)
            k_gin[here, cut] = (nt(top, rows(w_outer, part)) * slope_i[:, cut]).astype(BF16)
        back = nt(k_gin[here, :], w_inner[...].reshape(width, -1))
        sum_wide[0:1] += jnp.sum(back * plain_mid, axis=0, keepdims=True)
        g_mid = top.astype(F32) + norm_back(back, plain_mid, inv_mid, gain_two)
        g_middle[here, :] = g_mid
        branch = g_mid.astype(BF16)
        k_branch[here, :] = branch
        dp_p = jnp.zeros((length, length), F32)
        dp_c = jnp.zeros((length, 2 * length), F32)
        for part in range(parts):
            cut = slice(part * CHUNK, (part + 1) * CHUNK)
            gated_back = nt(branch, rows(w_hidden, part))
            gate, slope = silu_pair(reset_pre[:, cut])
            g_mix = (gated_back * gate).astype(BF16)
            k_greset[here, cut] = (gated_back * mixed[:, cut] * slope).astype(BF16)
            dp_p += nt(g_mix[:length], values[:length, cut])
            dp_c += nt(g_mix[length:], jnp.concatenate((t_values[m, :, cut], values[length:, cut]), axis=0))
            dv_p = tn(p_low, g_mix[:length])
            dv_c = tn(c_low, g_mix[length:])
            t_dv[m, :, cut] += dv_c[:length]
            dv = jnp.concatenate((dv_p, dv_c[length:]), axis=0)
            k_gvalue[here, cut] = (dv * slope_v[:, cut].astype(F32)).astype(BF16)
        g_act[here, :] = nt(k_greset[here, :], w_reset[...].reshape(width, -1))

        def score_back(probs, grads):
            return (probs * (grads - jnp.sum(grads * probs, axis=-1, keepdims=True))).astype(BF16)

        p_ds, c_ds = score_back(p_probs, dp_p), score_back(c_probs, dp_c)
        d_q = jnp.concatenate((nn(p_ds, p_k), nn(c_ds, jnp.concatenate((e_k, c_k), axis=0))), axis=0) * scale
        dk_c = tn(c_ds, c_q) * scale
        t_dk[m] += dk_c[:length]
        d_k = jnp.concatenate((tn(p_ds, p_q) * scale, dk_c[length:]), axis=0)
        sum_head[0:1] += jnp.sum(d_q * shared, axis=0, keepdims=True)
        sum_head[1:2] += jnp.sum(d_q, axis=0, keepdims=True)
        sum_head[2:3] += jnp.sum(d_k * shared, axis=0, keepdims=True)
        g_base[here, :] = d_q * q_mul + d_k * k_mul
        return carry

    lax.fori_loop(0, sets, set_step, 0)
    tail_keys[...] = t_dk[...].astype(BF16)

    def tail_back(m, carry):
        at = pl.multiple_of(own + m * length, length)
        k_gvalue[pl.ds(at, length), :] = (t_dv[m] * t_slope[m].astype(F32)).astype(BF16)
        return carry

    lax.fori_loop(0, sets, tail_back, 0)

    def units_step(i, carry):
        here = pl.ds(pl.multiple_of(i * CHUNK, CHUNK), CHUNK)
        g_units[here, :] = nt(k_gvalue[here, :], w_value[...].reshape(width, -1))
        return carry

    lax.fori_loop(0, total // CHUNK, units_step, 0) if total % CHUNK == 0 else None
    if total % CHUNK:
        here = slice(total // CHUNK * CHUNK, total)
        lax.fori_loop(0, total // CHUNK, units_step, 0)
        g_units[here, :] = nt(k_gvalue[here, :], w_value[...].reshape(width, -1))

    def weight_grad(lhs, rhs, out, count):
        per = CHUNK // out.shape[1]

        def step(i, carry):
            block = tn(lhs[0:count, pl.ds(pl.multiple_of(i * CHUNK, CHUNK), CHUNK)], rhs[0:count, :])
            out[pl.ds(i * per, per)] = block.astype(BF16).reshape(per, out.shape[1], out.shape[2])
            return carry

        lax.fori_loop(0, lhs.shape[1] // CHUNK, step, 0)

    weight_grad(k_inner, cot, o_outer, own)
    weight_grad(k_mid, k_gin, o_inner, own)
    weight_grad(k_gated, k_branch, o_hidden, own)
    weight_grad(k_activ, k_greset, o_reset, own)
    weight_grad(k_units, k_gvalue, o_value, total)


def dense_call(n, tok, tail, ema, cot, mats_a, mats_b, w_shared, vec_wide, vec_head, target):
    own, width = tok.shape
    rows_t = tail.shape[0]
    total = own + rows_t
    sets = target.shape[0]
    length = rows_t // sets
    hv = mats_a.shape[2]
    chan = mats_a.shape[1] // 3
    rows_b = mats_b.shape[1] // 2
    shape = jax.ShapeDtypeStruct
    vm = pltpu.VMEM
    outs = [
        shape((own, width), BF16), shape((own, width), F32), shape((own, width), F32), shape((own, 128), F32),
        shape((own, 128), F32), shape((own, 128), F32), shape((total, width), F32),
        shape((n, rows_b, width), BF16), shape((n, chan, hv), BF16), shape((n, rows_b, width), BF16),
        shape((n, chan, hv), BF16), shape((n, chan, hv), BF16),
        shape((sets, length, 128), BF16), shape((8, width), F32), shape((8, 128), F32),
    ]
    scratch = [
        vm((n, chan, hv), BF16), vm((n, chan, hv), BF16), vm((n, chan, hv), BF16),
        vm((n, rows_b, width), BF16), vm((n, rows_b, width), BF16),
        vm((2 * length, hv), BF16), vm((2 * length, hv), BF16),
        vm((sets, length, hv), BF16), vm((sets, length, hv), BF16), vm((sets, length, 128), BF16),
        vm((sets, length, hv), F32), vm((sets, length, 128), F32),
        vm((total, width), BF16), vm((own, width), BF16), vm((own, hv), BF16), vm((own, width), BF16),
        vm((own, hv), BF16), vm((own, width), BF16), vm((own, hv), BF16), vm((own, hv), BF16), vm((total, hv), BF16),
        vm((2 * length, hv), F32), vm((2 * length, hv), F32), vm((2 * length, hv), F32),
        pltpu.SemaphoreType.DMA((5,)),
    ]
    return pl.pallas_call(
        functools.partial(dense_kernel, n),
        out_shape=outs,
        in_specs=[VMEM] * 4 + [ANY] * 2 + [VMEM] * 3 + [SMEM],
        out_specs=[VMEM] * len(outs),
        scratch_shapes=scratch,
        compiler_params=pltpu.CompilerParams(vmem_limit_bytes=60 << 20),
        name="dense",
    )(tok, tail, ema, cot, mats_a, mats_b, w_shared, vec_wide, vec_head, target)


def lanes_first(rows):
    return rows.reshape(-1, 4, 128).transpose(1, 0, 2).reshape(-1, 128)


def rows_first(lanes):
    return lanes.reshape(4, -1, 128).transpose(1, 0, 2).reshape(-1, 512)


def dot(lhs, rhs, dims):
    return lax.dot_general(lhs, rhs, ((dims[:1], dims[1:]), ((), ())), preferred_element_type=F32)


def local(
    hidden_in, cotangent, cont_prompt, value_proj, shared_proj, reset_proj, hidden_proj, inner_proj,
    outer_proj, ema_alpha, ema_delta, ema_beta, ema_eta, ema_omega, norm_gain, ffn_gain, query_scale,
    query_shift, key_scale,
):
    n, groups = lax.axis_size("seq"), lax.axis_size("grp")
    nq = n // 4
    seq_index = lax.axis_index("seq")
    sets, kinds, length, width = hidden_in.shape[1:]
    chan = width // n
    heads = query_scale.shape[0]
    tokens_low = hidden_in[0]
    vectors = jnp.stack((query_scale, query_shift, key_scale), axis=1)
    small = jnp.concatenate(
        (
            ema_alpha, ema_delta, ema_beta, ema_eta, ema_omega[:, None], norm_gain[:, None], ffn_gain[:, None],
            jnp.pad(vectors, ((0, chan - heads), (0, 0))), jnp.zeros((chan, 58), BF16),
        ),
        axis=1,
    )
    small = jnp.concatenate((small, shared_proj), axis=0)
    mat_a = jnp.concatenate((value_proj, reset_proj, inner_proj), axis=0)
    mat_b = jnp.concatenate((hidden_proj, outer_proj), axis=0)
    rows_b = hidden_proj.shape[0]
    all_small, all_a, all_b, tail_low = gather_call(
        n, groups, small, mat_a, mat_b, tokens_low[:, 0].reshape(4, sets * length // 4, width)
    )
    mat_shared = all_small[:, chan:].reshape(width, 128)
    flat = all_small[:, :chan].astype(F32)
    table = flat.reshape(width, 128).T
    vecs = flat[:, :heads, 67:70].reshape(-1, 3)
    query_mul, query_add, key_mul = vecs[:, 0], vecs[:, 1], vecs[:, 2]

    def by_lane(part):
        return part.reshape(16, 4, 128).transpose(1, 0, 2).reshape(64, 128)

    alpha, delta, beta, eta = (by_lane(table[16 * i : 16 * i + 16]) for i in range(4))
    omega, gain_one, gain_two = table[64], table[65], table[66]
    omega_lanes = omega.reshape(4, 128)
    decay = 1.0 - alpha * delta
    decay2 = decay * decay
    decay4 = decay2 * decay2
    decay8 = decay4 * decay4
    decay16 = decay8 * decay8
    decay32 = decay16 * decay16
    decay64 = decay32 * decay32
    decay128 = decay64 * decay64
    decay256 = decay128 * decay128
    dec = jnp.stack((decay, decay16, decay32, decay64))
    far = jnp.stack((decay128, decay256, decay256 * decay128, decay256 * decay256))
    steps = [jnp.ones_like(decay), decay16, decay32, decay32 * decay16, decay64, decay64 * decay16, decay64 * decay32, decay64 * decay32 * decay16]
    power = jnp.stack(steps, axis=1).reshape(512, 128)
    power_rev = jnp.stack(steps[::-1], axis=1).reshape(512, 128)
    ab = alpha * beta
    mix = ab * eta
    targets = lax.dynamic_slice_in_dim(
        cont_prompt[0].reshape(sets, nq), seq_index // 4, 1, 1
    )[:, 0]
    select = (targets[:, None] == jnp.arange(sets, dtype=jnp.int32)[None, :]).astype(F32)
    sel = select.reshape(-1)
    own_rows = sets * kinds * length
    rows_low = jnp.concatenate((tokens_low.reshape(own_rows, width), tail_low.reshape(-1, width)), axis=0)
    tokens = rows_low.astype(F32)
    plain_in, inv_in = norm_rows(tokens)
    normed = plain_in * gain_one
    x_lanes = lanes_first(normed)
    inner, finals = local_pass_call(9, False, x_lanes, dec)
    starts = forward_exchange_call(n, groups, finals[: 6 * 64].reshape(3, 2, 64, 128), ab, far, sel)
    starts = starts.reshape(9 * 64, 128)
    ema_lanes = apply_pass_call(9, x_lanes, dec, mix, omega_lanes, power, inner, starts)
    grad_outer = cotangent[0].reshape(own_rows, width)
    vec_wide = jnp.pad(jnp.stack((gain_one, gain_two)), ((0, 6), (0, 0)))
    vec_head = jnp.pad(jnp.stack((query_mul, query_add, key_mul)), ((0, 5), (0, 0)))
    (
        result, grad_middle, grad_act, grad_base, slope_shared, shared, grad_units, sum_outer, sum_inner, sum_hidden,
        sum_reset, sum_value, sent_keys, sum_wide, sum_head,
    ) = dense_call(
        n, rows_low[:own_rows], rows_low[own_rows:], ema_lanes, grad_outer, all_a, all_b, mat_shared, vec_wide, vec_head, targets
    )
    sum_gain_two = sum_wide[0]
    tail_keys = keys_call(n, groups, sent_keys.reshape(2, 2, sets * length // 4, 128))
    tail_keys = tail_keys.reshape(sets, length, 128).astype(F32)
    zeros = jnp.zeros_like(tail_keys)
    tail_rows = jnp.stack((tail_keys, zeros), axis=1).reshape(own_rows, 128)
    sum_query_mul, sum_query_add = sum_head[0], sum_head[1]
    sum_key_mul = sum_head[2] + jnp.sum(tail_rows * shared, axis=0)
    grad_shared_pre = ((grad_base + tail_rows * key_mul) * slope_shared).astype(BF16)
    ema_own = rows_first(ema_lanes.reshape(4, -1, 128)[:, :own_rows].reshape(-1, 128))
    activ = jax.nn.silu(ema_own).astype(BF16)
    sum_shared = dot(activ, grad_shared_pre, (0, 0))
    grad_act = grad_act + dot(grad_shared_pre, mat_shared, (1, 1))
    grad_ema = grad_act * silu_grad(ema_own)
    g_lanes = lanes_first(grad_ema)
    back_inner, back_flow = local_pass_call(6, True, g_lanes, dec)
    back_start = backward_exchange_call(n, groups, back_flow.reshape(3, 2, 64, 128), far, sel)
    dx_lanes, acc_in, acc_decay, acc_out = back_pass_call(
        6, 9, x_lanes, g_lanes, dec, mix, omega_lanes, power, inner, starts, power_rev, back_inner,
        back_start.reshape(6 * 64, 128),
    )
    grad_units = jnp.concatenate((grad_units[:own_rows] + rows_first(dx_lanes), grad_units[own_rows:]), axis=0)
    sum_gain_one = jnp.sum(grad_units * plain_in, axis=0)
    grad_in = norm_back(grad_units, plain_in, inv_in, gain_one)
    m_sum, q_sum = eta * acc_in, eta * ab * acc_decay
    sum_alpha = beta * m_sum - delta * q_sum
    sum_delta = -alpha * q_sum
    sum_beta = alpha * m_sum
    sum_eta = ab * acc_out
    sum_omega = jnp.sum(grad_ema * normed[:own_rows], axis=0)

    def by_channel(part):
        return part.reshape(4, 16, 128).transpose(1, 0, 2).reshape(16, 512)

    top = jnp.concatenate(
        [by_channel(part) for part in (sum_alpha, sum_delta, sum_beta, sum_eta)]
        + [sum_omega[None], sum_gain_one[None], sum_gain_two[None], jnp.zeros((61, width), F32)],
        axis=0,
    ).T.reshape(n, chan, 128)
    triple = jnp.stack((sum_query_mul, sum_query_add, sum_key_mul), axis=1).reshape(n, heads, 3)
    top = top + jnp.pad(triple, ((0, 0), (0, chan - heads), (67, 58)))
    small_grad = jnp.concatenate((top, sum_shared.reshape(n, chan, 128)), axis=1)
    small_grad = jnp.concatenate((small_grad, jnp.zeros_like(small_grad)), axis=2)

    def shards(grad):
        return grad.reshape(nq, 2, 2, -1, grad.shape[-1])

    grads = [shards(part) for part in (sum_outer, sum_inner, sum_hidden, sum_reset, sum_value)]
    grads.append(small_grad.astype(BF16).reshape(nq, 2, 2, 2 * chan, 256))
    tail_grad = grad_in[own_rows:].astype(BF16).reshape(2, 2, sets * length // 4, width)
    *sums, tail_sum = sums_call(n, groups, grads, tail_grad)
    d_outer, d_inner, d_hidden, d_reset, d_value, d_small = [part.astype(F32) for part in sums]
    add_tail = tail_sum.reshape(sets, length, width).astype(F32)
    input_grad = (grad_middle + grad_in[:own_rows]).reshape(sets, 2, length, width)
    input_grad = jnp.stack((input_grad[:, 0] + add_tail, input_grad[:, 1]), axis=1).astype(BF16)
    return (
        result.reshape(hidden_in.shape), input_grad[None], d_value, d_small[chan:, :128], d_reset, d_hidden, d_inner, d_outer,
        d_small[:chan, 0:16], d_small[:chan, 16:32], d_small[:chan, 32:48], d_small[:chan, 48:64],
        d_small[:chan, 64], d_small[:chan, 65], d_small[:chan, 66],
        d_small[:heads, 67], d_small[:heads, 68], d_small[:heads, 69],
    )


def solution(mesh):
    mat, vec = P("seq", None), P("seq")
    tok = P("grp", None, None, "seq", None)
    in_specs = (tok, tok, P("grp", None)) + (mat,) * 10 + (vec,) * 6
    out_specs = (tok, tok) + (mat,) * 10 + (vec,) * 6
    return jax.shard_map(local, mesh=mesh, in_specs=in_specs, out_specs=out_specs, check_vma=False)
```

```python
import functools
import math

import jax
import jax.numpy as jnp
from jax import lax
from jax.experimental import pallas as pl
from jax.experimental.pallas import tpu as pltpu
from jax.sharding import PartitionSpec as P

CLEN = 512
NORM_EPS = 1e-05
MASKED_SCORE = -1e30
MESH = pl.DeviceIdType.MESH
SUB = 16
NJ = 16
TINY = 1e-20
F32 = jnp.float32
BF16 = jnp.bfloat16
VMEM = pl.BlockSpec(memory_space=pltpu.VMEM)
ANY = pl.BlockSpec(memory_space=pl.ANY)
SMEM = pl.BlockSpec(memory_space=pltpu.SMEM)


def shift_down(value, count):
    rows = lax.broadcasted_iota(jnp.int32, value.shape, 0)
    return jnp.where(rows >= count, pltpu.roll(value, count, 0), 0.0)


def shift_up(value, count):
    rows = lax.broadcasted_iota(jnp.int32, value.shape, 0)
    return jnp.where(rows < 8 - count, pltpu.roll(value, 8 - count, 0), 0.0)


def row_of(ref, row):
    return jnp.broadcast_to(ref[pl.ds(row, 1), :], (8, 128))


def ema_local_pass(rows, pick_rows, x_ref, decay, decay16, decay32, decay64, inner_ref, final_ref, backward):
    shift = shift_up if backward else shift_down

    first, stride, many = pick_rows

    def body(turn, carry):
        row, lane = first + stride * (turn // 4), turn % 4
        item = row * 4 + lane
        base = lane * (rows * 128) + row * 128
        dec = [row_of(decay, lane * 16 + j) for j in range(NJ)]
        state = [jnp.zeros((8, 128), F32)] * NJ
        for step in range(SUB - 1, -1, -1) if backward else range(SUB):
            x = x_ref[pl.ds(base + step, 8, stride=SUB), :]
            if backward:
                state = [dec[j] * (state[j] + x) for j in range(NJ)]
            else:
                state = [dec[j] * state[j] + x for j in range(NJ)]
        for j in range(NJ):
            total = state[j]
            total = total + row_of(decay16, lane * 16 + j) * shift(total, 1)
            total = total + row_of(decay32, lane * 16 + j) * shift(total, 2)
            total = total + row_of(decay64, lane * 16 + j) * shift(total, 4)
            inner_ref[pl.ds((item * 16 + j) * 8, 8), :] = shift(total, 1)
            final_ref[pl.ds(row * 64 + lane * 16 + j, 1), :] = total[0:1] if backward else total[7:8]
        return carry

    lax.fori_loop(0, many * 4, body, 0)


def ema_apply_pass(rows, x_ref, decay, mix, omega, power, inner_ref, start_ref, y_ref):
    def body(item, carry):
        row, lane = item // 4, item % 4
        base = lane * (rows * 128) + row * 128
        state = [
            inner_ref[pl.ds((item * 16 + j) * 8, 8), :]
            + power[pl.ds((lane * 16 + j) * 8, 8), :] * row_of(start_ref, row * 64 + lane * 16 + j)
            for j in range(NJ)
        ]
        skip = row_of(omega, lane)
        for step in range(SUB):
            x = x_ref[pl.ds(base + step, 8, stride=SUB), :]
            sums = [skip * x, None]
            for j in range(NJ):
                state[j] = row_of(decay, lane * 16 + j) * state[j] + x
                term = row_of(mix, lane * 16 + j) * state[j]
                sums[j % 2] = term if sums[j % 2] is None else sums[j % 2] + term
            y_ref[pl.ds(base + step, 8, stride=SUB), :] = sums[0] + sums[1]
        return carry

    lax.fori_loop(0, rows * 4, body, 0)


def ema_back_pass(
    rows, x_rows, row, x_ref, g_ref, decay, mix, omega, power, inner_ref, start_ref, power_rev,
    back_inner_ref, back_start_ref, dx_ref, sum_in, sum_decay, sum_out, kept,
):
    half = 8

    def body(lane, carry):
        item = row * 4 + lane
        base = lane * (rows * 128) + row * 128
        x_base = lane * (x_rows * 128) + row * 128
        skip = row_of(omega, 4 + lane)
        for part in range(NJ // half):
            js = range(part * half, part * half + half)
            dec = [row_of(decay, lane * 16 + j) for j in js]
            state = [
                inner_ref[pl.ds((item * 16 + j) * 8, 8), :]
                + power[pl.ds((lane * 16 + j) * 8, 8), :] * row_of(start_ref, row * 64 + lane * 16 + j)
                for j in js
            ]
            for step in range(SUB):
                x = x_ref[pl.ds(x_base + step, 8, stride=SUB), :]
                for i in range(half):
                    kept[step * half + i] = state[i]
                    state[i] = dec[i] * state[i] + x
            adj = [
                back_inner_ref[pl.ds((item * 16 + j) * 8, 8), :]
                + power_rev[pl.ds((lane * 16 + j) * 8, 8), :]
                * row_of(back_start_ref, row * 64 + lane * 16 + j)
                for j in js
            ]
            weight = [row_of(mix, lane * 16 + j) for j in js]
            edge = [-(adj[i] * state[i]) for i in range(half)]
            first, second = [None] * half, [None] * half
            for step in range(SUB - 1, -1, -1):
                x = x_ref[pl.ds(x_base + step, 8, stride=SUB), :]
                g = g_ref[pl.ds(base + step, 8, stride=SUB), :]
                sums = [skip * g if part == 0 else dx_ref[pl.ds(base + step, 8, stride=SUB), :], None]
                for i in range(half):
                    full = adj[i] + g
                    term = weight[i] * full
                    sums[i % 2] = term if sums[i % 2] is None else sums[i % 2] + term
                    with_x, with_s = full * x, full * kept[step * half + i]
                    first[i] = with_x if first[i] is None else first[i] + with_x
                    second[i] = with_s if second[i] is None else second[i] + with_s
                    adj[i] = dec[i] * full
                dx_ref[pl.ds(base + step, 8, stride=SUB), :] = sums[0] + sums[1]
            for i, j in enumerate(js):
                at = pl.ds(lane * 16 + j, 1)
                flow = edge[i] + adj[i] * kept[i]
                total = jnp.sum(first[i], axis=0, keepdims=True)
                sum_in[at, :] += total
                sum_decay[at, :] += jnp.sum(second[i], axis=0, keepdims=True)
                sum_out[at, :] += total + jnp.sum(flow, axis=0, keepdims=True)
        return carry

    lax.fori_loop(0, 4, body, 0)


class Place:
    def __init__(self, n, groups):
        self.n, self.nq, self.groups = n, n // 4, groups
        self.g, self.s = lax.axis_index("grp"), lax.axis_index("seq")
        self.c, self.y, self.q, self.x = self.s % 2, (self.s // 2) % 2, self.s // 4, self.g % 2
        self.pos = self.s % 4
        self.core = (self.g, self.s + 1 - 2 * self.c)
        self.side = (self.g, self.s + 2 - 4 * self.y)
        self.cross = (self.g + 1 - 2 * self.x, self.s)
        self.is_last = self.s == n - 1

    def quad(self, k):
        return (self.q + k) % self.nq

    def at_quad(self, q):
        return (self.g, q * 4 + self.pos)

    def group_peers(self):
        return [(self.g, (self.s + k) % self.n) for k in range(1, self.n)]

    def cross_bit(self, bit):
        return (self.g + bit - 2 * bit * ((self.g // bit) % 2), self.s)

    def cross_bits(self):
        return [1 << b for b in range(self.groups.bit_length() - 1)]


def meet(peers):
    barrier = pltpu.get_barrier_semaphore()
    for peer in peers:
        pl.semaphore_signal(barrier, inc=1, device_id=peer, device_id_type=MESH)
    pl.semaphore_wait(barrier, len(peers))


def remote(src, dst, send, recv, device):
    return pltpu.make_async_remote_copy(
        src_ref=src, dst_ref=dst, send_sem=send, recv_sem=recv, device_id=device, device_id_type=MESH
    )


def gather_kernel(n, groups, s_in, a_in, b_in, x_in, s_out, a_out, b_out, x_out, ss, sr, zs, zr, ys, yr, xs, xr, cs, cr, ts, tr, ls):
    me = Place(n, groups)
    nq = me.nq
    meet(me.group_peers() + [me.cross])
    mats = ((a_in, a_out, a_in.shape[-1] // 2), (b_in, b_out, b_in.shape[-1] // 2))
    sent = []

    def send(*args):
        copy = remote(*args)
        copy.start()
        sent.append(copy)

    def got(ref, recv):
        remote(ref, ref, ls.at[0], recv, me.core).wait_recv()

    own = [pltpu.make_async_copy(s_in, s_out.at[me.s], ls.at[0])]
    own += [pltpu.make_async_copy(w_in, w_out.at[me.s], ls.at[1 + i]) for i, (w_in, w_out, _) in enumerate(mats)]
    for copy in own:
        copy.start()
    for k in range(1, n):
        send(s_in, s_out.at[me.s], ss.at[k - 1], sr.at[k - 1], (me.g, (me.s + k) % n))

    @pl.when(me.is_last)
    def _():
        for j in range(3):
            remote(x_in.at[j], x_out.at[j], ts.at[j], tr.at[0], (me.g, 4 * (nq - 1) + j)).start()
        pltpu.make_async_copy(x_in.at[3], x_out.at[3], ls.at[3]).start()

    def half(ref, width, which):
        return ref.at[:, pl.ds(pl.multiple_of(which * width, 128), width)]

    for k in range(1, nq):
        for i, (w_in, w_out, width) in enumerate(mats):
            send(half(w_in, width, me.x), half(w_out.at[me.s], width, me.x), zs.at[k - 1, i], zr.at[k - 1, i], me.at_quad(me.quad(k)))
    for i, (w_in, w_out, width) in enumerate(mats):
        send(w_in, w_out.at[me.s], ys.at[0, i], yr.at[0, i], me.side)
        send(w_in, w_out.at[me.s], cs.at[0, i], cr.at[0, i], me.core)

    @pl.when(me.q == nq - 1)
    def _():
        @pl.when(me.is_last)
        def _():
            pltpu.make_async_copy(x_in.at[3], x_out.at[3], ls.at[3]).wait()

        @pl.when(jnp.logical_not(me.is_last))
        def _():
            got(x_out.at[me.pos], tr.at[0])

        for k in range(1, nq):
            remote(x_out.at[me.pos], x_out.at[me.pos], ts.at[2 + k], tr.at[1], me.at_quad(me.quad(k))).start()

    other = 1 - me.x
    for k in range(1, nq):
        shard = me.quad(nq - k) * 4 + me.pos
        for i, (w_in, w_out, width) in enumerate(mats):
            piece = half(w_out.at[shard], width, me.x)
            got(piece, zr.at[k - 1, i])
            send(piece, piece, ys.at[k, i], yr.at[k, i], me.side)
            send(piece, piece, xs.at[k - 1, i], xr.at[k - 1, i], me.cross)
            send(piece, piece, cs.at[k, i], cr.at[k, i], me.core)

    @pl.when(me.q != nq - 1)
    def _():
        got(x_out.at[me.pos], tr.at[1])

    mine = x_out.at[me.pos]
    send(mine, mine, ts.at[nq + 2], tr.at[2], me.side)
    send(mine, mine, ts.at[nq + 3], tr.at[3], me.core)

    side_pos = me.pos + 2 - 4 * me.y
    for k in range(nq):
        shard = me.quad(nq - k) * 4 + side_pos
        for i, (w_in, w_out, width) in enumerate(mats):
            piece = w_out.at[shard] if k == 0 else half(w_out.at[shard], width, me.x)
            got(piece, yr.at[k, i])
            if k:
                send(piece, piece, xs.at[nq - 2 + k, i], xr.at[nq - 2 + k, i], me.cross)
            send(piece, piece, cs.at[nq + k, i], cr.at[nq + k, i], me.core)
    theirs = x_out.at[side_pos]
    got(theirs, tr.at[2])
    send(theirs, theirs, ts.at[nq + 4], tr.at[4], me.core)
    for group, pos in ((0, me.pos), (1, side_pos)):
        for k in range(1, nq):
            shard = me.quad(nq - k) * 4 + pos
            at = group * (nq - 1) + k - 1
            for i, (w_in, w_out, width) in enumerate(mats):
                piece = half(w_out.at[shard], width, other)
                got(piece, xr.at[at, i])
                send(piece, piece, cs.at[2 * nq + at, i], cr.at[2 * nq + at, i], me.core)
    flip = 1 - 2 * me.c
    for group, pos in ((0, me.pos + flip), (1, side_pos + flip)):
        for k in range(nq):
            shard = me.quad(nq - k) * 4 + pos
            for i, (w_in, w_out, width) in enumerate(mats):
                if k == 0:
                    got(w_out.at[shard], cr.at[group * nq, i])
                else:
                    got(half(w_out.at[shard], width, me.x), cr.at[group * nq + k, i])
                    at = 2 * nq + group * (nq - 1) + k - 1
                    got(half(w_out.at[shard], width, other), cr.at[at, i])
    got(x_out.at[me.pos + flip], tr.at[3])
    got(x_out.at[side_pos + flip], tr.at[4])
    for k in range(1, n):
        got(s_out.at[(me.s + n - k) % n], sr.at[k - 1])
    for copy in own:
        copy.wait()
    for copy in sent:
        copy.wait_send()

    @pl.when(me.is_last)
    def _():
        for j in range(3):
            remote(x_in.at[j], x_out.at[j], ts.at[j], tr.at[0], (me.g, 4 * (nq - 1) + j)).wait_send()

    @pl.when(me.q == nq - 1)
    def _():
        for k in range(1, nq):
            remote(x_out.at[me.pos], x_out.at[me.pos], ts.at[2 + k], tr.at[1], me.at_quad(me.quad(k))).wait_send()


def gather_call(n, groups, small, mat_a, mat_b, tail):
    nq = n // 4
    sems = [(n - 1,), (n - 1,), (nq - 1, 2), (nq - 1, 2), (nq, 2), (nq, 2), (2 * nq - 2, 2), (2 * nq - 2, 2), (4 * nq - 2, 2), (4 * nq - 2, 2), (nq + 5,), (5,), (4,)]
    return pl.pallas_call(
        functools.partial(gather_kernel, n, groups),
        out_shape=[
            jax.ShapeDtypeStruct((n,) + small.shape, BF16),
            jax.ShapeDtypeStruct((n,) + mat_a.shape, BF16),
            jax.ShapeDtypeStruct((n,) + mat_b.shape, BF16),
            jax.ShapeDtypeStruct(tail.shape, BF16),
        ],
        in_specs=[ANY] * 4,
        out_specs=[ANY] * 4,
        scratch_shapes=[pltpu.SemaphoreType.DMA(shape) for shape in sems],
        compiler_params=pltpu.CompilerParams(collective_id=0, has_side_effects=True),
        name="gather_weights",
    )(small, mat_a, mat_b, tail)


def pick(index, values):
    out = values[0]
    for k in range(1, len(values)):
        out = jnp.where(index == k, values[k], out)
    return out


def forward_exchange(n, groups, f_ref, ab_ref, d_ref, sel_ref, s_ref, m0, r0, m1, r1, m2, r2, ss, rs, zs, zr, ps, pr):
    me = Place(n, groups)
    nq = me.nq
    meet(me.group_peers())
    one, two, three, four = d_ref[0], d_ref[1], d_ref[2], d_ref[3]
    m0[...] = f_ref[0:3].astype(BF16)
    copy = remote(m0, r0, ss.at[0], rs.at[0], me.core)
    copy.start()
    copy.wait()
    upper_core, upper_side = me.c == 1, me.y == 1
    mine = f_ref[0:3]
    other = r0[...].astype(F32)
    lower = jnp.where(upper_core, other, mine)
    upper = jnp.where(upper_core, mine, other)
    pair = one * lower + upper
    before = jnp.where(upper_core, other, 0.0)
    m1[0] = pair.astype(BF16)
    m1[1, :, 0] = lower[:, 0].astype(BF16)
    copy = remote(m1, r1, ss.at[1], rs.at[1], me.side)
    m1[1, :, 1] = jnp.zeros_like(m1[1, :, 1])
    copy.start()
    copy.wait()
    far = r1[0].astype(F32)
    low_pair = jnp.where(upper_side, far, pair)
    high_pair = jnp.where(upper_side, pair, far)
    total = two * low_pair + high_pair
    before = jnp.where(upper_side, jnp.where(upper_core, one * far, far), 0.0) + before
    third = jnp.where(upper_side, lower[:, 0], r1[1, :, 0].astype(F32))
    last_in = one * low_pair[:, 0] + third
    m2[0] = total[:, 0].astype(BF16)
    m2[1] = last_in.astype(BF16)
    sends = []
    for k in range(1, nq):
        copy = remote(m2.at[0], r2.at[me.q], zs.at[k - 1], zr.at[k - 1], me.at_quad(me.quad(k)))
        copy.start()
        sends.append(copy)

    @pl.when(me.q == nq - 1)
    def _():
        for k in range(1, nq):
            remote(m2.at[1], r2.at[nq], ps.at[k - 1], pr.at[0], me.at_quad(me.quad(k))).start()
        r2[nq] = m2[1]

    r2[me.q] = m2[0]
    for k in range(1, nq):
        src = r2.at[me.quad(nq - k)]
        remote(src, src, zs.at[k - 1], zr.at[k - 1], me.core).wait_recv()

    @pl.when(me.q != nq - 1)
    def _():
        remote(r2.at[nq], r2.at[nq], ps.at[0], pr.at[0], me.core).wait_recv()

    run = jnp.zeros((3, 64, 128), F32)
    carry, tail_in = run, run
    for k in range(nq):
        carry = jnp.where(me.q == k, run, carry)
        if k == nq - 1:
            tail_in = three * run + r2[nq].astype(F32)
        run = four * run + r2[k].astype(F32)
    low = (ab_ref[...] * run).astype(BF16).astype(F32)
    safe = jnp.abs(ab_ref[...]) >= TINY
    begin = jnp.where(safe, low / jnp.where(safe, ab_ref[...], 1.0), run)
    lead = pick(me.pos, [jnp.ones_like(one), one, two, three])
    for p in range(3):
        start = sel_ref[p * 3] * begin[0] + sel_ref[p * 3 + 1] * begin[1] + sel_ref[p * 3 + 2] * begin[2]
        s_ref[2 * p] = lead * carry[p] + before[p, 0]
        s_ref[2 * p + 1] = lead * start + before[p, 1]
        s_ref[6 + p] = tail_in[p]
    for copy in sends:
        copy.wait_send()

    @pl.when(me.q == nq - 1)
    def _():
        for k in range(1, nq):
            remote(m2.at[1], r2.at[nq], ps.at[k - 1], pr.at[0], me.at_quad(me.quad(k))).wait_send()


def forward_exchange_call(n, groups, finals, ab, decays, sel):
    nq = n // 4
    dma = pltpu.SemaphoreType.DMA
    return pl.pallas_call(
        functools.partial(forward_exchange, n, groups),
        out_shape=jax.ShapeDtypeStruct((9, 64, 128), F32),
        in_specs=[VMEM, VMEM, VMEM, SMEM],
        out_specs=VMEM,
        scratch_shapes=[
            pltpu.VMEM((3, 2, 64, 128), BF16), pltpu.VMEM((3, 2, 64, 128), BF16),
            pltpu.VMEM((2, 3, 2, 64, 128), BF16), pltpu.VMEM((2, 3, 2, 64, 128), BF16),
            pltpu.VMEM((2, 3, 64, 128), BF16), pltpu.VMEM((nq + 1, 3, 64, 128), BF16),
            dma((2,)), dma((2,)), dma((nq - 1,)), dma((nq - 1,)), dma((nq - 1,)), dma((1,)),
        ],
        compiler_params=pltpu.CompilerParams(collective_id=1, has_side_effects=True, vmem_limit_bytes=40 << 20),
        name="forward_exchange",
    )(finals, ab, decays, sel)


def tail_flow(me, t, r1, w1, r2, w2, r3, out, send, recv):
    nq = me.nq
    last = me.q == nq - 1
    out[...] = jnp.zeros_like(out)
    copy1 = remote(t.at[:, 1 - me.c], r1, send.at[0], recv.at[0], me.core)
    copy1.start()
    yield
    copy1.wait()
    for i in range(2):
        w1[i] = (t[i, me.c].astype(F32) + r1[i].astype(F32)).astype(BF16)
    copy2 = remote(w1.at[1 - me.y], r2, send.at[1], recv.at[1], me.side)
    copy2.start()
    yield
    copy2.wait()
    w2[...] = (w1[me.y].astype(F32) + r2[...].astype(F32)).astype(BF16)
    top = (me.g, (nq - 1) * 4 + me.pos)
    end = (me.g, nq * 4 - 1)
    for k in range(nq - 1):
        @pl.when(me.q == k)
        def _():
            remote(w2, r3.at[k], send.at[2], recv.at[2 + k], top).start()
    yield

    @pl.when(last)
    def _():
        total = w2[...].astype(F32)
        for k in range(nq - 1):
            remote(r3.at[k], r3.at[k], send.at[2], recv.at[2 + k], me.core).wait_recv()
            total = total + r3[k].astype(F32)
        w2[...] = total.astype(BF16)

        @pl.when(jnp.logical_not(me.is_last))
        def _():
            for j in range(3):
                @pl.when(me.pos == j)
                def _():
                    remote(w2, out.at[j // 2, j % 2], send.at[2], recv.at[nq + 1 + j], end).start()

        @pl.when(me.is_last)
        def _():
            out[1, 1] = w2[...]
    yield

    @pl.when(me.is_last)
    def _():
        for j in range(3):
            dst = out.at[j // 2, j % 2]
            remote(dst, dst, send.at[2], recv.at[nq + 1 + j], me.core).wait_recv()

    @pl.when(jnp.logical_not(me.is_last))
    def _():
        remote(w2, w2, send.at[2], recv.at[2], me.core).wait_send()


def tail_scratch(nq, rows, width):
    return [
        pltpu.VMEM((2, rows, width), BF16), pltpu.VMEM((2, rows, width), BF16),
        pltpu.VMEM((rows, width), BF16), pltpu.VMEM((rows, width), BF16),
        pltpu.VMEM((nq - 1, rows, width), BF16),
    ]


def ema_call(kernel, name, outs, ins, scratch=()):
    return pl.pallas_call(
        kernel,
        out_shape=[jax.ShapeDtypeStruct(shape, F32) for shape in outs],
        in_specs=[VMEM] * len(ins),
        out_specs=[VMEM] * len(outs),
        scratch_shapes=scratch,
        compiler_params=pltpu.CompilerParams(vmem_limit_bytes=56 << 20),
        name=name,
    )(*ins)


def local_pass_call(rows, backward, x, dec):
    def kernel(x_ref, d_ref, inner_ref, final_ref):
        ema_local_pass(rows, (0, 1, rows), x_ref, d_ref.at[0], d_ref.at[1], d_ref.at[2], d_ref.at[3], inner_ref, final_ref, backward)

    return ema_call(kernel, "ema_local", [(rows * 512, 128), (rows * 64, 128)], (x, dec))


def apply_pass_call(rows, x, dec, mix, omega, power, inner, start):
    def kernel(x_ref, d_ref, mix_ref, omega_ref, power_ref, inner_ref, start_ref, y_ref):
        ema_apply_pass(rows, x_ref, d_ref.at[0], mix_ref, omega_ref, power_ref, inner_ref, start_ref, y_ref)

    return ema_call(kernel, "ema_apply", [(rows * 512, 128)], (x, dec, mix, omega, power, inner, start))[0]


def silu_grad(pre_act):
    sigmoid_val = jax.nn.sigmoid(pre_act)
    return sigmoid_val * (1.0 + pre_act * (1.0 - sigmoid_val))


def norm_rows(row_data):
    centered = row_data - jnp.mean(row_data, axis=-1, keepdims=True)
    scale_inv = lax.rsqrt(jnp.mean(centered * centered, axis=-1, keepdims=True) + NORM_EPS)
    return (centered * scale_inv, scale_inv)


def norm_back(grad_rows, plain, scale_inv, gain_vec):
    grad_norm = grad_rows * gain_vec
    inner_term = (
        grad_norm
        - jnp.mean(grad_norm, axis=-1, keepdims=True)
        - plain * jnp.mean(grad_norm * plain, axis=-1, keepdims=True)
    )
    return inner_term * scale_inv


def nt(lhs, rhs):
    return lax.dot_general(lhs, rhs, (((1,), (1,)), ((), ())), preferred_element_type=F32)


def tn(lhs, rhs):
    return lax.dot_general(lhs, rhs, (((0,), (0,)), ((), ())), preferred_element_type=F32)


def nn(lhs, rhs):
    return lax.dot_general(lhs, rhs, (((1,), (0,)), ((), ())), preferred_element_type=F32)


def silu_pair(pre):
    sig = jax.nn.sigmoid(pre)
    return pre * sig, sig * (1.0 + pre * (1.0 - sig))


CHUNK = 256


def dense_kernel(
    n, tok, tail, ema, cot, mats_a, mats_b, w_shared, vec_wide, vec_head, target,
    result, g_middle, g_act, g_base, slope_s, shared_out, g_units, o_outer, o_inner, o_hidden, o_reset, o_value,
    tail_keys, sum_wide, sum_head,
    w_value, w_reset, w_inner, w_hidden, w_outer, values, slope_v, t_values, t_slope, t_keys, t_dv, t_dk,
    k_units, k_activ, k_gated, k_mid, k_inner, k_branch, k_gin, k_greset, k_gvalue, reset_pre, mixed, slope_i, sem,
):
    sets = t_keys.shape[0]
    length = t_keys.shape[1]
    own = tok.shape[0]
    total = own + tail.shape[0]
    width = tok.shape[1]
    chan = w_value.shape[1]
    rows_b = w_hidden.shape[1]
    hv = w_value.shape[2]
    parts = hv // CHUNK
    scale = 1.0 / math.sqrt(128.0)
    copies = [
        pltpu.make_async_copy(mats_a.at[:, 0:chan], w_value, sem.at[0]),
        pltpu.make_async_copy(mats_a.at[:, chan : 2 * chan], w_reset, sem.at[1]),
        pltpu.make_async_copy(mats_b.at[:, 0:rows_b], w_hidden, sem.at[2]),
        pltpu.make_async_copy(mats_a.at[:, 2 * chan : 3 * chan], w_inner, sem.at[3]),
        pltpu.make_async_copy(mats_b.at[:, rows_b : 2 * rows_b], w_outer, sem.at[4]),
    ]
    for copy in copies:
        copy.start()
    gain_one, gain_two = vec_wide[0:1], vec_wide[1:2]
    q_mul, q_add, k_mul = vec_head[0:1], vec_head[1:2], vec_head[2:3]
    t_dv[...] = jnp.zeros_like(t_dv)
    t_dk[...] = jnp.zeros_like(t_dk)
    sum_wide[...] = jnp.zeros_like(sum_wide)
    sum_head[...] = jnp.zeros_like(sum_head)

    def columns(ref, at):
        block = ref[:, :, at * CHUNK : (at + 1) * CHUNK]
        return block.reshape(block.shape[0] * block.shape[1], CHUNK)

    def rows(ref, at):
        per = CHUNK // rows_b
        return ref[at * per : (at + 1) * per].reshape(CHUNK, ref.shape[2])

    def ema_rows(start, count):
        return jnp.concatenate([ema[pl.ds(lane * total + start, count), :] for lane in range(4)], axis=1)

    copies[0].wait()

    def tail_step(m, carry):
        at = pl.multiple_of(m * length, length)
        here = pl.ds(at, length)
        plain, _ = norm_rows(tail[here, :].astype(F32))
        units = (plain * gain_one).astype(BF16)
        k_units[pl.ds(own + at, length), :] = units
        for part in range(parts):
            value, slope = silu_pair(nn(units, columns(w_value, part)))
            t_values[m, :, part * CHUNK : (part + 1) * CHUNK] = value.astype(BF16)
            t_slope[m, :, part * CHUNK : (part + 1) * CHUNK] = slope.astype(BF16)
        pre = ema_rows(own + at, length)
        activ = (pre * jax.nn.sigmoid(pre)).astype(BF16)
        shared = nn(activ, w_shared[...])
        t_keys[m] = (shared * jax.nn.sigmoid(shared) * k_mul).astype(BF16)
        return carry

    lax.fori_loop(0, sets, tail_step, 0)
    for copy in copies[1:]:
        copy.wait()
    causal = lax.broadcasted_iota(jnp.int32, (length, length), 0) >= lax.broadcasted_iota(jnp.int32, (length, length), 1)

    def set_step(p, carry):
        here = pl.ds(pl.multiple_of(p * 2 * length, 2 * length), 2 * length)
        m = target[p]
        x = tok[here, :].astype(F32)
        plain, _ = norm_rows(x)
        units = (plain * gain_one).astype(BF16)
        k_units[here, :] = units
        for part in range(parts):
            cut = slice(part * CHUNK, (part + 1) * CHUNK)
            value, slope = silu_pair(nn(units, columns(w_value, part)))
            values[:, cut] = value.astype(BF16)
            slope_v[:, cut] = slope.astype(BF16)
        pre = ema_rows(p * 2 * length, 2 * length)
        activ = (pre * jax.nn.sigmoid(pre)).astype(BF16)
        k_activ[here, :] = activ
        shared, slope = silu_pair(nn(activ, w_shared[...]))
        slope_s[here, :] = slope
        shared_out[here, :] = shared
        queries = (shared * q_mul + q_add).astype(BF16)
        keys = (shared * k_mul).astype(BF16)
        for part in range(parts):
            reset_pre[:, part * CHUNK : (part + 1) * CHUNK] = nn(activ, columns(w_reset, part))
        p_q, c_q, p_k, c_k = queries[:length], queries[length:], keys[:length], keys[length:]
        e_k = t_keys[m]

        def weights(scores):
            expo = jnp.exp(scores - jnp.max(scores, axis=-1, keepdims=True))
            return expo * (1.0 / jnp.sum(expo, axis=-1, keepdims=True))

        p_probs = weights(jnp.where(causal, nt(p_q, p_k) * scale, MASKED_SCORE))
        c_probs = weights(
            jnp.concatenate((nt(c_q, e_k) * scale, jnp.where(causal, nt(c_q, c_k) * scale, MASKED_SCORE)), axis=1)
        )
        p_low, c_low = p_probs.astype(BF16), c_probs.astype(BF16)
        for part in range(parts):
            cut = slice(part * CHUNK, (part + 1) * CHUNK)
            mix_p = nn(p_low, values[:length, cut])
            mix_c = nn(c_low, jnp.concatenate((t_values[m, :, cut], values[length:, cut]), axis=0))
            mix = jnp.concatenate((mix_p, mix_c), axis=0)
            mixed[:, cut] = mix
            gate = reset_pre[:, cut]
            k_gated[here, cut] = (gate * jax.nn.sigmoid(gate) * mix).astype(BF16)
        middle = x + nn(k_gated[here, :], w_hidden[...].reshape(-1, width))
        plain_mid, inv_mid = norm_rows(middle)
        mid_low = (plain_mid * gain_two).astype(BF16)
        k_mid[here, :] = mid_low
        for part in range(parts):
            cut = slice(part * CHUNK, (part + 1) * CHUNK)
            inner, slope = silu_pair(nn(mid_low, columns(w_inner, part)))
            k_inner[here, cut] = inner.astype(BF16)
            slope_i[:, cut] = slope
        result[here, :] = (middle + nn(k_inner[here, :], w_outer[...].reshape(-1, width))).astype(BF16)
        top = cot[here, :]
        for part in range(parts):
            cut = slice(part * CHUNK, (part + 1) * CHUNK)
            k_gin[here, cut] = (nt(top, rows(w_outer, part)) * slope_i[:, cut]).astype(BF16)
        back = nt(k_gin[here, :], w_inner[...].reshape(width, -1))
        sum_wide[0:1] += jnp.sum(back * plain_mid, axis=0, keepdims=True)
        g_mid = top.astype(F32) + norm_back(back, plain_mid, inv_mid, gain_two)
        g_middle[here, :] = g_mid
        branch = g_mid.astype(BF16)
        k_branch[here, :] = branch
        dp_p = jnp.zeros((length, length), F32)
        dp_c = jnp.zeros((length, 2 * length), F32)
        for part in range(parts):
            cut = slice(part * CHUNK, (part + 1) * CHUNK)
            gated_back = nt(branch, rows(w_hidden, part))
            gate, slope = silu_pair(reset_pre[:, cut])
            g_mix = (gated_back * gate).astype(BF16)
            k_greset[here, cut] = (gated_back * mixed[:, cut] * slope).astype(BF16)
            dp_p += nt(g_mix[:length], values[:length, cut])
            dp_c += nt(g_mix[length:], jnp.concatenate((t_values[m, :, cut], values[length:, cut]), axis=0))
            dv_p = tn(p_low, g_mix[:length])
            dv_c = tn(c_low, g_mix[length:])
            t_dv[m, :, cut] += dv_c[:length]
            dv = jnp.concatenate((dv_p, dv_c[length:]), axis=0)
            k_gvalue[here, cut] = (dv * slope_v[:, cut].astype(F32)).astype(BF16)
        g_act[here, :] = nt(k_greset[here, :], w_reset[...].reshape(width, -1))

        def score_back(probs, grads):
            return (probs * (grads - jnp.sum(grads * probs, axis=-1, keepdims=True))).astype(BF16)

        p_ds, c_ds = score_back(p_probs, dp_p), score_back(c_probs, dp_c)
        d_q = jnp.concatenate((nn(p_ds, p_k), nn(c_ds, jnp.concatenate((e_k, c_k), axis=0))), axis=0) * scale
        dk_c = tn(c_ds, c_q) * scale
        t_dk[m] += dk_c[:length]
        d_k = jnp.concatenate((tn(p_ds, p_q) * scale, dk_c[length:]), axis=0)
        sum_head[0:1] += jnp.sum(d_q * shared, axis=0, keepdims=True)
        sum_head[1:2] += jnp.sum(d_q, axis=0, keepdims=True)
        sum_head[2:3] += jnp.sum(d_k * shared, axis=0, keepdims=True)
        g_base[here, :] = d_q * q_mul + d_k * k_mul
        return carry

    lax.fori_loop(0, sets, set_step, 0)
    tail_keys[...] = t_dk[...].astype(BF16)

    def tail_back(m, carry):
        at = pl.multiple_of(own + m * length, length)
        k_gvalue[pl.ds(at, length), :] = (t_dv[m] * t_slope[m].astype(F32)).astype(BF16)
        return carry

    lax.fori_loop(0, sets, tail_back, 0)

    def units_step(i, carry):
        here = pl.ds(pl.multiple_of(i * CHUNK, CHUNK), CHUNK)
        g_units[here, :] = nt(k_gvalue[here, :], w_value[...].reshape(width, -1))
        return carry

    lax.fori_loop(0, total // CHUNK, units_step, 0) if total % CHUNK == 0 else None
    if total % CHUNK:
        here = slice(total // CHUNK * CHUNK, total)
        lax.fori_loop(0, total // CHUNK, units_step, 0)
        g_units[here, :] = nt(k_gvalue[here, :], w_value[...].reshape(width, -1))

    def weight_grad(lhs, rhs, out, count):
        per = CHUNK // out.shape[1]

        def step(i, carry):
            block = tn(lhs[0:count, pl.ds(pl.multiple_of(i * CHUNK, CHUNK), CHUNK)], rhs[0:count, :])
            out[pl.ds(i * per, per)] = block.astype(BF16).reshape(per, out.shape[1], out.shape[2])
            return carry

        lax.fori_loop(0, lhs.shape[1] // CHUNK, step, 0)

    weight_grad(k_inner, cot, o_outer, own)
    weight_grad(k_mid, k_gin, o_inner, own)
    weight_grad(k_gated, k_branch, o_hidden, own)
    weight_grad(k_activ, k_greset, o_reset, own)
    weight_grad(k_units, k_gvalue, o_value, total)


def dense_call(n, tok, tail, ema, cot, mats_a, mats_b, w_shared, vec_wide, vec_head, target):
    own, width = tok.shape
    rows_t = tail.shape[0]
    total = own + rows_t
    sets = target.shape[0]
    length = rows_t // sets
    hv = mats_a.shape[2]
    chan = mats_a.shape[1] // 3
    rows_b = mats_b.shape[1] // 2
    shape = jax.ShapeDtypeStruct
    vm = pltpu.VMEM
    outs = [
        shape((own, width), BF16), shape((own, width), F32), shape((own, width), F32), shape((own, 128), F32),
        shape((own, 128), F32), shape((own, 128), F32), shape((total, width), F32),
        shape((n, rows_b, width), BF16), shape((n, chan, hv), BF16), shape((n, rows_b, width), BF16),
        shape((n, chan, hv), BF16), shape((n, chan, hv), BF16),
        shape((sets, length, 128), BF16), shape((8, width), F32), shape((8, 128), F32),
    ]
    scratch = [
        vm((n, chan, hv), BF16), vm((n, chan, hv), BF16), vm((n, chan, hv), BF16),
        vm((n, rows_b, width), BF16), vm((n, rows_b, width), BF16),
        vm((2 * length, hv), BF16), vm((2 * length, hv), BF16),
        vm((sets, length, hv), BF16), vm((sets, length, hv), BF16), vm((sets, length, 128), BF16),
        vm((sets, length, hv), F32), vm((sets, length, 128), F32),
        vm((total, width), BF16), vm((own, width), BF16), vm((own, hv), BF16), vm((own, width), BF16),
        vm((own, hv), BF16), vm((own, width), BF16), vm((own, hv), BF16), vm((own, hv), BF16), vm((total, hv), BF16),
        vm((2 * length, hv), F32), vm((2 * length, hv), F32), vm((2 * length, hv), F32),
        pltpu.SemaphoreType.DMA((5,)),
    ]
    return pl.pallas_call(
        functools.partial(dense_kernel, n),
        out_shape=outs,
        in_specs=[VMEM] * 4 + [ANY] * 2 + [VMEM] * 3 + [SMEM],
        out_specs=[VMEM] * len(outs),
        scratch_shapes=scratch,
        compiler_params=pltpu.CompilerParams(vmem_limit_bytes=60 << 20),
        name="dense",
    )(tok, tail, ema, cot, mats_a, mats_b, w_shared, vec_wide, vec_head, target)


def big_flow(me, cross_first, grads, r1, w1, r2, w2, r3, w3, r4, rx, out, send, recv, local_sem):
    nq = me.nq
    rows, width = out.shape
    wide = width // 2
    ours = pl.ds(pl.multiple_of(me.x * wide, 128), wide)
    others = pl.ds(pl.multiple_of((1 - me.x) * wide, 128), wide)
    copy1 = remote(grads.at[:, :, 1 - me.c], r1, send.at[0], recv.at[0], me.core)
    copy1.start()
    kept = pltpu.make_async_copy(grads.at[:, :, me.c], w1, local_sem)
    kept.start()
    yield
    kept.wait()
    copy1.wait()

    def add1(i, carry):
        w1[i // 2, i % 2] = (w1[i // 2, i % 2].astype(F32) + r1[i // 2, i % 2].astype(F32)).astype(BF16)
        return carry

    lax.fori_loop(0, 2 * nq, add1, 0)
    if cross_first:
        copy2 = remote(w1.at[:, :, :, others], r2, send.at[1], recv.at[1], me.cross)
    else:
        copy2 = remote(w1.at[:, 1 - me.y], r2, send.at[1], recv.at[1], me.side)
    copy2.start()
    yield
    copy2.wait()
    if cross_first:
        def add2(i, carry):
            w2[i // 2, i % 2] = (w1[i // 2, i % 2, :, ours].astype(F32) + r2[i // 2, i % 2].astype(F32)).astype(BF16)
            return carry

        lax.fori_loop(0, 2 * nq, add2, 0)
        copy3 = remote(w2.at[:, 1 - me.y], r3, send.at[2], recv.at[2], me.side)
    else:
        def add2(i, carry):
            w2[i] = (w1[i, me.y].astype(F32) + r2[i].astype(F32)).astype(BF16)
            return carry

        lax.fori_loop(0, nq, add2, 0)
        copy3 = remote(w2.at[:, :, others], r3, send.at[2], recv.at[2], me.cross)
    copy3.start()
    yield
    copy3.wait()

    def add3(i, carry):
        mine = w2[i, me.y] if cross_first else w2[i, :, ours]
        w3[i] = (mine.astype(F32) + r3[i].astype(F32)).astype(BF16)
        return carry

    lax.fori_loop(0, nq, add3, 0)
    copies = []
    for k in range(1, nq):
        copy = remote(w3.at[me.quad(k)], r4.at[k - 1], send.at[2 + k], recv.at[2 + k], me.at_quad(me.quad(k)))
        copy.start()
        copies.append(copy)
    yield
    total = w3[me.q].astype(F32)
    for k in range(1, nq):
        copies[k - 1].wait()
        total = total + r4[k - 1].astype(F32)
    out[:, ours] = total.astype(BF16)
    copy5 = remote(out.at[:, ours], out.at[:, ours], send.at[nq + 2], recv.at[nq + 2], me.cross)
    copy5.start()
    yield
    remote(out.at[:, others], out.at[:, others], send.at[nq + 2], recv.at[nq + 2], me.cross).wait_recv()
    copy5.wait_send()
    for at, bit in enumerate(me.cross_bits()[1:]):
        copy = remote(out, rx.at[at], send.at[nq + 3 + at], recv.at[nq + 3 + at], me.cross_bit(bit))
        copy.start()
        copy.wait()
        out[...] = (out[...].astype(F32) + rx[at].astype(F32)).astype(BF16)


def big_scratch(nq, groups, cross_first, rows, width):
    extra = max(groups.bit_length() - 2, 1)
    half = width // 2
    full = [pltpu.VMEM((nq, 2, rows, width), BF16)] * 2
    if cross_first:
        mid = [pltpu.VMEM((nq, 2, rows, half), BF16)] * 2
    else:
        mid = [pltpu.VMEM((nq, rows, width), BF16)] * 2
    return full + mid + [
        pltpu.VMEM((nq, rows, half), BF16), pltpu.VMEM((nq, rows, half), BF16),
        pltpu.VMEM((nq - 1, rows, half), BF16), pltpu.VMEM((extra, rows, width), BF16),
    ]


def small_flow(me, grads, r1, w1, r2, w2, rx, out, send, recv):
    many = 2 * me.nq
    copy1 = remote(grads.at[:, 1 - me.c], r1, send.at[0], recv.at[0], me.core)
    copy1.start()
    yield
    copy1.wait()

    def add(i, carry):
        w1[i] = (grads[i, me.c].astype(F32) + r1[i].astype(F32)).astype(BF16)
        return carry

    lax.fori_loop(0, many, add, 0)
    mine = me.q * 2 + me.y
    copies = []
    for k in range(1, many):
        to = (mine + k) % many
        copy = remote(w1.at[to], r2.at[k - 1], send.at[k], recv.at[k], (me.g, to * 2 + me.c))
        copy.start()
        copies.append(copy)
    yield
    total = w1[mine].astype(F32)
    for k in range(1, many):
        copies[k - 1].wait()
        total = total + r2[k - 1].astype(F32)
    bits = me.cross_bits()
    for at, bit in enumerate(bits):
        w2[at] = total.astype(BF16)
        copy = remote(w2.at[at], rx.at[at], send.at[many + at], recv.at[many + at], me.cross_bit(bit))
        copy.start()
        if at == 0:
            yield
        copy.wait()
        total = total + rx[at].astype(F32)
    out[...] = total.astype(BF16)


def small_scratch(nq, groups, rows):
    bits = groups.bit_length() - 1
    return [
        pltpu.VMEM((2 * nq, rows, 128), BF16), pltpu.VMEM((2 * nq, rows, 128), BF16),
        pltpu.VMEM((2 * nq - 1, rows, 128), BF16), pltpu.VMEM((bits, rows, 128), BF16), pltpu.VMEM((bits, rows, 128), BF16),
    ]


def adjoint_flow(me, f_ref, tabs, sel_ref, s_ref, m0, r0, m1, r1, m2, r2, ss, rs, zs, zr):
    nq = me.nq
    one, two, three, four = tabs[4], tabs[5], tabs[6], tabs[7]
    mine = f_ref[...].reshape(3, 2, 64, 128)
    m0[...] = mine.astype(BF16)
    copy = remote(m0, r0, ss.at[0], rs.at[0], me.core)
    copy.start()
    yield
    copy.wait()
    upper_core, upper_side = me.c == 1, me.y == 1
    other = r0[...].astype(F32)
    lower = jnp.where(upper_core, other, mine)
    upper = jnp.where(upper_core, mine, other)
    pair = lower + one * upper
    after = jnp.where(upper_core, 0.0, other)
    m1[...] = pair.astype(BF16)
    copy = remote(m1, r1, ss.at[1], rs.at[1], me.side)
    copy.start()
    yield
    copy.wait()
    far = r1[...].astype(F32)
    low_pair = jnp.where(upper_side, far, pair)
    high_pair = jnp.where(upper_side, pair, far)
    total = low_pair + two * high_pair
    after = jnp.where(upper_side, 0.0, jnp.where(upper_core, far, one * far)) + after
    m2[0] = total[:, 0].astype(BF16)
    for m in range(3):
        m2[1, m] = (sel_ref[m] * total[0, 1] + sel_ref[3 + m] * total[1, 1] + sel_ref[6 + m] * total[2, 1]).astype(BF16)
    sends = []
    for k in range(1, nq):
        copy = remote(m2, r2.at[me.q], zs.at[k - 1], zr.at[k - 1], me.at_quad(me.quad(k)))
        copy.start()
        sends.append(copy)
    r2[me.q] = m2[...]
    yield
    for k in range(1, nq):
        src = r2.at[me.quad(nq - k)]
        remote(src, src, zs.at[k - 1], zr.at[k - 1], me.core).wait_recv()
    run = r2[0, 1].astype(F32)
    for k in range(1, nq):
        run = run + r2[k, 1].astype(F32)
    carry = run
    for k in range(nq - 1, -1, -1):
        carry = jnp.where(me.q == k, run, carry)
        run = four * run + r2[k, 0].astype(F32)
    lead = pick(me.pos, [three, two, one, jnp.ones_like(one)])
    for p in range(3):
        s_ref[2 * p * 64 : (2 * p + 1) * 64] = lead * carry[p] + after[p, 0]
        s_ref[(2 * p + 1) * 64 : (2 * p + 2) * 64] = after[p, 1]
    for copy in sends:
        copy.wait_send()


class Steps:
    def __init__(self, flows):
        self.flows, self.live = flows, [True] * len(flows)

    def __call__(self, *which):
        for i in which:
            if self.live[i]:
                try:
                    next(self.flows[i])
                except StopIteration:
                    self.live[i] = False

    def finish(self):
        while any(self.live):
            self(*range(len(self.flows)))


ORDERS = (True, False, True, False, True)
N_BIG = 5


def back_kernel(n, groups, *refs):
    refs = list(refs)

    def take(count):
        got = refs[:count]
        del refs[:count]
        return got

    base, slope_s, shared, t_keys, w_shared, tabs, power, power_rev, vec_wide, vec_head, starts, sum_wide, sum_head, sel = take(14)
    h_act, h_ema, h_x, h_inner, h_units, h_middle, h_tokens = take(7)
    grads = take(N_BIG)
    (input_grad,) = take(1)
    outs = take(N_BIG)
    (out_small,) = take(1)
    loads = take(7)
    g_act, ema, x_lanes, inner, g_units, g_middle, tokens = loads
    g_lanes, k_activ, k_gs, b_inner, b_flow, b_start, dx_lanes, acc_in, acc_decay, acc_out, kept, omega_acc, gain_acc = take(13)
    t_sum, t_rows, t_grad, t_out, grad_in, g_small = take(6)
    big = [take(8) for _ in range(N_BIG)]
    small = take(5)
    keys_s, tail_s = take(5), take(5)
    exchange = take(6)
    load_sem, big_send, big_recv, big_local, small_send, small_recv, k_send, k_recv, t_send, t_recv, ess, ers, ezs, ezr = take(14)

    me = Place(n, groups)
    own = base.shape[0]
    total = tokens.shape[0]
    width = tokens.shape[1]
    length = 128
    count = own // length
    lanes = width // 128
    chan = width // n
    hbm = [h_act, h_ema, h_x, h_inner, h_units, h_middle, h_tokens]
    arrive = [pltpu.make_async_copy(src, dst, load_sem.at[i]) for i, (src, dst) in enumerate(zip(hbm, loads))]
    for copy in arrive:
        copy.start()
    meet(me.group_peers() + [me.cross_bit(bit) for bit in me.cross_bits()])
    keys = tail_flow(me, t_keys, *keys_s, t_sum, k_send, k_recv)
    next(keys)
    steps = Steps(
        [
            big_flow(me, ORDERS[i], grads[i], *big[i], outs[i], big_send.at[i], big_recv.at[i], big_local.at[i])
            for i in range(N_BIG)
        ]
    )
    steps(*range(N_BIG))
    k_mul = vec_head[2:3]
    gain_one = vec_wide[0:1]
    for ref in (omega_acc, gain_acc, acc_in, acc_decay, acc_out):
        ref[...] = jnp.zeros_like(ref)
    for i in range(3):
        arrive[i].wait()

    def grad_rows(row, with_tail):
        at = pl.multiple_of(row * length, length)
        here = pl.ds(at, length)
        d_shared = base[here, :]
        if with_tail:
            extra = t_rows[pl.ds(pl.multiple_of(row // 2 * length, length), length), :]
            d_shared = d_shared + extra * k_mul
            gain_acc[1:2, 0:128] += jnp.sum(extra * shared[here, :], axis=0, keepdims=True)
        gs = (d_shared * slope_s[here, :]).astype(BF16)
        k_gs[here, :] = gs
        for lane in range(lanes):
            cut = slice(lane * 128, (lane + 1) * 128)
            pre = ema[pl.ds(lane * total + at, length), :]
            sig = jax.nn.sigmoid(pre)
            k_activ[here, cut] = (pre * sig).astype(BF16)
            back = g_act[here, cut] + nt(gs, w_shared[cut, :])
            back = back * (sig * (1.0 + pre * (1.0 - sig)))
            g_lanes[pl.ds(lane * own + at, length), :] = back
            x = x_lanes[pl.ds(lane * total + at, length), :]
            omega_acc[lane : lane + 1] += jnp.sum(back * x, axis=0, keepdims=True)

    def local_pass(first):
        ema_local_pass(
            count, (first, 2, count // 2), g_lanes, tabs.at[0], tabs.at[1], tabs.at[2], tabs.at[3], b_inner, b_flow, True
        )

    def cont_rows(p, carry):
        grad_rows(2 * p + 1, False)
        return carry

    def prompt_rows(p, carry):
        grad_rows(2 * p, True)
        return carry

    def norm_rows_back(at, size, extra):
        here = pl.ds(at, size)
        plain, inv = norm_rows(tokens[here, :].astype(F32))
        units = g_units[here, :]
        if extra is not None:
            units = units + extra
        gain_acc[0:1] += jnp.sum(units * plain, axis=0, keepdims=True)
        return norm_back(units, plain, inv, gain_one)

    lax.fori_loop(0, count // 2, cont_rows, 0)
    next(keys)
    steps(0, 1)
    local_pass(1)
    next(keys)
    steps(2, 3)
    arrive[4].wait()
    arrive[6].wait()
    piece = (total - own) // 4
    for part in range(4):
        t_grad[part // 2, part % 2] = norm_rows_back(own + part * piece, piece, None).astype(BF16)
    tail = tail_flow(me, t_grad, *tail_s, t_out, t_send, t_recv)
    next(tail)
    next(keys)
    steps(4)
    for _ in keys:
        pass
    for part in range(4):
        t_rows[part * piece : (part + 1) * piece] = t_sum[part // 2, part % 2].astype(F32)
    lax.fori_loop(0, count // 2, prompt_rows, 0)
    local_pass(0)
    adjoint = adjoint_flow(me, b_flow, tabs, sel, b_start, *exchange, ess, ers, ezs, ezr)
    next(adjoint)
    steps(0, 1)
    next(adjoint)
    next(tail)
    steps(2)
    next(adjoint)
    next(tail)
    steps(3)
    for _ in adjoint:
        pass
    arrive[3].wait()
    for row in range(count):
        ema_back_pass(
            count, total // length, row, x_lanes, g_lanes, tabs.at[0], tabs.at[8], vec_head, power, inner, starts,
            power_rev, b_inner, b_start, dx_lanes, acc_in, acc_decay, acc_out, kept,
        )
        if row == 0:
            steps(4)
            next(tail)
        elif row < count - 1:
            steps(*range(N_BIG))
    arrive[5].wait()

    def own_rows(row, carry):
        at = pl.multiple_of(row * length, length)
        extra = jnp.concatenate([dx_lanes[pl.ds(lane * own + at, length), :] for lane in range(lanes)], axis=1)
        grad_in[pl.ds(at, length), :] = g_middle[pl.ds(at, length), :] + norm_rows_back(at, length, extra)
        return carry

    lax.fori_loop(0, count, own_rows, 0)
    alpha, beta, delta, eta, ab = (tabs[9 + i] for i in range(5))
    m_sum, q_sum = eta * acc_in[...], eta * ab * acc_decay[...]
    parts = (beta * m_sum - delta * q_sum, -alpha * q_sum, alpha * m_sum, ab * acc_out[...])
    per = 128 // chan // 2
    for lane in range(lanes):
        cut = slice(lane * 128, (lane + 1) * 128)
        block = [part[lane * 16 : lane * 16 + 16] for part in parts]
        block += [omega_acc[lane : lane + 1], gain_acc[0:1, cut], sum_wide[0:1, cut], jnp.zeros((61, 128), F32)]
        block = jnp.concatenate(block, axis=0).T.astype(BF16)
        g_small[lane * per : (lane + 1) * per, :, 0:chan] = block.reshape(per, 2, chan, 128)
    block = tn(k_activ[...], k_gs[...]).astype(BF16)
    g_small[:, :, chan : 2 * chan] = block.reshape(n // 2, 2, chan, 128)
    heads = jnp.concatenate((sum_head[0:2], sum_head[2:3] + gain_acc[1:2, 0:128], jnp.zeros((13, 128), F32)), axis=0)
    heads = jnp.broadcast_to(heads.astype(BF16)[None, None], (n // 2, 2, 16, 128))
    g_small[:, :, 2 * chan :] = heads
    little = small_flow(me, g_small, *small, out_small, small_send, small_recv)
    next(little)
    for _ in tail:
        pass
    next(little)
    steps(*range(N_BIG))

    def cast_rows(row, carry):
        here = pl.ds(pl.multiple_of(row * length, length), length)
        input_grad[here, :] = grad_in[here, :].astype(BF16)
        return carry

    for part in range(4):
        t_wide = t_out[part // 2, part % 2].astype(F32)
        at = part * piece
        while at < (part + 1) * piece:
            m = at // length
            stop = min((m + 1) * length, (part + 1) * piece)
            here = slice(at + m * length, stop + m * length)
            grad_in[here] = grad_in[here] + t_wide[at - part * piece : stop - part * piece]
            at = stop
    lax.fori_loop(0, count, cast_rows, 0)
    next(little)
    steps(*range(N_BIG))
    for _ in little:
        pass
    steps.finish()


def back_call(n, groups, ins, hbm, grads):
    nq = n // 4
    dma = pltpu.SemaphoreType.DMA
    vm = pltpu.VMEM
    shape = jax.ShapeDtypeStruct
    own, total, width = ins[0].shape[0], hbm[6].shape[0], hbm[6].shape[1]
    chan = width // n
    small_rows = 2 * chan + 16
    piece = (total - own) // 4
    outs = [shape((own, width), BF16)] + [shape(grad.shape[-2:], BF16) for grad in grads] + [shape((small_rows, 128), BF16)]
    scratch = [vm(part.shape, part.dtype) for part in hbm]
    scratch += [
        vm((own * 4, 128), F32), vm((own, width), BF16), vm((own, 128), BF16), vm((own * 4, 128), F32),
        vm((own // 2, 128), F32), vm((own // 2, 128), F32), vm((own * 4, 128), F32), vm((64, 128), F32), vm((64, 128), F32),
        vm((64, 128), F32), vm((128, 8, 128), F32), vm((8, 128), F32), vm((8, width), F32),
        vm((2, 2, piece, 128), BF16), vm((4 * piece, 128), F32), vm((2, 2, piece, width), BF16), vm((2, 2, piece, width), BF16),
        vm((own, width), F32), vm((n // 2, 2, small_rows, 128), BF16),
    ]
    for i, grad in enumerate(grads):
        scratch += big_scratch(nq, groups, ORDERS[i], grad.shape[-2], grad.shape[-1])
    scratch += small_scratch(nq, groups, small_rows)
    scratch += tail_scratch(nq, piece, 128) + tail_scratch(nq, piece, width)
    scratch += [vm((3, 2, 64, 128), BF16)] * 4 + [vm((2, 3, 64, 128), BF16), vm((nq, 2, 3, 64, 128), BF16)]
    sems = nq + 3 + max(groups.bit_length() - 2, 1)
    small_sems = 2 * nq + groups.bit_length() - 1
    scratch += [
        dma((7,)), dma((N_BIG, sems)), dma((N_BIG, sems)), dma((N_BIG,)), dma((small_sems,)), dma((small_sems,)),
        dma((3,)), dma((nq + 4,)), dma((3,)), dma((nq + 4,)), dma((2,)), dma((2,)), dma((nq - 1,)), dma((nq - 1,)),
    ]
    return pl.pallas_call(
        functools.partial(back_kernel, n, groups),
        out_shape=outs,
        in_specs=[VMEM] * 13 + [SMEM] + [ANY] * (7 + N_BIG),
        out_specs=[VMEM] * len(outs),
        scratch_shapes=scratch,
        compiler_params=pltpu.CompilerParams(collective_id=2, has_side_effects=True, vmem_limit_bytes=60 << 20),
        name="back",
    )(*ins, *hbm, *grads)


def lanes_first(rows):
    return rows.reshape(-1, 4, 128).transpose(1, 0, 2).reshape(-1, 128)


def rows_first(lanes):
    return lanes.reshape(4, -1, 128).transpose(1, 0, 2).reshape(-1, 512)


def dot(lhs, rhs, dims):
    return lax.dot_general(lhs, rhs, ((dims[:1], dims[1:]), ((), ())), preferred_element_type=F32)


def local(
    hidden_in, cotangent, cont_prompt, value_proj, shared_proj, reset_proj, hidden_proj, inner_proj,
    outer_proj, ema_alpha, ema_delta, ema_beta, ema_eta, ema_omega, norm_gain, ffn_gain, query_scale,
    query_shift, key_scale,
):
    n, groups = lax.axis_size("seq"), lax.axis_size("grp")
    nq = n // 4
    seq_index = lax.axis_index("seq")
    sets, kinds, length, width = hidden_in.shape[1:]
    chan = width // n
    heads = query_scale.shape[0]
    tokens_low = hidden_in[0]
    vectors = jnp.stack((query_scale, query_shift, key_scale), axis=1)
    small = jnp.concatenate(
        (
            ema_alpha, ema_delta, ema_beta, ema_eta, ema_omega[:, None], norm_gain[:, None], ffn_gain[:, None],
            jnp.pad(vectors, ((0, chan - heads), (0, 0))), jnp.zeros((chan, 58), BF16),
        ),
        axis=1,
    )
    small = jnp.concatenate((small, shared_proj), axis=0)
    mat_a = jnp.concatenate((value_proj, reset_proj, inner_proj), axis=0)
    mat_b = jnp.concatenate((hidden_proj, outer_proj), axis=0)
    rows_b = hidden_proj.shape[0]
    all_small, all_a, all_b, tail_low = gather_call(
        n, groups, small, mat_a, mat_b, tokens_low[:, 0].reshape(4, sets * length // 4, width)
    )
    mat_shared = all_small[:, chan:].reshape(width, 128)
    flat = all_small[:, :chan].astype(F32)
    table = flat.reshape(width, 128).T
    vecs = flat[:, :heads, 67:70].reshape(-1, 3)
    query_mul, query_add, key_mul = vecs[:, 0], vecs[:, 1], vecs[:, 2]

    def by_lane(part):
        return part.reshape(16, 4, 128).transpose(1, 0, 2).reshape(64, 128)

    alpha, delta, beta, eta = (by_lane(table[16 * i : 16 * i + 16]) for i in range(4))
    omega, gain_one, gain_two = table[64], table[65], table[66]
    omega_lanes = omega.reshape(4, 128)
    decay = 1.0 - alpha * delta
    decay2 = decay * decay
    decay4 = decay2 * decay2
    decay8 = decay4 * decay4
    decay16 = decay8 * decay8
    decay32 = decay16 * decay16
    decay64 = decay32 * decay32
    decay128 = decay64 * decay64
    decay256 = decay128 * decay128
    dec = jnp.stack((decay, decay16, decay32, decay64))
    far = jnp.stack((decay128, decay256, decay256 * decay128, decay256 * decay256))
    steps = [jnp.ones_like(decay), decay16, decay32, decay32 * decay16, decay64, decay64 * decay16, decay64 * decay32, decay64 * decay32 * decay16]
    power = jnp.stack(steps, axis=1).reshape(512, 128)
    power_rev = jnp.stack(steps[::-1], axis=1).reshape(512, 128)
    ab = alpha * beta
    mix = ab * eta
    targets = lax.dynamic_slice_in_dim(
        cont_prompt[0].reshape(sets, nq), seq_index // 4, 1, 1
    )[:, 0]
    select = (targets[:, None] == jnp.arange(sets, dtype=jnp.int32)[None, :]).astype(F32)
    sel = select.reshape(-1)
    own_rows = sets * kinds * length
    rows_low = jnp.concatenate((tokens_low.reshape(own_rows, width), tail_low.reshape(-1, width)), axis=0)
    tokens = rows_low.astype(F32)
    plain_in, inv_in = norm_rows(tokens)
    normed = plain_in * gain_one
    x_lanes = lanes_first(normed)
    inner, finals = local_pass_call(9, False, x_lanes, dec)
    starts = forward_exchange_call(n, groups, finals[: 6 * 64].reshape(3, 2, 64, 128), ab, far, sel)
    starts = starts.reshape(9 * 64, 128)
    ema_lanes = apply_pass_call(9, x_lanes, dec, mix, omega_lanes, power, inner, starts)
    grad_outer = cotangent[0].reshape(own_rows, width)
    vec_wide = jnp.pad(jnp.stack((gain_one, gain_two)), ((0, 6), (0, 0)))
    vec_head = jnp.concatenate((jnp.stack((query_mul, query_add, key_mul, key_mul)), omega_lanes), axis=0)
    (
        result, grad_middle, grad_act, grad_base, slope_shared, shared, grad_units, sum_outer, sum_inner, sum_hidden,
        sum_reset, sum_value, sent_keys, sum_wide, sum_head,
    ) = dense_call(
        n, rows_low[:own_rows], rows_low[own_rows:], ema_lanes, grad_outer, all_a, all_b, mat_shared, vec_wide, vec_head, targets
    )
    tabs = jnp.concatenate((dec, far, jnp.stack((mix, alpha, beta, delta, eta, ab))))

    def shards(grad):
        return grad.reshape(nq, 2, 2, -1, grad.shape[-1])

    ins = (
        grad_base, slope_shared, shared, sent_keys.reshape(2, 2, -1, 128), mat_shared, tabs, power, power_rev, vec_wide,
        vec_head, starts, sum_wide, sum_head, sel,
    )
    hbm = (grad_act, ema_lanes, x_lanes, inner[: own_rows * 4], grad_units, grad_middle, rows_low)
    grads = [shards(part) for part in (sum_outer, sum_inner, sum_hidden, sum_reset, sum_value)]
    input_grad, *sums, d_small = back_call(n, groups, ins, hbm, grads)
    d_outer, d_inner, d_hidden, d_reset, d_value, d_small = [part.astype(F32) for part in (*sums, d_small)]
    d_heads = lax.dynamic_slice(d_small, (2 * chan, seq_index * heads), (3, heads))
    return (
        result.reshape(hidden_in.shape), input_grad.reshape(hidden_in.shape), d_value, d_small[chan : 2 * chan], d_reset,
        d_hidden, d_inner, d_outer, d_small[:chan, 0:16], d_small[:chan, 16:32], d_small[:chan, 32:48],
        d_small[:chan, 48:64], d_small[:chan, 64], d_small[:chan, 65], d_small[:chan, 66],
        d_heads[0], d_heads[1], d_heads[2],
    )


def solution(mesh):
    mat, vec = P("seq", None), P("seq")
    tok = P("grp", None, None, "seq", None)
    in_specs = (tok, tok, P("grp", None)) + (mat,) * 10 + (vec,) * 6
    out_specs = (tok, tok) + (mat,) * 10 + (vec,) * 6
    return jax.shard_map(local, mesh=mesh, in_specs=in_specs, out_specs=out_specs, check_vma=False)
```

```python
import functools
import math

import jax
import jax.numpy as jnp
from jax import lax
from jax.experimental import pallas as pl
from jax.experimental.pallas import tpu as pltpu
from jax.sharding import PartitionSpec as P

CLEN = 512
NORM_EPS = 1e-05
MASKED_SCORE = -1e30
MESH = pl.DeviceIdType.MESH
SUB = 16
NJ = 16
TINY = 1e-20
F32 = jnp.float32
BF16 = jnp.bfloat16
VMEM = pl.BlockSpec(memory_space=pltpu.VMEM)
HBM = pl.BlockSpec(memory_space=pltpu.HBM)
SMEM = pl.BlockSpec(memory_space=pltpu.SMEM)


def shift_down(value, count):
    rows = lax.broadcasted_iota(jnp.int32, value.shape, 0)
    return jnp.where(rows >= count, pltpu.roll(value, count, 0), 0.0)


def shift_up(value, count):
    rows = lax.broadcasted_iota(jnp.int32, value.shape, 0)
    return jnp.where(rows < 8 - count, pltpu.roll(value, 8 - count, 0), 0.0)


def row_of(ref, row):
    return jnp.broadcast_to(ref[pl.ds(row, 1), :], (8, 128))


def ema_local_pass(rows, pick_rows, x_ref, decay, decay16, decay32, decay64, inner_ref, final_ref, backward):
    shift = shift_up if backward else shift_down

    first, stride, many = pick_rows

    def body(turn, carry):
        row, lane = first + stride * (turn // 4), turn % 4
        item = row * 4 + lane
        base = lane * (rows * 128) + row * 128
        dec = [row_of(decay, lane * 16 + j) for j in range(NJ)]
        state = [jnp.zeros((8, 128), F32)] * NJ
        for step in range(SUB - 1, -1, -1) if backward else range(SUB):
            x = x_ref[pl.ds(base + step, 8, stride=SUB), :]
            if backward:
                state = [dec[j] * (state[j] + x) for j in range(NJ)]
            else:
                state = [dec[j] * state[j] + x for j in range(NJ)]
        for j in range(NJ):
            total = state[j]
            total = total + row_of(decay16, lane * 16 + j) * shift(total, 1)
            total = total + row_of(decay32, lane * 16 + j) * shift(total, 2)
            total = total + row_of(decay64, lane * 16 + j) * shift(total, 4)
            inner_ref[pl.ds((item * 16 + j) * 8, 8), :] = shift(total, 1)
            final_ref[pl.ds(row * 64 + lane * 16 + j, 1), :] = total[0:1] if backward else total[7:8]
        return carry

    lax.fori_loop(0, many * 4, body, 0)


def ema_apply_pass(rows, pick_rows, x_ref, decay, mix, omega, power, inner_ref, start_ref, y_ref):
    first, many = pick_rows

    def body(turn, carry):
        row, lane = first + turn // 4, turn % 4
        item = row * 4 + lane
        base = lane * (rows * 128) + row * 128
        state = [
            inner_ref[pl.ds((item * 16 + j) * 8, 8), :]
            + power[pl.ds((lane * 16 + j) * 8, 8), :] * row_of(start_ref, row * 64 + lane * 16 + j)
            for j in range(NJ)
        ]
        skip = row_of(omega, 4 + lane)
        for step in range(SUB):
            x = x_ref[pl.ds(base + step, 8, stride=SUB), :]
            sums = [skip * x, None]
            for j in range(NJ):
                state[j] = row_of(decay, lane * 16 + j) * state[j] + x
                term = row_of(mix, lane * 16 + j) * state[j]
                sums[j % 2] = term if sums[j % 2] is None else sums[j % 2] + term
            y_ref[pl.ds(base + step, 8, stride=SUB), :] = sums[0] + sums[1]
        return carry

    lax.fori_loop(0, many * 4, body, 0)


def ema_back_pass(
    rows, x_rows, row, x_ref, g_ref, decay, mix, omega, power, inner_ref, start_ref, power_rev,
    back_inner_ref, back_start_ref, dx_ref, sum_in, sum_decay, sum_out, kept,
):
    half = 8

    def body(lane, carry):
        item = row * 4 + lane
        base = lane * (rows * 128) + row * 128
        x_base = lane * (x_rows * 128) + row * 128
        skip = row_of(omega, 4 + lane)
        for part in range(NJ // half):
            js = range(part * half, part * half + half)
            dec = [row_of(decay, lane * 16 + j) for j in js]
            state = [
                inner_ref[pl.ds((item * 16 + j) * 8, 8), :]
                + power[pl.ds((lane * 16 + j) * 8, 8), :] * row_of(start_ref, row * 64 + lane * 16 + j)
                for j in js
            ]
            for step in range(SUB):
                x = x_ref[pl.ds(x_base + step, 8, stride=SUB), :]
                for i in range(half):
                    kept[step * half + i] = state[i]
                    state[i] = dec[i] * state[i] + x
            adj = [
                back_inner_ref[pl.ds((item * 16 + j) * 8, 8), :]
                + power_rev[pl.ds((lane * 16 + j) * 8, 8), :]
                * row_of(back_start_ref, row * 64 + lane * 16 + j)
                for j in js
            ]
            weight = [row_of(mix, lane * 16 + j) for j in js]
            edge = [-(adj[i] * state[i]) for i in range(half)]
            first, second = [None] * half, [None] * half
            for step in range(SUB - 1, -1, -1):
                x = x_ref[pl.ds(x_base + step, 8, stride=SUB), :]
                g = g_ref[pl.ds(base + step, 8, stride=SUB), :]
                sums = [skip * g if part == 0 else dx_ref[pl.ds(base + step, 8, stride=SUB), :], None]
                for i in range(half):
                    full = adj[i] + g
                    term = weight[i] * full
                    sums[i % 2] = term if sums[i % 2] is None else sums[i % 2] + term
                    with_x, with_s = full * x, full * kept[step * half + i]
                    first[i] = with_x if first[i] is None else first[i] + with_x
                    second[i] = with_s if second[i] is None else second[i] + with_s
                    adj[i] = dec[i] * full
                dx_ref[pl.ds(base + step, 8, stride=SUB), :] = sums[0] + sums[1]
            for i, j in enumerate(js):
                at = pl.ds(lane * 16 + j, 1)
                flow = edge[i] + adj[i] * kept[i]
                total = jnp.sum(first[i], axis=0, keepdims=True)
                sum_in[at, :] += total
                sum_decay[at, :] += jnp.sum(second[i], axis=0, keepdims=True)
                sum_out[at, :] += total + jnp.sum(flow, axis=0, keepdims=True)
        return carry

    lax.fori_loop(0, 4, body, 0)


class Place:
    def __init__(self, n, groups):
        self.n, self.nq, self.groups = n, n // 4, groups
        self.g, self.s = lax.axis_index("grp"), lax.axis_index("seq")
        self.c, self.y, self.q, self.x = self.s % 2, (self.s // 2) % 2, self.s // 4, self.g % 2
        self.pos = self.s % 4
        self.core = (self.g, self.s + 1 - 2 * self.c)
        self.side = (self.g, self.s + 2 - 4 * self.y)
        self.cross = (self.g + 1 - 2 * self.x, self.s)
        self.is_last = self.s == n - 1

    def quad(self, k):
        return (self.q + k) % self.nq

    def at_quad(self, q):
        return (self.g, q * 4 + self.pos)

    def group_peers(self):
        return [(self.g, (self.s + k) % self.n) for k in range(1, self.n)]

    def cross_bit(self, bit):
        return (self.g + bit - 2 * bit * ((self.g // bit) % 2), self.s)

    def cross_bits(self):
        return [1 << b for b in range(self.groups.bit_length() - 1)]


def chosen(resumed, me):
    def at(p, m):
        return jnp.where(resumed[0, p * me.nq + me.q] == m, 1.0, 0.0)

    return at


def meet(peers):
    barrier = pltpu.get_barrier_semaphore()
    for peer in peers:
        pl.semaphore_signal(barrier, inc=1, device_id=peer, device_id_type=MESH)
    pl.semaphore_wait(barrier, len(peers))


def remote(src, dst, send, recv, device):
    return pltpu.make_async_remote_copy(
        src_ref=src, dst_ref=dst, send_sem=send, recv_sem=recv, device_id=device, device_id_type=MESH
    )


def pick(index, values):
    out = values[0]
    for k in range(1, len(values)):
        out = jnp.where(index == k, values[k], out)
    return out


def tail_flow(me, t, r1, w1, r2, w2, r3, out, send, recv):
    nq = me.nq
    last = me.q == nq - 1
    out[...] = jnp.zeros_like(out)
    copy1 = remote(t.at[:, 1 - me.c], r1, send.at[0], recv.at[0], me.core)
    copy1.start()
    yield
    copy1.wait()
    for i in range(2):
        w1[i] = (t[i, me.c].astype(F32) + r1[i].astype(F32)).astype(BF16)
    copy2 = remote(w1.at[1 - me.y], r2, send.at[1], recv.at[1], me.side)
    copy2.start()
    yield
    copy2.wait()
    w2[...] = (w1[me.y].astype(F32) + r2[...].astype(F32)).astype(BF16)
    top = (me.g, (nq - 1) * 4 + me.pos)
    end = (me.g, nq * 4 - 1)
    for k in range(nq - 1):
        @pl.when(me.q == k)
        def _():
            remote(w2, r3.at[k], send.at[2], recv.at[2 + k], top).start()
    yield

    @pl.when(last)
    def _():
        total = w2[...].astype(F32)
        for k in range(nq - 1):
            remote(r3.at[k], r3.at[k], send.at[2], recv.at[2 + k], me.core).wait_recv()
            total = total + r3[k].astype(F32)
        w2[...] = total.astype(BF16)

        @pl.when(jnp.logical_not(me.is_last))
        def _():
            for j in range(3):
                @pl.when(me.pos == j)
                def _():
                    remote(w2, out.at[j // 2, j % 2], send.at[2], recv.at[nq + 1 + j], end).start()

        @pl.when(me.is_last)
        def _():
            out[1, 1] = w2[...]
    yield

    @pl.when(me.is_last)
    def _():
        for j in range(3):
            dst = out.at[j // 2, j % 2]
            remote(dst, dst, send.at[2], recv.at[nq + 1 + j], me.core).wait_recv()

    @pl.when(jnp.logical_not(me.is_last))
    def _():
        remote(w2, w2, send.at[2], recv.at[2], me.core).wait_send()


def tail_scratch(nq, rows, width):
    return [
        pltpu.VMEM((2, rows, width), BF16), pltpu.VMEM((2, rows, width), BF16),
        pltpu.VMEM((rows, width), BF16), pltpu.VMEM((rows, width), BF16),
        pltpu.VMEM((nq - 1, rows, width), BF16),
    ]


class Sender:
    def __init__(self, spare):
        self.spare, self.started = spare, []

    def send(self, src, dst, send, recv, device, when=None):
        copy = remote(src, dst, send, recv, device)
        if when is None:
            copy.start()
        else:
            pl.when(when)(copy.start)
        self.started.append((copy, when))

    def got(self, ref, recv):
        remote(ref, ref, self.spare, recv, self.device).wait_recv()

    def finish(self):
        for copy, when in self.started:
            if when is None:
                copy.wait_send()
            else:
                pl.when(when)(copy.wait_send)


def small_gather(me, out, post, ss, sr):
    for k in range(1, me.n):
        post.send(out.at[me.s], out.at[me.s], ss.at[k - 1], sr.at[k - 1], (me.g, (me.s + k) % me.n))


def small_arrive(me, out, post, sr):
    for k in range(1, me.n):
        post.got(out.at[(me.s + me.n - k) % me.n], sr.at[k - 1])


def gather_flow(me, post, a_own, b_own, a_out, b_out, x_in, x_out, zs, zr, ys, yr, xs, xr, cs, cr, ts, tr, local_sem):
    nq = me.nq
    mats = ((a_out, a_out.shape[-1] // 2), (b_out, b_out.shape[-1] // 2))
    other = 1 - me.x
    piece_rows = x_out.shape[1] // 4

    def half(ref, width, which):
        return ref.at[:, pl.ds(pl.multiple_of(which * width, 128), width)]

    def quarter(ref, pos):
        return ref.at[:, pl.ds(pl.multiple_of(pos * piece_rows, piece_rows), piece_rows)]

    up, down = (me.g, me.s + 4), (me.g, me.s - 4)
    has_up, has_down = me.q < nq - 1, me.q > 0
    ours = (a_own, b_own)
    for i, (w_out, width) in enumerate(mats):
        piece, place = half(ours[i], width, me.x), half(w_out.at[me.s], width, me.x)
        post.send(piece, place, zs.at[0, 0, i], zr.at[0, 0, i], up, has_up)
        post.send(piece, place, zs.at[1, 0, i], zr.at[1, 0, i], down, has_down)
        post.send(ours[i], w_out.at[me.s], ys.at[0, i], yr.at[0, i], me.side)
    for i, (w_out, width) in enumerate(mats):
        post.send(ours[i], w_out.at[me.s], cs.at[0, i], cr.at[0, i], me.core)
    in_last = me.q == nq - 1
    keep = pltpu.make_async_copy(quarter(x_in, me.pos), quarter(x_out, me.pos), local_sem)
    pl.when(me.is_last)(keep.start)
    for j in range(3):
        post.send(quarter(x_in, j), quarter(x_out, j), ts.at[j], tr.at[0], (me.g, 4 * (nq - 1) + j), me.is_last)
    yield

    @pl.when(jnp.logical_and(in_last, jnp.logical_not(me.is_last)))
    def _():
        post.got(quarter(x_out, me.pos), tr.at[0])

    pl.when(me.is_last)(keep.wait)
    mine = quarter(x_out, me.pos)
    for k in range(1, nq):
        post.send(mine, mine, ts.at[2 + k], tr.at[1], me.at_quad(me.quad(k)), in_last)

    def arrival(side, hop):
        there = me.q - hop if side == 0 else me.q + hop
        here = there >= 0 if side == 0 else there < nq
        onward, to = (has_up, up) if side == 0 else (has_down, down)

        def pieces(pos, which):
            shard = jnp.clip(there, 0, nq - 1) * 4 + pos
            return [half(w_out.at[shard], width, which) for w_out, width in mats]

        return here, jnp.logical_and(here, onward), to, pieces

    arrivals = [(hop, side) for hop in range(1, nq) for side in range(2)]
    side_pos = me.pos + 2 - 4 * me.y
    for hop, side in arrivals:
        here, onward, to, pieces = arrival(side, hop)
        at = (hop - 1) * 2 + side
        for i, piece in enumerate(pieces(me.pos, me.x)):
            pl.when(here)(functools.partial(post.got, piece, zr.at[side, hop - 1, i]))
            if hop < nq - 1:
                post.send(piece, piece, zs.at[side, hop, i], zr.at[side, hop, i], to, onward)
            post.send(piece, piece, ys.at[1 + at, i], yr.at[1 + at, i], me.side, here)
            post.send(piece, piece, xs.at[at, i], xr.at[at, i], me.cross, here)
            post.send(piece, piece, cs.at[1 + at, i], cr.at[1 + at, i], me.core, here)
        if side:
            yield

    @pl.when(jnp.logical_not(in_last))
    def _():
        post.got(mine, tr.at[1])

    post.send(mine, mine, ts.at[nq + 2], tr.at[2], me.side)
    post.send(mine, mine, ts.at[nq + 3], tr.at[3], me.core)
    count = len(arrivals)
    for i, (w_out, width) in enumerate(mats):
        block = w_out.at[me.q * 4 + side_pos]
        post.got(block, yr.at[0, i])
        post.send(block, block, cs.at[1 + count, i], cr.at[1 + count, i], me.core)
    for hop, side in arrivals:
        here, _, _, pieces = arrival(side, hop)
        at = (hop - 1) * 2 + side
        for i, piece in enumerate(pieces(side_pos, me.x)):
            pl.when(here)(functools.partial(post.got, piece, yr.at[1 + at, i]))
            post.send(piece, piece, xs.at[count + at, i], xr.at[count + at, i], me.cross, here)
            post.send(piece, piece, cs.at[2 + count + at, i], cr.at[2 + count + at, i], me.core, here)
        if side:
            yield
    theirs = quarter(x_out, side_pos)
    post.got(theirs, tr.at[2])
    post.send(theirs, theirs, ts.at[nq + 4], tr.at[4], me.core)
    flip = 1 - 2 * me.c
    post.got(quarter(x_out, me.pos + flip), tr.at[3])
    post.got(quarter(x_out, side_pos + flip), tr.at[4])
    yield
    for group, pos in ((0, me.pos), (1, side_pos)):
        for hop, side in arrivals:
            here, _, _, pieces = arrival(side, hop)
            at = group * count + (hop - 1) * 2 + side
            to = 2 + 2 * count + at
            for i, piece in enumerate(pieces(pos, other)):
                pl.when(here)(functools.partial(post.got, piece, xr.at[at, i]))
                post.send(piece, piece, cs.at[to, i], cr.at[to, i], me.core, here)
        yield
    for group, pos in ((0, me.pos + flip), (1, side_pos + flip)):
        for i, (w_out, width) in enumerate(mats):
            post.got(w_out.at[me.q * 4 + pos], cr.at[group * (1 + count), i])
        for hop, side in arrivals:
            here, _, _, pieces = arrival(side, hop)
            at = (hop - 1) * 2 + side
            for i, piece in enumerate(pieces(pos, me.x)):
                pl.when(here)(functools.partial(post.got, piece, cr.at[group * (1 + count) + 1 + at, i]))
            for i, piece in enumerate(pieces(pos, other)):
                pl.when(here)(functools.partial(post.got, piece, cr.at[2 + 2 * count + group * count + at, i]))


def gather_sems(nq):
    count = 2 * (nq - 1)
    shapes = [(2, nq - 1, 2)] * 2 + [(1 + count, 2)] * 2 + [(2 * count, 2)] * 2 + [(2 + 4 * count, 2)] * 2 + [(nq + 5,), (5,)]
    return [pltpu.SemaphoreType.DMA(shape) for shape in shapes]


def state_flow(me, f_ref, tabs, sel, s_ref, m0, r0, m1, r1, m2, r2, ss, rs, zs, zr, ps, pr):
    nq = me.nq
    one, two, three, four = tabs[4], tabs[5], tabs[6], tabs[7]
    ab = tabs[13]
    mine = f_ref[0:384].reshape(3, 2, 64, 128)
    m0[...] = mine.astype(BF16)
    copy = remote(m0, r0, ss.at[0], rs.at[0], me.core)
    copy.start()
    yield
    copy.wait()
    upper_core, upper_side = me.c == 1, me.y == 1
    other = r0[...].astype(F32)
    lower = jnp.where(upper_core, other, mine)
    upper = jnp.where(upper_core, mine, other)
    pair = one * lower + upper
    before = jnp.where(upper_core, other, 0.0)
    m1[0] = pair.astype(BF16)
    m1[1, :, 0] = lower[:, 0].astype(BF16)
    m1[1, :, 1] = jnp.zeros((3, 64, 128), BF16)
    copy = remote(m1, r1, ss.at[1], rs.at[1], me.side)
    copy.start()
    yield
    copy.wait()
    far = r1[0].astype(F32)
    low_pair = jnp.where(upper_side, far, pair)
    high_pair = jnp.where(upper_side, pair, far)
    total = two * low_pair + high_pair
    before = jnp.where(upper_side, jnp.where(upper_core, one * far, far), 0.0) + before
    third = jnp.where(upper_side, lower[:, 0], r1[1, :, 0].astype(F32))
    last_in = one * low_pair[:, 0] + third
    m2[0] = total[:, 0].astype(BF16)
    m2[1] = last_in.astype(BF16)
    sends = []
    for k in range(1, nq):
        copy = remote(m2.at[0], r2.at[me.q], zs.at[k - 1], zr.at[k - 1], me.at_quad(me.quad(k)))
        copy.start()
        sends.append(copy)

    @pl.when(me.q == nq - 1)
    def _():
        for k in range(1, nq):
            remote(m2.at[1], r2.at[nq], ps.at[k - 1], pr.at[0], me.at_quad(me.quad(k))).start()
        r2[nq] = m2[1]

    r2[me.q] = m2[0]
    yield
    for k in range(1, nq):
        src = r2.at[me.quad(nq - k)]
        remote(src, src, zs.at[k - 1], zr.at[k - 1], me.core).wait_recv()

    @pl.when(me.q != nq - 1)
    def _():
        remote(r2.at[nq], r2.at[nq], ps.at[0], pr.at[0], me.core).wait_recv()

    run = jnp.zeros((3, 64, 128), F32)
    carry, tail_in = run, run
    for k in range(nq):
        carry = jnp.where(me.q == k, run, carry)
        if k == nq - 1:
            tail_in = three * run + r2[nq].astype(F32)
        run = four * run + r2[k].astype(F32)
    low = (ab * run).astype(BF16).astype(F32)
    safe = jnp.abs(ab) >= TINY
    begin = jnp.where(safe, low / jnp.where(safe, ab, 1.0), run)
    lead = pick(me.pos, [jnp.ones_like(one), one, two, three])
    for p in range(3):
        start = sel(p, 0) * begin[0] + sel(p, 1) * begin[1] + sel(p, 2) * begin[2]
        s_ref[128 * p : 128 * p + 64] = lead * carry[p] + before[p, 0]
        s_ref[128 * p + 64 : 128 * p + 128] = lead * start + before[p, 1]
        s_ref[384 + 64 * p : 448 + 64 * p] = tail_in[p]
    for copy in sends:
        copy.wait_send()

    @pl.when(me.q == nq - 1)
    def _():
        for k in range(1, nq):
            remote(m2.at[1], r2.at[nq], ps.at[k - 1], pr.at[0], me.at_quad(me.quad(k))).wait_send()


def front_kernel(n, groups, *refs):
    refs = list(refs)

    def take(count):
        got = refs[:count]
        del refs[:count]
        return got

    p_rates, p_vecs, (resumed,) = take(4), take(6), take(1)
    h_tokens, i_value, i_reset, i_inner, i_hidden, i_outer, i_shared = take(7)
    tabs, power, power_rev, vec_wide, vec_head, starts, w_shared = take(7)
    o_ema, o_x, o_inner, a_out, b_out, x_out = take(6)
    gathered, lift, a_own, b_own, tokens, tail, x_lanes, ema, inner, finals = take(10)
    exchange = take(6)
    load_sem, ss, sr, hs, hr = take(5)
    gather_sem = take(10)
    ess, ers, ezs, ezr, eps, epr = take(6)

    me = Place(n, groups)
    length = 128
    width = tokens.shape[1]
    lanes = width // 128
    own = tokens.shape[0]
    total = own + tail.shape[0] * length
    count = own // length
    chan = width // n
    heads = 128 // n
    rows_b = i_hidden.shape[0]
    sets = count // 2
    sel = chosen(resumed, me)

    def local_copy(src, dst, at):
        copy = pltpu.make_async_copy(src, dst, load_sem.at[at])
        copy.start()
        return copy

    x_in = h_tokens.at[:, 0]
    packing = [
        local_copy(i_value, a_own.at[0:chan], 0),
        local_copy(i_reset, a_own.at[chan : 2 * chan], 1),
        local_copy(i_inner, a_own.at[2 * chan : 3 * chan], 2),
        local_copy(i_hidden, b_own.at[0:rows_b], 3),
        local_copy(i_outer, b_own.at[rows_b : 2 * rows_b], 4),
        local_copy(i_shared, w_shared.at[me.s], 5),
    ]
    fetch = [local_copy(h_tokens.at[p, k], tokens.at[(p * 2 + k) * length : (p * 2 + k + 1) * length], 6 + p * 2 + k) for p in range(sets) for k in range(2)]
    lift[...] = jnp.zeros_like(lift)
    block = jnp.zeros((16, 128), F32)
    for i, ref in enumerate(p_rates):
        lift[i, :, 0:chan] = ref[...].astype(F32)
        block = block + pltpu.roll(lift[i], 32 * i, 1)
    for i, ref in enumerate(p_vecs):
        lift[4, i : i + 1, 0 : ref.shape[1]] = ref[...].astype(F32)
    gathered[me.s, 0:16] = block.astype(BF16)
    gathered[me.s, 16:32] = lift[4].astype(BF16)
    meet(me.group_peers() + [me.cross])
    post = Sender(load_sem.at[12])
    post.device = me.core
    small_gather(me, gathered, post, ss, sr)
    for copy in packing:
        copy.wait()
    placing = [local_copy(a_own, a_out.at[me.s], 14), local_copy(b_own, b_out.at[me.s], 15)]
    gather = gather_flow(me, post, a_own, b_own, a_out, b_out, x_in, x_out, *gather_sem, load_sem.at[13])
    next(gather)
    small_gather(me, w_shared, post, hs, hr)
    for copy in fetch:
        copy.wait()

    def norm_step(row, carry):
        here = pl.ds(pl.multiple_of(row * length, length), length)
        plain, _ = norm_rows(tokens[here, :].astype(F32))
        for lane in range(lanes):
            x_lanes[pl.ds(lane * total + row * length, length), :] = plain[:, lane * 128 : (lane + 1) * 128]
        return carry

    lax.fori_loop(0, count, norm_step, 0)
    small_arrive(me, gathered, post, sr)
    per = 128 // chan
    column = lax.broadcasted_iota(jnp.int32, (16, 128), 1)
    head_sum = jnp.zeros((16, 128), F32)
    for lane in range(lanes):
        rates = [jnp.zeros((16, 128), F32)] * 4
        wide = jnp.zeros((16, 128), F32)
        for k in range(per):
            block = gathered[lane * per + k, 0:16].astype(F32)
            for i in range(4):
                mine = jnp.where((column >= 32 * i) & (column < 32 * i + chan), block, 0.0)
                rates[i] = rates[i] + pltpu.roll(mine, (chan * k - 32 * i) % 128, 1)
            rows = gathered[lane * per + k, 16:32].astype(F32)
            wide = wide + pltpu.roll(rows, chan * k, 1)
            head_sum = head_sum + pltpu.roll(rows, heads * (lane * per + k), 1)
        for i in range(4):
            tabs[9 + i, lane * 16 : lane * 16 + 16] = rates[i]
        vec_wide[:, lane * 128 : (lane + 1) * 128] = wide[0:8]
        vec_head[4 + lane : 5 + lane] = wide[2:3]
    vec_head[0:3] = head_sum[3:6]
    vec_head[3:4] = head_sum[3:4]
    alpha, delta, beta, eta = tabs[9], tabs[10], tabs[11], tabs[12]
    decay = 1.0 - alpha * delta
    chain = [decay]
    for _ in range(9):
        chain.append(chain[-1] * chain[-1])
    ab = alpha * beta
    tabs[10], tabs[11] = beta, delta
    tabs[0], tabs[1], tabs[2], tabs[3] = decay, chain[4], chain[5], chain[6]
    tabs[4], tabs[5], tabs[6], tabs[7] = chain[7], chain[8], chain[8] * chain[7], chain[9]
    tabs[8], tabs[13] = ab * eta, ab
    d16, d32, d64 = chain[4], chain[5], chain[6]
    steps = [jnp.ones_like(decay), d16, d32, d32 * d16, d64, d64 * d16, d64 * d32, d64 * d32 * d16]
    for k in range(8):
        power[pl.ds(k, 64, stride=8), :] = steps[k]
        power_rev[pl.ds(7 - k, 64, stride=8), :] = steps[k]
    for lane in range(lanes):
        x_lanes[lane * total : lane * total + own] = x_lanes[lane * total : lane * total + own] * vec_wide[0:1, lane * 128 : (lane + 1) * 128]

    def local_pass(first, many):
        ema_local_pass(
            total // length, (first, 1, many), x_lanes, tabs.at[0], tabs.at[1], tabs.at[2], tabs.at[3], inner, finals, False
        )

    def apply_pass(first, many):
        ema_apply_pass(total // length, (first, many), x_lanes, tabs.at[0], tabs.at[8], vec_head, power, inner, starts, ema)

    def more():
        next(gather, None)

    for part in range(2):
        local_pass(part * (count // 2), count // 2)
        more()
    state = state_flow(me, finals, tabs, sel, starts, *exchange, ess, ers, ezs, ezr, eps, epr)
    next(state)
    keep = local_copy(inner.at[0 : own * 4], o_inner, 5)
    more()
    next(state)
    more()
    next(state)
    more()
    for _ in state:
        pass
    for part in range(3):
        apply_pass(part * (count // 3), count // 3)
        if part < 2:
            more()
    bring = local_copy(x_out, tail, 6)
    bring.wait()
    small_arrive(me, w_shared, post, hr)

    def tail_norm(m, carry):
        plain, _ = norm_rows(tail[m].astype(F32))
        plain = plain * vec_wide[0:1]
        for lane in range(lanes):
            x_lanes[pl.ds(lane * total + own + m * length, length), :] = plain[:, lane * 128 : (lane + 1) * 128]
        return carry

    lax.fori_loop(0, sets, tail_norm, 0)
    local_pass(count, sets)
    keep_x = local_copy(x_lanes, o_x, 7)
    more()
    apply_pass(count, sets)
    keep_ema = local_copy(ema, o_ema, 8)
    for _ in gather:
        pass
    for copy in (keep, keep_x, keep_ema, *placing):
        copy.wait()
    post.finish()


def front_call(n, groups, rates, vectors, resumed, tokens, weights):
    nq = n // 4
    dma = pltpu.SemaphoreType.DMA
    vm = pltpu.VMEM
    shape = jax.ShapeDtypeStruct
    sets, kinds, length, width = tokens.shape
    own = sets * kinds * length
    total = own + sets * length
    chan, hv = weights[0].shape
    rows_b = weights[3].shape[0]
    outs = [
        shape((14, 64, 128), F32), shape((512, 128), F32), shape((512, 128), F32), shape((8, width), F32), shape((8, 128), F32),
        shape((total // 2, 128), F32), shape((n, chan, 128), BF16),
        shape((total * 4, 128), F32), shape((total * 4, 128), F32), shape((own * 4, 128), F32),
        shape((n, 3 * chan, hv), BF16), shape((n, 2 * rows_b, width), BF16), shape((sets, length, width), BF16),
    ]
    scratch = [
        vm((n, 32, 128), BF16), vm((5, 16, 128), F32), vm((3 * chan, hv), BF16), vm((2 * rows_b, width), BF16), vm((own, width), BF16), vm((sets, length, width), BF16),
        vm((total * 4, 128), F32), vm((total * 4, 128), F32), vm((total * 4, 128), F32), vm((total // 2, 128), F32),
    ]
    scratch += [vm((3, 2, 64, 128), BF16)] * 2 + [vm((2, 3, 2, 64, 128), BF16)] * 2
    scratch += [vm((2, 3, 64, 128), BF16), vm((nq + 1, 3, 64, 128), BF16)]
    scratch += [dma((16,)), dma((n - 1,)), dma((n - 1,)), dma((n - 1,)), dma((n - 1,))]
    scratch += gather_sems(nq)
    scratch += [dma((2,)), dma((2,)), dma((nq - 1,)), dma((nq - 1,)), dma((nq - 1,)), dma((1,))]
    return pl.pallas_call(
        functools.partial(front_kernel, n, groups),
        out_shape=outs,
        in_specs=[VMEM] * 10 + [SMEM] + [HBM] * 7,
        out_specs=[VMEM] * 7 + [HBM] * 6,
        scratch_shapes=scratch,
        compiler_params=pltpu.CompilerParams(collective_id=0, has_side_effects=True, vmem_limit_bytes=60 << 20),
        name="front",
    )(*rates, *vectors, resumed, tokens, *weights)


def silu_grad(pre_act):
    sigmoid_val = jax.nn.sigmoid(pre_act)
    return sigmoid_val * (1.0 + pre_act * (1.0 - sigmoid_val))


def norm_rows(row_data):
    centered = row_data - jnp.mean(row_data, axis=-1, keepdims=True)
    scale_inv = lax.rsqrt(jnp.mean(centered * centered, axis=-1, keepdims=True) + NORM_EPS)
    return (centered * scale_inv, scale_inv)


def norm_back(grad_rows, plain, scale_inv, gain_vec):
    grad_norm = grad_rows * gain_vec
    inner_term = (
        grad_norm
        - jnp.mean(grad_norm, axis=-1, keepdims=True)
        - plain * jnp.mean(grad_norm * plain, axis=-1, keepdims=True)
    )
    return inner_term * scale_inv


def nt(lhs, rhs):
    return lax.dot_general(lhs, rhs, (((1,), (1,)), ((), ())), preferred_element_type=F32)


def tn(lhs, rhs):
    return lax.dot_general(lhs, rhs, (((0,), (0,)), ((), ())), preferred_element_type=F32)


def nn(lhs, rhs):
    return lax.dot_general(lhs, rhs, (((1,), (0,)), ((), ())), preferred_element_type=F32)


def silu_pair(pre):
    sig = jax.nn.sigmoid(pre)
    return pre * sig, sig * (1.0 + pre * (1.0 - sig))


CHUNK = 256


def dense_kernel(
    n, tok, tail, ema, cot, mats_a, mats_b, w_shared, vec_wide, vec_head, target,
    result, g_middle, g_act, g_base, slope_s, shared_out, g_units, o_outer, o_inner, o_hidden, o_reset, o_value,
    tail_keys, sum_wide, sum_head,
    w_value, w_reset, w_inner, w_hidden, w_outer, values, slope_v, t_values, t_slope, t_keys, t_dv, t_dk,
    k_units, k_activ, k_gated, k_mid, k_inner, k_branch, k_gin, k_greset, k_gvalue, reset_pre, mixed, slope_i, sem,
):
    sets = t_keys.shape[0]
    length = t_keys.shape[1]
    own = tok.shape[0]
    total = own + tail.shape[0]
    width = tok.shape[1]
    chan = w_value.shape[1]
    rows_b = w_hidden.shape[1]
    hv = w_value.shape[2]
    parts = hv // CHUNK
    scale = 1.0 / math.sqrt(128.0)
    copies = [
        pltpu.make_async_copy(mats_a.at[:, 0:chan], w_value, sem.at[0]),
        pltpu.make_async_copy(mats_a.at[:, chan : 2 * chan], w_reset, sem.at[1]),
        pltpu.make_async_copy(mats_b.at[:, 0:rows_b], w_hidden, sem.at[2]),
        pltpu.make_async_copy(mats_a.at[:, 2 * chan : 3 * chan], w_inner, sem.at[3]),
        pltpu.make_async_copy(mats_b.at[:, rows_b : 2 * rows_b], w_outer, sem.at[4]),
    ]
    for copy in copies:
        copy.start()
    gain_one, gain_two = vec_wide[0:1], vec_wide[1:2]
    q_mul, q_add, k_mul = vec_head[0:1], vec_head[1:2], vec_head[2:3]
    t_dv[...] = jnp.zeros_like(t_dv)
    t_dk[...] = jnp.zeros_like(t_dk)
    sum_wide[...] = jnp.zeros_like(sum_wide)
    sum_head[...] = jnp.zeros_like(sum_head)

    def columns(ref, at):
        block = ref[:, :, at * CHUNK : (at + 1) * CHUNK]
        return block.reshape(block.shape[0] * block.shape[1], CHUNK)

    def rows(ref, at):
        per = CHUNK // rows_b
        return ref[at * per : (at + 1) * per].reshape(CHUNK, ref.shape[2])

    def ema_rows(start, count):
        return jnp.concatenate([ema[pl.ds(lane * total + start, count), :] for lane in range(4)], axis=1)

    copies[0].wait()

    def tail_step(m, carry):
        at = pl.multiple_of(m * length, length)
        here = pl.ds(at, length)
        plain, _ = norm_rows(tail[here, :].astype(F32))
        units = (plain * gain_one).astype(BF16)
        k_units[pl.ds(own + at, length), :] = units
        for part in range(parts):
            value, slope = silu_pair(nn(units, columns(w_value, part)))
            t_values[m, :, part * CHUNK : (part + 1) * CHUNK] = value.astype(BF16)
            t_slope[m, :, part * CHUNK : (part + 1) * CHUNK] = slope.astype(BF16)
        pre = ema_rows(own + at, length)
        activ = (pre * jax.nn.sigmoid(pre)).astype(BF16)
        shared = nn(activ, w_shared[...])
        t_keys[m] = (shared * jax.nn.sigmoid(shared) * k_mul).astype(BF16)
        return carry

    lax.fori_loop(0, sets, tail_step, 0)
    for copy in copies[1:]:
        copy.wait()
    causal = lax.broadcasted_iota(jnp.int32, (length, length), 0) >= lax.broadcasted_iota(jnp.int32, (length, length), 1)

    def set_step(p, carry):
        here = pl.ds(pl.multiple_of(p * 2 * length, 2 * length), 2 * length)
        m = target[0, p * (n // 4) + lax.axis_index("seq") // 4]
        x = tok[here, :].astype(F32)
        plain, _ = norm_rows(x)
        units = (plain * gain_one).astype(BF16)
        k_units[here, :] = units
        for part in range(parts):
            cut = slice(part * CHUNK, (part + 1) * CHUNK)
            value, slope = silu_pair(nn(units, columns(w_value, part)))
            values[:, cut] = value.astype(BF16)
            slope_v[:, cut] = slope.astype(BF16)
        pre = ema_rows(p * 2 * length, 2 * length)
        activ = (pre * jax.nn.sigmoid(pre)).astype(BF16)
        k_activ[here, :] = activ
        shared, slope = silu_pair(nn(activ, w_shared[...]))
        slope_s[here, :] = slope
        shared_out[here, :] = shared
        queries = (shared * q_mul + q_add).astype(BF16)
        keys = (shared * k_mul).astype(BF16)
        for part in range(parts):
            reset_pre[:, part * CHUNK : (part + 1) * CHUNK] = nn(activ, columns(w_reset, part))
        p_q, c_q, p_k, c_k = queries[:length], queries[length:], keys[:length], keys[length:]
        e_k = t_keys[m]

        def weights(scores):
            expo = jnp.exp(scores - jnp.max(scores, axis=-1, keepdims=True))
            return expo * (1.0 / jnp.sum(expo, axis=-1, keepdims=True))

        p_probs = weights(jnp.where(causal, nt(p_q, p_k) * scale, MASKED_SCORE))
        c_probs = weights(
            jnp.concatenate((nt(c_q, e_k) * scale, jnp.where(causal, nt(c_q, c_k) * scale, MASKED_SCORE)), axis=1)
        )
        p_low, c_low = p_probs.astype(BF16), c_probs.astype(BF16)
        for part in range(parts):
            cut = slice(part * CHUNK, (part + 1) * CHUNK)
            mix_p = nn(p_low, values[:length, cut])
            mix_c = nn(c_low, jnp.concatenate((t_values[m, :, cut], values[length:, cut]), axis=0))
            mix = jnp.concatenate((mix_p, mix_c), axis=0)
            mixed[:, cut] = mix
            gate = reset_pre[:, cut]
            k_gated[here, cut] = (gate * jax.nn.sigmoid(gate) * mix).astype(BF16)
        middle = x + nn(k_gated[here, :], w_hidden[...].reshape(-1, width))
        plain_mid, inv_mid = norm_rows(middle)
        mid_low = (plain_mid * gain_two).astype(BF16)
        k_mid[here, :] = mid_low
        for part in range(parts):
            cut = slice(part * CHUNK, (part + 1) * CHUNK)
            inner, slope = silu_pair(nn(mid_low, columns(w_inner, part)))
            k_inner[here, cut] = inner.astype(BF16)
            slope_i[:, cut] = slope
        result[here, :] = (middle + nn(k_inner[here, :], w_outer[...].reshape(-1, width))).astype(BF16)
        top = cot[here, :]
        for part in range(parts):
            cut = slice(part * CHUNK, (part + 1) * CHUNK)
            k_gin[here, cut] = (nt(top, rows(w_outer, part)) * slope_i[:, cut]).astype(BF16)
        back = nt(k_gin[here, :], w_inner[...].reshape(width, -1))
        sum_wide[0:1] += jnp.sum(back * plain_mid, axis=0, keepdims=True)
        g_mid = top.astype(F32) + norm_back(back, plain_mid, inv_mid, gain_two)
        g_middle[here, :] = g_mid
        branch = g_mid.astype(BF16)
        k_branch[here, :] = branch
        dp_p = jnp.zeros((length, length), F32)
        dp_c = jnp.zeros((length, 2 * length), F32)
        for part in range(parts):
            cut = slice(part * CHUNK, (part + 1) * CHUNK)
            gated_back = nt(branch, rows(w_hidden, part))
            gate, slope = silu_pair(reset_pre[:, cut])
            g_mix = (gated_back * gate).astype(BF16)
            k_greset[here, cut] = (gated_back * mixed[:, cut] * slope).astype(BF16)
            dp_p += nt(g_mix[:length], values[:length, cut])
            dp_c += nt(g_mix[length:], jnp.concatenate((t_values[m, :, cut], values[length:, cut]), axis=0))
            dv_p = tn(p_low, g_mix[:length])
            dv_c = tn(c_low, g_mix[length:])
            t_dv[m, :, cut] += dv_c[:length]
            dv = jnp.concatenate((dv_p, dv_c[length:]), axis=0)
            k_gvalue[here, cut] = (dv * slope_v[:, cut].astype(F32)).astype(BF16)
        g_act[here, :] = nt(k_greset[here, :], w_reset[...].reshape(width, -1))

        def score_back(probs, grads):
            return (probs * (grads - jnp.sum(grads * probs, axis=-1, keepdims=True))).astype(BF16)

        p_ds, c_ds = score_back(p_probs, dp_p), score_back(c_probs, dp_c)
        d_q = jnp.concatenate((nn(p_ds, p_k), nn(c_ds, jnp.concatenate((e_k, c_k), axis=0))), axis=0) * scale
        dk_c = tn(c_ds, c_q) * scale
        t_dk[m] += dk_c[:length]
        d_k = jnp.concatenate((tn(p_ds, p_q) * scale, dk_c[length:]), axis=0)
        sum_head[0:1] += jnp.sum(d_q * shared, axis=0, keepdims=True)
        sum_head[1:2] += jnp.sum(d_q, axis=0, keepdims=True)
        sum_head[2:3] += jnp.sum(d_k * shared, axis=0, keepdims=True)
        g_base[here, :] = d_q * q_mul + d_k * k_mul
        return carry

    lax.fori_loop(0, sets, set_step, 0)
    tail_keys[...] = t_dk[...].astype(BF16)

    def tail_back(m, carry):
        at = pl.multiple_of(own + m * length, length)
        k_gvalue[pl.ds(at, length), :] = (t_dv[m] * t_slope[m].astype(F32)).astype(BF16)
        return carry

    lax.fori_loop(0, sets, tail_back, 0)

    def units_step(i, carry):
        here = pl.ds(pl.multiple_of(i * CHUNK, CHUNK), CHUNK)
        g_units[here, :] = nt(k_gvalue[here, :], w_value[...].reshape(width, -1))
        return carry

    lax.fori_loop(0, total // CHUNK, units_step, 0) if total % CHUNK == 0 else None
    if total % CHUNK:
        here = slice(total // CHUNK * CHUNK, total)
        lax.fori_loop(0, total // CHUNK, units_step, 0)
        g_units[here, :] = nt(k_gvalue[here, :], w_value[...].reshape(width, -1))

    def weight_grad(lhs, rhs, out, count):
        per = CHUNK // out.shape[1]

        def step(i, carry):
            block = tn(lhs[0:count, pl.ds(pl.multiple_of(i * CHUNK, CHUNK), CHUNK)], rhs[0:count, :])
            out[pl.ds(i * per, per)] = block.astype(BF16).reshape(per, out.shape[1], out.shape[2])
            return carry

        lax.fori_loop(0, lhs.shape[1] // CHUNK, step, 0)

    weight_grad(k_inner, cot, o_outer, own)
    weight_grad(k_mid, k_gin, o_inner, own)
    weight_grad(k_gated, k_branch, o_hidden, own)
    weight_grad(k_activ, k_greset, o_reset, own)
    weight_grad(k_units, k_gvalue, o_value, total)


def dense_call(n, tok, tail, ema, cot, mats_a, mats_b, w_shared, vec_wide, vec_head, target):
    own, width = tok.shape
    rows_t = tail.shape[0]
    total = own + rows_t
    length = 128
    sets = rows_t // length
    hv = mats_a.shape[2]
    chan = mats_a.shape[1] // 3
    rows_b = mats_b.shape[1] // 2
    shape = jax.ShapeDtypeStruct
    vm = pltpu.VMEM
    outs = [
        shape((own, width), BF16), shape((own, width), F32), shape((own, width), F32), shape((own, 128), F32),
        shape((own, 128), F32), shape((own, 128), F32), shape((total, width), F32),
        shape((n, rows_b, width), BF16), shape((n, chan, hv), BF16), shape((n, rows_b, width), BF16),
        shape((n, chan, hv), BF16), shape((n, chan, hv), BF16),
        shape((sets, length, 128), BF16), shape((8, width), F32), shape((8, 128), F32),
    ]
    scratch = [
        vm((n, chan, hv), BF16), vm((n, chan, hv), BF16), vm((n, chan, hv), BF16),
        vm((n, rows_b, width), BF16), vm((n, rows_b, width), BF16),
        vm((2 * length, hv), BF16), vm((2 * length, hv), BF16),
        vm((sets, length, hv), BF16), vm((sets, length, hv), BF16), vm((sets, length, 128), BF16),
        vm((sets, length, hv), F32), vm((sets, length, 128), F32),
        vm((total, width), BF16), vm((own, width), BF16), vm((own, hv), BF16), vm((own, width), BF16),
        vm((own, hv), BF16), vm((own, width), BF16), vm((own, hv), BF16), vm((own, hv), BF16), vm((total, hv), BF16),
        vm((2 * length, hv), F32), vm((2 * length, hv), F32), vm((2 * length, hv), F32),
        pltpu.SemaphoreType.DMA((5,)),
    ]
    return pl.pallas_call(
        functools.partial(dense_kernel, n),
        out_shape=outs,
        in_specs=[VMEM] * 4 + [HBM] * 2 + [VMEM] * 3 + [SMEM],
        out_specs=[VMEM] * len(outs),
        scratch_shapes=scratch,
        compiler_params=pltpu.CompilerParams(vmem_limit_bytes=60 << 20),
        name="dense",
    )(tok, tail, ema, cot, mats_a, mats_b, w_shared, vec_wide, vec_head, target)


def big_flow(me, cross_first, grads, r1, w1, r2, w2, r3, w3, r4, rx, out, send, recv, local_sem):
    nq = me.nq
    rows, width = out.shape
    wide = width // 2
    ours = pl.ds(pl.multiple_of(me.x * wide, 128), wide)
    others = pl.ds(pl.multiple_of((1 - me.x) * wide, 128), wide)
    copy1 = remote(grads.at[:, :, 1 - me.c], r1, send.at[0], recv.at[0], me.core)
    copy1.start()
    kept = pltpu.make_async_copy(grads.at[:, :, me.c], w1, local_sem)
    kept.start()
    yield
    kept.wait()
    copy1.wait()

    def add1(i, carry):
        w1[i // 2, i % 2] = (w1[i // 2, i % 2].astype(F32) + r1[i // 2, i % 2].astype(F32)).astype(BF16)
        return carry

    lax.fori_loop(0, 2 * nq, add1, 0)
    if cross_first:
        copy2 = remote(w1.at[:, :, :, others], r2, send.at[1], recv.at[1], me.cross)
    else:
        copy2 = remote(w1.at[:, 1 - me.y], r2, send.at[1], recv.at[1], me.side)
    copy2.start()
    yield
    copy2.wait()
    if cross_first:
        def add2(i, carry):
            w2[i // 2, i % 2] = (w1[i // 2, i % 2, :, ours].astype(F32) + r2[i // 2, i % 2].astype(F32)).astype(BF16)
            return carry

        lax.fori_loop(0, 2 * nq, add2, 0)
        copy3 = remote(w2.at[:, 1 - me.y], r3, send.at[2], recv.at[2], me.side)
    else:
        def add2(i, carry):
            w2[i] = (w1[i, me.y].astype(F32) + r2[i].astype(F32)).astype(BF16)
            return carry

        lax.fori_loop(0, nq, add2, 0)
        copy3 = remote(w2.at[:, :, others], r3, send.at[2], recv.at[2], me.cross)
    copy3.start()
    yield
    copy3.wait()

    def add3(i, carry):
        mine = w2[i, me.y] if cross_first else w2[i, :, ours]
        w3[i] = (mine.astype(F32) + r3[i].astype(F32)).astype(BF16)
        return carry

    lax.fori_loop(0, nq, add3, 0)
    copies = []
    for k in range(1, nq):
        copy = remote(w3.at[me.quad(k)], r4.at[k - 1], send.at[2 + k], recv.at[2 + k], me.at_quad(me.quad(k)))
        copy.start()
        copies.append(copy)
    yield
    total = w3[me.q].astype(F32)
    for k in range(1, nq):
        copies[k - 1].wait()
        total = total + r4[k - 1].astype(F32)
    out[:, ours] = total.astype(BF16)
    copy5 = remote(out.at[:, ours], out.at[:, ours], send.at[nq + 2], recv.at[nq + 2], me.cross)
    copy5.start()
    yield
    remote(out.at[:, others], out.at[:, others], send.at[nq + 2], recv.at[nq + 2], me.cross).wait_recv()
    copy5.wait_send()
    for at, bit in enumerate(me.cross_bits()[1:]):
        copy = remote(out, rx.at[at], send.at[nq + 3 + at], recv.at[nq + 3 + at], me.cross_bit(bit))
        copy.start()
        copy.wait()
        out[...] = (out[...].astype(F32) + rx[at].astype(F32)).astype(BF16)


def big_scratch(nq, groups, cross_first, rows, width):
    extra = max(groups.bit_length() - 2, 1)
    half = width // 2
    full = [pltpu.VMEM((nq, 2, rows, width), BF16)] * 2
    if cross_first:
        mid = [pltpu.VMEM((nq, 2, rows, half), BF16)] * 2
    else:
        mid = [pltpu.VMEM((nq, rows, width), BF16)] * 2
    return full + mid + [
        pltpu.VMEM((nq, rows, half), BF16), pltpu.VMEM((nq, rows, half), BF16),
        pltpu.VMEM((nq - 1, rows, half), BF16), pltpu.VMEM((extra, rows, width), BF16),
    ]


def small_flow(me, grads, r1, w1, r2, w2, rx, out, send, recv):
    many = 2 * me.nq
    copy1 = remote(grads.at[:, 1 - me.c], r1, send.at[0], recv.at[0], me.core)
    copy1.start()
    yield
    copy1.wait()

    def add(i, carry):
        w1[i] = (grads[i, me.c].astype(F32) + r1[i].astype(F32)).astype(BF16)
        return carry

    lax.fori_loop(0, many, add, 0)
    mine = me.q * 2 + me.y
    copies = []
    for k in range(1, many):
        to = (mine + k) % many
        copy = remote(w1.at[to], r2.at[k - 1], send.at[k], recv.at[k], (me.g, to * 2 + me.c))
        copy.start()
        copies.append(copy)
    yield
    total = w1[mine].astype(F32)
    for k in range(1, many):
        copies[k - 1].wait()
        total = total + r2[k - 1].astype(F32)
    bits = me.cross_bits()
    for at, bit in enumerate(bits):
        w2[at] = total.astype(BF16)
        copy = remote(w2.at[at], rx.at[at], send.at[many + at], recv.at[many + at], me.cross_bit(bit))
        copy.start()
        if at == 0:
            yield
        copy.wait()
        total = total + rx[at].astype(F32)
    out[...] = total.astype(BF16)


def small_scratch(nq, groups, rows):
    bits = groups.bit_length() - 1
    return [
        pltpu.VMEM((2 * nq, rows, 128), BF16), pltpu.VMEM((2 * nq, rows, 128), BF16),
        pltpu.VMEM((2 * nq - 1, rows, 128), BF16), pltpu.VMEM((bits, rows, 128), BF16), pltpu.VMEM((bits, rows, 128), BF16),
    ]


def adjoint_flow(me, f_ref, tabs, sel, s_ref, m0, r0, m1, r1, m2, r2, ss, rs, zs, zr):
    nq = me.nq
    one, two, three, four = tabs[4], tabs[5], tabs[6], tabs[7]
    mine = f_ref[...].reshape(3, 2, 64, 128)
    m0[...] = mine.astype(BF16)
    copy = remote(m0, r0, ss.at[0], rs.at[0], me.core)
    copy.start()
    yield
    copy.wait()
    upper_core, upper_side = me.c == 1, me.y == 1
    other = r0[...].astype(F32)
    lower = jnp.where(upper_core, other, mine)
    upper = jnp.where(upper_core, mine, other)
    pair = lower + one * upper
    after = jnp.where(upper_core, 0.0, other)
    m1[...] = pair.astype(BF16)
    copy = remote(m1, r1, ss.at[1], rs.at[1], me.side)
    copy.start()
    yield
    copy.wait()
    far = r1[...].astype(F32)
    low_pair = jnp.where(upper_side, far, pair)
    high_pair = jnp.where(upper_side, pair, far)
    total = low_pair + two * high_pair
    after = jnp.where(upper_side, 0.0, jnp.where(upper_core, far, one * far)) + after
    m2[0] = total[:, 0].astype(BF16)
    for m in range(3):
        m2[1, m] = (sel(0, m) * total[0, 1] + sel(1, m) * total[1, 1] + sel(2, m) * total[2, 1]).astype(BF16)
    sends = []
    for k in range(1, nq):
        copy = remote(m2, r2.at[me.q], zs.at[k - 1], zr.at[k - 1], me.at_quad(me.quad(k)))
        copy.start()
        sends.append(copy)
    r2[me.q] = m2[...]
    yield
    for k in range(1, nq):
        src = r2.at[me.quad(nq - k)]
        remote(src, src, zs.at[k - 1], zr.at[k - 1], me.core).wait_recv()
    run = r2[0, 1].astype(F32)
    for k in range(1, nq):
        run = run + r2[k, 1].astype(F32)
    carry = run
    for k in range(nq - 1, -1, -1):
        carry = jnp.where(me.q == k, run, carry)
        run = four * run + r2[k, 0].astype(F32)
    lead = pick(me.pos, [three, two, one, jnp.ones_like(one)])
    for p in range(3):
        s_ref[2 * p * 64 : (2 * p + 1) * 64] = lead * carry[p] + after[p, 0]
        s_ref[(2 * p + 1) * 64 : (2 * p + 2) * 64] = after[p, 1]
    for copy in sends:
        copy.wait_send()


class Steps:
    def __init__(self, flows):
        self.flows, self.live = flows, [True] * len(flows)

    def __call__(self, *which):
        for i in which:
            if self.live[i]:
                try:
                    next(self.flows[i])
                except StopIteration:
                    self.live[i] = False

    def finish(self):
        while any(self.live):
            self(*range(len(self.flows)))


ORDERS = (True, False, True, False, True)
N_BIG = 5


def back_kernel(n, groups, *refs):
    refs = list(refs)

    def take(count):
        got = refs[:count]
        del refs[:count]
        return got

    base, slope_s, shared, t_keys, w_shared, tabs, power, power_rev, vec_wide, vec_head, starts, sum_wide, sum_head, resumed = take(14)
    h_act, h_ema, h_x, h_inner, h_units, h_middle, h_tokens, h_tail = take(8)
    grads = take(N_BIG)
    (input_grad,) = take(1)
    outs = take(N_BIG)
    (out_small,) = take(1)
    loads = take(7)
    g_act, ema, x_lanes, inner, g_units, g_middle, tokens = loads
    g_lanes, k_activ, k_gs, b_inner, b_flow, b_start, dx_lanes, acc_in, acc_decay, acc_out, kept, omega_acc, gain_acc = take(13)
    t_sum, t_rows, t_grad, t_out, grad_in, g_small = take(6)
    big = [take(8) for _ in range(N_BIG)]
    small = take(5)
    keys_s, tail_s = take(5), take(5)
    exchange = take(6)
    load_sem, big_send, big_recv, big_local, small_send, small_recv, k_send, k_recv, t_send, t_recv, ess, ers, ezs, ezr = take(14)

    me = Place(n, groups)
    own = base.shape[0]
    total = tokens.shape[0]
    width = tokens.shape[1]
    length = 128
    count = own // length
    lanes = width // 128
    chan = width // n
    sel = chosen(resumed, me)
    hbm = [h_act, h_ema, h_x, h_inner, h_units, h_middle, h_tokens, h_tail]
    places = loads[:6] + [tokens.at[0:own], tokens.at[own:total]]
    arrive = [pltpu.make_async_copy(src, dst, load_sem.at[i]) for i, (src, dst) in enumerate(zip(hbm, places))]
    for copy in arrive:
        copy.start()
    meet(me.group_peers() + [me.cross_bit(bit) for bit in me.cross_bits()])
    keys = tail_flow(me, t_keys, *keys_s, t_sum, k_send, k_recv)
    next(keys)
    steps = Steps(
        [
            big_flow(me, ORDERS[i], grads[i], *big[i], outs[i], big_send.at[i], big_recv.at[i], big_local.at[i])
            for i in range(N_BIG)
        ]
    )
    steps(*range(N_BIG))
    k_mul = vec_head[2:3]
    gain_one = vec_wide[0:1]
    for ref in (omega_acc, gain_acc, acc_in, acc_decay, acc_out):
        ref[...] = jnp.zeros_like(ref)
    for i in range(3):
        arrive[i].wait()

    def grad_rows(row, with_tail):
        at = pl.multiple_of(row * length, length)
        here = pl.ds(at, length)
        d_shared = base[here, :]
        if with_tail:
            extra = t_rows[pl.ds(pl.multiple_of(row // 2 * length, length), length), :]
            d_shared = d_shared + extra * k_mul
            gain_acc[1:2, 0:128] += jnp.sum(extra * shared[here, :], axis=0, keepdims=True)
        gs = (d_shared * slope_s[here, :]).astype(BF16)
        k_gs[here, :] = gs
        for lane in range(lanes):
            cut = slice(lane * 128, (lane + 1) * 128)
            pre = ema[pl.ds(lane * total + at, length), :]
            sig = jax.nn.sigmoid(pre)
            k_activ[here, cut] = (pre * sig).astype(BF16)
            back = g_act[here, cut] + nt(gs, w_shared[cut, :])
            back = back * (sig * (1.0 + pre * (1.0 - sig)))
            g_lanes[pl.ds(lane * own + at, length), :] = back
            x = x_lanes[pl.ds(lane * total + at, length), :]
            omega_acc[lane : lane + 1] += jnp.sum(back * x, axis=0, keepdims=True)

    def local_pass(first):
        ema_local_pass(
            count, (first, 2, count // 2), g_lanes, tabs.at[0], tabs.at[1], tabs.at[2], tabs.at[3], b_inner, b_flow, True
        )

    def cont_rows(p, carry):
        grad_rows(2 * p + 1, False)
        return carry

    def prompt_rows(p, carry):
        grad_rows(2 * p, True)
        return carry

    def norm_rows_back(at, size, extra):
        here = pl.ds(at, size)
        plain, inv = norm_rows(tokens[here, :].astype(F32))
        units = g_units[here, :]
        if extra is not None:
            units = units + extra
        gain_acc[0:1] += jnp.sum(units * plain, axis=0, keepdims=True)
        return norm_back(units, plain, inv, gain_one)

    lax.fori_loop(0, count // 2, cont_rows, 0)
    next(keys)
    steps(0, 1)
    local_pass(1)
    next(keys)
    steps(2, 3)
    arrive[4].wait()
    arrive[6].wait()
    arrive[7].wait()
    piece = (total - own) // 4
    for part in range(4):
        t_grad[part // 2, part % 2] = norm_rows_back(own + part * piece, piece, None).astype(BF16)
    tail = tail_flow(me, t_grad, *tail_s, t_out, t_send, t_recv)
    next(tail)
    next(keys)
    steps(4)
    for _ in keys:
        pass
    for part in range(4):
        t_rows[part * piece : (part + 1) * piece] = t_sum[part // 2, part % 2].astype(F32)
    lax.fori_loop(0, count // 2, prompt_rows, 0)
    local_pass(0)
    adjoint = adjoint_flow(me, b_flow, tabs, sel, b_start, *exchange, ess, ers, ezs, ezr)
    next(adjoint)
    steps(0, 1)
    next(adjoint)
    next(tail)
    steps(2)
    next(adjoint)
    next(tail)
    steps(3)
    for _ in adjoint:
        pass
    arrive[3].wait()
    for row in range(count):
        ema_back_pass(
            count, total // length, row, x_lanes, g_lanes, tabs.at[0], tabs.at[8], vec_head, power, inner, starts,
            power_rev, b_inner, b_start, dx_lanes, acc_in, acc_decay, acc_out, kept,
        )
        if row == 0:
            steps(4)
            next(tail)
        elif row < count - 1:
            steps(*range(N_BIG))
    arrive[5].wait()

    def own_rows(row, carry):
        at = pl.multiple_of(row * length, length)
        extra = jnp.concatenate([dx_lanes[pl.ds(lane * own + at, length), :] for lane in range(lanes)], axis=1)
        grad_in[pl.ds(at, length), :] = g_middle[pl.ds(at, length), :] + norm_rows_back(at, length, extra)
        return carry

    lax.fori_loop(0, count, own_rows, 0)
    alpha, beta, delta, eta, ab = (tabs[9 + i] for i in range(5))
    m_sum, q_sum = eta * acc_in[...], eta * ab * acc_decay[...]
    parts = (beta * m_sum - delta * q_sum, -alpha * q_sum, alpha * m_sum, ab * acc_out[...])
    per = 128 // chan // 2
    for lane in range(lanes):
        cut = slice(lane * 128, (lane + 1) * 128)
        block = [part[lane * 16 : lane * 16 + 16] for part in parts]
        block += [omega_acc[lane : lane + 1], gain_acc[0:1, cut], sum_wide[0:1, cut], jnp.zeros((61, 128), F32)]
        block = jnp.concatenate(block, axis=0).T.astype(BF16)
        g_small[lane * per : (lane + 1) * per, :, 0:chan] = block.reshape(per, 2, chan, 128)
    block = tn(k_activ[...], k_gs[...]).astype(BF16)
    g_small[:, :, chan : 2 * chan] = block.reshape(n // 2, 2, chan, 128)
    heads = jnp.concatenate((sum_head[0:2], sum_head[2:3] + gain_acc[1:2, 0:128], jnp.zeros((13, 128), F32)), axis=0)
    heads = jnp.broadcast_to(heads.astype(BF16)[None, None], (n // 2, 2, 16, 128))
    g_small[:, :, 2 * chan :] = heads
    little = small_flow(me, g_small, *small, out_small, small_send, small_recv)
    next(little)
    for _ in tail:
        pass
    next(little)
    steps(*range(N_BIG))

    def cast_rows(row, carry):
        here = pl.ds(pl.multiple_of(row * length, length), length)
        input_grad[here, :] = grad_in[here, :].astype(BF16)
        return carry

    for part in range(4):
        t_wide = t_out[part // 2, part % 2].astype(F32)
        at = part * piece
        while at < (part + 1) * piece:
            m = at // length
            stop = min((m + 1) * length, (part + 1) * piece)
            here = slice(at + m * length, stop + m * length)
            grad_in[here] = grad_in[here] + t_wide[at - part * piece : stop - part * piece]
            at = stop
    lax.fori_loop(0, count, cast_rows, 0)
    next(little)
    steps(*range(N_BIG))
    for _ in little:
        pass
    steps.finish()


def back_call(n, groups, ins, hbm, grads):
    nq = n // 4
    dma = pltpu.SemaphoreType.DMA
    vm = pltpu.VMEM
    shape = jax.ShapeDtypeStruct
    own, width = hbm[6].shape
    total = own + hbm[7].shape[0]
    chan = width // n
    small_rows = 2 * chan + 16
    piece = (total - own) // 4
    outs = [shape((own, width), BF16)] + [shape(grad.shape[-2:], BF16) for grad in grads] + [shape((small_rows, 128), BF16)]
    scratch = [vm(part.shape, part.dtype) for part in hbm[:6]] + [vm((total, width), BF16)]
    scratch += [
        vm((own * 4, 128), F32), vm((own, width), BF16), vm((own, 128), BF16), vm((own * 4, 128), F32),
        vm((own // 2, 128), F32), vm((own // 2, 128), F32), vm((own * 4, 128), F32), vm((64, 128), F32), vm((64, 128), F32),
        vm((64, 128), F32), vm((128, 8, 128), F32), vm((8, 128), F32), vm((8, width), F32),
        vm((2, 2, piece, 128), BF16), vm((4 * piece, 128), F32), vm((2, 2, piece, width), BF16), vm((2, 2, piece, width), BF16),
        vm((own, width), F32), vm((n // 2, 2, small_rows, 128), BF16),
    ]
    for i, grad in enumerate(grads):
        scratch += big_scratch(nq, groups, ORDERS[i], grad.shape[-2], grad.shape[-1])
    scratch += small_scratch(nq, groups, small_rows)
    scratch += tail_scratch(nq, piece, 128) + tail_scratch(nq, piece, width)
    scratch += [vm((3, 2, 64, 128), BF16)] * 4 + [vm((2, 3, 64, 128), BF16), vm((nq, 2, 3, 64, 128), BF16)]
    sems = nq + 3 + max(groups.bit_length() - 2, 1)
    small_sems = 2 * nq + groups.bit_length() - 1
    scratch += [
        dma((8,)), dma((N_BIG, sems)), dma((N_BIG, sems)), dma((N_BIG,)), dma((small_sems,)), dma((small_sems,)),
        dma((3,)), dma((nq + 4,)), dma((3,)), dma((nq + 4,)), dma((2,)), dma((2,)), dma((nq - 1,)), dma((nq - 1,)),
    ]
    return pl.pallas_call(
        functools.partial(back_kernel, n, groups),
        out_shape=outs,
        in_specs=[VMEM] * 13 + [SMEM] + [HBM] * (8 + N_BIG),
        out_specs=[VMEM] * len(outs),
        scratch_shapes=scratch,
        compiler_params=pltpu.CompilerParams(collective_id=2, has_side_effects=True, vmem_limit_bytes=60 << 20),
        name="back",
    )(*ins, *hbm, *grads)


def finish_kernel(heads, grad_in, *refs):
    sums, small, grad_out = refs[:N_BIG], refs[N_BIG], refs[N_BIG + 1]
    outs = refs[N_BIG + 2 : 2 * N_BIG + 2]
    shared, rates, vecs = refs[2 * N_BIG + 2], refs[2 * N_BIG + 3 : 2 * N_BIG + 7], refs[2 * N_BIG + 7 : 2 * N_BIG + 13]
    grad_out[...] = grad_in[...]
    for src, dst in zip(sums, outs):
        dst[...] = src[...].astype(F32)
    chan = shared.shape[0]
    shared[...] = small[chan : 2 * chan].astype(F32)
    block = small[0:chan].astype(F32).T
    for i, ref in enumerate(rates):
        ref[...] = block[16 * i : 16 * i + 16]
    for i in range(3):
        vecs[i][...] = block[64 + i : 65 + i]
    mine = lax.axis_index("seq") * heads
    rows = pltpu.roll(small[2 * chan : 2 * chan + 16].astype(F32), (128 - mine) % 128, 1)
    for i in range(3):
        vecs[3 + i][...] = rows[i : i + 1, 0:heads]


def finish_call(n, heads, input_grad, sums, small):
    shape = jax.ShapeDtypeStruct
    chan = (small.shape[0] - 16) // 2
    outs = [shape(input_grad.shape, BF16)] + [shape(part.shape, F32) for part in sums] + [shape((chan, 128), F32)]
    outs += [shape((16, chan), F32)] * 4 + [shape((1, chan), F32)] * 3 + [shape((1, heads), F32)] * 3
    return pl.pallas_call(
        functools.partial(finish_kernel, heads),
        out_shape=outs,
        in_specs=[VMEM] * (N_BIG + 2),
        out_specs=[VMEM] * len(outs),
        compiler_params=pltpu.CompilerParams(vmem_limit_bytes=60 << 20),
        name="finish",
    )(input_grad, *sums, small)


def local(
    hidden_in, cotangent, cont_prompt, value_proj, shared_proj, reset_proj, hidden_proj, inner_proj,
    outer_proj, ema_alpha, ema_delta, ema_beta, ema_eta, ema_omega, norm_gain, ffn_gain, query_scale,
    query_shift, key_scale,
):
    n, groups = lax.axis_size("seq"), lax.axis_size("grp")
    nq = n // 4
    seq_index = lax.axis_index("seq")
    sets, kinds, length, width = hidden_in.shape[1:]
    chan = width // n
    heads = query_scale.shape[0]
    own_rows = sets * kinds * length
    vectors = (norm_gain, ffn_gain, ema_omega, query_scale, query_shift, key_scale)
    (
        tabs, power, power_rev, vec_wide, vec_head, starts, mat_shared, ema_lanes, x_lanes, inner, all_a, all_b, tail_low,
    ) = front_call(
        n, groups, [part.T for part in (ema_alpha, ema_delta, ema_beta, ema_eta)], [part[None] for part in vectors],
        cont_prompt, hidden_in[0],
        (value_proj, reset_proj, inner_proj, hidden_proj, outer_proj, shared_proj),
    )
    mat_shared = mat_shared.reshape(width, 128)
    own_low, tail_low = hidden_in[0].reshape(own_rows, width), tail_low.reshape(-1, width)
    grad_outer = cotangent[0].reshape(own_rows, width)
    (
        result, grad_middle, grad_act, grad_base, slope_shared, shared, grad_units, sum_outer, sum_inner, sum_hidden,
        sum_reset, sum_value, sent_keys, sum_wide, sum_head,
    ) = dense_call(
        n, own_low, tail_low, ema_lanes, grad_outer, all_a, all_b, mat_shared, vec_wide, vec_head, cont_prompt
    )

    def shards(grad):
        return grad.reshape(nq, 2, 2, -1, grad.shape[-1])

    ins = (
        grad_base, slope_shared, shared, sent_keys.reshape(2, 2, -1, 128), mat_shared, tabs, power, power_rev, vec_wide,
        vec_head, starts, sum_wide, sum_head, cont_prompt,
    )
    hbm = (grad_act, ema_lanes, x_lanes, inner, grad_units, grad_middle, own_low, tail_low)
    grads = [shards(part) for part in (sum_outer, sum_inner, sum_hidden, sum_reset, sum_value)]
    input_grad, *sums, d_small = back_call(n, groups, ins, hbm, grads)
    wide = finish_call(n, heads, input_grad, sums, d_small)
    input_grad, d_outer, d_inner, d_hidden, d_reset, d_value, d_shared = wide[:7]
    rates = [part.T for part in wide[7:11]]
    vecs = [part.reshape(part.shape[1]) for part in wide[11:17]]
    return (
        result.reshape(hidden_in.shape), input_grad.reshape(hidden_in.shape), d_value, d_shared, d_reset, d_hidden, d_inner,
        d_outer, *rates, *vecs,
    )


def solution(mesh):
    mat, vec = P("seq", None), P("seq")
    tok = P("grp", None, None, "seq", None)
    in_specs = (tok, tok, P("grp", None)) + (mat,) * 10 + (vec,) * 6
    out_specs = (tok, tok) + (mat,) * 10 + (vec,) * 6
    return jax.shard_map(local, mesh=mesh, in_specs=in_specs, out_specs=out_specs, check_vma=False)
```

```python
import functools
import math

import jax
import jax.numpy as jnp
from jax import lax
from jax.experimental import pallas as pl
from jax.experimental.pallas import tpu as pltpu
from jax.sharding import PartitionSpec as P

CLEN = 512
NORM_EPS = 1e-05
MASKED_SCORE = -1e30
MESH = pl.DeviceIdType.MESH
SUB = 16
NJ = 16
TINY = 1e-20
F32 = jnp.float32
BF16 = jnp.bfloat16
VMEM = pl.BlockSpec(memory_space=pltpu.VMEM)
HBM = pl.BlockSpec(memory_space=pltpu.HBM)
SMEM = pl.BlockSpec(memory_space=pltpu.SMEM)


def shift_down(value, count):
    rows = lax.broadcasted_iota(jnp.int32, value.shape, 0)
    return jnp.where(rows >= count, pltpu.roll(value, count, 0), 0.0)


def shift_up(value, count):
    rows = lax.broadcasted_iota(jnp.int32, value.shape, 0)
    return jnp.where(rows < 8 - count, pltpu.roll(value, 8 - count, 0), 0.0)


def row_of(ref, row):
    return jnp.broadcast_to(ref[pl.ds(row, 1), :], (8, 128))


def ema_local_pass(rows, pick_rows, x_ref, decay, decay16, decay32, decay64, inner_ref, final_ref, backward):
    shift = shift_up if backward else shift_down

    first, stride, many = pick_rows

    def body(turn, carry):
        row, lane = first + stride * (turn // 4), turn % 4
        item = row * 4 + lane
        base = lane * (rows * 128) + row * 128
        dec = [row_of(decay, lane * 16 + j) for j in range(NJ)]
        state = [jnp.zeros((8, 128), F32)] * NJ
        for step in range(SUB - 1, -1, -1) if backward else range(SUB):
            x = x_ref[pl.ds(base + step, 8, stride=SUB), :]
            if backward:
                state = [dec[j] * (state[j] + x) for j in range(NJ)]
            else:
                state = [dec[j] * state[j] + x for j in range(NJ)]
        for j in range(NJ):
            total = state[j]
            total = total + row_of(decay16, lane * 16 + j) * shift(total, 1)
            total = total + row_of(decay32, lane * 16 + j) * shift(total, 2)
            total = total + row_of(decay64, lane * 16 + j) * shift(total, 4)
            inner_ref[pl.ds((item * 16 + j) * 8, 8), :] = shift(total, 1)
            final_ref[pl.ds(row * 64 + lane * 16 + j, 1), :] = total[0:1] if backward else total[7:8]
        return carry

    lax.fori_loop(0, many * 4, body, 0)


def ema_apply_pass(rows, pick_rows, x_ref, decay, mix, omega, power, inner_ref, start_ref, y_ref):
    first, many = pick_rows

    def body(turn, carry):
        row, lane = first + turn // 4, turn % 4
        item = row * 4 + lane
        base = lane * (rows * 128) + row * 128
        state = [
            inner_ref[pl.ds((item * 16 + j) * 8, 8), :]
            + power[pl.ds((lane * 16 + j) * 8, 8), :] * row_of(start_ref, row * 64 + lane * 16 + j)
            for j in range(NJ)
        ]
        skip = row_of(omega, 4 + lane)
        for step in range(SUB):
            x = x_ref[pl.ds(base + step, 8, stride=SUB), :]
            sums = [skip * x, None]
            for j in range(NJ):
                state[j] = row_of(decay, lane * 16 + j) * state[j] + x
                term = row_of(mix, lane * 16 + j) * state[j]
                sums[j % 2] = term if sums[j % 2] is None else sums[j % 2] + term
            y_ref[pl.ds(base + step, 8, stride=SUB), :] = sums[0] + sums[1]
        return carry

    lax.fori_loop(0, many * 4, body, 0)


def ema_back_pass(
    rows, x_rows, row, x_ref, g_ref, decay, mix, omega, power, inner_ref, start_ref, power_rev,
    back_inner_ref, back_start_ref, dx_ref, sum_in, sum_decay, sum_out, kept,
):
    half = 8

    def body(lane, carry):
        item = row * 4 + lane
        base = lane * (rows * 128) + row * 128
        x_base = lane * (x_rows * 128) + row * 128
        skip = row_of(omega, 4 + lane)
        for part in range(NJ // half):
            js = range(part * half, part * half + half)
            dec = [row_of(decay, lane * 16 + j) for j in js]
            state = [
                inner_ref[pl.ds((item * 16 + j) * 8, 8), :]
                + power[pl.ds((lane * 16 + j) * 8, 8), :] * row_of(start_ref, row * 64 + lane * 16 + j)
                for j in js
            ]
            for step in range(SUB):
                x = x_ref[pl.ds(x_base + step, 8, stride=SUB), :]
                for i in range(half):
                    kept[step * half + i] = state[i]
                    state[i] = dec[i] * state[i] + x
            adj = [
                back_inner_ref[pl.ds((item * 16 + j) * 8, 8), :]
                + power_rev[pl.ds((lane * 16 + j) * 8, 8), :]
                * row_of(back_start_ref, row * 64 + lane * 16 + j)
                for j in js
            ]
            weight = [row_of(mix, lane * 16 + j) for j in js]
            edge = [-(adj[i] * state[i]) for i in range(half)]
            first, second = [None] * half, [None] * half
            for step in range(SUB - 1, -1, -1):
                x = x_ref[pl.ds(x_base + step, 8, stride=SUB), :]
                g = g_ref[pl.ds(base + step, 8, stride=SUB), :]
                sums = [skip * g if part == 0 else dx_ref[pl.ds(base + step, 8, stride=SUB), :], None]
                for i in range(half):
                    full = adj[i] + g
                    term = weight[i] * full
                    sums[i % 2] = term if sums[i % 2] is None else sums[i % 2] + term
                    with_x, with_s = full * x, full * kept[step * half + i]
                    first[i] = with_x if first[i] is None else first[i] + with_x
                    second[i] = with_s if second[i] is None else second[i] + with_s
                    adj[i] = dec[i] * full
                dx_ref[pl.ds(base + step, 8, stride=SUB), :] = sums[0] + sums[1]
            for i, j in enumerate(js):
                at = pl.ds(lane * 16 + j, 1)
                flow = edge[i] + adj[i] * kept[i]
                total = jnp.sum(first[i], axis=0, keepdims=True)
                sum_in[at, :] += total
                sum_decay[at, :] += jnp.sum(second[i], axis=0, keepdims=True)
                sum_out[at, :] += total + jnp.sum(flow, axis=0, keepdims=True)
        return carry

    lax.fori_loop(0, 4, body, 0)


class Place:
    def __init__(self, n, groups):
        self.n, self.nq, self.groups = n, n // 4, groups
        self.g, self.s = lax.axis_index("grp"), lax.axis_index("seq")
        self.c, self.y, self.q, self.x = self.s % 2, (self.s // 2) % 2, self.s // 4, self.g % 2
        self.pos = self.s % 4
        self.core = (self.g, self.s + 1 - 2 * self.c)
        self.side = (self.g, self.s + 2 - 4 * self.y)
        self.cross = (self.g + 1 - 2 * self.x, self.s)
        self.is_last = self.s == n - 1

    def quad(self, k):
        return (self.q + k) % self.nq

    def at_quad(self, q):
        return (self.g, q * 4 + self.pos)

    def group_peers(self):
        return [(self.g, (self.s + k) % self.n) for k in range(1, self.n)]

    def cross_bit(self, bit):
        return (self.g + bit - 2 * bit * ((self.g // bit) % 2), self.s)

    def cross_bits(self):
        return [1 << b for b in range(self.groups.bit_length() - 1)]


def chosen(resumed, me):
    def at(p, m):
        return jnp.where(resumed[0, p * me.nq + me.q] == m, 1.0, 0.0)

    return at


def meet(peers):
    barrier = pltpu.get_barrier_semaphore()
    for peer in peers:
        pl.semaphore_signal(barrier, inc=1, device_id=peer, device_id_type=MESH)
    pl.semaphore_wait(barrier, len(peers))


def remote(src, dst, send, recv, device):
    return pltpu.make_async_remote_copy(
        src_ref=src, dst_ref=dst, send_sem=send, recv_sem=recv, device_id=device, device_id_type=MESH
    )


def pick(index, values):
    out = values[0]
    for k in range(1, len(values)):
        out = jnp.where(index == k, values[k], out)
    return out


def tail_flow(me, t, r1, w1, r2, w2, r3, out, send, recv):
    nq = me.nq
    last = me.q == nq - 1
    out[...] = jnp.zeros_like(out)
    copy1 = remote(t.at[:, 1 - me.c], r1, send.at[0], recv.at[0], me.core)
    copy1.start()
    yield
    copy1.wait()
    for i in range(2):
        w1[i] = (t[i, me.c].astype(F32) + r1[i].astype(F32)).astype(BF16)
    copy2 = remote(w1.at[1 - me.y], r2, send.at[1], recv.at[1], me.side)
    copy2.start()
    yield
    copy2.wait()
    w2[...] = (w1[me.y].astype(F32) + r2[...].astype(F32)).astype(BF16)
    top = (me.g, (nq - 1) * 4 + me.pos)
    end = (me.g, nq * 4 - 1)
    for k in range(nq - 1):
        @pl.when(me.q == k)
        def _():
            remote(w2, r3.at[k], send.at[2], recv.at[2 + k], top).start()
    yield

    @pl.when(last)
    def _():
        total = w2[...].astype(F32)
        for k in range(nq - 1):
            remote(r3.at[k], r3.at[k], send.at[2], recv.at[2 + k], me.core).wait_recv()
            total = total + r3[k].astype(F32)
        w2[...] = total.astype(BF16)

        @pl.when(jnp.logical_not(me.is_last))
        def _():
            for j in range(3):
                @pl.when(me.pos == j)
                def _():
                    remote(w2, out.at[j // 2, j % 2], send.at[2], recv.at[nq + 1 + j], end).start()

        @pl.when(me.is_last)
        def _():
            out[1, 1] = w2[...]
    yield

    @pl.when(me.is_last)
    def _():
        for j in range(3):
            dst = out.at[j // 2, j % 2]
            remote(dst, dst, send.at[2], recv.at[nq + 1 + j], me.core).wait_recv()

    @pl.when(jnp.logical_not(me.is_last))
    def _():
        remote(w2, w2, send.at[2], recv.at[2], me.core).wait_send()


def tail_scratch(nq, rows, width):
    return [
        pltpu.VMEM((2, rows, width), BF16), pltpu.VMEM((2, rows, width), BF16),
        pltpu.VMEM((rows, width), BF16), pltpu.VMEM((rows, width), BF16),
        pltpu.VMEM((nq - 1, rows, width), BF16),
    ]


class Sender:
    def __init__(self, spare):
        self.spare, self.started = spare, []

    def send(self, src, dst, send, recv, device, when=None):
        copy = remote(src, dst, send, recv, device)
        if when is None:
            copy.start()
        else:
            pl.when(when)(copy.start)
        self.started.append((copy, when))

    def got(self, ref, recv):
        remote(ref, ref, self.spare, recv, self.device).wait_recv()

    def finish(self):
        for copy, when in self.started:
            if when is None:
                copy.wait_send()
            else:
                pl.when(when)(copy.wait_send)


def small_gather(me, out, post, ss, sr):
    for k in range(1, me.n):
        post.send(out.at[me.s], out.at[me.s], ss.at[k - 1], sr.at[k - 1], (me.g, (me.s + k) % me.n))


def small_arrive(me, out, post, sr):
    for k in range(1, me.n):
        post.got(out.at[(me.s + me.n - k) % me.n], sr.at[k - 1])


def gather_flow(me, post, mats, zs, zr, ys, yr, xs, xr, cs, cr):
    nq = me.nq
    mats = [(own, out, out.shape[-1] // 2) for own, out in mats]
    other = 1 - me.x

    def half(ref, width, which):
        return ref.at[:, pl.ds(pl.multiple_of(which * width, 128), width)]

    up, down = (me.g, me.s + 4), (me.g, me.s - 4)
    has_up, has_down = me.q < nq - 1, me.q > 0
    for i, (own, out, width) in enumerate(mats):
        piece, place = half(own, width, me.x), half(out.at[me.s], width, me.x)
        post.send(piece, place, zs.at[0, 0, i], zr.at[0, 0, i], up, has_up)
        post.send(piece, place, zs.at[1, 0, i], zr.at[1, 0, i], down, has_down)
        post.send(own, out.at[me.s], ys.at[0, i], yr.at[0, i], me.side)
    for i, (own, out, width) in enumerate(mats):
        post.send(own, out.at[me.s], cs.at[0, i], cr.at[0, i], me.core)
    yield

    def arrival(side, hop):
        there = me.q - hop if side == 0 else me.q + hop
        here = there >= 0 if side == 0 else there < nq
        onward, to = (has_up, up) if side == 0 else (has_down, down)

        def pieces(pos, which):
            shard = jnp.clip(there, 0, nq - 1) * 4 + pos
            return [half(out.at[shard], width, which) for _, out, width in mats]

        return here, jnp.logical_and(here, onward), to, pieces

    arrivals = [(hop, side) for hop in range(1, nq) for side in range(2)]
    side_pos = me.pos + 2 - 4 * me.y
    for hop, side in arrivals:
        here, onward, to, pieces = arrival(side, hop)
        at = (hop - 1) * 2 + side
        for i, piece in enumerate(pieces(me.pos, me.x)):
            pl.when(here)(functools.partial(post.got, piece, zr.at[side, hop - 1, i]))
            if hop < nq - 1:
                post.send(piece, piece, zs.at[side, hop, i], zr.at[side, hop, i], to, onward)
            post.send(piece, piece, ys.at[1 + at, i], yr.at[1 + at, i], me.side, here)
            post.send(piece, piece, xs.at[at, i], xr.at[at, i], me.cross, here)
            post.send(piece, piece, cs.at[1 + at, i], cr.at[1 + at, i], me.core, here)
        if side:
            yield
    count = len(arrivals)
    for i, (_, out, _) in enumerate(mats):
        block = out.at[me.q * 4 + side_pos]
        post.got(block, yr.at[0, i])
        post.send(block, block, cs.at[1 + count, i], cr.at[1 + count, i], me.core)
    for hop, side in arrivals:
        here, _, _, pieces = arrival(side, hop)
        at = (hop - 1) * 2 + side
        for i, piece in enumerate(pieces(side_pos, me.x)):
            pl.when(here)(functools.partial(post.got, piece, yr.at[1 + at, i]))
            post.send(piece, piece, xs.at[count + at, i], xr.at[count + at, i], me.cross, here)
            post.send(piece, piece, cs.at[2 + count + at, i], cr.at[2 + count + at, i], me.core, here)
        if side:
            yield
    flip = 1 - 2 * me.c
    for group, pos in ((0, me.pos), (1, side_pos)):
        for hop, side in arrivals:
            here, _, _, pieces = arrival(side, hop)
            at = group * count + (hop - 1) * 2 + side
            to = 2 + 2 * count + at
            for i, piece in enumerate(pieces(pos, other)):
                pl.when(here)(functools.partial(post.got, piece, xr.at[at, i]))
                post.send(piece, piece, cs.at[to, i], cr.at[to, i], me.core, here)
        yield
    for group, pos in ((0, me.pos + flip), (1, side_pos + flip)):
        for i, (_, out, _) in enumerate(mats):
            post.got(out.at[me.q * 4 + pos], cr.at[group * (1 + count), i])
        for hop, side in arrivals:
            here, _, _, pieces = arrival(side, hop)
            at = (hop - 1) * 2 + side
            for i, piece in enumerate(pieces(pos, me.x)):
                pl.when(here)(functools.partial(post.got, piece, cr.at[group * (1 + count) + 1 + at, i]))
            for i, piece in enumerate(pieces(pos, other)):
                pl.when(here)(functools.partial(post.got, piece, cr.at[2 + 2 * count + group * count + at, i]))


def tokens_flow(me, post, x_in, x_out, ts, tr, local_sem):
    nq = me.nq
    rows = x_out.shape[1] // 4

    def quarter(ref, pos):
        return ref.at[:, pl.ds(pl.multiple_of(pos * rows, rows), rows)]

    in_last = me.q == nq - 1
    side_pos, flip = me.pos + 2 - 4 * me.y, 1 - 2 * me.c
    keep = pltpu.make_async_copy(quarter(x_in, me.pos), quarter(x_out, me.pos), local_sem)
    pl.when(me.is_last)(keep.start)
    for j in range(3):
        post.send(quarter(x_in, j), quarter(x_out, j), ts.at[j], tr.at[0], (me.g, 4 * (nq - 1) + j), me.is_last)
    yield

    @pl.when(jnp.logical_and(in_last, jnp.logical_not(me.is_last)))
    def _():
        post.got(quarter(x_out, me.pos), tr.at[0])

    pl.when(me.is_last)(keep.wait)
    mine = quarter(x_out, me.pos)
    for k in range(1, nq):
        post.send(mine, mine, ts.at[2 + k], tr.at[1], me.at_quad(me.quad(k)), in_last)
    yield

    @pl.when(jnp.logical_not(in_last))
    def _():
        post.got(mine, tr.at[1])

    post.send(mine, mine, ts.at[nq + 2], tr.at[2], me.side)
    post.send(mine, mine, ts.at[nq + 3], tr.at[3], me.core)
    yield
    theirs = quarter(x_out, side_pos)
    post.got(theirs, tr.at[2])
    post.send(theirs, theirs, ts.at[nq + 4], tr.at[4], me.core)
    yield
    post.got(quarter(x_out, me.pos + flip), tr.at[3])
    post.got(quarter(x_out, side_pos + flip), tr.at[4])


def gather_sems(nq, mats):
    count = 2 * (nq - 1)
    shapes = [(2, nq - 1, mats)] * 2 + [(1 + count, mats)] * 2 + [(2 * count, mats)] * 2 + [(2 + 4 * count, mats)] * 2
    return [pltpu.SemaphoreType.DMA(shape) for shape in shapes]


def state_flow(me, f_ref, tabs, sel, s_ref, m0, r0, m1, r1, m2, r2, ss, rs, zs, zr, ps, pr):
    nq = me.nq
    one, two, three, four = tabs[4], tabs[5], tabs[6], tabs[7]
    ab = tabs[13]
    mine = f_ref[0:384].reshape(3, 2, 64, 128)
    m0[...] = mine.astype(BF16)
    copy = remote(m0, r0, ss.at[0], rs.at[0], me.core)
    copy.start()
    yield
    copy.wait()
    upper_core, upper_side = me.c == 1, me.y == 1
    other = r0[...].astype(F32)
    lower = jnp.where(upper_core, other, mine)
    upper = jnp.where(upper_core, mine, other)
    pair = one * lower + upper
    before = jnp.where(upper_core, other, 0.0)
    m1[0] = pair.astype(BF16)
    m1[1, :, 0] = lower[:, 0].astype(BF16)
    m1[1, :, 1] = jnp.zeros((3, 64, 128), BF16)
    copy = remote(m1, r1, ss.at[1], rs.at[1], me.side)
    copy.start()
    yield
    copy.wait()
    far = r1[0].astype(F32)
    low_pair = jnp.where(upper_side, far, pair)
    high_pair = jnp.where(upper_side, pair, far)
    total = two * low_pair + high_pair
    before = jnp.where(upper_side, jnp.where(upper_core, one * far, far), 0.0) + before
    third = jnp.where(upper_side, lower[:, 0], r1[1, :, 0].astype(F32))
    last_in = one * low_pair[:, 0] + third
    m2[0] = total[:, 0].astype(BF16)
    m2[1] = last_in.astype(BF16)
    sends = []
    for k in range(1, nq):
        copy = remote(m2.at[0], r2.at[me.q], zs.at[k - 1], zr.at[k - 1], me.at_quad(me.quad(k)))
        copy.start()
        sends.append(copy)

    @pl.when(me.q == nq - 1)
    def _():
        for k in range(1, nq):
            remote(m2.at[1], r2.at[nq], ps.at[k - 1], pr.at[0], me.at_quad(me.quad(k))).start()
        r2[nq] = m2[1]

    r2[me.q] = m2[0]
    yield
    for k in range(1, nq):
        src = r2.at[me.quad(nq - k)]
        remote(src, src, zs.at[k - 1], zr.at[k - 1], me.core).wait_recv()

    @pl.when(me.q != nq - 1)
    def _():
        remote(r2.at[nq], r2.at[nq], ps.at[0], pr.at[0], me.core).wait_recv()

    run = jnp.zeros((3, 64, 128), F32)
    carry, tail_in = run, run
    for k in range(nq):
        carry = jnp.where(me.q == k, run, carry)
        if k == nq - 1:
            tail_in = three * run + r2[nq].astype(F32)
        run = four * run + r2[k].astype(F32)
    low = (ab * run).astype(BF16).astype(F32)
    safe = jnp.abs(ab) >= TINY
    begin = jnp.where(safe, low / jnp.where(safe, ab, 1.0), run)
    lead = pick(me.pos, [jnp.ones_like(one), one, two, three])
    for p in range(3):
        start = sel(p, 0) * begin[0] + sel(p, 1) * begin[1] + sel(p, 2) * begin[2]
        s_ref[128 * p : 128 * p + 64] = lead * carry[p] + before[p, 0]
        s_ref[128 * p + 64 : 128 * p + 128] = lead * start + before[p, 1]
        s_ref[384 + 64 * p : 448 + 64 * p] = tail_in[p]
    for copy in sends:
        copy.wait_send()

    @pl.when(me.q == nq - 1)
    def _():
        for k in range(1, nq):
            remote(m2.at[1], r2.at[nq], ps.at[k - 1], pr.at[0], me.at_quad(me.quad(k))).wait_send()


def silu_grad(pre_act):
    sigmoid_val = jax.nn.sigmoid(pre_act)
    return sigmoid_val * (1.0 + pre_act * (1.0 - sigmoid_val))


def norm_rows(row_data):
    centered = row_data - jnp.mean(row_data, axis=-1, keepdims=True)
    scale_inv = lax.rsqrt(jnp.mean(centered * centered, axis=-1, keepdims=True) + NORM_EPS)
    return (centered * scale_inv, scale_inv)


def norm_back(grad_rows, plain, scale_inv, gain_vec):
    grad_norm = grad_rows * gain_vec
    inner_term = (
        grad_norm
        - jnp.mean(grad_norm, axis=-1, keepdims=True)
        - plain * jnp.mean(grad_norm * plain, axis=-1, keepdims=True)
    )
    return inner_term * scale_inv


def nt(lhs, rhs):
    return lax.dot_general(lhs, rhs, (((1,), (1,)), ((), ())), preferred_element_type=F32)


def tn(lhs, rhs):
    return lax.dot_general(lhs, rhs, (((0,), (0,)), ((), ())), preferred_element_type=F32)


def nn(lhs, rhs):
    return lax.dot_general(lhs, rhs, (((1,), (0,)), ((), ())), preferred_element_type=F32)


def silu_pair(pre):
    sig = jax.nn.sigmoid(pre)
    return pre * sig, sig * (1.0 + pre * (1.0 - sig))


CHUNK = 256


def layer_kernel(n, groups, *refs):
    refs = list(refs)

    def take(count):
        got = refs[:count]
        del refs[:count]
        return got

    p_rates, p_vecs, (resumed,) = take(4), take(6), take(1)
    cot, h_tokens, i_value, i_reset, i_inner, i_hidden, i_outer, i_shared = take(8)
    tabs, power, power_rev, vec_wide, vec_head, starts, w_shared = take(7)
    (
        result, g_middle, g_act, g_base, slope_s, shared_out, g_units, o_outer, o_inner, o_hidden, o_reset, o_value,
        tail_keys, sum_wide, sum_head,
    ) = take(15)
    o_ema, o_x, o_state, o_tail = take(4)
    gathered, lift, tok, tail, x_lanes, ema, inner, finals = take(8)
    early_own, hidden_own, inner_own, outer_own, early_all, w_hidden, w_inner, w_outer = take(8)
    (
        values, slope_v, t_values, t_slope, t_keys, t_dv, t_dk, k_units, k_activ, k_gated, k_mid, k_inner, k_branch, k_gin,
        k_greset, k_gvalue, reset_pre, mixed, slope_i,
    ) = take(19)
    exchange = take(6)
    load_sem, ss, sr, hs, hr, ts, tr = take(7)
    early_sem, late_sem = take(8), take(8)
    ess, ers, ezs, ezr, eps, epr = take(6)

    me = Place(n, groups)
    length = 128
    width = tok.shape[1]
    lanes = width // 128
    own = tok.shape[0]
    total = own + tail.shape[0] * length
    count = own // length
    chan = width // n
    heads = 128 // n
    rows_b = i_hidden.shape[0]
    sets = count // 2
    sel = chosen(resumed, me)

    def local_copy(src, dst, at):
        copy = pltpu.make_async_copy(src, dst, load_sem.at[at])
        copy.start()
        return copy

    x_in = h_tokens.at[:, 0]
    packing = [
        local_copy(i_value, early_own.at[0:chan], 0),
        local_copy(i_reset, early_own.at[chan : 2 * chan], 1),
        local_copy(i_hidden, hidden_own, 2),
        local_copy(i_inner, inner_own, 3),
        local_copy(i_outer, outer_own, 4),
        local_copy(i_shared, w_shared.at[me.s], 5),
    ]
    fetch = [local_copy(h_tokens.at[p, k], tok.at[(p * 2 + k) * length : (p * 2 + k + 1) * length], 6 + p * 2 + k) for p in range(sets) for k in range(2)]
    lift[...] = jnp.zeros_like(lift)
    block = jnp.zeros((16, 128), F32)
    for i, ref in enumerate(p_rates):
        lift[i, :, 0:chan] = ref[...].astype(F32)
        block = block + pltpu.roll(lift[i], 32 * i, 1)
    for i, ref in enumerate(p_vecs):
        lift[4, i : i + 1, 0 : ref.shape[1]] = ref[...].astype(F32)
    gathered[me.s, 0:16] = block.astype(BF16)
    gathered[me.s, 16:32] = lift[4].astype(BF16)
    meet(me.group_peers() + [me.cross])
    post = Sender(load_sem.at[12])
    post.device = me.core
    small_gather(me, gathered, post, ss, sr)
    for copy in packing:
        copy.wait()
    pairs = ((early_own, early_all), (hidden_own, w_hidden), (inner_own, w_inner), (outer_own, w_outer))
    early = gather_flow(me, post, pairs[:1], *early_sem)
    late = gather_flow(me, post, pairs[1:], *late_sem)
    words = tokens_flow(me, post, x_in, tail, ts, tr, load_sem.at[13])
    next(early)
    next(words)
    next(late)
    placing = [local_copy(own_part, all_part.at[me.s], 14 + i) for i, (own_part, all_part) in enumerate(pairs)]
    small_gather(me, w_shared, post, hs, hr)
    for copy in fetch:
        copy.wait()

    def norm_step(row, carry):
        here = pl.ds(pl.multiple_of(row * length, length), length)
        plain, _ = norm_rows(tok[here, :].astype(F32))
        for lane in range(lanes):
            x_lanes[pl.ds(lane * total + row * length, length), :] = plain[:, lane * 128 : (lane + 1) * 128]
        return carry

    lax.fori_loop(0, count, norm_step, 0)
    small_arrive(me, gathered, post, sr)
    per = 128 // chan
    column = lax.broadcasted_iota(jnp.int32, (16, 128), 1)
    head_sum = jnp.zeros((16, 128), F32)
    for lane in range(lanes):
        rates = [jnp.zeros((16, 128), F32)] * 4
        wide = jnp.zeros((16, 128), F32)
        for k in range(per):
            block = gathered[lane * per + k, 0:16].astype(F32)
            for i in range(4):
                mine = jnp.where((column >= 32 * i) & (column < 32 * i + chan), block, 0.0)
                rates[i] = rates[i] + pltpu.roll(mine, (chan * k - 32 * i) % 128, 1)
            rows = gathered[lane * per + k, 16:32].astype(F32)
            wide = wide + pltpu.roll(rows, chan * k, 1)
            head_sum = head_sum + pltpu.roll(rows, heads * (lane * per + k), 1)
        for i in range(4):
            tabs[9 + i, lane * 16 : lane * 16 + 16] = rates[i]
        vec_wide[:, lane * 128 : (lane + 1) * 128] = wide[0:8]
        vec_head[4 + lane : 5 + lane] = wide[2:3]
    vec_head[0:3] = head_sum[3:6]
    vec_head[3:4] = head_sum[3:4]
    alpha, delta, beta, eta = tabs[9], tabs[10], tabs[11], tabs[12]
    decay = 1.0 - alpha * delta
    chain = [decay]
    for _ in range(9):
        chain.append(chain[-1] * chain[-1])
    ab = alpha * beta
    tabs[10], tabs[11] = beta, delta
    tabs[0], tabs[1], tabs[2], tabs[3] = decay, chain[4], chain[5], chain[6]
    tabs[4], tabs[5], tabs[6], tabs[7] = chain[7], chain[8], chain[8] * chain[7], chain[9]
    tabs[8], tabs[13] = ab * eta, ab
    d16, d32, d64 = chain[4], chain[5], chain[6]
    steps = [jnp.ones_like(decay), d16, d32, d32 * d16, d64, d64 * d16, d64 * d32, d64 * d32 * d16]
    for k in range(8):
        power[pl.ds(k, 64, stride=8), :] = steps[k]
        power_rev[pl.ds(7 - k, 64, stride=8), :] = steps[k]
    for lane in range(lanes):
        x_lanes[lane * total : lane * total + own] = x_lanes[lane * total : lane * total + own] * vec_wide[0:1, lane * 128 : (lane + 1) * 128]

    def local_pass(first, many):
        ema_local_pass(
            total // length, (first, 1, many), x_lanes, tabs.at[0], tabs.at[1], tabs.at[2], tabs.at[3], inner, finals, False
        )

    def apply_pass(first, many):
        ema_apply_pass(total // length, (first, many), x_lanes, tabs.at[0], tabs.at[8], vec_head, power, inner, starts, ema)

    def step(*flows):
        for flow in flows:
            next(flow, None)

    step(words, early)
    local_pass(0, count // 2)
    step(late, early)
    local_pass(count // 2, count // 2)
    state = state_flow(me, finals, tabs, sel, starts, *exchange, ess, ers, ezs, ezr, eps, epr)
    step(state)
    keep = [local_copy(inner.at[0 : own * 4], o_state, 0)]
    step(late, early)
    step(state)
    step(words, early, late)
    step(state)
    step(early, early)
    step(state)
    step(words)
    for part in range(3):
        apply_pass(part * (count // 3), count // 3)
        step(early)
        if part:
            step(late)
    for _ in words:
        pass
    keep.append(local_copy(tail, o_tail, 1))

    def tail_norm(m, carry):
        plain, _ = norm_rows(tail[m].astype(F32))
        plain = plain * vec_wide[0:1]
        for lane in range(lanes):
            x_lanes[pl.ds(lane * total + own + m * length, length), :] = plain[:, lane * 128 : (lane + 1) * 128]
        return carry

    lax.fori_loop(0, sets, tail_norm, 0)
    local_pass(count, sets)
    keep.append(local_copy(x_lanes, o_x, 2))
    step(late)
    apply_pass(count, sets)
    keep.append(local_copy(ema, o_ema, 3))
    small_arrive(me, w_shared, post, hr)
    for _ in early:
        pass
    for copy in placing:
        copy.wait()
    w_value, w_reset = early_all.at[:, 0:chan], early_all.at[:, chan : 2 * chan]
    hv = w_value.shape[2]
    parts = hv // CHUNK
    scale = 1.0 / math.sqrt(128.0)

    def ready(name):
        if name == "hidden":
            for _ in late:
                pass
        elif name in ("tail", "reset"):
            step(late)

    gain_one, gain_two = vec_wide[0:1], vec_wide[1:2]
    q_mul, q_add, k_mul = vec_head[0:1], vec_head[1:2], vec_head[2:3]
    t_dv[...] = jnp.zeros_like(t_dv)
    t_dk[...] = jnp.zeros_like(t_dk)
    sum_wide[...] = jnp.zeros_like(sum_wide)
    sum_head[...] = jnp.zeros_like(sum_head)

    def columns(ref, at):
        block = ref[:, :, at * CHUNK : (at + 1) * CHUNK]
        return block.reshape(block.shape[0] * block.shape[1], CHUNK)

    def rows(ref, at):
        per = CHUNK // rows_b
        return ref[at * per : (at + 1) * per].reshape(CHUNK, ref.shape[2])

    def ema_rows(start, count):
        return jnp.concatenate([ema[pl.ds(lane * total + start, count), :] for lane in range(4)], axis=1)

    def tail_step(m, carry):
        at = pl.multiple_of(m * length, length)
        plain, _ = norm_rows(tail[m].astype(F32))
        units = (plain * gain_one).astype(BF16)
        k_units[pl.ds(own + at, length), :] = units
        for part in range(parts):
            value, slope = silu_pair(nn(units, columns(w_value, part)))
            t_values[m, :, part * CHUNK : (part + 1) * CHUNK] = value.astype(BF16)
            t_slope[m, :, part * CHUNK : (part + 1) * CHUNK] = slope.astype(BF16)
        pre = ema_rows(own + at, length)
        activ = (pre * jax.nn.sigmoid(pre)).astype(BF16)
        shared = nn(activ, w_shared[...].reshape(width, 128))
        t_keys[m] = (shared * jax.nn.sigmoid(shared) * k_mul).astype(BF16)
        return carry

    lax.fori_loop(0, sets, tail_step, 0)
    ready("tail")
    causal = lax.broadcasted_iota(jnp.int32, (length, length), 0) >= lax.broadcasted_iota(jnp.int32, (length, length), 1)

    def set_step(p, ready):
        here = pl.ds(pl.multiple_of(p * 2 * length, 2 * length), 2 * length)
        m = resumed[0, p * me.nq + me.q]
        x = tok[here, :].astype(F32)
        plain, _ = norm_rows(x)
        units = (plain * gain_one).astype(BF16)
        k_units[here, :] = units
        for part in range(parts):
            cut = slice(part * CHUNK, (part + 1) * CHUNK)
            value, slope = silu_pair(nn(units, columns(w_value, part)))
            values[:, cut] = value.astype(BF16)
            slope_v[:, cut] = slope.astype(BF16)
        ready("reset")
        pre = ema_rows(p * 2 * length, 2 * length)
        activ = (pre * jax.nn.sigmoid(pre)).astype(BF16)
        k_activ[here, :] = activ
        shared, slope = silu_pair(nn(activ, w_shared[...].reshape(width, 128)))
        slope_s[here, :] = slope
        shared_out[here, :] = shared
        queries = (shared * q_mul + q_add).astype(BF16)
        keys = (shared * k_mul).astype(BF16)
        for part in range(parts):
            reset_pre[:, part * CHUNK : (part + 1) * CHUNK] = nn(activ, columns(w_reset, part))
        p_q, c_q, p_k, c_k = queries[:length], queries[length:], keys[:length], keys[length:]
        e_k = t_keys[m]

        def weights(scores):
            expo = jnp.exp(scores - jnp.max(scores, axis=-1, keepdims=True))
            return expo * (1.0 / jnp.sum(expo, axis=-1, keepdims=True))

        p_probs = weights(jnp.where(causal, nt(p_q, p_k) * scale, MASKED_SCORE))
        c_probs = weights(
            jnp.concatenate((nt(c_q, e_k) * scale, jnp.where(causal, nt(c_q, c_k) * scale, MASKED_SCORE)), axis=1)
        )
        p_low, c_low = p_probs.astype(BF16), c_probs.astype(BF16)
        for part in range(parts):
            cut = slice(part * CHUNK, (part + 1) * CHUNK)
            mix_p = nn(p_low, values[:length, cut])
            mix_c = nn(c_low, jnp.concatenate((t_values[m, :, cut], values[length:, cut]), axis=0))
            mix = jnp.concatenate((mix_p, mix_c), axis=0)
            mixed[:, cut] = mix
            gate = reset_pre[:, cut]
            k_gated[here, cut] = (gate * jax.nn.sigmoid(gate) * mix).astype(BF16)
        ready("hidden")
        middle = x + nn(k_gated[here, :], w_hidden[...].reshape(-1, width))
        plain_mid, inv_mid = norm_rows(middle)
        mid_low = (plain_mid * gain_two).astype(BF16)
        k_mid[here, :] = mid_low
        ready("inner")
        for part in range(parts):
            cut = slice(part * CHUNK, (part + 1) * CHUNK)
            inner, slope = silu_pair(nn(mid_low, columns(w_inner, part)))
            k_inner[here, cut] = inner.astype(BF16)
            slope_i[:, cut] = slope
        ready("outer")
        result[here, :] = (middle + nn(k_inner[here, :], w_outer[...].reshape(-1, width))).astype(BF16)
        top = cot[here, :]
        for part in range(parts):
            cut = slice(part * CHUNK, (part + 1) * CHUNK)
            k_gin[here, cut] = (nt(top, rows(w_outer, part)) * slope_i[:, cut]).astype(BF16)
        back = nt(k_gin[here, :], w_inner[...].reshape(width, -1))
        sum_wide[0:1] += jnp.sum(back * plain_mid, axis=0, keepdims=True)
        g_mid = top.astype(F32) + norm_back(back, plain_mid, inv_mid, gain_two)
        g_middle[here, :] = g_mid
        branch = g_mid.astype(BF16)
        k_branch[here, :] = branch
        dp_p = jnp.zeros((length, length), F32)
        dp_c = jnp.zeros((length, 2 * length), F32)
        for part in range(parts):
            cut = slice(part * CHUNK, (part + 1) * CHUNK)
            gated_back = nt(branch, rows(w_hidden, part))
            gate, slope = silu_pair(reset_pre[:, cut])
            g_mix = (gated_back * gate).astype(BF16)
            k_greset[here, cut] = (gated_back * mixed[:, cut] * slope).astype(BF16)
            dp_p += nt(g_mix[:length], values[:length, cut])
            dp_c += nt(g_mix[length:], jnp.concatenate((t_values[m, :, cut], values[length:, cut]), axis=0))
            dv_p = tn(p_low, g_mix[:length])
            dv_c = tn(c_low, g_mix[length:])
            for to in range(sets):
                t_dv[to, :, cut] += sel(p, to) * dv_c[:length]
            dv = jnp.concatenate((dv_p, dv_c[length:]), axis=0)
            k_gvalue[here, cut] = (dv * slope_v[:, cut].astype(F32)).astype(BF16)
        g_act[here, :] = nt(k_greset[here, :], w_reset[...].reshape(width, -1))

        def score_back(probs, grads):
            return (probs * (grads - jnp.sum(grads * probs, axis=-1, keepdims=True))).astype(BF16)

        p_ds, c_ds = score_back(p_probs, dp_p), score_back(c_probs, dp_c)
        d_q = jnp.concatenate((nn(p_ds, p_k), nn(c_ds, jnp.concatenate((e_k, c_k), axis=0))), axis=0) * scale
        dk_c = tn(c_ds, c_q) * scale
        for to in range(sets):
            t_dk[to] += sel(p, to) * dk_c[:length]
        d_k = jnp.concatenate((tn(p_ds, p_q) * scale, dk_c[length:]), axis=0)
        sum_head[0:1] += jnp.sum(d_q * shared, axis=0, keepdims=True)
        sum_head[1:2] += jnp.sum(d_q, axis=0, keepdims=True)
        sum_head[2:3] += jnp.sum(d_k * shared, axis=0, keepdims=True)
        g_base[here, :] = d_q * q_mul + d_k * k_mul

    def quiet(name):
        return None

    def later_step(p, carry):
        set_step(p, quiet)
        return carry

    set_step(0, ready)
    lax.fori_loop(1, sets, later_step, 0)
    tail_keys[...] = t_dk[...].astype(BF16)

    def tail_back(m, carry):
        at = pl.multiple_of(own + m * length, length)
        k_gvalue[pl.ds(at, length), :] = (t_dv[m] * t_slope[m].astype(F32)).astype(BF16)
        return carry

    lax.fori_loop(0, sets, tail_back, 0)

    def units_step(i, carry):
        here = pl.ds(pl.multiple_of(i * CHUNK, CHUNK), CHUNK)
        g_units[here, :] = nt(k_gvalue[here, :], w_value[...].reshape(width, -1))
        return carry

    lax.fori_loop(0, total // CHUNK, units_step, 0)
    if total % CHUNK:
        here = slice(total // CHUNK * CHUNK, total)
        g_units[here, :] = nt(k_gvalue[here, :], w_value[...].reshape(width, -1))

    def weight_grad(lhs, rhs, out, count):
        per = CHUNK // out.shape[1]

        def step(i, carry):
            block = tn(lhs[0:count, pl.ds(pl.multiple_of(i * CHUNK, CHUNK), CHUNK)], rhs[0:count, :])
            out[pl.ds(i * per, per)] = block.astype(BF16).reshape(per, out.shape[1], out.shape[2])
            return carry

        lax.fori_loop(0, lhs.shape[1] // CHUNK, step, 0)

    weight_grad(k_inner, cot, o_outer, own)
    weight_grad(k_mid, k_gin, o_inner, own)
    weight_grad(k_gated, k_branch, o_hidden, own)
    weight_grad(k_activ, k_greset, o_reset, own)
    weight_grad(k_units, k_gvalue, o_value, total)


    for copy in keep:
        copy.wait()
    post.finish()


def layer_call(n, groups, rates, vectors, resumed, cot, tokens, weights):
    nq = n // 4
    dma = pltpu.SemaphoreType.DMA
    vm = pltpu.VMEM
    shape = jax.ShapeDtypeStruct
    sets, kinds, length, width = tokens.shape
    own = sets * kinds * length
    total = own + sets * length
    chan, hv = weights[0].shape
    rows_b = weights[3].shape[0]
    outs = [
        shape((14, 64, 128), F32), shape((512, 128), F32), shape((512, 128), F32), shape((8, width), F32), shape((8, 128), F32),
        shape((total // 2, 128), F32), shape((n, chan, 128), BF16),
        shape((own, width), BF16), shape((own, width), F32), shape((own, width), F32), shape((own, 128), F32),
        shape((own, 128), F32), shape((own, 128), F32), shape((total, width), F32),
        shape((n, rows_b, width), BF16), shape((n, chan, hv), BF16), shape((n, rows_b, width), BF16),
        shape((n, chan, hv), BF16), shape((n, chan, hv), BF16),
        shape((sets, length, 128), BF16), shape((8, width), F32), shape((8, 128), F32),
        shape((total * 4, 128), F32), shape((total * 4, 128), F32), shape((own * 4, 128), F32), shape((sets, length, width), BF16),
    ]
    scratch = [
        vm((n, 32, 128), BF16), vm((5, 16, 128), F32), vm((own, width), BF16), vm((sets, length, width), BF16),
        vm((total * 4, 128), F32), vm((total * 4, 128), F32), vm((total * 4, 128), F32), vm((total // 2, 128), F32),
        vm((2 * chan, hv), BF16), vm((rows_b, width), BF16), vm((chan, hv), BF16), vm((rows_b, width), BF16),
        vm((n, 2 * chan, hv), BF16), vm((n, rows_b, width), BF16), vm((n, chan, hv), BF16), vm((n, rows_b, width), BF16),
        vm((2 * length, hv), BF16), vm((2 * length, hv), BF16),
        vm((sets, length, hv), BF16), vm((sets, length, hv), BF16), vm((sets, length, 128), BF16),
        vm((sets, length, hv), F32), vm((sets, length, 128), F32),
        vm((total, width), BF16), vm((own, width), BF16), vm((own, hv), BF16), vm((own, width), BF16),
        vm((own, hv), BF16), vm((own, width), BF16), vm((own, hv), BF16), vm((own, hv), BF16), vm((total, hv), BF16),
        vm((2 * length, hv), F32), vm((2 * length, hv), F32), vm((2 * length, hv), F32),
    ]
    scratch += [vm((3, 2, 64, 128), BF16)] * 2 + [vm((2, 3, 2, 64, 128), BF16)] * 2
    scratch += [vm((2, 3, 64, 128), BF16), vm((nq + 1, 3, 64, 128), BF16)]
    scratch += [dma((18,)), dma((n - 1,)), dma((n - 1,)), dma((n - 1,)), dma((n - 1,)), dma((nq + 5,)), dma((5,))]
    scratch += gather_sems(nq, 1) + gather_sems(nq, 3)
    scratch += [dma((2,)), dma((2,)), dma((nq - 1,)), dma((nq - 1,)), dma((nq - 1,)), dma((1,))]
    return pl.pallas_call(
        functools.partial(layer_kernel, n, groups),
        out_shape=outs,
        in_specs=[VMEM] * 10 + [SMEM, VMEM] + [HBM] * 7,
        out_specs=[VMEM] * 22 + [HBM] * 4,
        scratch_shapes=scratch,
        compiler_params=pltpu.CompilerParams(collective_id=0, has_side_effects=True, vmem_limit_bytes=62 << 20),
        name="layer",
    )(*rates, *vectors, resumed, cot, tokens, *weights)


def big_flow(me, cross_first, grads, r1, w1, r2, w2, r3, w3, r4, rx, out, send, recv, local_sem):
    nq = me.nq
    rows, width = out.shape
    wide = width // 2
    ours = pl.ds(pl.multiple_of(me.x * wide, 128), wide)
    others = pl.ds(pl.multiple_of((1 - me.x) * wide, 128), wide)
    copy1 = remote(grads.at[:, :, 1 - me.c], r1, send.at[0], recv.at[0], me.core)
    copy1.start()
    kept = pltpu.make_async_copy(grads.at[:, :, me.c], w1, local_sem)
    kept.start()
    yield
    kept.wait()
    copy1.wait()

    def add1(i, carry):
        w1[i // 2, i % 2] = (w1[i // 2, i % 2].astype(F32) + r1[i // 2, i % 2].astype(F32)).astype(BF16)
        return carry

    lax.fori_loop(0, 2 * nq, add1, 0)
    if cross_first:
        copy2 = remote(w1.at[:, :, :, others], r2, send.at[1], recv.at[1], me.cross)
    else:
        copy2 = remote(w1.at[:, 1 - me.y], r2, send.at[1], recv.at[1], me.side)
    copy2.start()
    yield
    copy2.wait()
    if cross_first:
        def add2(i, carry):
            w2[i // 2, i % 2] = (w1[i // 2, i % 2, :, ours].astype(F32) + r2[i // 2, i % 2].astype(F32)).astype(BF16)
            return carry

        lax.fori_loop(0, 2 * nq, add2, 0)
        copy3 = remote(w2.at[:, 1 - me.y], r3, send.at[2], recv.at[2], me.side)
    else:
        def add2(i, carry):
            w2[i] = (w1[i, me.y].astype(F32) + r2[i].astype(F32)).astype(BF16)
            return carry

        lax.fori_loop(0, nq, add2, 0)
        copy3 = remote(w2.at[:, :, others], r3, send.at[2], recv.at[2], me.cross)
    copy3.start()
    yield
    copy3.wait()

    def add3(i, carry):
        mine = w2[i, me.y] if cross_first else w2[i, :, ours]
        w3[i] = (mine.astype(F32) + r3[i].astype(F32)).astype(BF16)
        return carry

    lax.fori_loop(0, nq, add3, 0)
    copies = []
    for k in range(1, nq):
        copy = remote(w3.at[me.quad(k)], r4.at[k - 1], send.at[2 + k], recv.at[2 + k], me.at_quad(me.quad(k)))
        copy.start()
        copies.append(copy)
    yield
    total = w3[me.q].astype(F32)
    for k in range(1, nq):
        copies[k - 1].wait()
        total = total + r4[k - 1].astype(F32)
    out[:, ours] = total.astype(BF16)
    copy5 = remote(out.at[:, ours], out.at[:, ours], send.at[nq + 2], recv.at[nq + 2], me.cross)
    copy5.start()
    yield
    remote(out.at[:, others], out.at[:, others], send.at[nq + 2], recv.at[nq + 2], me.cross).wait_recv()
    copy5.wait_send()
    for at, bit in enumerate(me.cross_bits()[1:]):
        copy = remote(out, rx.at[at], send.at[nq + 3 + at], recv.at[nq + 3 + at], me.cross_bit(bit))
        copy.start()
        copy.wait()
        out[...] = (out[...].astype(F32) + rx[at].astype(F32)).astype(BF16)


def big_scratch(nq, groups, cross_first, rows, width):
    extra = max(groups.bit_length() - 2, 1)
    half = width // 2
    full = [pltpu.VMEM((nq, 2, rows, width), BF16)] * 2
    if cross_first:
        mid = [pltpu.VMEM((nq, 2, rows, half), BF16)] * 2
    else:
        mid = [pltpu.VMEM((nq, rows, width), BF16)] * 2
    return full + mid + [
        pltpu.VMEM((nq, rows, half), BF16), pltpu.VMEM((nq, rows, half), BF16),
        pltpu.VMEM((nq - 1, rows, half), BF16), pltpu.VMEM((extra, rows, width), BF16),
    ]


def small_flow(me, grads, r1, w1, r2, w2, rx, out, send, recv):
    many = 2 * me.nq
    copy1 = remote(grads.at[:, 1 - me.c], r1, send.at[0], recv.at[0], me.core)
    copy1.start()
    yield
    copy1.wait()

    def add(i, carry):
        w1[i] = (grads[i, me.c].astype(F32) + r1[i].astype(F32)).astype(BF16)
        return carry

    lax.fori_loop(0, many, add, 0)
    mine = me.q * 2 + me.y
    copies = []
    for k in range(1, many):
        to = (mine + k) % many
        copy = remote(w1.at[to], r2.at[k - 1], send.at[k], recv.at[k], (me.g, to * 2 + me.c))
        copy.start()
        copies.append(copy)
    yield
    total = w1[mine].astype(F32)
    for k in range(1, many):
        copies[k - 1].wait()
        total = total + r2[k - 1].astype(F32)
    bits = me.cross_bits()
    for at, bit in enumerate(bits):
        w2[at] = total.astype(BF16)
        copy = remote(w2.at[at], rx.at[at], send.at[many + at], recv.at[many + at], me.cross_bit(bit))
        copy.start()
        if at == 0:
            yield
        copy.wait()
        total = total + rx[at].astype(F32)
    out[...] = total.astype(BF16)


def small_scratch(nq, groups, rows):
    bits = groups.bit_length() - 1
    return [
        pltpu.VMEM((2 * nq, rows, 128), BF16), pltpu.VMEM((2 * nq, rows, 128), BF16),
        pltpu.VMEM((2 * nq - 1, rows, 128), BF16), pltpu.VMEM((bits, rows, 128), BF16), pltpu.VMEM((bits, rows, 128), BF16),
    ]


def adjoint_flow(me, f_ref, tabs, sel, s_ref, m0, r0, m1, r1, m2, r2, ss, rs, zs, zr):
    nq = me.nq
    one, two, three, four = tabs[4], tabs[5], tabs[6], tabs[7]
    mine = f_ref[...].reshape(3, 2, 64, 128)
    m0[...] = mine.astype(BF16)
    copy = remote(m0, r0, ss.at[0], rs.at[0], me.core)
    copy.start()
    yield
    copy.wait()
    upper_core, upper_side = me.c == 1, me.y == 1
    other = r0[...].astype(F32)
    lower = jnp.where(upper_core, other, mine)
    upper = jnp.where(upper_core, mine, other)
    pair = lower + one * upper
    after = jnp.where(upper_core, 0.0, other)
    m1[...] = pair.astype(BF16)
    copy = remote(m1, r1, ss.at[1], rs.at[1], me.side)
    copy.start()
    yield
    copy.wait()
    far = r1[...].astype(F32)
    low_pair = jnp.where(upper_side, far, pair)
    high_pair = jnp.where(upper_side, pair, far)
    total = low_pair + two * high_pair
    after = jnp.where(upper_side, 0.0, jnp.where(upper_core, far, one * far)) + after
    m2[0] = total[:, 0].astype(BF16)
    for m in range(3):
        m2[1, m] = (sel(0, m) * total[0, 1] + sel(1, m) * total[1, 1] + sel(2, m) * total[2, 1]).astype(BF16)
    sends = []
    for k in range(1, nq):
        copy = remote(m2, r2.at[me.q], zs.at[k - 1], zr.at[k - 1], me.at_quad(me.quad(k)))
        copy.start()
        sends.append(copy)
    r2[me.q] = m2[...]
    yield
    for k in range(1, nq):
        src = r2.at[me.quad(nq - k)]
        remote(src, src, zs.at[k - 1], zr.at[k - 1], me.core).wait_recv()
    run = r2[0, 1].astype(F32)
    for k in range(1, nq):
        run = run + r2[k, 1].astype(F32)
    carry = run
    for k in range(nq - 1, -1, -1):
        carry = jnp.where(me.q == k, run, carry)
        run = four * run + r2[k, 0].astype(F32)
    lead = pick(me.pos, [three, two, one, jnp.ones_like(one)])
    for p in range(3):
        s_ref[2 * p * 64 : (2 * p + 1) * 64] = lead * carry[p] + after[p, 0]
        s_ref[(2 * p + 1) * 64 : (2 * p + 2) * 64] = after[p, 1]
    for copy in sends:
        copy.wait_send()


class Steps:
    def __init__(self, flows):
        self.flows, self.live = flows, [True] * len(flows)

    def __call__(self, *which):
        for i in which:
            if self.live[i]:
                try:
                    next(self.flows[i])
                except StopIteration:
                    self.live[i] = False

    def finish(self):
        while any(self.live):
            self(*range(len(self.flows)))


ORDERS = (True, False, True, False, True)
N_BIG = 5


def back_kernel(n, groups, *refs):
    refs = list(refs)

    def take(count):
        got = refs[:count]
        del refs[:count]
        return got

    base, slope_s, shared, t_keys, w_shared, tabs, power, power_rev, vec_wide, vec_head, starts, sum_wide, sum_head, resumed = take(14)
    h_act, h_ema, h_x, h_inner, h_units, h_middle, h_tokens, h_tail = take(8)
    grads = take(N_BIG)
    (input_grad,) = take(1)
    outs = take(N_BIG)
    (out_small,) = take(1)
    loads = take(7)
    g_act, ema, x_lanes, inner, g_units, g_middle, tokens = loads
    g_lanes, k_activ, k_gs, b_inner, b_flow, b_start, dx_lanes, acc_in, acc_decay, acc_out, kept, omega_acc, gain_acc = take(13)
    t_sum, t_rows, t_grad, t_out, grad_in, g_small = take(6)
    big = [take(8) for _ in range(N_BIG)]
    small = take(5)
    keys_s, tail_s = take(5), take(5)
    exchange = take(6)
    load_sem, big_send, big_recv, big_local, small_send, small_recv, k_send, k_recv, t_send, t_recv, ess, ers, ezs, ezr = take(14)

    me = Place(n, groups)
    own = base.shape[0]
    total = tokens.shape[0]
    width = tokens.shape[1]
    length = 128
    count = own // length
    lanes = width // 128
    chan = width // n
    sel = chosen(resumed, me)
    hbm = [h_act, h_ema, h_x, h_inner, h_units, h_middle, h_tokens, h_tail]
    places = loads[:6] + [tokens.at[0:own], tokens.at[own:total]]
    arrive = [pltpu.make_async_copy(src, dst, load_sem.at[i]) for i, (src, dst) in enumerate(zip(hbm, places))]
    for copy in arrive:
        copy.start()
    meet(me.group_peers() + [me.cross_bit(bit) for bit in me.cross_bits()])
    keys = tail_flow(me, t_keys, *keys_s, t_sum, k_send, k_recv)
    next(keys)
    steps = Steps(
        [
            big_flow(me, ORDERS[i], grads[i], *big[i], outs[i], big_send.at[i], big_recv.at[i], big_local.at[i])
            for i in range(N_BIG)
        ]
    )
    steps(*range(N_BIG))
    k_mul = vec_head[2:3]
    gain_one = vec_wide[0:1]
    for ref in (omega_acc, gain_acc, acc_in, acc_decay, acc_out):
        ref[...] = jnp.zeros_like(ref)
    for i in range(3):
        arrive[i].wait()

    def grad_rows(row, with_tail):
        at = pl.multiple_of(row * length, length)
        here = pl.ds(at, length)
        d_shared = base[here, :]
        if with_tail:
            extra = t_rows[pl.ds(pl.multiple_of(row // 2 * length, length), length), :]
            d_shared = d_shared + extra * k_mul
            gain_acc[1:2, 0:128] += jnp.sum(extra * shared[here, :], axis=0, keepdims=True)
        gs = (d_shared * slope_s[here, :]).astype(BF16)
        k_gs[here, :] = gs
        for lane in range(lanes):
            cut = slice(lane * 128, (lane + 1) * 128)
            pre = ema[pl.ds(lane * total + at, length), :]
            sig = jax.nn.sigmoid(pre)
            k_activ[here, cut] = (pre * sig).astype(BF16)
            back = g_act[here, cut] + nt(gs, w_shared[cut, :])
            back = back * (sig * (1.0 + pre * (1.0 - sig)))
            g_lanes[pl.ds(lane * own + at, length), :] = back
            x = x_lanes[pl.ds(lane * total + at, length), :]
            omega_acc[lane : lane + 1] += jnp.sum(back * x, axis=0, keepdims=True)

    def local_pass(first):
        ema_local_pass(
            count, (first, 2, count // 2), g_lanes, tabs.at[0], tabs.at[1], tabs.at[2], tabs.at[3], b_inner, b_flow, True
        )

    def cont_rows(p, carry):
        grad_rows(2 * p + 1, False)
        return carry

    def prompt_rows(p, carry):
        grad_rows(2 * p, True)
        return carry

    def norm_rows_back(at, size, extra):
        here = pl.ds(at, size)
        plain, inv = norm_rows(tokens[here, :].astype(F32))
        units = g_units[here, :]
        if extra is not None:
            units = units + extra
        gain_acc[0:1] += jnp.sum(units * plain, axis=0, keepdims=True)
        return norm_back(units, plain, inv, gain_one)

    lax.fori_loop(0, count // 2, cont_rows, 0)
    next(keys)
    steps(0, 1)
    local_pass(1)
    next(keys)
    steps(2, 3)
    arrive[4].wait()
    arrive[6].wait()
    arrive[7].wait()
    piece = (total - own) // 4
    for part in range(4):
        t_grad[part // 2, part % 2] = norm_rows_back(own + part * piece, piece, None).astype(BF16)
    tail = tail_flow(me, t_grad, *tail_s, t_out, t_send, t_recv)
    next(tail)
    next(keys)
    steps(4)
    for _ in keys:
        pass
    for part in range(4):
        t_rows[part * piece : (part + 1) * piece] = t_sum[part // 2, part % 2].astype(F32)
    lax.fori_loop(0, count // 2, prompt_rows, 0)
    local_pass(0)
    adjoint = adjoint_flow(me, b_flow, tabs, sel, b_start, *exchange, ess, ers, ezs, ezr)
    next(adjoint)
    steps(0, 1)
    next(adjoint)
    next(tail)
    steps(2)
    next(adjoint)
    next(tail)
    steps(3)
    for _ in adjoint:
        pass
    arrive[3].wait()
    for row in range(count):
        ema_back_pass(
            count, total // length, row, x_lanes, g_lanes, tabs.at[0], tabs.at[8], vec_head, power, inner, starts,
            power_rev, b_inner, b_start, dx_lanes, acc_in, acc_decay, acc_out, kept,
        )
        if row == 0:
            steps(4)
            next(tail)
        elif row < count - 1:
            steps(*range(N_BIG))
    arrive[5].wait()

    def own_rows(row, carry):
        at = pl.multiple_of(row * length, length)
        extra = jnp.concatenate([dx_lanes[pl.ds(lane * own + at, length), :] for lane in range(lanes)], axis=1)
        grad_in[pl.ds(at, length), :] = g_middle[pl.ds(at, length), :] + norm_rows_back(at, length, extra)
        return carry

    lax.fori_loop(0, count, own_rows, 0)
    alpha, beta, delta, eta, ab = (tabs[9 + i] for i in range(5))
    m_sum, q_sum = eta * acc_in[...], eta * ab * acc_decay[...]
    parts = (beta * m_sum - delta * q_sum, -alpha * q_sum, alpha * m_sum, ab * acc_out[...])
    per = 128 // chan // 2
    for lane in range(lanes):
        cut = slice(lane * 128, (lane + 1) * 128)
        block = [part[lane * 16 : lane * 16 + 16] for part in parts]
        block += [omega_acc[lane : lane + 1], gain_acc[0:1, cut], sum_wide[0:1, cut], jnp.zeros((61, 128), F32)]
        block = jnp.concatenate(block, axis=0).T.astype(BF16)
        g_small[lane * per : (lane + 1) * per, :, 0:chan] = block.reshape(per, 2, chan, 128)
    block = tn(k_activ[...], k_gs[...]).astype(BF16)
    g_small[:, :, chan : 2 * chan] = block.reshape(n // 2, 2, chan, 128)
    heads = jnp.concatenate((sum_head[0:2], sum_head[2:3] + gain_acc[1:2, 0:128], jnp.zeros((13, 128), F32)), axis=0)
    heads = jnp.broadcast_to(heads.astype(BF16)[None, None], (n // 2, 2, 16, 128))
    g_small[:, :, 2 * chan :] = heads
    little = small_flow(me, g_small, *small, out_small, small_send, small_recv)
    next(little)
    for _ in tail:
        pass
    next(little)
    steps(*range(N_BIG))

    def cast_rows(row, carry):
        here = pl.ds(pl.multiple_of(row * length, length), length)
        input_grad[here, :] = grad_in[here, :].astype(BF16)
        return carry

    for part in range(4):
        t_wide = t_out[part // 2, part % 2].astype(F32)
        at = part * piece
        while at < (part + 1) * piece:
            m = at // length
            stop = min((m + 1) * length, (part + 1) * piece)
            here = slice(at + m * length, stop + m * length)
            grad_in[here] = grad_in[here] + t_wide[at - part * piece : stop - part * piece]
            at = stop
    lax.fori_loop(0, count, cast_rows, 0)
    next(little)
    steps(*range(N_BIG))
    for _ in little:
        pass
    steps.finish()


def back_call(n, groups, ins, hbm, grads):
    nq = n // 4
    dma = pltpu.SemaphoreType.DMA
    vm = pltpu.VMEM
    shape = jax.ShapeDtypeStruct
    own, width = hbm[6].shape
    total = own + hbm[7].shape[0]
    chan = width // n
    small_rows = 2 * chan + 16
    piece = (total - own) // 4
    outs = [shape((own, width), BF16)] + [shape(grad.shape[-2:], BF16) for grad in grads] + [shape((small_rows, 128), BF16)]
    scratch = [vm(part.shape, part.dtype) for part in hbm[:6]] + [vm((total, width), BF16)]
    scratch += [
        vm((own * 4, 128), F32), vm((own, width), BF16), vm((own, 128), BF16), vm((own * 4, 128), F32),
        vm((own // 2, 128), F32), vm((own // 2, 128), F32), vm((own * 4, 128), F32), vm((64, 128), F32), vm((64, 128), F32),
        vm((64, 128), F32), vm((128, 8, 128), F32), vm((8, 128), F32), vm((8, width), F32),
        vm((2, 2, piece, 128), BF16), vm((4 * piece, 128), F32), vm((2, 2, piece, width), BF16), vm((2, 2, piece, width), BF16),
        vm((own, width), F32), vm((n // 2, 2, small_rows, 128), BF16),
    ]
    for i, grad in enumerate(grads):
        scratch += big_scratch(nq, groups, ORDERS[i], grad.shape[-2], grad.shape[-1])
    scratch += small_scratch(nq, groups, small_rows)
    scratch += tail_scratch(nq, piece, 128) + tail_scratch(nq, piece, width)
    scratch += [vm((3, 2, 64, 128), BF16)] * 4 + [vm((2, 3, 64, 128), BF16), vm((nq, 2, 3, 64, 128), BF16)]
    sems = nq + 3 + max(groups.bit_length() - 2, 1)
    small_sems = 2 * nq + groups.bit_length() - 1
    scratch += [
        dma((8,)), dma((N_BIG, sems)), dma((N_BIG, sems)), dma((N_BIG,)), dma((small_sems,)), dma((small_sems,)),
        dma((3,)), dma((nq + 4,)), dma((3,)), dma((nq + 4,)), dma((2,)), dma((2,)), dma((nq - 1,)), dma((nq - 1,)),
    ]
    return pl.pallas_call(
        functools.partial(back_kernel, n, groups),
        out_shape=outs,
        in_specs=[VMEM] * 13 + [SMEM] + [HBM] * (8 + N_BIG),
        out_specs=[VMEM] * len(outs),
        scratch_shapes=scratch,
        compiler_params=pltpu.CompilerParams(collective_id=2, has_side_effects=True, vmem_limit_bytes=60 << 20),
        name="back",
    )(*ins, *hbm, *grads)


def finish_kernel(heads, grad_in, *refs):
    sums, small, grad_out = refs[:N_BIG], refs[N_BIG], refs[N_BIG + 1]
    outs = refs[N_BIG + 2 : 2 * N_BIG + 2]
    shared, rates, vecs = refs[2 * N_BIG + 2], refs[2 * N_BIG + 3 : 2 * N_BIG + 7], refs[2 * N_BIG + 7 : 2 * N_BIG + 13]
    grad_out[...] = grad_in[...]
    for src, dst in zip(sums, outs):
        dst[...] = src[...].astype(F32)
    chan = shared.shape[0]
    shared[...] = small[chan : 2 * chan].astype(F32)
    block = small[0:chan].astype(F32).T
    for i, ref in enumerate(rates):
        ref[...] = block[16 * i : 16 * i + 16]
    for i in range(3):
        vecs[i][...] = block[64 + i : 65 + i]
    mine = lax.axis_index("seq") * heads
    rows = pltpu.roll(small[2 * chan : 2 * chan + 16].astype(F32), (128 - mine) % 128, 1)
    for i in range(3):
        vecs[3 + i][...] = rows[i : i + 1, 0:heads]


def finish_call(n, heads, input_grad, sums, small):
    shape = jax.ShapeDtypeStruct
    chan = (small.shape[0] - 16) // 2
    outs = [shape(input_grad.shape, BF16)] + [shape(part.shape, F32) for part in sums] + [shape((chan, 128), F32)]
    outs += [shape((16, chan), F32)] * 4 + [shape((1, chan), F32)] * 3 + [shape((1, heads), F32)] * 3
    return pl.pallas_call(
        functools.partial(finish_kernel, heads),
        out_shape=outs,
        in_specs=[VMEM] * (N_BIG + 2),
        out_specs=[VMEM] * len(outs),
        compiler_params=pltpu.CompilerParams(vmem_limit_bytes=60 << 20),
        name="finish",
    )(input_grad, *sums, small)


def local(
    hidden_in, cotangent, cont_prompt, value_proj, shared_proj, reset_proj, hidden_proj, inner_proj,
    outer_proj, ema_alpha, ema_delta, ema_beta, ema_eta, ema_omega, norm_gain, ffn_gain, query_scale,
    query_shift, key_scale,
):
    n, groups = lax.axis_size("seq"), lax.axis_size("grp")
    nq = n // 4
    seq_index = lax.axis_index("seq")
    sets, kinds, length, width = hidden_in.shape[1:]
    chan = width // n
    heads = query_scale.shape[0]
    own_rows = sets * kinds * length
    vectors = (norm_gain, ffn_gain, ema_omega, query_scale, query_shift, key_scale)
    own_low = hidden_in[0].reshape(own_rows, width)
    (
        tabs, power, power_rev, vec_wide, vec_head, starts, mat_shared,
        result, grad_middle, grad_act, grad_base, slope_shared, shared, grad_units, sum_outer, sum_inner, sum_hidden,
        sum_reset, sum_value, sent_keys, sum_wide, sum_head, ema_lanes, x_lanes, inner, tail_low,
    ) = layer_call(
        n, groups, [part.T for part in (ema_alpha, ema_delta, ema_beta, ema_eta)], [part[None] for part in vectors],
        cont_prompt, cotangent[0].reshape(own_rows, width), hidden_in[0],
        (value_proj, reset_proj, inner_proj, hidden_proj, outer_proj, shared_proj),
    )
    mat_shared, tail_low = mat_shared.reshape(width, 128), tail_low.reshape(-1, width)

    def shards(grad):
        return grad.reshape(nq, 2, 2, -1, grad.shape[-1])

    ins = (
        grad_base, slope_shared, shared, sent_keys.reshape(2, 2, -1, 128), mat_shared, tabs, power, power_rev, vec_wide,
        vec_head, starts, sum_wide, sum_head, cont_prompt,
    )
    hbm = (grad_act, ema_lanes, x_lanes, inner, grad_units, grad_middle, own_low, tail_low)
    grads = [shards(part) for part in (sum_outer, sum_inner, sum_hidden, sum_reset, sum_value)]
    input_grad, *sums, d_small = back_call(n, groups, ins, hbm, grads)
    wide = finish_call(n, heads, input_grad, sums, d_small)
    input_grad, d_outer, d_inner, d_hidden, d_reset, d_value, d_shared = wide[:7]
    rates = [part.T for part in wide[7:11]]
    vecs = [part.reshape(part.shape[1]) for part in wide[11:17]]
    return (
        result.reshape(hidden_in.shape), input_grad.reshape(hidden_in.shape), d_value, d_shared, d_reset, d_hidden, d_inner,
        d_outer, *rates, *vecs,
    )


def solution(mesh):
    mat, vec = P("seq", None), P("seq")
    tok = P("grp", None, None, "seq", None)
    in_specs = (tok, tok, P("grp", None)) + (mat,) * 10 + (vec,) * 6
    out_specs = (tok, tok) + (mat,) * 10 + (vec,) * 6
    return jax.shard_map(local, mesh=mesh, in_specs=in_specs, out_specs=out_specs, check_vma=False)
```

```python
import functools
import math

import jax
import jax.numpy as jnp
from jax import lax
from jax.experimental import pallas as pl
from jax.experimental.pallas import tpu as pltpu
from jax.sharding import PartitionSpec as P

CLEN = 512
NORM_EPS = 1e-05
MASKED_SCORE = -1e30
MESH = pl.DeviceIdType.MESH
SUB = 16
NJ = 16
TINY = 1e-20
F32 = jnp.float32
BF16 = jnp.bfloat16
VMEM = pl.BlockSpec(memory_space=pltpu.VMEM)
HBM = pl.BlockSpec(memory_space=pltpu.HBM)
SMEM = pl.BlockSpec(memory_space=pltpu.SMEM)


def shift_down(value, count):
    rows = lax.broadcasted_iota(jnp.int32, value.shape, 0)
    return jnp.where(rows >= count, pltpu.roll(value, count, 0), 0.0)


def shift_up(value, count):
    rows = lax.broadcasted_iota(jnp.int32, value.shape, 0)
    return jnp.where(rows < 8 - count, pltpu.roll(value, 8 - count, 0), 0.0)


def row_of(ref, row):
    return jnp.broadcast_to(ref[pl.ds(row, 1), :], (8, 128))


def ema_local_pass(rows, pick_rows, x_ref, decay, decay16, decay32, decay64, inner_ref, final_ref, backward):
    shift = shift_up if backward else shift_down

    first, stride, many = pick_rows

    def body(turn, carry):
        row, lane = first + stride * (turn // 4), turn % 4
        item = row * 4 + lane
        base = lane * (rows * 128) + row * 128
        dec = [row_of(decay, lane * 16 + j) for j in range(NJ)]
        state = [jnp.zeros((8, 128), F32)] * NJ
        for step in range(SUB - 1, -1, -1) if backward else range(SUB):
            x = x_ref[pl.ds(base + step, 8, stride=SUB), :]
            if backward:
                state = [dec[j] * (state[j] + x) for j in range(NJ)]
            else:
                state = [dec[j] * state[j] + x for j in range(NJ)]
        for j in range(NJ):
            total = state[j]
            total = total + row_of(decay16, lane * 16 + j) * shift(total, 1)
            total = total + row_of(decay32, lane * 16 + j) * shift(total, 2)
            total = total + row_of(decay64, lane * 16 + j) * shift(total, 4)
            inner_ref[pl.ds((item * 16 + j) * 8, 8), :] = shift(total, 1)
            final_ref[pl.ds(row * 64 + lane * 16 + j, 1), :] = total[0:1] if backward else total[7:8]
        return carry

    lax.fori_loop(0, many * 4, body, 0)


def ema_apply_pass(rows, pick_rows, x_ref, decay, mix, omega, power, inner_ref, start_ref, y_ref):
    first, many = pick_rows

    def body(turn, carry):
        row, lane = first + turn // 4, turn % 4
        item = row * 4 + lane
        base = lane * (rows * 128) + row * 128
        state = [
            inner_ref[pl.ds((item * 16 + j) * 8, 8), :]
            + power[pl.ds((lane * 16 + j) * 8, 8), :] * row_of(start_ref, row * 64 + lane * 16 + j)
            for j in range(NJ)
        ]
        skip = row_of(omega, 4 + lane)
        for step in range(SUB):
            x = x_ref[pl.ds(base + step, 8, stride=SUB), :]
            sums = [skip * x, None]
            for j in range(NJ):
                state[j] = row_of(decay, lane * 16 + j) * state[j] + x
                term = row_of(mix, lane * 16 + j) * state[j]
                sums[j % 2] = term if sums[j % 2] is None else sums[j % 2] + term
            y_ref[pl.ds(base + step, 8, stride=SUB), :] = sums[0] + sums[1]
        return carry

    lax.fori_loop(0, many * 4, body, 0)


def ema_back_pass(
    rows, x_rows, row, x_ref, g_ref, decay, mix, omega, power, inner_ref, start_ref, power_rev,
    back_inner_ref, back_start_ref, dx_ref, sum_in, sum_decay, sum_out, kept,
):
    half = 8

    def body(lane, carry):
        item = row * 4 + lane
        base = lane * (rows * 128) + row * 128
        x_base = lane * (x_rows * 128) + row * 128
        skip = row_of(omega, 4 + lane)
        for part in range(NJ // half):
            js = range(part * half, part * half + half)
            dec = [row_of(decay, lane * 16 + j) for j in js]
            state = [
                inner_ref[pl.ds((item * 16 + j) * 8, 8), :]
                + power[pl.ds((lane * 16 + j) * 8, 8), :] * row_of(start_ref, row * 64 + lane * 16 + j)
                for j in js
            ]
            for step in range(SUB):
                x = x_ref[pl.ds(x_base + step, 8, stride=SUB), :]
                for i in range(half):
                    kept[step * half + i] = state[i]
                    state[i] = dec[i] * state[i] + x
            adj = [
                back_inner_ref[pl.ds((item * 16 + j) * 8, 8), :]
                + power_rev[pl.ds((lane * 16 + j) * 8, 8), :]
                * row_of(back_start_ref, row * 64 + lane * 16 + j)
                for j in js
            ]
            weight = [row_of(mix, lane * 16 + j) for j in js]
            edge = [-(adj[i] * state[i]) for i in range(half)]
            first, second = [None] * half, [None] * half
            for step in range(SUB - 1, -1, -1):
                x = x_ref[pl.ds(x_base + step, 8, stride=SUB), :]
                g = g_ref[pl.ds(base + step, 8, stride=SUB), :]
                sums = [dx_ref[pl.ds(base + step, 8, stride=SUB), :], skip * g if part == 0 else None]
                for i in range(half):
                    full = adj[i] + g
                    term = weight[i] * full
                    sums[i % 2] = term if sums[i % 2] is None else sums[i % 2] + term
                    with_x, with_s = full * x, full * kept[step * half + i]
                    first[i] = with_x if first[i] is None else first[i] + with_x
                    second[i] = with_s if second[i] is None else second[i] + with_s
                    adj[i] = dec[i] * full
                dx_ref[pl.ds(base + step, 8, stride=SUB), :] = sums[0] + sums[1]
            for i, j in enumerate(js):
                at = pl.ds(lane * 16 + j, 1)
                flow = edge[i] + adj[i] * kept[i]
                total = jnp.sum(first[i], axis=0, keepdims=True)
                sum_in[at, :] += total
                sum_decay[at, :] += jnp.sum(second[i], axis=0, keepdims=True)
                sum_out[at, :] += total + jnp.sum(flow, axis=0, keepdims=True)
        return carry

    lax.fori_loop(0, 4, body, 0)


class Place:
    def __init__(self, n, groups):
        self.n, self.nq, self.groups = n, n // 4, groups
        self.g, self.s = lax.axis_index("grp"), lax.axis_index("seq")
        self.c, self.y, self.q, self.x = self.s % 2, (self.s // 2) % 2, self.s // 4, self.g % 2
        self.pos = self.s % 4
        self.core = (self.g, self.s + 1 - 2 * self.c)
        self.side = (self.g, self.s + 2 - 4 * self.y)
        self.cross = (self.g + 1 - 2 * self.x, self.s)
        self.is_last = self.s == n - 1

    def quad(self, k):
        return (self.q + k) % self.nq

    def at_quad(self, q):
        return (self.g, q * 4 + self.pos)

    def group_peers(self):
        return [(self.g, (self.s + k) % self.n) for k in range(1, self.n)]

    def cross_bit(self, bit):
        return (self.g + bit - 2 * bit * ((self.g // bit) % 2), self.s)

    def cross_bits(self):
        return [1 << b for b in range(self.groups.bit_length() - 1)]


def chosen(resumed, me):
    def at(p, m):
        return jnp.where(resumed[0, p * me.nq + me.q] == m, 1.0, 0.0)

    return at


def meet(peers):
    barrier = pltpu.get_barrier_semaphore()
    for peer in peers:
        pl.semaphore_signal(barrier, inc=1, device_id=peer, device_id_type=MESH)
    pl.semaphore_wait(barrier, len(peers))


def remote(src, dst, send, recv, device):
    return pltpu.make_async_remote_copy(
        src_ref=src, dst_ref=dst, send_sem=send, recv_sem=recv, device_id=device, device_id_type=MESH
    )


def pick(index, values):
    out = values[0]
    for k in range(1, len(values)):
        out = jnp.where(index == k, values[k], out)
    return out


def tail_flow(me, t, r1, w1, r2, w2, r3, out, send, recv):
    nq = me.nq
    last = me.q == nq - 1
    out[...] = jnp.zeros_like(out)
    copy1 = remote(t.at[:, 1 - me.c], r1, send.at[0], recv.at[0], me.core)
    copy1.start()
    yield
    copy1.wait()
    for i in range(2):
        w1[i] = (t[i, me.c].astype(F32) + r1[i].astype(F32)).astype(BF16)
    copy2 = remote(w1.at[1 - me.y], r2, send.at[1], recv.at[1], me.side)
    copy2.start()
    yield
    copy2.wait()
    w2[...] = (w1[me.y].astype(F32) + r2[...].astype(F32)).astype(BF16)
    top = (me.g, (nq - 1) * 4 + me.pos)
    end = (me.g, nq * 4 - 1)
    for k in range(nq - 1):
        @pl.when(me.q == k)
        def _():
            remote(w2, r3.at[k], send.at[2], recv.at[2 + k], top).start()
    yield

    @pl.when(last)
    def _():
        total = w2[...].astype(F32)
        for k in range(nq - 1):
            remote(r3.at[k], r3.at[k], send.at[2], recv.at[2 + k], me.core).wait_recv()
            total = total + r3[k].astype(F32)
        w2[...] = total.astype(BF16)

        @pl.when(jnp.logical_not(me.is_last))
        def _():
            for j in range(3):
                @pl.when(me.pos == j)
                def _():
                    remote(w2, out.at[j // 2, j % 2], send.at[2], recv.at[nq + 1 + j], end).start()

        @pl.when(me.is_last)
        def _():
            out[1, 1] = w2[...]
    yield

    @pl.when(me.is_last)
    def _():
        for j in range(3):
            dst = out.at[j // 2, j % 2]
            remote(dst, dst, send.at[2], recv.at[nq + 1 + j], me.core).wait_recv()

    @pl.when(jnp.logical_not(me.is_last))
    def _():
        remote(w2, w2, send.at[2], recv.at[2], me.core).wait_send()


def tail_scratch(nq, shape):
    vm = pltpu.VMEM
    return [vm((2, *shape), BF16), vm((2, *shape), BF16), vm(shape, BF16), vm(shape, BF16), vm((nq - 1, *shape), BF16)]


class Sender:
    def __init__(self, spare):
        self.spare, self.started = spare, []

    def send(self, src, dst, send, recv, device, when=None):
        copy = remote(src, dst, send, recv, device)
        if when is None:
            copy.start()
        else:
            pl.when(when)(copy.start)
        self.started.append((copy, when))

    def got(self, ref, recv):
        remote(ref, ref, self.spare, recv, self.device).wait_recv()

    def finish(self):
        for copy, when in self.started:
            if when is None:
                copy.wait_send()
            else:
                pl.when(when)(copy.wait_send)


def small_gather(me, out, post, ss, sr):
    for k in range(1, me.n):
        post.send(out.at[me.s], out.at[me.s], ss.at[k - 1], sr.at[k - 1], (me.g, (me.s + k) % me.n))


def small_arrive(me, out, post, sr):
    for k in range(1, me.n):
        post.got(out.at[(me.s + me.n - k) % me.n], sr.at[k - 1])


def gather_flow(me, post, mats, zs, zr, ys, yr, xs, xr, cs, cr):
    nq = me.nq
    mats = [(out, out.shape[-1] // 2) for out in mats]
    other = 1 - me.x

    def half(ref, width, which):
        return ref.at[:, pl.ds(pl.multiple_of(which * width, 128), width)]

    up, down = (me.g, me.s + 4), (me.g, me.s - 4)
    has_up, has_down = me.q < nq - 1, me.q > 0
    for i, (out, width) in enumerate(mats):
        mine = out.at[me.s]
        piece = half(mine, width, me.x)
        post.send(piece, piece, zs.at[0, 0, i], zr.at[0, 0, i], up, has_up)
        post.send(piece, piece, zs.at[1, 0, i], zr.at[1, 0, i], down, has_down)
        post.send(mine, mine, ys.at[0, i], yr.at[0, i], me.side)
    for i, (out, width) in enumerate(mats):
        post.send(out.at[me.s], out.at[me.s], cs.at[0, i], cr.at[0, i], me.core)
    yield

    def arrival(side, hop):
        there = me.q - hop if side == 0 else me.q + hop
        here = there >= 0 if side == 0 else there < nq
        onward, to = (has_up, up) if side == 0 else (has_down, down)

        def pieces(pos, which):
            shard = jnp.clip(there, 0, nq - 1) * 4 + pos
            return [half(out.at[shard], width, which) for out, width in mats]

        return here, jnp.logical_and(here, onward), to, pieces

    arrivals = [(hop, side) for hop in range(1, nq) for side in range(2)]
    side_pos = me.pos + 2 - 4 * me.y
    for hop, side in arrivals:
        here, onward, to, pieces = arrival(side, hop)
        at = (hop - 1) * 2 + side
        for i, piece in enumerate(pieces(me.pos, me.x)):
            pl.when(here)(functools.partial(post.got, piece, zr.at[side, hop - 1, i]))
            if hop < nq - 1:
                post.send(piece, piece, zs.at[side, hop, i], zr.at[side, hop, i], to, onward)
            post.send(piece, piece, ys.at[1 + at, i], yr.at[1 + at, i], me.side, here)
            post.send(piece, piece, xs.at[at, i], xr.at[at, i], me.cross, here)
            post.send(piece, piece, cs.at[1 + at, i], cr.at[1 + at, i], me.core, here)
        if side:
            yield
    count = len(arrivals)
    for i, (out, _) in enumerate(mats):
        block = out.at[me.q * 4 + side_pos]
        post.got(block, yr.at[0, i])
        post.send(block, block, cs.at[1 + count, i], cr.at[1 + count, i], me.core)
    for hop, side in arrivals:
        here, _, _, pieces = arrival(side, hop)
        at = (hop - 1) * 2 + side
        for i, piece in enumerate(pieces(side_pos, me.x)):
            pl.when(here)(functools.partial(post.got, piece, yr.at[1 + at, i]))
            post.send(piece, piece, xs.at[count + at, i], xr.at[count + at, i], me.cross, here)
            post.send(piece, piece, cs.at[2 + count + at, i], cr.at[2 + count + at, i], me.core, here)
        if side:
            yield
    flip = 1 - 2 * me.c
    for group, pos in ((0, me.pos), (1, side_pos)):
        for hop, side in arrivals:
            here, _, _, pieces = arrival(side, hop)
            at = group * count + (hop - 1) * 2 + side
            to = 2 + 2 * count + at
            for i, piece in enumerate(pieces(pos, other)):
                pl.when(here)(functools.partial(post.got, piece, xr.at[at, i]))
                post.send(piece, piece, cs.at[to, i], cr.at[to, i], me.core, here)
        yield
    for group, pos in ((0, me.pos + flip), (1, side_pos + flip)):
        for i, (out, _) in enumerate(mats):
            post.got(out.at[me.q * 4 + pos], cr.at[group * (1 + count), i])
        for hop, side in arrivals:
            here, _, _, pieces = arrival(side, hop)
            at = (hop - 1) * 2 + side
            for i, piece in enumerate(pieces(pos, me.x)):
                pl.when(here)(functools.partial(post.got, piece, cr.at[group * (1 + count) + 1 + at, i]))
            for i, piece in enumerate(pieces(pos, other)):
                pl.when(here)(functools.partial(post.got, piece, cr.at[2 + 2 * count + group * count + at, i]))


def tokens_flow(me, post, x_in, x_out, ts, tr, local_sem):
    nq = me.nq
    rows = x_out.shape[1] // 4

    def quarter(ref, pos):
        return ref.at[:, pl.ds(pl.multiple_of(pos * rows, rows), rows)]

    in_last = me.q == nq - 1
    side_pos, flip = me.pos + 2 - 4 * me.y, 1 - 2 * me.c
    keep = pltpu.make_async_copy(quarter(x_in, me.pos), quarter(x_out, me.pos), local_sem)
    pl.when(me.is_last)(keep.start)
    for j in range(3):
        post.send(quarter(x_in, j), quarter(x_out, j), ts.at[j], tr.at[0], (me.g, 4 * (nq - 1) + j), me.is_last)
    yield

    @pl.when(jnp.logical_and(in_last, jnp.logical_not(me.is_last)))
    def _():
        post.got(quarter(x_out, me.pos), tr.at[0])

    pl.when(me.is_last)(keep.wait)
    mine = quarter(x_out, me.pos)
    for k in range(1, nq):
        post.send(mine, mine, ts.at[2 + k], tr.at[1], me.at_quad(me.quad(k)), in_last)
    yield

    @pl.when(jnp.logical_not(in_last))
    def _():
        post.got(mine, tr.at[1])

    post.send(mine, mine, ts.at[nq + 2], tr.at[2], me.side)
    post.send(mine, mine, ts.at[nq + 3], tr.at[3], me.core)
    yield
    theirs = quarter(x_out, side_pos)
    post.got(theirs, tr.at[2])
    post.send(theirs, theirs, ts.at[nq + 4], tr.at[4], me.core)
    yield
    post.got(quarter(x_out, me.pos + flip), tr.at[3])
    post.got(quarter(x_out, side_pos + flip), tr.at[4])


def gather_sems(nq, mats):
    count = 2 * (nq - 1)
    shapes = [(2, nq - 1, mats)] * 2 + [(1 + count, mats)] * 2 + [(2 * count, mats)] * 2 + [(2 + 4 * count, mats)] * 2
    return [pltpu.SemaphoreType.DMA(shape) for shape in shapes]


def state_flow(me, f_ref, tabs, sel, s_ref, m0, r0, m1, r1, m2, r2, ss, rs, zs, zr, ps, pr):
    nq = me.nq
    one, two, three, four = tabs[4], tabs[5], tabs[6], tabs[7]
    ab = tabs[13]
    mine = f_ref[0:384].reshape(3, 2, 64, 128)
    m0[...] = mine.astype(BF16)
    copy = remote(m0, r0, ss.at[0], rs.at[0], me.core)
    copy.start()
    yield
    copy.wait()
    upper_core, upper_side = me.c == 1, me.y == 1
    other = r0[...].astype(F32)
    lower = jnp.where(upper_core, other, mine)
    upper = jnp.where(upper_core, mine, other)
    pair = one * lower + upper
    before = jnp.where(upper_core, other, 0.0)
    m1[0] = pair.astype(BF16)
    m1[1, :, 0] = lower[:, 0].astype(BF16)
    m1[1, :, 1] = jnp.zeros((3, 64, 128), BF16)
    copy = remote(m1, r1, ss.at[1], rs.at[1], me.side)
    copy.start()
    yield
    copy.wait()
    far = r1[0].astype(F32)
    low_pair = jnp.where(upper_side, far, pair)
    high_pair = jnp.where(upper_side, pair, far)
    total = two * low_pair + high_pair
    before = jnp.where(upper_side, jnp.where(upper_core, one * far, far), 0.0) + before
    third = jnp.where(upper_side, lower[:, 0], r1[1, :, 0].astype(F32))
    last_in = one * low_pair[:, 0] + third
    m2[0] = total[:, 0].astype(BF16)
    m2[1] = last_in.astype(BF16)
    sends = []
    for k in range(1, nq):
        copy = remote(m2.at[0], r2.at[me.q], zs.at[k - 1], zr.at[k - 1], me.at_quad(me.quad(k)))
        copy.start()
        sends.append(copy)

    @pl.when(me.q == nq - 1)
    def _():
        for k in range(1, nq):
            remote(m2.at[1], r2.at[nq], ps.at[k - 1], pr.at[0], me.at_quad(me.quad(k))).start()
        r2[nq] = m2[1]

    r2[me.q] = m2[0]
    yield
    for k in range(1, nq):
        src = r2.at[me.quad(nq - k)]
        remote(src, src, zs.at[k - 1], zr.at[k - 1], me.core).wait_recv()

    @pl.when(me.q != nq - 1)
    def _():
        remote(r2.at[nq], r2.at[nq], ps.at[0], pr.at[0], me.core).wait_recv()

    run = jnp.zeros((3, 64, 128), F32)
    carry, tail_in = run, run
    for k in range(nq):
        carry = jnp.where(me.q == k, run, carry)
        if k == nq - 1:
            tail_in = three * run + r2[nq].astype(F32)
        run = four * run + r2[k].astype(F32)
    low = (ab * run).astype(BF16).astype(F32)
    safe = jnp.abs(ab) >= TINY
    begin = jnp.where(safe, low / jnp.where(safe, ab, 1.0), run)
    lead = pick(me.pos, [jnp.ones_like(one), one, two, three])
    for p in range(3):
        start = sel(p, 0) * begin[0] + sel(p, 1) * begin[1] + sel(p, 2) * begin[2]
        s_ref[128 * p : 128 * p + 64] = lead * carry[p] + before[p, 0]
        s_ref[128 * p + 64 : 128 * p + 128] = lead * start + before[p, 1]
        s_ref[384 + 64 * p : 448 + 64 * p] = tail_in[p]
    for copy in sends:
        copy.wait_send()

    @pl.when(me.q == nq - 1)
    def _():
        for k in range(1, nq):
            remote(m2.at[1], r2.at[nq], ps.at[k - 1], pr.at[0], me.at_quad(me.quad(k))).wait_send()


def silu_grad(pre_act):
    sigmoid_val = jax.nn.sigmoid(pre_act)
    return sigmoid_val * (1.0 + pre_act * (1.0 - sigmoid_val))


def norm_rows(row_data):
    centered = row_data - jnp.mean(row_data, axis=-1, keepdims=True)
    scale_inv = lax.rsqrt(jnp.mean(centered * centered, axis=-1, keepdims=True) + NORM_EPS)
    return (centered * scale_inv, scale_inv)


def norm_back(grad_rows, plain, scale_inv, gain_vec):
    grad_norm = grad_rows * gain_vec
    inner_term = (
        grad_norm
        - jnp.mean(grad_norm, axis=-1, keepdims=True)
        - plain * jnp.mean(grad_norm * plain, axis=-1, keepdims=True)
    )
    return inner_term * scale_inv


def nt(lhs, rhs):
    return lax.dot_general(lhs, rhs, (((1,), (1,)), ((), ())), preferred_element_type=F32)


def tn(lhs, rhs):
    return lax.dot_general(lhs, rhs, (((0,), (0,)), ((), ())), preferred_element_type=F32)


def nn(lhs, rhs):
    return lax.dot_general(lhs, rhs, (((1,), (0,)), ((), ())), preferred_element_type=F32)


def silu_pair(pre):
    sig = jax.nn.sigmoid(pre)
    return pre * sig, sig * (1.0 + pre * (1.0 - sig))


CHUNK = 256


def big_flow(me, cross_first, grads, r1, r2, r3, r4, rx, out, send, recv):
    nq = me.nq
    rows, width = out.shape
    wide = width // 2
    ours = pl.ds(pl.multiple_of(me.x * wide, 128), wide)
    others = pl.ds(pl.multiple_of((1 - me.x) * wide, 128), wide)
    copy1 = remote(grads.at[:, 1 - me.c], r1, send.at[0], recv.at[0], me.core)
    copy1.start()
    yield
    copy1.wait()

    def add1(i, carry):
        r1[i] = (grads[i, me.c].astype(F32) + r1[i].astype(F32)).astype(BF16)
        return carry

    lax.fori_loop(0, 2 * nq, add1, 0)
    if cross_first:
        copy2 = remote(r1.at[:, :, others], r2, send.at[1], recv.at[1], me.cross)
        copy2.start()
    else:
        copies2 = []
        for k in range(nq):
            copy = remote(r1.at[2 * k + 1 - me.y], r2.at[k], send.at[nq + 3 + k], recv.at[nq + 3 + k], me.side)
            copy.start()
            copies2.append(copy)
    yield
    if cross_first:
        copy2.wait()

        def add2(i, carry):
            r2[i] = (r1[i, :, ours].astype(F32) + r2[i].astype(F32)).astype(BF16)
            return carry

        lax.fori_loop(0, 2 * nq, add2, 0)
        copies3 = []
        for k in range(nq):
            copy = remote(r2.at[2 * k + 1 - me.y], r3.at[k], send.at[nq + 3 + k], recv.at[nq + 3 + k], me.side)
            copy.start()
            copies3.append(copy)
    else:
        for copy in copies2:
            copy.wait()

        def add2(i, carry):
            r2[i] = (r1[2 * i + me.y].astype(F32) + r2[i].astype(F32)).astype(BF16)
            return carry

        lax.fori_loop(0, nq, add2, 0)
        copies3 = [remote(r2.at[:, :, others], r3, send.at[2], recv.at[2], me.cross)]
        copies3[0].start()
    yield
    for copy in copies3:
        copy.wait()

    def add3(i, carry):
        mine = r2[2 * i + me.y] if cross_first else r2[i, :, ours]
        r3[i] = (mine.astype(F32) + r3[i].astype(F32)).astype(BF16)
        return carry

    lax.fori_loop(0, nq, add3, 0)
    copies = []
    for k in range(1, nq):
        copy = remote(r3.at[me.quad(k)], r4.at[k - 1], send.at[2 + k], recv.at[2 + k], me.at_quad(me.quad(k)))
        copy.start()
        copies.append(copy)
    yield
    total = r3[me.q].astype(F32)
    for k in range(1, nq):
        copies[k - 1].wait()
        total = total + r4[k - 1].astype(F32)
    out[:, ours] = total.astype(BF16)
    copy5 = remote(out.at[:, ours], out.at[:, ours], send.at[nq + 2], recv.at[nq + 2], me.cross)
    copy5.start()
    yield
    remote(out.at[:, others], out.at[:, others], send.at[nq + 2], recv.at[nq + 2], me.cross).wait_recv()
    copy5.wait_send()
    for at, bit in enumerate(me.cross_bits()[1:]):
        copy = remote(out, rx.at[at], send.at[2 * nq + 3 + at], recv.at[2 * nq + 3 + at], me.cross_bit(bit))
        copy.start()
        copy.wait()
        out[...] = (out[...].astype(F32) + rx[at].astype(F32)).astype(BF16)


def big_scratch(nq, groups, cross_first, rows, width):
    extra = max(groups.bit_length() - 2, 1)
    half = width // 2
    second = (2 * nq, rows, half) if cross_first else (nq, rows, width)
    spare = (extra, rows, width) if groups > 2 else (1, 16, 128)
    shapes = [(2 * nq, rows, width), second, (nq, rows, half), (nq - 1, rows, half), spare]
    return [pltpu.VMEM(shape, BF16) for shape in shapes]


def small_flow(me, grads, r1, w1, r2, w2, rx, out, send, recv):
    many = 2 * me.nq
    copy1 = remote(grads.at[:, 1 - me.c], r1, send.at[0], recv.at[0], me.core)
    copy1.start()
    yield
    copy1.wait()

    def add(i, carry):
        w1[i] = (grads[i, me.c].astype(F32) + r1[i].astype(F32)).astype(BF16)
        return carry

    lax.fori_loop(0, many, add, 0)
    mine = me.q * 2 + me.y
    copies = []
    for k in range(1, many):
        to = (mine + k) % many
        copy = remote(w1.at[to], r2.at[k - 1], send.at[k], recv.at[k], (me.g, to * 2 + me.c))
        copy.start()
        copies.append(copy)
    yield
    total = w1[mine].astype(F32)
    for k in range(1, many):
        copies[k - 1].wait()
        total = total + r2[k - 1].astype(F32)
    bits = me.cross_bits()
    for at, bit in enumerate(bits):
        w2[at] = total.astype(BF16)
        copy = remote(w2.at[at], rx.at[at], send.at[many + at], recv.at[many + at], me.cross_bit(bit))
        copy.start()
        if at == 0:
            yield
        copy.wait()
        total = total + rx[at].astype(F32)
    out[...] = total.astype(BF16)


def small_scratch(nq, groups, rows):
    bits = groups.bit_length() - 1
    return [
        pltpu.VMEM((2 * nq, rows, 128), BF16), pltpu.VMEM((2 * nq, rows, 128), BF16),
        pltpu.VMEM((2 * nq - 1, rows, 128), BF16), pltpu.VMEM((bits, rows, 128), BF16), pltpu.VMEM((bits, rows, 128), BF16),
    ]


def adjoint_flow(me, f_ref, tabs, sel, s_ref, m0, r0, m1, r1, m2, r2, ss, rs, zs, zr):
    nq = me.nq
    one, two, three, four = tabs[4], tabs[5], tabs[6], tabs[7]
    mine = f_ref[...].reshape(3, 2, 64, 128)
    m0[...] = mine.astype(BF16)
    copy = remote(m0, r0, ss.at[0], rs.at[0], me.core)
    copy.start()
    yield
    copy.wait()
    upper_core, upper_side = me.c == 1, me.y == 1
    other = r0[...].astype(F32)
    lower = jnp.where(upper_core, other, mine)
    upper = jnp.where(upper_core, mine, other)
    pair = lower + one * upper
    after = jnp.where(upper_core, 0.0, other)
    m1[...] = pair.astype(BF16)
    copy = remote(m1, r1, ss.at[1], rs.at[1], me.side)
    copy.start()
    yield
    copy.wait()
    far = r1[...].astype(F32)
    low_pair = jnp.where(upper_side, far, pair)
    high_pair = jnp.where(upper_side, pair, far)
    total = low_pair + two * high_pair
    after = jnp.where(upper_side, 0.0, jnp.where(upper_core, far, one * far)) + after
    m2[0] = total[:, 0].astype(BF16)
    for m in range(3):
        m2[1, m] = (sel(0, m) * total[0, 1] + sel(1, m) * total[1, 1] + sel(2, m) * total[2, 1]).astype(BF16)
    sends = []
    for k in range(1, nq):
        copy = remote(m2, r2.at[me.q], zs.at[k - 1], zr.at[k - 1], me.at_quad(me.quad(k)))
        copy.start()
        sends.append(copy)
    r2[me.q] = m2[...]
    yield
    for k in range(1, nq):
        src = r2.at[me.quad(nq - k)]
        remote(src, src, zs.at[k - 1], zr.at[k - 1], me.core).wait_recv()
    run = r2[0, 1].astype(F32)
    for k in range(1, nq):
        run = run + r2[k, 1].astype(F32)
    carry = run
    for k in range(nq - 1, -1, -1):
        carry = jnp.where(me.q == k, run, carry)
        run = four * run + r2[k, 0].astype(F32)
    lead = pick(me.pos, [three, two, one, jnp.ones_like(one)])
    for p in range(3):
        s_ref[2 * p * 64 : (2 * p + 1) * 64] = lead * carry[p] + after[p, 0]
        s_ref[(2 * p + 1) * 64 : (2 * p + 2) * 64] = after[p, 1]
    for copy in sends:
        copy.wait_send()


class Steps:
    def __init__(self, flows):
        self.flows, self.live = flows, [True] * len(flows)

    def __call__(self, *which):
        for i in which:
            if self.live[i]:
                try:
                    next(self.flows[i])
                except StopIteration:
                    self.live[i] = False

    def finish(self):
        while any(self.live):
            self(*range(len(self.flows)))


ORDERS = (True, False, True, False, True)
N_BIG = 5


def layer_kernel(n, groups, *refs):
    refs = list(refs)

    def take(count):
        got = refs[:count]
        del refs[:count]
        return got

    p_rates, p_vecs, (resumed,) = take(4), take(6), take(1)
    cot, h_tokens, i_value, i_reset, i_inner, i_hidden, i_outer, i_shared = take(8)
    o_result, o_input = take(2)
    sums, (out_small,), (staged,) = take(N_BIG), take(1), take(1)
    tabs, power, power_rev, vec_wide, vec_head, starts, w_shared = take(7)
    g_middle, g_act, g_base, slope_s, shared_out = take(5)
    grads, (t_keys_sent, sum_wide, sum_head) = take(N_BIG), take(3)
    gathered, lift, tok, tail, x_lanes, ema, inner, finals = take(8)
    early_all, w_hidden, w_inner, w_outer = take(4)
    (
        values, slope_v, t_values, t_slope, t_keys, t_dv, t_dk, k_units, k_activ, k_gated, k_mid, k_inner, k_branch, k_gin,
        k_greset, k_gvalue,
    ) = take(16)
    g_lanes, b_inner, dx_lanes, k_gs, b_start, acc_in, acc_decay, acc_out, kept, omega_acc, gain_acc = take(11)
    b_flow = finals.at[0:384]
    t_sum, t_grad, t_out, g_small = take(4)
    big = [take(5) for _ in range(N_BIG)]
    small, keys_s, tail_s, back_exchange = take(5), take(5), take(5), take(6)
    exchange = take(6)
    load_sem, ss, sr, hs, hr, ts, tr = take(7)
    early_sem, late_sem = take(8), take(8)
    ess, ers, ezs, ezr, eps, epr = take(6)
    big_send, big_recv, small_send, small_recv, k_send, k_recv, t_send, t_recv, bss, brs, bzs, bzr = take(12)

    me = Place(n, groups)
    length = 128
    width = tok.shape[1]
    lanes = width // 128
    own = tok.shape[0]
    total = own + tail.shape[0] * length
    count = own // length
    chan = width // n
    heads = 128 // n
    rows_b = i_hidden.shape[0]
    sets = count // 2
    sel = chosen(resumed, me)

    def local_copy(src, dst, at):
        copy = pltpu.make_async_copy(src, dst, load_sem.at[at])
        copy.start()
        return copy

    x_in = h_tokens.at[:, 0]
    packing = [
        local_copy(i_value, early_all.at[me.s, 0:chan], 0),
        local_copy(i_reset, early_all.at[me.s, chan : 2 * chan], 1),
        local_copy(i_hidden, w_hidden.at[me.s], 2),
        local_copy(i_inner, w_inner.at[me.s], 3),
        local_copy(i_outer, w_outer.at[me.s], 4),
        local_copy(i_shared, w_shared.at[me.s], 5),
    ]
    fetch = [local_copy(h_tokens.at[p, k], tok.at[(p * 2 + k) * length : (p * 2 + k + 1) * length], 6 + p * 2 + k) for p in range(sets) for k in range(2)]
    lift[...] = jnp.zeros_like(lift)
    block = jnp.zeros((16, 128), F32)
    for i, ref in enumerate(p_rates):
        lift[i, :, 0:chan] = ref[...].astype(F32)
        block = block + pltpu.roll(lift[i], 32 * i, 1)
    for i, ref in enumerate(p_vecs):
        lift[4, i : i + 1, 0 : ref.shape[1]] = ref[...].astype(F32)
    gathered[me.s, 0:16] = block.astype(BF16)
    gathered[me.s, 16:32] = lift[4].astype(BF16)
    meet(me.group_peers() + [me.cross_bit(bit) for bit in me.cross_bits()])
    post = Sender(load_sem.at[12])
    post.device = me.core
    small_gather(me, gathered, post, ss, sr)
    for copy in packing:
        copy.wait()
    early = gather_flow(me, post, [early_all], *early_sem)
    late = gather_flow(me, post, [w_hidden, w_inner, w_outer], *late_sem)
    words = tokens_flow(me, post, x_in, tail, ts, tr, load_sem.at[13])
    next(early)
    next(words)
    next(late)
    small_gather(me, w_shared, post, hs, hr)
    for copy in fetch:
        copy.wait()

    def norm_step(row, carry):
        here = pl.ds(pl.multiple_of(row * length, length), length)
        plain, _ = norm_rows(tok[here, :].astype(F32))
        for lane in range(lanes):
            x_lanes[pl.ds(lane * total + row * length, length), :] = plain[:, lane * 128 : (lane + 1) * 128]
        return carry

    lax.fori_loop(0, count, norm_step, 0)
    small_arrive(me, gathered, post, sr)
    per = 128 // chan
    column = lax.broadcasted_iota(jnp.int32, (16, 128), 1)
    head_sum = jnp.zeros((16, 128), F32)
    for lane in range(lanes):
        rates = [jnp.zeros((16, 128), F32)] * 4
        wide = jnp.zeros((16, 128), F32)
        for k in range(per):
            block = gathered[lane * per + k, 0:16].astype(F32)
            for i in range(4):
                mine = jnp.where((column >= 32 * i) & (column < 32 * i + chan), block, 0.0)
                rates[i] = rates[i] + pltpu.roll(mine, (chan * k - 32 * i) % 128, 1)
            rows = gathered[lane * per + k, 16:32].astype(F32)
            wide = wide + pltpu.roll(rows, chan * k, 1)
            head_sum = head_sum + pltpu.roll(rows, heads * (lane * per + k), 1)
        for i in range(4):
            tabs[9 + i, lane * 16 : lane * 16 + 16] = rates[i]
        vec_wide[:, lane * 128 : (lane + 1) * 128] = wide[0:8]
        vec_head[4 + lane : 5 + lane] = wide[2:3]
    vec_head[0:3] = head_sum[3:6]
    vec_head[3:4] = head_sum[3:4]
    alpha, delta, beta, eta = tabs[9], tabs[10], tabs[11], tabs[12]
    decay = 1.0 - alpha * delta
    chain = [decay]
    for _ in range(9):
        chain.append(chain[-1] * chain[-1])
    ab = alpha * beta
    tabs[10], tabs[11] = beta, delta
    tabs[0], tabs[1], tabs[2], tabs[3] = decay, chain[4], chain[5], chain[6]
    tabs[4], tabs[5], tabs[6], tabs[7] = chain[7], chain[8], chain[8] * chain[7], chain[9]
    tabs[8], tabs[13] = ab * eta, ab
    d16, d32, d64 = chain[4], chain[5], chain[6]
    steps = [jnp.ones_like(decay), d16, d32, d32 * d16, d64, d64 * d16, d64 * d32, d64 * d32 * d16]
    for k in range(8):
        power[pl.ds(k, 64, stride=8), :] = steps[k]
        power_rev[pl.ds(7 - k, 64, stride=8), :] = steps[k]
    for lane in range(lanes):
        x_lanes[lane * total : lane * total + own] = x_lanes[lane * total : lane * total + own] * vec_wide[0:1, lane * 128 : (lane + 1) * 128]

    def local_pass(first, many):
        ema_local_pass(
            total // length, (first, 1, many), x_lanes, tabs.at[0], tabs.at[1], tabs.at[2], tabs.at[3], inner, finals, False
        )

    def apply_pass(first, many):
        ema_apply_pass(total // length, (first, many), x_lanes, tabs.at[0], tabs.at[8], vec_head, power, inner, starts, ema)

    def step(*flows):
        for flow in flows:
            next(flow, None)

    step(words, early)
    local_pass(0, count // 2)
    step(late, early)
    local_pass(count // 2, count // 2)
    state = state_flow(me, finals, tabs, sel, starts, *exchange, ess, ers, ezs, ezr, eps, epr)
    step(state)
    step(late, early)
    step(state)
    step(words, early, late)
    step(state)
    step(early, early)
    step(state)
    step(words)
    for part in range(3):
        apply_pass(part * (count // 3), count // 3)
        step(early)
        if part:
            step(late)
    for _ in words:
        pass

    def tail_norm(m, carry):
        plain, _ = norm_rows(tail[m].astype(F32))
        plain = plain * vec_wide[0:1]
        for lane in range(lanes):
            x_lanes[pl.ds(lane * total + own + m * length, length), :] = plain[:, lane * 128 : (lane + 1) * 128]
        return carry

    lax.fori_loop(0, sets, tail_norm, 0)
    local_pass(count, sets)
    step(late)
    apply_pass(count, sets)
    small_arrive(me, w_shared, post, hr)
    for _ in early:
        pass
    w_value, w_reset = early_all.at[:, 0:chan], early_all.at[:, chan : 2 * chan]
    hv = w_value.shape[2]
    parts = hv // CHUNK
    scale = 1.0 / math.sqrt(128.0)

    def ready(name):
        if name == "hidden":
            for _ in late:
                pass
        elif name in ("tail", "reset"):
            step(late)

    gain_one, gain_two = vec_wide[0:1], vec_wide[1:2]
    q_mul, q_add, k_mul = vec_head[0:1], vec_head[1:2], vec_head[2:3]
    t_dv[...] = jnp.zeros_like(t_dv)
    t_dk[...] = jnp.zeros_like(t_dk)
    sum_wide[...] = jnp.zeros_like(sum_wide)
    sum_head[...] = jnp.zeros_like(sum_head)

    def columns(ref, at):
        block = ref[:, :, at * CHUNK : (at + 1) * CHUNK]
        return block.reshape(block.shape[0] * block.shape[1], CHUNK)

    def rows(ref, at):
        per = CHUNK // rows_b
        return ref[at * per : (at + 1) * per].reshape(CHUNK, ref.shape[2])

    def ema_rows(start, count):
        return jnp.concatenate([ema[pl.ds(lane * total + start, count), :] for lane in range(4)], axis=1)

    def tail_step(m, carry):
        at = pl.multiple_of(m * length, length)
        plain, _ = norm_rows(tail[m].astype(F32))
        units = (plain * gain_one).astype(BF16)
        k_units[pl.ds(own + at, length), :] = units
        for part in range(parts):
            value, slope = silu_pair(nn(units, columns(w_value, part)))
            t_values[m, :, part * CHUNK : (part + 1) * CHUNK] = value.astype(BF16)
            t_slope[m, :, part * CHUNK : (part + 1) * CHUNK] = slope.astype(BF16)
        pre = ema_rows(own + at, length)
        activ = (pre * jax.nn.sigmoid(pre)).astype(BF16)
        shared = nn(activ, w_shared[...].reshape(width, 128))
        t_keys[m] = (shared * jax.nn.sigmoid(shared) * k_mul).astype(BF16)
        return carry

    lax.fori_loop(0, sets, tail_step, 0)
    ready("tail")
    causal = lax.broadcasted_iota(jnp.int32, (length, length), 0) >= lax.broadcasted_iota(jnp.int32, (length, length), 1)

    reset_pre, mixed, slope_i = g_lanes, b_inner, dx_lanes

    def put(ref, part, value):
        for i in range(CHUNK // 128):
            at = (part * (CHUNK // 128) + i) * 2 * length
            ref[at : at + 2 * length] = value[:, i * 128 : (i + 1) * 128]

    def get(ref, part):
        at = [(part * (CHUNK // 128) + i) * 2 * length for i in range(CHUNK // 128)]
        return jnp.concatenate([ref[start : start + 2 * length] for start in at], axis=1)

    def set_step(p, ready):
        here = pl.ds(pl.multiple_of(p * 2 * length, 2 * length), 2 * length)
        m = resumed[0, p * me.nq + me.q]
        x = tok[here, :].astype(F32)
        plain, _ = norm_rows(x)
        units = (plain * gain_one).astype(BF16)
        k_units[here, :] = units
        for part in range(parts):
            cut = slice(part * CHUNK, (part + 1) * CHUNK)
            value, slope = silu_pair(nn(units, columns(w_value, part)))
            values[:, cut] = value.astype(BF16)
            slope_v[:, cut] = slope.astype(BF16)
        ready("reset")
        pre = ema_rows(p * 2 * length, 2 * length)
        activ = (pre * jax.nn.sigmoid(pre)).astype(BF16)
        k_activ[here, :] = activ
        shared, slope = silu_pair(nn(activ, w_shared[...].reshape(width, 128)))
        slope_s[here, :] = slope
        shared_out[here, :] = shared
        queries = (shared * q_mul + q_add).astype(BF16)
        keys = (shared * k_mul).astype(BF16)
        for part in range(parts):
            put(reset_pre, part, nn(activ, columns(w_reset, part)))
        p_q, c_q, p_k, c_k = queries[:length], queries[length:], keys[:length], keys[length:]
        e_k = t_keys[m]

        def weights(scores):
            expo = jnp.exp(scores - jnp.max(scores, axis=-1, keepdims=True))
            return expo * (1.0 / jnp.sum(expo, axis=-1, keepdims=True))

        p_probs = weights(jnp.where(causal, nt(p_q, p_k) * scale, MASKED_SCORE))
        c_probs = weights(
            jnp.concatenate((nt(c_q, e_k) * scale, jnp.where(causal, nt(c_q, c_k) * scale, MASKED_SCORE)), axis=1)
        )
        p_low, c_low = p_probs.astype(BF16), c_probs.astype(BF16)
        for part in range(parts):
            cut = slice(part * CHUNK, (part + 1) * CHUNK)
            mix_p = nn(p_low, values[:length, cut])
            mix_c = nn(c_low, jnp.concatenate((t_values[m, :, cut], values[length:, cut]), axis=0))
            mix = jnp.concatenate((mix_p, mix_c), axis=0)
            put(mixed, part, mix)
            gate = get(reset_pre, part)
            k_gated[here, cut] = (gate * jax.nn.sigmoid(gate) * mix).astype(BF16)
        ready("hidden")
        middle = x + nn(k_gated[here, :], w_hidden[...].reshape(-1, width))
        plain_mid, inv_mid = norm_rows(middle)
        mid_low = (plain_mid * gain_two).astype(BF16)
        k_mid[here, :] = mid_low
        ready("inner")
        for part in range(parts):
            cut = slice(part * CHUNK, (part + 1) * CHUNK)
            inner, slope = silu_pair(nn(mid_low, columns(w_inner, part)))
            k_inner[here, cut] = inner.astype(BF16)
            put(slope_i, part, slope)
        ready("outer")
        staged[here, :] = (middle + nn(k_inner[here, :], w_outer[...].reshape(-1, width))).astype(BF16)
        top = cot[here, :]
        for part in range(parts):
            cut = slice(part * CHUNK, (part + 1) * CHUNK)
            k_gin[here, cut] = (nt(top, rows(w_outer, part)) * get(slope_i, part)).astype(BF16)
        back = nt(k_gin[here, :], w_inner[...].reshape(width, -1))
        sum_wide[0:1] += jnp.sum(back * plain_mid, axis=0, keepdims=True)
        g_mid = top.astype(F32) + norm_back(back, plain_mid, inv_mid, gain_two)
        g_middle[here, :] = g_mid
        branch = g_mid.astype(BF16)
        k_branch[here, :] = branch
        dp_p = jnp.zeros((length, length), F32)
        dp_c = jnp.zeros((length, 2 * length), F32)
        for part in range(parts):
            cut = slice(part * CHUNK, (part + 1) * CHUNK)
            gated_back = nt(branch, rows(w_hidden, part))
            gate, slope = silu_pair(get(reset_pre, part))
            g_mix = (gated_back * gate).astype(BF16)
            k_greset[here, cut] = (gated_back * get(mixed, part) * slope).astype(BF16)
            dp_p += nt(g_mix[:length], values[:length, cut])
            dp_c += nt(g_mix[length:], jnp.concatenate((t_values[m, :, cut], values[length:, cut]), axis=0))
            dv_p = tn(p_low, g_mix[:length])
            dv_c = tn(c_low, g_mix[length:])
            for to in range(sets):
                t_dv[to, :, cut] += sel(p, to) * dv_c[:length]
            dv = jnp.concatenate((dv_p, dv_c[length:]), axis=0)
            k_gvalue[here, cut] = (dv * slope_v[:, cut].astype(F32)).astype(BF16)
        g_act[here, :] = nt(k_greset[here, :], w_reset[...].reshape(width, -1))

        def score_back(probs, grads):
            return (probs * (grads - jnp.sum(grads * probs, axis=-1, keepdims=True))).astype(BF16)

        p_ds, c_ds = score_back(p_probs, dp_p), score_back(c_probs, dp_c)
        d_q = jnp.concatenate((nn(p_ds, p_k), nn(c_ds, jnp.concatenate((e_k, c_k), axis=0))), axis=0) * scale
        dk_c = tn(c_ds, c_q) * scale
        for to in range(sets):
            t_dk[to] += sel(p, to) * dk_c[:length]
        d_k = jnp.concatenate((tn(p_ds, p_q) * scale, dk_c[length:]), axis=0)
        sum_head[0:1] += jnp.sum(d_q * shared, axis=0, keepdims=True)
        sum_head[1:2] += jnp.sum(d_q, axis=0, keepdims=True)
        sum_head[2:3] += jnp.sum(d_k * shared, axis=0, keepdims=True)
        g_base[here, :] = d_q * q_mul + d_k * k_mul

    def quiet(name):
        return None

    def later_step(p, carry):
        set_step(p, quiet)
        return carry

    set_step(0, ready)
    lax.fori_loop(1, sets, later_step, 0)
    leave = local_copy(staged, o_result, 0)
    tail_rows = length // 4
    for part in range(4):
        t_keys_sent[part // 2, part % 2] = t_dk[:, part * tail_rows : (part + 1) * tail_rows].astype(BF16)
    keys = tail_flow(me, t_keys_sent, *keys_s, t_sum, k_send, k_recv)
    next(keys)
    for ref in (omega_acc, gain_acc, acc_in, acc_decay, acc_out):
        ref[...] = jnp.zeros_like(ref)

    def grad_rows(row, with_tail):
        at = pl.multiple_of(row * length, length)
        here = pl.ds(at, length)
        d_shared = g_base[here, :]
        if with_tail:
            extra = jnp.concatenate([t_sum[part // 2, part % 2, row // 2] for part in range(4)], axis=0).astype(F32)
            d_shared = d_shared + extra * k_mul
            gain_acc[1:2, 0:128] += jnp.sum(extra * shared_out[here, :], axis=0, keepdims=True)
        gs = (d_shared * slope_s[here, :]).astype(BF16)
        k_gs[here, :] = gs
        for lane in range(lanes):
            cut = slice(lane * 128, (lane + 1) * 128)
            pre = ema[pl.ds(lane * total + at, length), :]
            sig = jax.nn.sigmoid(pre)
            back = g_act[here, cut] + nt(gs, w_shared[lane * per : (lane + 1) * per].reshape(128, 128))
            back = back * (sig * (1.0 + pre * (1.0 - sig)))
            g_lanes[pl.ds(lane * own + at, length), :] = back
            x = x_lanes[pl.ds(lane * total + at, length), :]
            omega_acc[lane : lane + 1] += jnp.sum(back * x, axis=0, keepdims=True)

    def local_back(first):
        ema_local_pass(
            count, (first, 2, count // 2), g_lanes, tabs.at[0], tabs.at[1], tabs.at[2], tabs.at[3], b_inner, b_flow, True
        )

    def cont_rows(p, carry):
        grad_rows(2 * p + 1, False)
        return carry

    def prompt_rows(p, carry):
        grad_rows(2 * p, True)
        return carry

    def norm_rows_back(x, units):
        plain, inv = norm_rows(x.astype(F32))
        gain_acc[0:1] += jnp.sum(units * plain, axis=0, keepdims=True)
        return norm_back(units, plain, inv, gain_one)

    def weight_grad(lhs, rhs, out, many):
        block_rows = CHUNK // out.shape[2] // 2

        def step(i, carry):
            block = tn(lhs[0:many, pl.ds(pl.multiple_of(i * CHUNK, CHUNK), CHUNK)], rhs[0:many, :])
            out[pl.ds(i * block_rows, block_rows)] = block.astype(BF16).reshape(block_rows, 2, out.shape[2], out.shape[3])
            return carry

        lax.fori_loop(0, lhs.shape[1] // CHUNK, step, 0)

    steps = Steps(
        [big_flow(me, ORDERS[i], grads[i], *big[i], sums[i], big_send.at[i], big_recv.at[i]) for i in range(N_BIG)]
    )
    weight_grad(k_inner, cot, grads[0], own)
    steps(0)
    next(keys)
    weight_grad(k_mid, k_gin, grads[1], own)
    steps(1, 0)
    lax.fori_loop(0, count // 2, cont_rows, 0)
    next(keys)
    weight_grad(k_gated, k_branch, grads[2], own)
    steps(2, 1)
    local_back(1)
    next(keys)
    weight_grad(k_activ, k_greset, grads[3], own)
    steps(3, 2)
    for _ in keys:
        pass
    lax.fori_loop(0, count // 2, prompt_rows, 0)
    local_back(0)
    adjoint = adjoint_flow(me, b_flow, tabs, sel, b_start, *back_exchange, bss, brs, bzs, bzr)
    next(adjoint)
    steps(3, 0)

    def tail_back(m, carry):
        at = pl.multiple_of(own + m * length, length)
        k_gvalue[pl.ds(at, length), :] = (t_dv[m] * t_slope[m].astype(F32)).astype(BF16)
        return carry

    lax.fori_loop(0, sets, tail_back, 0)
    next(adjoint)
    weight_grad(k_units, k_gvalue, grads[4], total)
    steps(4, 1)
    next(adjoint)

    def units_step(i, carry):
        at = pl.multiple_of(i * CHUNK, CHUNK)
        block = nt(k_gvalue[pl.ds(at, CHUNK), :], w_value[...].reshape(width, -1))
        for lane in range(lanes):
            dx_lanes[pl.ds(lane * own + at, CHUNK), :] = block[:, lane * 128 : (lane + 1) * 128]
        return carry

    lax.fori_loop(0, own // CHUNK, units_step, 0)

    def tail_grad_step(m, carry):
        at = pl.multiple_of(own + m * length, length)
        units = nt(k_gvalue[pl.ds(at, length), :], w_value[...].reshape(width, -1))
        block = norm_rows_back(tail[m], units).astype(BF16)
        for part in range(4):
            t_grad[part // 2, part % 2, m] = block[part * tail_rows : (part + 1) * tail_rows]
        return carry

    lax.fori_loop(0, sets, tail_grad_step, 0)
    ends = tail_flow(me, t_grad, *tail_s, t_out, t_send, t_recv)
    next(ends)
    steps(2, 4)
    for _ in adjoint:
        pass
    for row in range(count):
        ema_back_pass(
            count, total // length, row, x_lanes, g_lanes, tabs.at[0], tabs.at[8], vec_head, power, inner, starts,
            power_rev, b_inner, b_start, dx_lanes, acc_in, acc_decay, acc_out, kept,
        )
        if row < 3:
            next(ends)
        if row < count - 1:
            steps(*range(N_BIG))

    def own_rows(row, carry):
        here = pl.ds(pl.multiple_of(row * length, length), length)
        units = jnp.concatenate(
            [dx_lanes[pl.ds(lane * own + row * length, length), :] for lane in range(lanes)], axis=1
        )
        g_middle[here, :] = g_middle[here, :] + norm_rows_back(tok[here, :], units)
        return carry

    lax.fori_loop(0, count, own_rows, 0)
    alpha, beta, delta, eta, ab = (tabs[9 + i] for i in range(5))
    m_sum, q_sum = eta * acc_in[...], eta * ab * acc_decay[...]
    parts = (beta * m_sum - delta * q_sum, -alpha * q_sum, alpha * m_sum, ab * acc_out[...])
    per = 128 // chan // 2
    for lane in range(lanes):
        cut = slice(lane * 128, (lane + 1) * 128)
        block = [part[lane * 16 : lane * 16 + 16] for part in parts]
        block += [omega_acc[lane : lane + 1], gain_acc[0:1, cut], sum_wide[0:1, cut], jnp.zeros((61, 128), F32)]
        block = jnp.concatenate(block, axis=0).T.astype(BF16)
        g_small[lane * per : (lane + 1) * per, :, 0:chan] = block.reshape(per, 2, chan, 128)
    block = tn(k_activ[...], k_gs[...]).astype(BF16)
    g_small[:, :, chan : 2 * chan] = block.reshape(n // 2, 2, chan, 128)
    heads = jnp.concatenate((sum_head[0:2], sum_head[2:3] + gain_acc[1:2, 0:128], jnp.zeros((13, 128), F32)), axis=0)
    heads = jnp.broadcast_to(heads.astype(BF16)[None, None], (n // 2, 2, 16, 128))
    g_small[:, :, 2 * chan :] = heads
    little = small_flow(me, g_small, *small, out_small, small_send, small_recv)
    next(little)
    for _ in ends:
        pass
    next(little)
    steps(*range(N_BIG))
    for part in range(4):
        for m in range(sets):
            at = 2 * m * length + part * tail_rows
            here = slice(at, at + tail_rows)
            g_middle[here] = g_middle[here] + t_out[part // 2, part % 2, m].astype(F32)

    def cast_rows(row, carry):
        here = pl.ds(pl.multiple_of(row * length, length), length)
        staged[here, :] = g_middle[here, :].astype(BF16)
        return carry

    leave.wait()
    lax.fori_loop(0, count, cast_rows, 0)
    leave = local_copy(staged, o_input, 1)
    next(little)
    steps(*range(N_BIG))
    for _ in little:
        pass
    steps.finish()
    post.finish()
    leave.wait()


def layer_call(n, groups, rates, vectors, resumed, cot, tokens, weights):
    nq = n // 4
    dma = pltpu.SemaphoreType.DMA
    vm = pltpu.VMEM
    shape = jax.ShapeDtypeStruct
    sets, kinds, length, width = tokens.shape
    own = sets * kinds * length
    total = own + sets * length
    chan, hv = weights[0].shape
    rows_b = weights[3].shape[0]
    small_rows = 2 * chan + 16
    wide, tall = (n // 2, 2, chan, hv), (n // 2, 2, rows_b, width)
    shapes = [tall, wide, tall, wide, wide]
    piece = (sets, length // 4)
    outs = [shape((own, width), BF16)] * 2 + [shape(part[2:], BF16) for part in shapes] + [shape((small_rows, 128), BF16)]
    scratch = [
        vm((own, width), BF16), vm((14, 64, 128), F32), vm((512, 128), F32), vm((512, 128), F32), vm((8, width), F32), vm((8, 128), F32),
        vm((total // 2, 128), F32), vm((n, chan, 128), BF16),
        vm((own, width), F32), vm((own, width), F32), vm((own, 128), F32), vm((own, 128), F32), vm((own, 128), F32),
    ]
    scratch += [vm(part, BF16) for part in shapes]
    scratch += [vm((2, 2, *piece, 128), BF16), vm((8, width), F32), vm((8, 128), F32)]
    scratch += [
        vm((n, 32, 128), BF16), vm((5, 16, 128), F32), vm((own, width), BF16), vm((sets, length, width), BF16),
        vm((total * 4, 128), F32), vm((total * 4, 128), F32), vm((total * 4, 128), F32), vm((total // 2, 128), F32),
        vm((n, 2 * chan, hv), BF16), vm((n, rows_b, width), BF16), vm((n, chan, hv), BF16), vm((n, rows_b, width), BF16),
        vm((2 * length, hv), BF16), vm((2 * length, hv), BF16),
        vm((sets, length, hv), BF16), vm((sets, length, hv), BF16), vm((sets, length, 128), BF16),
        vm((sets, length, hv), F32), vm((sets, length, 128), F32),
        vm((total, width), BF16), vm((own, width), BF16), vm((own, hv), BF16), vm((own, width), BF16),
        vm((own, hv), BF16), vm((own, width), BF16), vm((own, hv), BF16), vm((own, hv), BF16), vm((total, hv), BF16),
    ]
    scratch += [vm((own * 4, 128), F32)] * 3 + [vm((own, 128), BF16), vm((own // 2, 128), F32)]
    scratch += [vm((64, 128), F32)] * 3 + [vm((128, 8, 128), F32), vm((8, 128), F32), vm((8, width), F32)]
    scratch += [
        vm((2, 2, *piece, 128), BF16), vm((2, 2, *piece, width), BF16),
        vm((2, 2, *piece, width), BF16), vm((n // 2, 2, small_rows, 128), BF16),
    ]
    for i, part in enumerate(shapes):
        scratch += big_scratch(nq, groups, ORDERS[i], *part[2:])
    scratch += small_scratch(nq, groups, small_rows)
    scratch += tail_scratch(nq, (*piece, 128)) + tail_scratch(nq, (*piece, width))
    scratch += [vm((3, 2, 64, 128), BF16)] * 4 + [vm((2, 3, 64, 128), BF16), vm((nq, 2, 3, 64, 128), BF16)]
    scratch += [vm((3, 2, 64, 128), BF16)] * 2 + [vm((2, 3, 2, 64, 128), BF16)] * 2
    scratch += [vm((2, 3, 64, 128), BF16), vm((nq + 1, 3, 64, 128), BF16)]
    scratch += [dma((18,)), dma((n - 1,)), dma((n - 1,)), dma((n - 1,)), dma((n - 1,)), dma((nq + 5,)), dma((5,))]
    scratch += gather_sems(nq, 1) + gather_sems(nq, 3)
    scratch += [dma((2,)), dma((2,)), dma((nq - 1,)), dma((nq - 1,)), dma((nq - 1,)), dma((1,))]
    sems = 2 * nq + 3 + max(groups.bit_length() - 2, 1)
    small_sems = 2 * nq + groups.bit_length() - 1
    scratch += [
        dma((N_BIG, sems)), dma((N_BIG, sems)), dma((small_sems,)), dma((small_sems,)), dma((3,)), dma((nq + 4,)),
        dma((3,)), dma((nq + 4,)), dma((2,)), dma((2,)), dma((nq - 1,)), dma((nq - 1,)),
    ]
    return pl.pallas_call(
        functools.partial(layer_kernel, n, groups),
        out_shape=outs,
        in_specs=[VMEM] * 10 + [SMEM, VMEM] + [HBM] * 7,
        out_specs=[HBM] * 2 + [VMEM] * (len(outs) - 2),
        scratch_shapes=scratch,
        compiler_params=pltpu.CompilerParams(collective_id=0, has_side_effects=True, vmem_limit_bytes=63 << 20),
        name="layer",
    )(*rates, *vectors, resumed, cot, tokens, *weights)


def finish_kernel(heads, grad_in, *refs):
    sums, small, grad_out = refs[:N_BIG], refs[N_BIG], refs[N_BIG + 1]
    outs = refs[N_BIG + 2 : 2 * N_BIG + 2]
    shared, rates, vecs = refs[2 * N_BIG + 2], refs[2 * N_BIG + 3 : 2 * N_BIG + 7], refs[2 * N_BIG + 7 : 2 * N_BIG + 13]
    grad_out[...] = grad_in[...]
    for src, dst in zip(sums, outs):
        dst[...] = src[...].astype(F32)
    chan = shared.shape[0]
    shared[...] = small[chan : 2 * chan].astype(F32)
    block = small[0:chan].astype(F32).T
    for i, ref in enumerate(rates):
        ref[...] = block[16 * i : 16 * i + 16]
    for i in range(3):
        vecs[i][...] = block[64 + i : 65 + i]
    mine = lax.axis_index("seq") * heads
    rows = pltpu.roll(small[2 * chan : 2 * chan + 16].astype(F32), (128 - mine) % 128, 1)
    for i in range(3):
        vecs[3 + i][...] = rows[i : i + 1, 0:heads]


def finish_call(n, heads, input_grad, sums, small):
    shape = jax.ShapeDtypeStruct
    chan = (small.shape[0] - 16) // 2
    outs = [shape(input_grad.shape, BF16)] + [shape(part.shape, F32) for part in sums] + [shape((chan, 128), F32)]
    outs += [shape((16, chan), F32)] * 4 + [shape((1, chan), F32)] * 3 + [shape((1, heads), F32)] * 3
    return pl.pallas_call(
        functools.partial(finish_kernel, heads),
        out_shape=outs,
        in_specs=[VMEM] * (N_BIG + 2),
        out_specs=[VMEM] * len(outs),
        compiler_params=pltpu.CompilerParams(vmem_limit_bytes=60 << 20),
        name="finish",
    )(input_grad, *sums, small)


def local(
    hidden_in, cotangent, cont_prompt, value_proj, shared_proj, reset_proj, hidden_proj, inner_proj,
    outer_proj, ema_alpha, ema_delta, ema_beta, ema_eta, ema_omega, norm_gain, ffn_gain, query_scale,
    query_shift, key_scale,
):
    n, groups = lax.axis_size("seq"), lax.axis_size("grp")
    sets, kinds, length, width = hidden_in.shape[1:]
    heads = query_scale.shape[0]
    own_rows = sets * kinds * length
    vectors = (norm_gain, ffn_gain, ema_omega, query_scale, query_shift, key_scale)
    result, input_grad, *sums, d_small = layer_call(
        n, groups, [part.T for part in (ema_alpha, ema_delta, ema_beta, ema_eta)], [part[None] for part in vectors],
        cont_prompt, cotangent[0].reshape(own_rows, width), hidden_in[0],
        (value_proj, reset_proj, inner_proj, hidden_proj, outer_proj, shared_proj),
    )
    wide = finish_call(n, heads, input_grad, sums, d_small)
    input_grad, d_outer, d_inner, d_hidden, d_reset, d_value, d_shared = wide[:7]
    rates = [part.T for part in wide[7:11]]
    vecs = [part.reshape(part.shape[1]) for part in wide[11:17]]
    return (
        result.reshape(hidden_in.shape), input_grad.reshape(hidden_in.shape), d_value, d_shared, d_reset, d_hidden, d_inner,
        d_outer, *rates, *vecs,
    )


def solution(mesh):
    mat, vec = P("seq", None), P("seq")
    tok = P("grp", None, None, "seq", None)
    in_specs = (tok, tok, P("grp", None)) + (mat,) * 10 + (vec,) * 6
    out_specs = (tok, tok) + (mat,) * 10 + (vec,) * 6
    return jax.shard_map(local, mesh=mesh, in_specs=in_specs, out_specs=out_specs, check_vma=False)
```

```python
import functools
import math

import jax
import jax.numpy as jnp
from jax import lax
from jax.experimental import pallas as pl
from jax.experimental.pallas import tpu as pltpu
from jax.sharding import PartitionSpec as P

CLEN = 512
NORM_EPS = 1e-05
MASKED_SCORE = -1e30
MESH = pl.DeviceIdType.MESH
SUB = 16
NJ = 16
TINY = 1e-20
F32 = jnp.float32
BF16 = jnp.bfloat16
VMEM = pl.BlockSpec(memory_space=pltpu.VMEM)
HBM = pl.BlockSpec(memory_space=pltpu.HBM)
SMEM = pl.BlockSpec(memory_space=pltpu.SMEM)


def shift_down(value, count):
    rows = lax.broadcasted_iota(jnp.int32, value.shape, 0)
    return jnp.where(rows >= count, pltpu.roll(value, count, 0), 0.0)


def shift_up(value, count):
    rows = lax.broadcasted_iota(jnp.int32, value.shape, 0)
    return jnp.where(rows < 8 - count, pltpu.roll(value, 8 - count, 0), 0.0)


def row_of(ref, row):
    return jnp.broadcast_to(ref[pl.ds(row, 1), :], (8, 128))


def ema_local_pass(rows, pick_rows, x_ref, decay, decay16, decay32, decay64, inner_ref, final_ref, backward):
    shift = shift_up if backward else shift_down

    first, stride, many = pick_rows

    def body(turn, carry):
        row, lane = first + stride * (turn // 4), turn % 4
        item = row * 4 + lane
        base = lane * (rows * 128) + row * 128
        dec = [row_of(decay, lane * 16 + j) for j in range(NJ)]
        state = [jnp.zeros((8, 128), F32)] * NJ
        for step in range(SUB - 1, -1, -1) if backward else range(SUB):
            x = x_ref[pl.ds(base + step, 8, stride=SUB), :]
            if backward:
                state = [dec[j] * (state[j] + x) for j in range(NJ)]
            else:
                state = [dec[j] * state[j] + x for j in range(NJ)]
        for j in range(NJ):
            total = state[j]
            total = total + row_of(decay16, lane * 16 + j) * shift(total, 1)
            total = total + row_of(decay32, lane * 16 + j) * shift(total, 2)
            total = total + row_of(decay64, lane * 16 + j) * shift(total, 4)
            inner_ref[pl.ds((item * 16 + j) * 8, 8), :] = shift(total, 1)
            final_ref[pl.ds(row * 64 + lane * 16 + j, 1), :] = total[0:1] if backward else total[7:8]
        return carry

    lax.fori_loop(0, many * 4, body, 0)


def ema_apply_pass(rows, pick_rows, x_ref, decay, mix, omega, power, inner_ref, start_ref, y_ref):
    first, many = pick_rows

    def body(turn, carry):
        row, lane = first + turn // 4, turn % 4
        item = row * 4 + lane
        base = lane * (rows * 128) + row * 128
        state = [
            inner_ref[pl.ds((item * 16 + j) * 8, 8), :]
            + power[pl.ds((lane * 16 + j) * 8, 8), :] * row_of(start_ref, row * 64 + lane * 16 + j)
            for j in range(NJ)
        ]
        skip = row_of(omega, 4 + lane)
        for step in range(SUB):
            x = x_ref[pl.ds(base + step, 8, stride=SUB), :]
            sums = [skip * x, None]
            for j in range(NJ):
                state[j] = row_of(decay, lane * 16 + j) * state[j] + x
                term = row_of(mix, lane * 16 + j) * state[j]
                sums[j % 2] = term if sums[j % 2] is None else sums[j % 2] + term
            y_ref[pl.ds(base + step, 8, stride=SUB), :] = sums[0] + sums[1]
        return carry

    lax.fori_loop(0, many * 4, body, 0)


def ema_back_pass(
    rows, x_rows, row, x_ref, g_ref, decay, mix, omega, power, inner_ref, start_ref, power_rev,
    back_inner_ref, back_start_ref, dx_ref, sum_in, sum_decay, sum_out, kept,
):
    half = 8

    def body(lane, carry):
        item = row * 4 + lane
        base = lane * (rows * 128) + row * 128
        x_base = lane * (x_rows * 128) + row * 128
        skip = row_of(omega, 4 + lane)
        for part in range(NJ // half):
            js = range(part * half, part * half + half)
            dec = [row_of(decay, lane * 16 + j) for j in js]
            state = [
                inner_ref[pl.ds((item * 16 + j) * 8, 8), :]
                + power[pl.ds((lane * 16 + j) * 8, 8), :] * row_of(start_ref, row * 64 + lane * 16 + j)
                for j in js
            ]
            for step in range(SUB):
                if part == 0:
                    x = x_ref[pl.ds(x_base + step, 8, stride=SUB), :]
                    kept[SUB * half + step] = x
                else:
                    x = kept[SUB * half + step]
                for i in range(half):
                    kept[step * half + i] = state[i]
                    state[i] = dec[i] * state[i] + x
            adj = [
                back_inner_ref[pl.ds((item * 16 + j) * 8, 8), :]
                + power_rev[pl.ds((lane * 16 + j) * 8, 8), :]
                * row_of(back_start_ref, row * 64 + lane * 16 + j)
                for j in js
            ]
            weight = [row_of(mix, lane * 16 + j) for j in js]
            edge = [-(adj[i] * state[i]) for i in range(half)]
            first, second = [None] * half, [None] * half
            for step in range(SUB - 1, -1, -1):
                x = kept[SUB * half + step]
                at = pl.ds(base + step, 8, stride=SUB)
                if part == 0:
                    g = g_ref[at, :]
                    kept[SUB * (half + 1) + step] = g
                    sums = [dx_ref[at, :], skip * g]
                else:
                    g = kept[SUB * (half + 1) + step]
                    sums = [kept[SUB * (half + 2) + step], None]
                for i in range(half):
                    full = adj[i] + g
                    term = weight[i] * full
                    sums[i % 2] = term if sums[i % 2] is None else sums[i % 2] + term
                    with_x, with_s = full * x, full * kept[step * half + i]
                    first[i] = with_x if first[i] is None else first[i] + with_x
                    second[i] = with_s if second[i] is None else second[i] + with_s
                    adj[i] = dec[i] * full
                if part == 0:
                    kept[SUB * (half + 2) + step] = sums[0] + sums[1]
                else:
                    dx_ref[at, :] = sums[0] + sums[1]
            for i, j in enumerate(js):
                at = pl.ds(lane * 16 + j, 1)
                flow = edge[i] + adj[i] * kept[i]
                total = jnp.sum(first[i], axis=0, keepdims=True)
                sum_in[at, :] += total
                sum_decay[at, :] += jnp.sum(second[i], axis=0, keepdims=True)
                sum_out[at, :] += total + jnp.sum(flow, axis=0, keepdims=True)
        return carry

    lax.fori_loop(0, 4, body, 0)


class Place:
    def __init__(self, n, groups):
        self.n, self.nq, self.groups = n, n // 4, groups
        self.g, self.s = lax.axis_index("grp"), lax.axis_index("seq")
        self.c, self.y, self.q, self.x = self.s % 2, (self.s // 2) % 2, self.s // 4, self.g % 2
        self.pos = self.s % 4
        self.core = (self.g, self.s + 1 - 2 * self.c)
        self.side = (self.g, self.s + 2 - 4 * self.y)
        self.cross = (self.g + 1 - 2 * self.x, self.s)
        self.is_last = self.s == n - 1

    def quad(self, k):
        return (self.q + k) % self.nq

    def at_quad(self, q):
        return (self.g, q * 4 + self.pos)

    def group_peers(self):
        return [(self.g, (self.s + k) % self.n) for k in range(1, self.n)]

    def cross_bit(self, bit):
        return (self.g + bit - 2 * bit * ((self.g // bit) % 2), self.s)

    def cross_bits(self):
        return [1 << b for b in range(self.groups.bit_length() - 1)]


def chosen(resumed, me):
    def at(p, m):
        return jnp.where(resumed[0, p * me.nq + me.q] == m, 1.0, 0.0)

    return at


def meet(peers):
    barrier = pltpu.get_barrier_semaphore()
    for peer in peers:
        pl.semaphore_signal(barrier, inc=1, device_id=peer, device_id_type=MESH)
    pl.semaphore_wait(barrier, len(peers))


def remote(src, dst, send, recv, device):
    return pltpu.make_async_remote_copy(
        src_ref=src, dst_ref=dst, send_sem=send, recv_sem=recv, device_id=device, device_id_type=MESH
    )


def pick(index, values):
    out = values[0]
    for k in range(1, len(values)):
        out = jnp.where(index == k, values[k], out)
    return out


def tail_flow(me, t, r1, w1, r2, w2, r3, out, send, recv):
    nq = me.nq
    last = me.q == nq - 1
    out[...] = jnp.zeros_like(out)
    copy1 = remote(t.at[:, 1 - me.c], r1, send.at[0], recv.at[0], me.core)
    copy1.start()
    yield
    copy1.wait()
    for i in range(2):
        w1[i] = (t[i, me.c].astype(F32) + r1[i].astype(F32)).astype(BF16)
    copy2 = remote(w1.at[1 - me.y], r2, send.at[1], recv.at[1], me.side)
    copy2.start()
    yield
    copy2.wait()
    w2[...] = (w1[me.y].astype(F32) + r2[...].astype(F32)).astype(BF16)
    top = (me.g, (nq - 1) * 4 + me.pos)
    end = (me.g, nq * 4 - 1)
    for k in range(nq - 1):
        @pl.when(me.q == k)
        def _():
            remote(w2, r3.at[k], send.at[2], recv.at[2 + k], top).start()
    yield

    @pl.when(last)
    def _():
        total = w2[...].astype(F32)
        for k in range(nq - 1):
            remote(r3.at[k], r3.at[k], send.at[2], recv.at[2 + k], me.core).wait_recv()
            total = total + r3[k].astype(F32)
        w2[...] = total.astype(BF16)

        @pl.when(jnp.logical_not(me.is_last))
        def _():
            for j in range(3):
                @pl.when(me.pos == j)
                def _():
                    remote(w2, out.at[j // 2, j % 2], send.at[2], recv.at[nq + 1 + j], end).start()

        @pl.when(me.is_last)
        def _():
            out[1, 1] = w2[...]
    yield

    @pl.when(me.is_last)
    def _():
        for j in range(3):
            dst = out.at[j // 2, j % 2]
            remote(dst, dst, send.at[2], recv.at[nq + 1 + j], me.core).wait_recv()

    @pl.when(jnp.logical_not(me.is_last))
    def _():
        remote(w2, w2, send.at[2], recv.at[2], me.core).wait_send()


def tail_scratch(nq, shape):
    vm = pltpu.VMEM
    return [vm((2, *shape), BF16), vm((2, *shape), BF16), vm(shape, BF16), vm(shape, BF16), vm((nq - 1, *shape), BF16)]


class Sender:
    def __init__(self, spare):
        self.spare, self.started = spare, []

    def send(self, src, dst, send, recv, device, when=None):
        copy = remote(src, dst, send, recv, device)
        if when is None:
            copy.start()
        else:
            pl.when(when)(copy.start)
        self.started.append((copy, when))

    def got(self, ref, recv):
        remote(ref, ref, self.spare, recv, self.device).wait_recv()

    def finish(self):
        for copy, when in self.started:
            if when is None:
                copy.wait_send()
            else:
                pl.when(when)(copy.wait_send)


def small_gather(me, out, post, ss, sr):
    for k in range(1, me.n):
        post.send(out.at[me.s], out.at[me.s], ss.at[k - 1], sr.at[k - 1], (me.g, (me.s + k) % me.n))


def small_arrive(me, out, post, sr):
    for k in range(1, me.n):
        post.got(out.at[(me.s + me.n - k) % me.n], sr.at[k - 1])


def gather_flow(me, post, mats, zs, zr, ys, yr, xs, xr, cs, cr):
    nq = me.nq
    mats = [(out, out.shape[-1] // 2) for out in mats]
    other = 1 - me.x

    def half(ref, width, which):
        return ref.at[:, pl.ds(pl.multiple_of(which * width, 128), width)]

    def pieces(k, pos, which):
        shard = me.quad(nq - k) * 4 + pos
        return [half(out.at[shard], width, which) for out, width in mats]

    for i, (out, width) in enumerate(mats):
        mine = out.at[me.s]
        piece = half(mine, width, me.x)
        for k in range(1, nq):
            post.send(piece, piece, zs.at[k - 1, i], zr.at[k - 1, i], me.at_quad(me.quad(k)))
        post.send(mine, mine, ys.at[0, i], yr.at[0, i], me.side)
    for i, (out, width) in enumerate(mats):
        post.send(out.at[me.s], out.at[me.s], cs.at[0, i], cr.at[0, i], me.core)
    yield
    side_pos = me.pos + 2 - 4 * me.y
    for k in range(1, nq):
        for i, piece in enumerate(pieces(k, me.pos, me.x)):
            post.got(piece, zr.at[k - 1, i])
            post.send(piece, piece, ys.at[k, i], yr.at[k, i], me.side)
            post.send(piece, piece, xs.at[k - 1, i], xr.at[k - 1, i], me.cross)
            post.send(piece, piece, cs.at[k, i], cr.at[k, i], me.core)
        yield
    for k in range(nq):
        blocks = pieces(k, side_pos, me.x) if k else [out.at[me.q * 4 + side_pos] for out, _ in mats]
        for i, piece in enumerate(blocks):
            post.got(piece, yr.at[k, i])
            if k:
                post.send(piece, piece, xs.at[nq - 2 + k, i], xr.at[nq - 2 + k, i], me.cross)
            post.send(piece, piece, cs.at[nq + k, i], cr.at[nq + k, i], me.core)
        if k:
            yield
    for group, pos in ((0, me.pos), (1, side_pos)):
        for k in range(1, nq):
            at = group * (nq - 1) + k - 1
            for i, piece in enumerate(pieces(k, pos, other)):
                post.got(piece, xr.at[at, i])
                post.send(piece, piece, cs.at[2 * nq + at, i], cr.at[2 * nq + at, i], me.core)
        yield
    flip = 1 - 2 * me.c
    for group, pos in ((0, me.pos + flip), (1, side_pos + flip)):
        for i, (out, _) in enumerate(mats):
            post.got(out.at[me.q * 4 + pos], cr.at[group * nq, i])
        for k in range(1, nq):
            for i, piece in enumerate(pieces(k, pos, me.x)):
                post.got(piece, cr.at[group * nq + k, i])
            for i, piece in enumerate(pieces(k, pos, other)):
                post.got(piece, cr.at[2 * nq + group * (nq - 1) + k - 1, i])


def tokens_flow(me, post, x_in, x_out, ts, tr, local_sem):
    nq = me.nq
    rows = x_out.shape[1] // 4

    def quarter(ref, pos):
        return ref.at[:, pl.ds(pl.multiple_of(pos * rows, rows), rows)]

    in_last = me.q == nq - 1
    side_pos, flip = me.pos + 2 - 4 * me.y, 1 - 2 * me.c
    keep = pltpu.make_async_copy(quarter(x_in, me.pos), quarter(x_out, me.pos), local_sem)
    pl.when(me.is_last)(keep.start)
    for j in range(3):
        post.send(quarter(x_in, j), quarter(x_out, j), ts.at[j], tr.at[0], (me.g, 4 * (nq - 1) + j), me.is_last)
    yield

    @pl.when(jnp.logical_and(in_last, jnp.logical_not(me.is_last)))
    def _():
        post.got(quarter(x_out, me.pos), tr.at[0])

    pl.when(me.is_last)(keep.wait)
    mine = quarter(x_out, me.pos)
    for k in range(1, nq):
        post.send(mine, mine, ts.at[2 + k], tr.at[1], me.at_quad(me.quad(k)), in_last)
    yield

    @pl.when(jnp.logical_not(in_last))
    def _():
        post.got(mine, tr.at[1])

    post.send(mine, mine, ts.at[nq + 2], tr.at[2], me.side)
    post.send(mine, mine, ts.at[nq + 3], tr.at[3], me.core)
    yield
    theirs = quarter(x_out, side_pos)
    post.got(theirs, tr.at[2])
    post.send(theirs, theirs, ts.at[nq + 4], tr.at[4], me.core)
    yield
    post.got(quarter(x_out, me.pos + flip), tr.at[3])
    post.got(quarter(x_out, side_pos + flip), tr.at[4])


def gather_sems(nq, mats):
    shapes = [(nq - 1, mats)] * 2 + [(nq, mats)] * 2 + [(2 * nq - 2, mats)] * 2 + [(4 * nq - 2, mats)] * 2
    return [pltpu.SemaphoreType.DMA(shape) for shape in shapes]


def state_flow(me, f_ref, tabs, sel, s_ref, m0, r0, m1, r1, m2, r2, ss, rs, zs, zr, ps, pr):
    nq = me.nq
    one, two, three, four = tabs[4], tabs[5], tabs[6], tabs[7]
    ab = tabs[13]
    mine = f_ref[0:384].reshape(3, 2, 64, 128)
    m0[...] = mine.astype(BF16)
    copy = remote(m0, r0, ss.at[0], rs.at[0], me.core)
    copy.start()
    yield
    copy.wait()
    upper_core, upper_side = me.c == 1, me.y == 1
    other = r0[...].astype(F32)
    lower = jnp.where(upper_core, other, mine)
    upper = jnp.where(upper_core, mine, other)
    pair = one * lower + upper
    before = jnp.where(upper_core, other, 0.0)
    m1[0] = pair.astype(BF16)
    m1[1, :, 0] = lower[:, 0].astype(BF16)
    m1[1, :, 1] = jnp.zeros((3, 64, 128), BF16)
    copy = remote(m1, r1, ss.at[1], rs.at[1], me.side)
    copy.start()
    yield
    copy.wait()
    far = r1[0].astype(F32)
    low_pair = jnp.where(upper_side, far, pair)
    high_pair = jnp.where(upper_side, pair, far)
    total = two * low_pair + high_pair
    before = jnp.where(upper_side, jnp.where(upper_core, one * far, far), 0.0) + before
    third = jnp.where(upper_side, lower[:, 0], r1[1, :, 0].astype(F32))
    last_in = one * low_pair[:, 0] + third
    m2[0] = total[:, 0].astype(BF16)
    m2[1] = last_in.astype(BF16)
    sends = []
    for k in range(1, nq):
        copy = remote(m2.at[0], r2.at[me.q], zs.at[k - 1], zr.at[k - 1], me.at_quad(me.quad(k)))
        copy.start()
        sends.append(copy)

    @pl.when(me.q == nq - 1)
    def _():
        for k in range(1, nq):
            remote(m2.at[1], r2.at[nq], ps.at[k - 1], pr.at[0], me.at_quad(me.quad(k))).start()
        r2[nq] = m2[1]

    r2[me.q] = m2[0]
    yield
    for k in range(1, nq):
        src = r2.at[me.quad(nq - k)]
        remote(src, src, zs.at[k - 1], zr.at[k - 1], me.core).wait_recv()

    @pl.when(me.q != nq - 1)
    def _():
        remote(r2.at[nq], r2.at[nq], ps.at[0], pr.at[0], me.core).wait_recv()

    run = jnp.zeros((3, 64, 128), F32)
    carry, tail_in = run, run
    for k in range(nq):
        carry = jnp.where(me.q == k, run, carry)
        if k == nq - 1:
            tail_in = three * run + r2[nq].astype(F32)
        run = four * run + r2[k].astype(F32)
    low = (ab * run).astype(BF16).astype(F32)
    safe = jnp.abs(ab) >= TINY
    begin = jnp.where(safe, low / jnp.where(safe, ab, 1.0), run)
    lead = pick(me.pos, [jnp.ones_like(one), one, two, three])
    for p in range(3):
        start = sel(p, 0) * begin[0] + sel(p, 1) * begin[1] + sel(p, 2) * begin[2]
        s_ref[128 * p : 128 * p + 64] = lead * carry[p] + before[p, 0]
        s_ref[128 * p + 64 : 128 * p + 128] = lead * start + before[p, 1]
        s_ref[384 + 64 * p : 448 + 64 * p] = tail_in[p]
    for copy in sends:
        copy.wait_send()

    @pl.when(me.q == nq - 1)
    def _():
        for k in range(1, nq):
            remote(m2.at[1], r2.at[nq], ps.at[k - 1], pr.at[0], me.at_quad(me.quad(k))).wait_send()


def silu_grad(pre_act):
    sigmoid_val = sigmoid(pre_act)
    return sigmoid_val * (1.0 + pre_act * (1.0 - sigmoid_val))


def norm_rows(row_data):
    centered = row_data - jnp.mean(row_data, axis=-1, keepdims=True)
    scale_inv = lax.rsqrt(jnp.mean(centered * centered, axis=-1, keepdims=True) + NORM_EPS)
    return (centered * scale_inv, scale_inv)


def norm_back(grad_rows, plain, scale_inv, gain_vec):
    grad_norm = grad_rows * gain_vec
    inner_term = (
        grad_norm
        - jnp.mean(grad_norm, axis=-1, keepdims=True)
        - plain * jnp.mean(grad_norm * plain, axis=-1, keepdims=True)
    )
    return inner_term * scale_inv


def nt(lhs, rhs):
    return lax.dot_general(lhs, rhs, (((1,), (1,)), ((), ())), preferred_element_type=F32)


def tn(lhs, rhs):
    return lax.dot_general(lhs, rhs, (((0,), (0,)), ((), ())), preferred_element_type=F32)


def nn(lhs, rhs):
    return lax.dot_general(lhs, rhs, (((1,), (0,)), ((), ())), preferred_element_type=F32)


def sigmoid(value):
    return 0.5 * jnp.tanh(0.5 * value) + 0.5


def silu_pair(pre):
    sig = sigmoid(pre)
    return pre * sig, sig * (1.0 + pre * (1.0 - sig))


CHUNK = 256


def big_flow(me, cross_first, grads, r1, r2, r3, r4, rx, out, send, recv):
    nq = me.nq
    rows, width = out.shape
    wide = width // 2
    ours = pl.ds(pl.multiple_of(me.x * wide, 128), wide)
    others = pl.ds(pl.multiple_of((1 - me.x) * wide, 128), wide)
    copy1 = remote(grads.at[:, :, 1 - me.c], r1, send.at[0], recv.at[0], me.core)
    copy1.start()
    yield
    copy1.wait()

    def add1(i, carry):
        r1[i // 2, i % 2] = (grads[i // 2, i % 2, me.c].astype(F32) + r1[i // 2, i % 2].astype(F32)).astype(BF16)
        return carry

    lax.fori_loop(0, 2 * nq, add1, 0)
    if cross_first:
        copy2 = remote(r1.at[:, :, :, others], r2, send.at[1], recv.at[1], me.cross)
    else:
        copy2 = remote(r1.at[:, 1 - me.y], r2, send.at[1], recv.at[1], me.side)
    copy2.start()
    yield
    copy2.wait()
    if cross_first:
        def add2(i, carry):
            r2[i // 2, i % 2] = (r1[i // 2, i % 2, :, ours].astype(F32) + r2[i // 2, i % 2].astype(F32)).astype(BF16)
            return carry

        lax.fori_loop(0, 2 * nq, add2, 0)
        copy3 = remote(r2.at[:, 1 - me.y], r3, send.at[2], recv.at[2], me.side)
    else:
        def add2(i, carry):
            r2[i] = (r1[i, me.y].astype(F32) + r2[i].astype(F32)).astype(BF16)
            return carry

        lax.fori_loop(0, nq, add2, 0)
        copy3 = remote(r2.at[:, :, others], r3, send.at[2], recv.at[2], me.cross)
    copy3.start()
    yield
    copy3.wait()

    def add3(i, carry):
        mine = r2[i, me.y] if cross_first else r2[i, :, ours]
        r3[i] = (mine.astype(F32) + r3[i].astype(F32)).astype(BF16)
        return carry

    lax.fori_loop(0, nq, add3, 0)
    copies = []
    for k in range(1, nq):
        copy = remote(r3.at[me.quad(k)], r4.at[k - 1], send.at[2 + k], recv.at[2 + k], me.at_quad(me.quad(k)))
        copy.start()
        copies.append(copy)
    yield
    total = r3[me.q].astype(F32)
    for k in range(1, nq):
        copies[k - 1].wait()
        total = total + r4[k - 1].astype(F32)
    out[:, ours] = total.astype(BF16)
    copy5 = remote(out.at[:, ours], out.at[:, ours], send.at[nq + 2], recv.at[nq + 2], me.cross)
    copy5.start()
    yield
    remote(out.at[:, others], out.at[:, others], send.at[nq + 2], recv.at[nq + 2], me.cross).wait_recv()
    copy5.wait_send()
    for at, bit in enumerate(me.cross_bits()[1:]):
        copy = remote(out, rx.at[at], send.at[nq + 3 + at], recv.at[nq + 3 + at], me.cross_bit(bit))
        copy.start()
        copy.wait()
        out[...] = (out[...].astype(F32) + rx[at].astype(F32)).astype(BF16)


def big_scratch(nq, groups, cross_first, rows, width):
    extra = max(groups.bit_length() - 2, 1)
    half = width // 2
    second = (nq, 2, rows, half) if cross_first else (nq, rows, width)
    spare = (extra, rows, width) if groups > 2 else (1, 16, 128)
    shapes = [(nq, 2, rows, width), second, (nq, rows, half), (nq - 1, rows, half), spare]
    return [pltpu.VMEM(shape, BF16) for shape in shapes]


def small_flow(me, grads, r1, w1, r2, w2, rx, out, send, recv):
    many = 2 * me.nq
    copy1 = remote(grads.at[:, 1 - me.c], r1, send.at[0], recv.at[0], me.core)
    copy1.start()
    yield
    copy1.wait()

    def add(i, carry):
        w1[i] = (grads[i, me.c].astype(F32) + r1[i].astype(F32)).astype(BF16)
        return carry

    lax.fori_loop(0, many, add, 0)
    mine = me.q * 2 + me.y
    copies = []
    for k in range(1, many):
        to = (mine + k) % many
        copy = remote(w1.at[to], r2.at[k - 1], send.at[k], recv.at[k], (me.g, to * 2 + me.c))
        copy.start()
        copies.append(copy)
    yield
    total = w1[mine].astype(F32)
    for k in range(1, many):
        copies[k - 1].wait()
        total = total + r2[k - 1].astype(F32)
    bits = me.cross_bits()
    for at, bit in enumerate(bits):
        w2[at] = total.astype(BF16)
        copy = remote(w2.at[at], rx.at[at], send.at[many + at], recv.at[many + at], me.cross_bit(bit))
        copy.start()
        if at == 0:
            yield
        copy.wait()
        total = total + rx[at].astype(F32)
    out[...] = total.astype(BF16)


def small_scratch(nq, groups, rows):
    bits = groups.bit_length() - 1
    return [
        pltpu.VMEM((2 * nq, rows, 128), BF16), pltpu.VMEM((2 * nq, rows, 128), BF16),
        pltpu.VMEM((2 * nq - 1, rows, 128), BF16), pltpu.VMEM((bits, rows, 128), BF16), pltpu.VMEM((bits, rows, 128), BF16),
    ]


def adjoint_flow(me, f_ref, tabs, sel, s_ref, m0, r0, m1, r1, m2, r2, ss, rs, zs, zr):
    nq = me.nq
    one, two, three, four = tabs[4], tabs[5], tabs[6], tabs[7]
    mine = f_ref[...].reshape(3, 2, 64, 128)
    m0[...] = mine.astype(BF16)
    copy = remote(m0, r0, ss.at[0], rs.at[0], me.core)
    copy.start()
    yield
    copy.wait()
    upper_core, upper_side = me.c == 1, me.y == 1
    other = r0[...].astype(F32)
    lower = jnp.where(upper_core, other, mine)
    upper = jnp.where(upper_core, mine, other)
    pair = lower + one * upper
    after = jnp.where(upper_core, 0.0, other)
    m1[...] = pair.astype(BF16)
    copy = remote(m1, r1, ss.at[1], rs.at[1], me.side)
    copy.start()
    yield
    copy.wait()
    far = r1[...].astype(F32)
    low_pair = jnp.where(upper_side, far, pair)
    high_pair = jnp.where(upper_side, pair, far)
    total = low_pair + two * high_pair
    after = jnp.where(upper_side, 0.0, jnp.where(upper_core, far, one * far)) + after
    m2[0] = total[:, 0].astype(BF16)
    for m in range(3):
        m2[1, m] = (sel(0, m) * total[0, 1] + sel(1, m) * total[1, 1] + sel(2, m) * total[2, 1]).astype(BF16)
    sends = []
    for k in range(1, nq):
        copy = remote(m2, r2.at[me.q], zs.at[k - 1], zr.at[k - 1], me.at_quad(me.quad(k)))
        copy.start()
        sends.append(copy)
    r2[me.q] = m2[...]
    yield
    for k in range(1, nq):
        src = r2.at[me.quad(nq - k)]
        remote(src, src, zs.at[k - 1], zr.at[k - 1], me.core).wait_recv()
    run = r2[0, 1].astype(F32)
    for k in range(1, nq):
        run = run + r2[k, 1].astype(F32)
    carry = run
    for k in range(nq - 1, -1, -1):
        carry = jnp.where(me.q == k, run, carry)
        run = four * run + r2[k, 0].astype(F32)
    lead = pick(me.pos, [three, two, one, jnp.ones_like(one)])
    for p in range(3):
        s_ref[2 * p * 64 : (2 * p + 1) * 64] = lead * carry[p] + after[p, 0]
        s_ref[(2 * p + 1) * 64 : (2 * p + 2) * 64] = after[p, 1]
    for copy in sends:
        copy.wait_send()


class Steps:
    def __init__(self, flows):
        self.flows, self.live = flows, [True] * len(flows)

    def __call__(self, *which):
        for i in which:
            if self.live[i]:
                try:
                    next(self.flows[i])
                except StopIteration:
                    self.live[i] = False

    def finish(self):
        while any(self.live):
            self(*range(len(self.flows)))


ORDERS = (True, True, True, True, True)
N_BIG = 5
TURNS = ((0, 1), (2, 3), (0, 1, 4), (2, 3), (0, 1, 4), (2, 3))


def layer_kernel(n, groups, *refs):
    refs = list(refs)

    def take(count):
        got = refs[:count]
        del refs[:count]
        return got

    p_rates, p_vecs, (resumed,) = take(4), take(6), take(1)
    cot, h_tokens, i_value, i_reset, i_inner, i_hidden, i_outer, i_shared = take(8)
    o_result, o_input = take(2)
    sums, (out_early, out_late), (staged,) = take(N_BIG), take(2), take(1)
    tabs, power, power_rev, vec_wide, vec_head, starts, w_shared = take(7)
    g_middle, g_act, g_base, slope_s, shared_out = take(5)
    grads, (t_keys_sent, sum_wide, sum_head) = take(N_BIG), take(3)
    gathered, lift, tok, tail, x_lanes, ema, inner, finals = take(8)
    early_all, late_all = take(2)
    (
        values, slope_v, t_values, t_slope, t_keys, t_dv, t_dk, k_units, k_activ, k_gated, k_mid, k_inner, k_branch, k_gin,
        k_greset, k_gvalue,
    ) = take(16)
    g_lanes, b_inner, dx_lanes, k_gs, b_start, acc_in, acc_decay, acc_out, kept, omega_acc, gain_acc = take(11)
    b_flow = finals.at[0:384]
    t_sum, t_grad, t_out, g_early, g_late = take(5)
    big = [take(5) for _ in range(N_BIG)]
    small_early, small_late, keys_s, tail_s, back_exchange = take(5), take(5), take(5), take(5), take(6)
    exchange = take(6)
    load_sem, ss, sr, hs, hr, ts, tr = take(7)
    early_sem, late_sem = take(8), take(8)
    ess, ers, ezs, ezr, eps, epr = take(6)
    big_send, big_recv, fs, fr, small_send, small_recv, k_send, k_recv, t_send, t_recv, bss, brs, bzs, bzr = take(14)

    me = Place(n, groups)
    length = 128
    width = tok.shape[1]
    lanes = width // 128
    own = tok.shape[0]
    total = own + tail.shape[0] * length
    count = own // length
    chan = width // n
    heads = 128 // n
    rows_b = i_hidden.shape[0]
    sets = count // 2
    sel = chosen(resumed, me)

    def local_copy(src, dst, at):
        copy = pltpu.make_async_copy(src, dst, load_sem.at[at])
        copy.start()
        return copy

    x_in = h_tokens.at[:, 0]
    packing = [
        local_copy(i_value, early_all.at[me.s, 0:chan], 0),
        local_copy(i_reset, early_all.at[me.s, chan : 2 * chan], 1),
        local_copy(i_hidden, late_all.at[me.s, 0:rows_b], 2),
        local_copy(i_outer, late_all.at[me.s, rows_b : 2 * rows_b], 3),
        local_copy(i_inner.at[:, 0:width], late_all.at[me.s, 2 * rows_b : 2 * rows_b + chan], 4),
        local_copy(i_inner.at[:, width : 2 * width], late_all.at[me.s, 2 * rows_b + chan : 2 * rows_b + 2 * chan], 14),
        local_copy(i_shared, w_shared.at[me.s], 5),
    ]
    fetch = [local_copy(h_tokens.at[p, k], tok.at[(p * 2 + k) * length : (p * 2 + k + 1) * length], 6 + p * 2 + k) for p in range(sets) for k in range(2)]
    lift[...] = jnp.zeros_like(lift)
    block = jnp.zeros((16, 128), F32)
    for i, ref in enumerate(p_rates):
        lift[i, :, 0:chan] = ref[...].astype(F32)
        block = block + pltpu.roll(lift[i], 32 * i, 1)
    for i, ref in enumerate(p_vecs):
        lift[4, i : i + 1, 0 : ref.shape[1]] = ref[...].astype(F32)
    gathered[me.s, 0:16] = block.astype(BF16)
    gathered[me.s, 16:32] = lift[4].astype(BF16)
    meet(me.group_peers() + [me.cross_bit(bit) for bit in me.cross_bits()])
    post = Sender(load_sem.at[12])
    post.device = me.core
    small_gather(me, gathered, post, ss, sr)
    for copy in packing:
        copy.wait()
    early = gather_flow(me, post, [early_all], *early_sem)
    late = gather_flow(me, post, [late_all], *late_sem)
    words = tokens_flow(me, post, x_in, tail, ts, tr, load_sem.at[13])
    next(early)
    next(words)
    next(late)
    small_gather(me, w_shared, post, hs, hr)
    for copy in fetch:
        copy.wait()

    def norm_step(row, carry):
        here = pl.ds(pl.multiple_of(row * length, length), length)
        plain, _ = norm_rows(tok[here, :].astype(F32))
        for lane in range(lanes):
            x_lanes[pl.ds(lane * total + row * length, length), :] = plain[:, lane * 128 : (lane + 1) * 128]
        return carry

    lax.fori_loop(0, count, norm_step, 0)
    small_arrive(me, gathered, post, sr)
    per = 128 // chan
    column = lax.broadcasted_iota(jnp.int32, (16, 128), 1)
    head_sum = jnp.zeros((16, 128), F32)
    for lane in range(lanes):
        rates = [jnp.zeros((16, 128), F32)] * 4
        wide = jnp.zeros((16, 128), F32)
        for k in range(per):
            block = gathered[lane * per + k, 0:16].astype(F32)
            for i in range(4):
                mine = jnp.where((column >= 32 * i) & (column < 32 * i + chan), block, 0.0)
                rates[i] = rates[i] + pltpu.roll(mine, (chan * k - 32 * i) % 128, 1)
            rows = gathered[lane * per + k, 16:32].astype(F32)
            wide = wide + pltpu.roll(rows, chan * k, 1)
            head_sum = head_sum + pltpu.roll(rows, heads * (lane * per + k), 1)
        for i in range(4):
            tabs[9 + i, lane * 16 : lane * 16 + 16] = rates[i]
        vec_wide[:, lane * 128 : (lane + 1) * 128] = wide[0:8]
        vec_head[4 + lane : 5 + lane] = wide[2:3]
    vec_head[0:3] = head_sum[3:6]
    vec_head[3:4] = head_sum[3:4]
    alpha, delta, beta, eta = tabs[9], tabs[10], tabs[11], tabs[12]
    decay = 1.0 - alpha * delta
    chain = [decay]
    for _ in range(9):
        chain.append(chain[-1] * chain[-1])
    ab = alpha * beta
    tabs[10], tabs[11] = beta, delta
    tabs[0], tabs[1], tabs[2], tabs[3] = decay, chain[4], chain[5], chain[6]
    tabs[4], tabs[5], tabs[6], tabs[7] = chain[7], chain[8], chain[8] * chain[7], chain[9]
    tabs[8], tabs[13] = ab * eta, ab
    d16, d32, d64 = chain[4], chain[5], chain[6]
    steps = [jnp.ones_like(decay), d16, d32, d32 * d16, d64, d64 * d16, d64 * d32, d64 * d32 * d16]
    for k in range(8):
        power[pl.ds(k, 64, stride=8), :] = steps[k]
        power_rev[pl.ds(7 - k, 64, stride=8), :] = steps[k]
    for lane in range(lanes):
        x_lanes[lane * total : lane * total + own] = x_lanes[lane * total : lane * total + own] * vec_wide[0:1, lane * 128 : (lane + 1) * 128]

    def local_pass(first, many):
        ema_local_pass(
            total // length, (first, 1, many), x_lanes, tabs.at[0], tabs.at[1], tabs.at[2], tabs.at[3], inner, finals, False
        )

    def apply_pass(first, many):
        ema_apply_pass(total // length, (first, many), x_lanes, tabs.at[0], tabs.at[8], vec_head, power, inner, starts, ema)

    def step(*flows):
        for flow in flows:
            next(flow, None)

    step(words, early)
    local_pass(0, count // 2)
    step(early, early)
    local_pass(count // 2, count // 2)
    state = state_flow(me, finals, tabs, sel, starts, *exchange, ess, ers, ezs, ezr, eps, epr)
    step(state)
    step(state)
    step(words, early)
    step(state)
    step(late, early, early)
    step(state)
    step(words, late, late)
    for part in range(3):
        apply_pass(part * (count // 3), count // 3)
        step(early)
    for _ in words:
        pass

    def tail_norm(m, carry):
        plain, _ = norm_rows(tail[m].astype(F32))
        plain = plain * vec_wide[0:1]
        for lane in range(lanes):
            x_lanes[pl.ds(lane * total + own + m * length, length), :] = plain[:, lane * 128 : (lane + 1) * 128]
        return carry

    step(late)
    lax.fori_loop(0, sets, tail_norm, 0)
    local_pass(count, sets)
    step(late)
    apply_pass(count, sets)
    step(late)
    small_arrive(me, w_shared, post, hr)
    for _ in early:
        pass
    w_value, w_reset = early_all.at[:, 0:chan], early_all.at[:, chan : 2 * chan]
    w_hidden, w_outer = late_all.at[:, 0:rows_b], late_all.at[:, rows_b : 2 * rows_b]
    w_inner = [late_all.at[:, 2 * rows_b + i * chan : 2 * rows_b + (i + 1) * chan] for i in range(2)]
    hv = w_value.shape[2]
    parts = hv // CHUNK
    scale = 1.0 / math.sqrt(128.0)

    def ready(name):
        if name == "hidden":
            for _ in late:
                pass
        elif name == "tail":
            step(late, late)
        elif name == "reset":
            step(late)

    gain_one, gain_two = vec_wide[0:1], vec_wide[1:2]
    q_mul, q_add, k_mul = vec_head[0:1], vec_head[1:2], vec_head[2:3]
    t_dv[...] = jnp.zeros_like(t_dv)
    t_dk[...] = jnp.zeros_like(t_dk)
    sum_wide[...] = jnp.zeros_like(sum_wide)
    sum_head[...] = jnp.zeros_like(sum_head)

    def columns(ref, at):
        block = ref[:, :, at * CHUNK : (at + 1) * CHUNK]
        return block.reshape(block.shape[0] * block.shape[1], CHUNK)

    def rows(ref, at):
        per = CHUNK // rows_b
        return ref[at * per : (at + 1) * per].reshape(CHUNK, ref.shape[2])

    def ema_rows(start, count):
        return jnp.concatenate([ema[pl.ds(lane * total + start, count), :] for lane in range(4)], axis=1)

    def tail_step(m, carry):
        at = pl.multiple_of(m * length, length)
        plain, _ = norm_rows(tail[m].astype(F32))
        units = (plain * gain_one).astype(BF16)
        k_units[pl.ds(own + at, length), :] = units
        for part in range(parts):
            value, slope = silu_pair(nn(units, columns(w_value, part)))
            t_values[m, :, part * CHUNK : (part + 1) * CHUNK] = value.astype(BF16)
            t_slope[m, :, part * CHUNK : (part + 1) * CHUNK] = slope.astype(BF16)
        pre = ema_rows(own + at, length)
        activ = (pre * sigmoid(pre)).astype(BF16)
        shared = nn(activ, w_shared[...].reshape(width, 128))
        t_keys[m] = (shared * sigmoid(shared) * k_mul).astype(BF16)
        return carry

    lax.fori_loop(0, sets, tail_step, 0)
    ready("tail")
    causal = lax.broadcasted_iota(jnp.int32, (length, length), 0) >= lax.broadcasted_iota(jnp.int32, (length, length), 1)

    reset_pre, mixed, slope_i = g_lanes, b_inner, dx_lanes

    def put(ref, part, value):
        for i in range(CHUNK // 128):
            at = (part * (CHUNK // 128) + i) * 2 * length
            ref[at : at + 2 * length] = value[:, i * 128 : (i + 1) * 128]

    def get(ref, part):
        at = [(part * (CHUNK // 128) + i) * 2 * length for i in range(CHUNK // 128)]
        return jnp.concatenate([ref[start : start + 2 * length] for start in at], axis=1)

    def set_step(p, ready):
        here = pl.ds(pl.multiple_of(p * 2 * length, 2 * length), 2 * length)
        m = resumed[0, p * me.nq + me.q]
        x = tok[here, :].astype(F32)
        plain, _ = norm_rows(x)
        units = (plain * gain_one).astype(BF16)
        k_units[here, :] = units
        for part in range(parts):
            cut = slice(part * CHUNK, (part + 1) * CHUNK)
            value, slope = silu_pair(nn(units, columns(w_value, part)))
            values[:, cut] = value.astype(BF16)
            slope_v[:, cut] = slope.astype(BF16)
        ready("reset")
        pre = ema_rows(p * 2 * length, 2 * length)
        activ = (pre * sigmoid(pre)).astype(BF16)
        k_activ[here, :] = activ
        shared, slope = silu_pair(nn(activ, w_shared[...].reshape(width, 128)))
        slope_s[here, :] = slope
        shared_out[here, :] = shared
        queries = (shared * q_mul + q_add).astype(BF16)
        keys = (shared * k_mul).astype(BF16)
        for part in range(parts):
            put(reset_pre, part, nn(activ, columns(w_reset, part)))
        p_q, c_q, p_k, c_k = queries[:length], queries[length:], keys[:length], keys[length:]
        e_k = t_keys[m]

        def weights(scores):
            expo = jnp.exp(scores - jnp.max(scores, axis=-1, keepdims=True))
            return expo * (1.0 / jnp.sum(expo, axis=-1, keepdims=True))

        p_probs = weights(jnp.where(causal, nt(p_q, p_k) * scale, MASKED_SCORE))
        c_probs = weights(
            jnp.concatenate((nt(c_q, e_k) * scale, jnp.where(causal, nt(c_q, c_k) * scale, MASKED_SCORE)), axis=1)
        )
        p_low, c_low = p_probs.astype(BF16), c_probs.astype(BF16)
        for part in range(parts):
            cut = slice(part * CHUNK, (part + 1) * CHUNK)
            mix_p = nn(p_low, values[:length, cut])
            mix_c = nn(c_low, jnp.concatenate((t_values[m, :, cut], values[length:, cut]), axis=0))
            mix = jnp.concatenate((mix_p, mix_c), axis=0)
            put(mixed, part, mix)
            gate = get(reset_pre, part)
            k_gated[here, cut] = (gate * sigmoid(gate) * mix).astype(BF16)
        ready("hidden")
        middle = x + nn(k_gated[here, :], w_hidden[...].reshape(-1, width))
        plain_mid, inv_mid = norm_rows(middle)
        mid_low = (plain_mid * gain_two).astype(BF16)
        k_mid[here, :] = mid_low
        ready("inner")
        for part in range(parts):
            cut = slice(part * CHUNK, (part + 1) * CHUNK)
            inner, slope = silu_pair(nn(mid_low, columns(w_inner[part * CHUNK // width], part % (width // CHUNK))))
            k_inner[here, cut] = inner.astype(BF16)
            put(slope_i, part, slope)
        ready("outer")
        staged[here, :] = (middle + nn(k_inner[here, :], w_outer[...].reshape(-1, width))).astype(BF16)
        top = cot[here, :]
        for part in range(parts):
            cut = slice(part * CHUNK, (part + 1) * CHUNK)
            k_gin[here, cut] = (nt(top, rows(w_outer, part)) * get(slope_i, part)).astype(BF16)
        back = nt(k_gin[here, 0:width], w_inner[0][...].reshape(width, width))
        back = back + nt(k_gin[here, width : 2 * width], w_inner[1][...].reshape(width, width))
        sum_wide[0:1] += jnp.sum(back * plain_mid, axis=0, keepdims=True)
        g_mid = top.astype(F32) + norm_back(back, plain_mid, inv_mid, gain_two)
        g_middle[here, :] = g_mid
        branch = g_mid.astype(BF16)
        k_branch[here, :] = branch
        dp_p = jnp.zeros((length, length), F32)
        dp_c = jnp.zeros((length, 2 * length), F32)
        for part in range(parts):
            cut = slice(part * CHUNK, (part + 1) * CHUNK)
            gated_back = nt(branch, rows(w_hidden, part))
            gate, slope = silu_pair(get(reset_pre, part))
            g_mix = (gated_back * gate).astype(BF16)
            k_greset[here, cut] = (gated_back * get(mixed, part) * slope).astype(BF16)
            dp_p += nt(g_mix[:length], values[:length, cut])
            dp_c += nt(g_mix[length:], jnp.concatenate((t_values[m, :, cut], values[length:, cut]), axis=0))
            dv_p = tn(p_low, g_mix[:length])
            dv_c = tn(c_low, g_mix[length:])
            for to in range(sets):
                t_dv[to, :, cut] += sel(p, to) * dv_c[:length]
            dv = jnp.concatenate((dv_p, dv_c[length:]), axis=0)
            k_gvalue[here, cut] = (dv * slope_v[:, cut].astype(F32)).astype(BF16)
        g_act[here, :] = nt(k_greset[here, :], w_reset[...].reshape(width, -1))

        def score_back(probs, grads):
            return (probs * (grads - jnp.sum(grads * probs, axis=-1, keepdims=True))).astype(BF16)

        p_ds, c_ds = score_back(p_probs, dp_p), score_back(c_probs, dp_c)
        d_q = jnp.concatenate((nn(p_ds, p_k), nn(c_ds, jnp.concatenate((e_k, c_k), axis=0))), axis=0) * scale
        dk_c = tn(c_ds, c_q) * scale
        for to in range(sets):
            t_dk[to] += sel(p, to) * dk_c[:length]
        d_k = jnp.concatenate((tn(p_ds, p_q) * scale, dk_c[length:]), axis=0)
        sum_head[0:1] += jnp.sum(d_q * shared, axis=0, keepdims=True)
        sum_head[1:2] += jnp.sum(d_q, axis=0, keepdims=True)
        sum_head[2:3] += jnp.sum(d_k * shared, axis=0, keepdims=True)
        g_base[here, :] = d_q * q_mul + d_k * k_mul

    def quiet(name):
        return None

    def later_step(p, carry):
        set_step(p, quiet)
        return carry

    set_step(0, ready)
    lax.fori_loop(1, sets, later_step, 0)
    leave = local_copy(staged, o_result, 0)
    tail_rows = length // 4
    for part in range(4):
        t_keys_sent[part // 2, part % 2] = t_dk[:, part * tail_rows : (part + 1) * tail_rows].astype(BF16)
    keys = tail_flow(me, t_keys_sent, *keys_s, t_sum, k_send, k_recv)
    next(keys)
    for ref in (omega_acc, gain_acc, acc_in, acc_decay, acc_out):
        ref[...] = jnp.zeros_like(ref)

    def grad_rows(row, with_tail):
        at = pl.multiple_of(row * length, length)
        here = pl.ds(at, length)
        d_shared = g_base[here, :]
        if with_tail:
            extra = jnp.concatenate([t_sum[part // 2, part % 2, row // 2] for part in range(4)], axis=0).astype(F32)
            d_shared = d_shared + extra * k_mul
            gain_acc[1:2, 0:128] += jnp.sum(extra * shared_out[here, :], axis=0, keepdims=True)
        gs = (d_shared * slope_s[here, :]).astype(BF16)
        k_gs[here, :] = gs
        for lane in range(lanes):
            cut = slice(lane * 128, (lane + 1) * 128)
            pre = ema[pl.ds(lane * total + at, length), :]
            sig = sigmoid(pre)
            back = g_act[here, cut] + nt(gs, w_shared[lane * per : (lane + 1) * per].reshape(128, 128))
            back = back * (sig * (1.0 + pre * (1.0 - sig)))
            g_lanes[pl.ds(lane * own + at, length), :] = back
            x = x_lanes[pl.ds(lane * total + at, length), :]
            omega_acc[lane : lane + 1] += jnp.sum(back * x, axis=0, keepdims=True)

    def local_back(first):
        ema_local_pass(
            count, (first, 2, count // 2), g_lanes, tabs.at[0], tabs.at[1], tabs.at[2], tabs.at[3], b_inner, b_flow, True
        )

    def cont_rows(p, carry):
        grad_rows(2 * p + 1, False)
        return carry

    def prompt_rows(p, carry):
        grad_rows(2 * p, True)
        return carry

    def norm_rows_back(x, units):
        plain, inv = norm_rows(x.astype(F32))
        gain_acc[0:1] += jnp.sum(units * plain, axis=0, keepdims=True)
        return norm_back(units, plain, inv, gain_one)

    def weight_grad(lhs, rhs, out, many):
        quads = CHUNK // out.shape[3] // 4

        def step(i, carry):
            block = tn(lhs[0:many, pl.ds(pl.multiple_of(i * CHUNK, CHUNK), CHUNK)], rhs[0:many, :])
            out[pl.ds(i * quads, quads)] = block.astype(BF16).reshape(quads, *out.shape[1:])
            return carry

        lax.fori_loop(0, lhs.shape[1] // CHUNK, step, 0)

    steps = Steps(
        [big_flow(me, ORDERS[i], grads[i], *big[i], sums[i], big_send.at[i], big_recv.at[i]) for i in range(N_BIG)]
    )
    weight_grad(k_inner, cot, grads[0], own)
    steps(0)
    next(keys)
    weight_grad(k_mid, k_gin, grads[1], own)
    steps(1, 0)
    lax.fori_loop(0, count // 2, cont_rows, 0)
    next(keys)
    weight_grad(k_gated, k_branch, grads[2], own)
    steps(2, 1)
    local_back(1)
    next(keys)
    weight_grad(k_activ, k_greset, grads[3], own)
    steps(3, 2)
    for _ in keys:
        pass
    lax.fori_loop(0, count // 2, prompt_rows, 0)
    local_back(0)
    adjoint = adjoint_flow(me, b_flow, tabs, sel, b_start, *back_exchange, bss, brs, bzs, bzr)
    next(adjoint)
    steps(3)

    def tail_back(m, carry):
        at = pl.multiple_of(own + m * length, length)
        k_gvalue[pl.ds(at, length), :] = (t_dv[m] * t_slope[m].astype(F32)).astype(BF16)
        return carry

    lax.fori_loop(0, sets, tail_back, 0)
    block = tn(k_activ[...], k_gs[...]).astype(BF16)
    g_early[:, :, 0:chan] = block.reshape(n // 2, 2, chan, 128)
    tops = jnp.concatenate((sum_head[0:2], sum_head[2:3] + gain_acc[1:2, 0:128], jnp.zeros((13, 128), F32)), axis=0)
    tops = jnp.broadcast_to(tops.astype(BF16)[None, None], (n // 2, 2, 16, 128))
    g_early[:, :, chan:] = tops
    first = small_flow(me, g_early, *small_early, out_early, fs, fr)
    next(first)
    next(adjoint)
    weight_grad(k_units, k_gvalue, grads[4], total)
    steps(4)
    next(adjoint)
    steps(0, 1)

    def units_step(i, carry):
        at = pl.multiple_of(i * CHUNK, CHUNK)
        block = nt(k_gvalue[pl.ds(at, CHUNK), :], w_value[...].reshape(width, -1))
        for lane in range(lanes):
            dx_lanes[pl.ds(lane * own + at, CHUNK), :] = block[:, lane * 128 : (lane + 1) * 128]
        return carry

    lax.fori_loop(0, own // CHUNK, units_step, 0)

    def tail_grad_step(m, carry):
        at = pl.multiple_of(own + m * length, length)
        units = nt(k_gvalue[pl.ds(at, length), :], w_value[...].reshape(width, -1))
        block = norm_rows_back(tail[m], units).astype(BF16)
        for part in range(4):
            t_grad[part // 2, part % 2, m] = block[part * tail_rows : (part + 1) * tail_rows]
        return carry

    lax.fori_loop(0, sets, tail_grad_step, 0)
    ends = tail_flow(me, t_grad, *tail_s, t_out, t_send, t_recv)
    next(ends)
    steps(2, 4)
    for _ in adjoint:
        pass
    for row in range(count):
        ema_back_pass(
            count, total // length, row, x_lanes, g_lanes, tabs.at[0], tabs.at[8], vec_head, power, inner, starts,
            power_rev, b_inner, b_start, dx_lanes, acc_in, acc_decay, acc_out, kept,
        )
        if row < 3:
            next(ends)
        next(first, None)
        steps(*TURNS[row])

    def own_rows(row, carry):
        here = pl.ds(pl.multiple_of(row * length, length), length)
        units = jnp.concatenate(
            [dx_lanes[pl.ds(lane * own + row * length, length), :] for lane in range(lanes)], axis=1
        )
        g_middle[here, :] = g_middle[here, :] + norm_rows_back(tok[here, :], units)
        return carry

    lax.fori_loop(0, count, own_rows, 0)
    alpha, beta, delta, eta, ab = (tabs[9 + i] for i in range(5))
    m_sum, q_sum = eta * acc_in[...], eta * ab * acc_decay[...]
    parts = (beta * m_sum - delta * q_sum, -alpha * q_sum, alpha * m_sum, ab * acc_out[...])
    per = 128 // chan // 2
    for lane in range(lanes):
        cut = slice(lane * 128, (lane + 1) * 128)
        block = [part[lane * 16 : lane * 16 + 16] for part in parts]
        block += [omega_acc[lane : lane + 1], gain_acc[0:1, cut], sum_wide[0:1, cut], jnp.zeros((61, 128), F32)]
        block = jnp.concatenate(block, axis=0).T.astype(BF16)
        g_late[lane * per : (lane + 1) * per] = block.reshape(per, 2, chan, 128)
    little = small_flow(me, g_late, *small_late, out_late, small_send, small_recv)
    next(little)
    for _ in ends:
        pass
    next(little)
    steps(*range(N_BIG))
    for part in range(4):
        for m in range(sets):
            at = 2 * m * length + part * tail_rows
            here = slice(at, at + tail_rows)
            g_middle[here] = g_middle[here] + t_out[part // 2, part % 2, m].astype(F32)

    def cast_rows(row, carry):
        here = pl.ds(pl.multiple_of(row * length, length), length)
        staged[here, :] = g_middle[here, :].astype(BF16)
        return carry

    leave.wait()
    lax.fori_loop(0, count, cast_rows, 0)
    leave = local_copy(staged, o_input, 1)
    next(little)
    steps(*range(N_BIG))
    for _ in little:
        pass
    steps.finish()
    post.finish()
    leave.wait()


def layer_call(n, groups, rates, vectors, resumed, cot, tokens, weights):
    nq = n // 4
    dma = pltpu.SemaphoreType.DMA
    vm = pltpu.VMEM
    shape = jax.ShapeDtypeStruct
    sets, kinds, length, width = tokens.shape
    own = sets * kinds * length
    total = own + sets * length
    chan, hv = weights[0].shape
    rows_b = weights[3].shape[0]
    early_rows = chan + 16
    wide, tall = (nq, 2, 2, chan, hv), (nq, 2, 2, rows_b, width)
    shapes = [tall, wide, tall, wide, wide]
    piece = (sets, length // 4)
    outs = [shape((own, width), BF16)] * 2 + [shape(part[3:], BF16) for part in shapes] + [shape((early_rows, 128), BF16), shape((chan, 128), BF16)]
    scratch = [
        vm((own, width), BF16), vm((14, 64, 128), F32), vm((512, 128), F32), vm((512, 128), F32), vm((8, width), F32), vm((8, 128), F32),
        vm((total // 2, 128), F32), vm((n, chan, 128), BF16),
        vm((own, width), F32), vm((own, width), F32), vm((own, 128), F32), vm((own, 128), F32), vm((own, 128), F32),
    ]
    scratch += [vm(part, BF16) for part in shapes]
    scratch += [vm((2, 2, *piece, 128), BF16), vm((8, width), F32), vm((8, 128), F32)]
    scratch += [
        vm((n, 32, 128), BF16), vm((5, 16, 128), F32), vm((own, width), BF16), vm((sets, length, width), BF16),
        vm((total * 4, 128), F32), vm((total * 4, 128), F32), vm((total * 4, 128), F32), vm((total // 2, 128), F32),
        vm((n, 2 * chan, hv), BF16), vm((n, 2 * rows_b + 2 * chan, width), BF16),
        vm((2 * length, hv), BF16), vm((2 * length, hv), BF16),
        vm((sets, length, hv), BF16), vm((sets, length, hv), BF16), vm((sets, length, 128), BF16),
        vm((sets, length, hv), F32), vm((sets, length, 128), F32),
        vm((total, width), BF16), vm((own, width), BF16), vm((own, hv), BF16), vm((own, width), BF16),
        vm((own, hv), BF16), vm((own, width), BF16), vm((own, hv), BF16), vm((own, hv), BF16), vm((total, hv), BF16),
    ]
    scratch += [vm((own * 4, 128), F32)] * 3 + [vm((own, 128), BF16), vm((own // 2, 128), F32)]
    scratch += [vm((64, 128), F32)] * 3 + [vm((SUB * 11, 8, 128), F32), vm((8, 128), F32), vm((8, width), F32)]
    scratch += [
        vm((2, 2, *piece, 128), BF16), vm((2, 2, *piece, width), BF16),
        vm((2, 2, *piece, width), BF16), vm((n // 2, 2, early_rows, 128), BF16), vm((n // 2, 2, chan, 128), BF16),
    ]
    for i, part in enumerate(shapes):
        scratch += big_scratch(nq, groups, ORDERS[i], *part[3:])
    scratch += small_scratch(nq, groups, early_rows) + small_scratch(nq, groups, chan)
    scratch += tail_scratch(nq, (*piece, 128)) + tail_scratch(nq, (*piece, width))
    scratch += [vm((3, 2, 64, 128), BF16)] * 4 + [vm((2, 3, 64, 128), BF16), vm((nq, 2, 3, 64, 128), BF16)]
    scratch += [vm((3, 2, 64, 128), BF16)] * 2 + [vm((2, 3, 2, 64, 128), BF16)] * 2
    scratch += [vm((2, 3, 64, 128), BF16), vm((nq + 1, 3, 64, 128), BF16)]
    scratch += [dma((18,)), dma((n - 1,)), dma((n - 1,)), dma((n - 1,)), dma((n - 1,)), dma((nq + 5,)), dma((5,))]
    scratch += gather_sems(nq, 1) + gather_sems(nq, 1)
    scratch += [dma((2,)), dma((2,)), dma((nq - 1,)), dma((nq - 1,)), dma((nq - 1,)), dma((1,))]
    sems = nq + 3 + max(groups.bit_length() - 2, 1)
    small_sems = 2 * nq + groups.bit_length() - 1
    scratch += [
        dma((N_BIG, sems)), dma((N_BIG, sems)), dma((small_sems,)), dma((small_sems,)), dma((small_sems,)), dma((small_sems,)), dma((3,)), dma((nq + 4,)),
        dma((3,)), dma((nq + 4,)), dma((2,)), dma((2,)), dma((nq - 1,)), dma((nq - 1,)),
    ]
    return pl.pallas_call(
        functools.partial(layer_kernel, n, groups),
        out_shape=outs,
        in_specs=[VMEM] * 10 + [SMEM, VMEM] + [HBM] * 7,
        out_specs=[HBM] * 2 + [VMEM] * (len(outs) - 2),
        scratch_shapes=scratch,
        compiler_params=pltpu.CompilerParams(collective_id=0, has_side_effects=True, vmem_limit_bytes=63 << 20),
        name="layer",
    )(*rates, *vectors, resumed, cot, tokens, *weights)


def finish_kernel(heads, result_in, grad_in, *refs):
    sums, early, late, result_out, grad_out = refs[:N_BIG], *refs[N_BIG : N_BIG + 4]
    refs = refs[2:]
    outs = refs[N_BIG + 2 : 2 * N_BIG + 2]
    shared, rates, vecs = refs[2 * N_BIG + 2], refs[2 * N_BIG + 3 : 2 * N_BIG + 7], refs[2 * N_BIG + 7 : 2 * N_BIG + 13]
    result_out[...] = result_in[...]
    grad_out[...] = grad_in[...]
    for src, dst in zip(sums, outs):
        dst[...] = src[...].astype(F32)
    chan = shared.shape[0]
    shared[...] = early[0:chan].astype(F32)
    block = late[...].astype(F32).T
    for i, ref in enumerate(rates):
        ref[...] = block[16 * i : 16 * i + 16]
    for i in range(3):
        vecs[i][...] = block[64 + i : 65 + i]
    mine = lax.axis_index("seq") * heads
    rows = pltpu.roll(early[chan : chan + 16].astype(F32), (128 - mine) % 128, 1)
    for i in range(3):
        vecs[3 + i][...] = rows[i : i + 1, 0:heads]


def finish_call(n, heads, result, input_grad, sums, early, late):
    shape = jax.ShapeDtypeStruct
    chan = late.shape[0]
    outs = [shape(input_grad.shape, BF16)] * 2 + [shape(part.shape, F32) for part in sums] + [shape((chan, 128), F32)]
    outs += [shape((16, chan), F32)] * 4 + [shape((1, chan), F32)] * 3 + [shape((1, heads), F32)] * 3
    return pl.pallas_call(
        functools.partial(finish_kernel, heads),
        out_shape=outs,
        in_specs=[VMEM] * (N_BIG + 4),
        out_specs=[VMEM] * len(outs),
        compiler_params=pltpu.CompilerParams(vmem_limit_bytes=60 << 20),
        name="finish",
    )(result, input_grad, *sums, early, late)


def local(
    hidden_in, cotangent, cont_prompt, value_proj, shared_proj, reset_proj, hidden_proj, inner_proj,
    outer_proj, ema_alpha, ema_delta, ema_beta, ema_eta, ema_omega, norm_gain, ffn_gain, query_scale,
    query_shift, key_scale,
):
    n, groups = lax.axis_size("seq"), lax.axis_size("grp")
    sets, kinds, length, width = hidden_in.shape[1:]
    heads = query_scale.shape[0]
    own_rows = sets * kinds * length
    vectors = (norm_gain, ffn_gain, ema_omega, query_scale, query_shift, key_scale)
    result, input_grad, *sums, early, late = layer_call(
        n, groups, [part.T for part in (ema_alpha, ema_delta, ema_beta, ema_eta)], [part[None] for part in vectors],
        cont_prompt, cotangent[0].reshape(own_rows, width), hidden_in[0],
        (value_proj, reset_proj, inner_proj, hidden_proj, outer_proj, shared_proj),
    )
    result, *wide = finish_call(n, heads, result, input_grad, sums, early, late)
    input_grad, d_outer, d_inner, d_hidden, d_reset, d_value, d_shared = wide[:7]
    rates = [part.T for part in wide[7:11]]
    vecs = [part.reshape(part.shape[1]) for part in wide[11:17]]
    return (
        result.reshape(hidden_in.shape), input_grad.reshape(hidden_in.shape), d_value, d_shared, d_reset, d_hidden, d_inner,
        d_outer, *rates, *vecs,
    )


def solution(mesh):
    mat, vec = P("seq", None), P("seq")
    tok = P("grp", None, None, "seq", None)
    in_specs = (tok, tok, P("grp", None)) + (mat,) * 10 + (vec,) * 6
    out_specs = (tok, tok) + (mat,) * 10 + (vec,) * 6
    return jax.shard_map(local, mesh=mesh, in_specs=in_specs, out_specs=out_specs, check_vma=False)
```

```python
import functools
import math

import jax
import jax.numpy as jnp
from jax import lax
from jax.experimental import pallas as pl
from jax.experimental.pallas import tpu as pltpu
from jax.sharding import PartitionSpec as P

CLEN = 512
NORM_EPS = 1e-05
MASKED_SCORE = -1e30
MESH = pl.DeviceIdType.MESH
SUB = 16
NJ = 16
TINY = 1e-20
F32 = jnp.float32
BF16 = jnp.bfloat16
VMEM = pl.BlockSpec(memory_space=pltpu.VMEM)
HBM = pl.BlockSpec(memory_space=pltpu.HBM)
SMEM = pl.BlockSpec(memory_space=pltpu.SMEM)


def shift_down(value, count):
    rows = lax.broadcasted_iota(jnp.int32, value.shape, 0)
    return jnp.where(rows >= count, pltpu.roll(value, count, 0), 0.0)


def shift_up(value, count):
    rows = lax.broadcasted_iota(jnp.int32, value.shape, 0)
    return jnp.where(rows < 8 - count, pltpu.roll(value, 8 - count, 0), 0.0)


def row_of(ref, row):
    return jnp.broadcast_to(ref[pl.ds(row, 1), :], (8, 128))


def ema_local_pass(rows, pick_rows, x_ref, decay, decay16, decay32, decay64, inner_ref, final_ref, backward):
    shift = shift_up if backward else shift_down

    first, stride, many = pick_rows

    def body(turn, carry):
        row, lane = first + stride * (turn // 4), turn % 4
        item = row * 4 + lane
        base = lane * (rows * 128) + row * 128
        dec = [row_of(decay, lane * 16 + j) for j in range(NJ)]
        state = [jnp.zeros((8, 128), F32)] * NJ
        for step in range(SUB - 1, -1, -1) if backward else range(SUB):
            x = x_ref[pl.ds(base + step, 8, stride=SUB), :]
            if backward:
                state = [dec[j] * (state[j] + x) for j in range(NJ)]
            else:
                state = [dec[j] * state[j] + x for j in range(NJ)]
        for j in range(NJ):
            total = state[j]
            total = total + row_of(decay16, lane * 16 + j) * shift(total, 1)
            total = total + row_of(decay32, lane * 16 + j) * shift(total, 2)
            total = total + row_of(decay64, lane * 16 + j) * shift(total, 4)
            inner_ref[pl.ds((item * 16 + j) * 8, 8), :] = shift(total, 1)
            final_ref[pl.ds(row * 64 + lane * 16 + j, 1), :] = total[0:1] if backward else total[7:8]
        return carry

    lax.fori_loop(0, many * 4, body, 0)


def ema_apply_pass(rows, pick_rows, x_ref, decay, mix, omega, power, inner_ref, start_ref, y_ref):
    first, many = pick_rows

    def body(turn, carry):
        row, lane = first + turn // 4, turn % 4
        item = row * 4 + lane
        base = lane * (rows * 128) + row * 128
        state = [
            inner_ref[pl.ds((item * 16 + j) * 8, 8), :]
            + power[pl.ds((lane * 16 + j) * 8, 8), :] * row_of(start_ref, row * 64 + lane * 16 + j)
            for j in range(NJ)
        ]
        skip = row_of(omega, 4 + lane)
        for step in range(SUB):
            x = x_ref[pl.ds(base + step, 8, stride=SUB), :]
            sums = [skip * x, None]
            for j in range(NJ):
                state[j] = row_of(decay, lane * 16 + j) * state[j] + x
                term = row_of(mix, lane * 16 + j) * state[j]
                sums[j % 2] = term if sums[j % 2] is None else sums[j % 2] + term
            y_ref[pl.ds(base + step, 8, stride=SUB), :] = sums[0] + sums[1]
        return carry

    lax.fori_loop(0, many * 4, body, 0)


def ema_back_pass(
    rows, x_rows, row, x_ref, g_ref, decay, mix, omega, power, inner_ref, start_ref, power_rev,
    back_inner_ref, back_start_ref, dx_ref, sum_in, sum_decay, sum_out, kept,
):
    half = 8

    def body(lane, carry):
        item = row * 4 + lane
        base = lane * (rows * 128) + row * 128
        x_base = lane * (x_rows * 128) + row * 128
        skip = row_of(omega, 4 + lane)
        for part in range(NJ // half):
            js = range(part * half, part * half + half)
            dec = [row_of(decay, lane * 16 + j) for j in js]
            state = [
                inner_ref[pl.ds((item * 16 + j) * 8, 8), :]
                + power[pl.ds((lane * 16 + j) * 8, 8), :] * row_of(start_ref, row * 64 + lane * 16 + j)
                for j in js
            ]
            for step in range(SUB):
                if part == 0:
                    x = x_ref[pl.ds(x_base + step, 8, stride=SUB), :]
                    kept[SUB * half + step] = x
                else:
                    x = kept[SUB * half + step]
                for i in range(half):
                    kept[step * half + i] = state[i]
                    state[i] = dec[i] * state[i] + x
            adj = [
                back_inner_ref[pl.ds((item * 16 + j) * 8, 8), :]
                + power_rev[pl.ds((lane * 16 + j) * 8, 8), :]
                * row_of(back_start_ref, row * 64 + lane * 16 + j)
                for j in js
            ]
            weight = [row_of(mix, lane * 16 + j) for j in js]
            edge = [-(adj[i] * state[i]) for i in range(half)]
            first, second = [None] * half, [None] * half
            for step in range(SUB - 1, -1, -1):
                x = kept[SUB * half + step]
                at = pl.ds(base + step, 8, stride=SUB)
                if part == 0:
                    g = g_ref[at, :]
                    kept[SUB * (half + 1) + step] = g
                    sums = [dx_ref[at, :], skip * g]
                else:
                    g = kept[SUB * (half + 1) + step]
                    sums = [kept[SUB * (half + 2) + step], None]
                for i in range(half):
                    full = adj[i] + g
                    term = weight[i] * full
                    sums[i % 2] = term if sums[i % 2] is None else sums[i % 2] + term
                    with_x, with_s = full * x, full * kept[step * half + i]
                    first[i] = with_x if first[i] is None else first[i] + with_x
                    second[i] = with_s if second[i] is None else second[i] + with_s
                    adj[i] = dec[i] * full
                if part == 0:
                    kept[SUB * (half + 2) + step] = sums[0] + sums[1]
                else:
                    dx_ref[at, :] = sums[0] + sums[1]
            for i, j in enumerate(js):
                at = pl.ds(lane * 16 + j, 1)
                flow = edge[i] + adj[i] * kept[i]
                total = jnp.sum(first[i], axis=0, keepdims=True)
                sum_in[at, :] += total
                sum_decay[at, :] += jnp.sum(second[i], axis=0, keepdims=True)
                sum_out[at, :] += total + jnp.sum(flow, axis=0, keepdims=True)
        return carry

    lax.fori_loop(0, 4, body, 0)


class Place:
    def __init__(self, n, groups):
        self.n, self.nq, self.groups = n, n // 4, groups
        self.g, self.s = lax.axis_index("grp"), lax.axis_index("seq")
        self.c, self.y, self.q, self.x = self.s % 2, (self.s // 2) % 2, self.s // 4, self.g % 2
        self.pos = self.s % 4
        self.core = (self.g, self.s + 1 - 2 * self.c)
        self.side = (self.g, self.s + 2 - 4 * self.y)
        self.cross = (self.g + 1 - 2 * self.x, self.s)
        self.is_last = self.s == n - 1

    def quad(self, k):
        return (self.q + k) % self.nq

    def at_quad(self, q):
        return (self.g, q * 4 + self.pos)

    def group_peers(self):
        return [(self.g, (self.s + k) % self.n) for k in range(1, self.n)]

    def cross_bit(self, bit):
        return (self.g + bit - 2 * bit * ((self.g // bit) % 2), self.s)

    def cross_bits(self):
        return [1 << b for b in range(self.groups.bit_length() - 1)]


def chosen(resumed, me):
    def at(p, m):
        return jnp.where(resumed[0, p * me.nq + me.q] == m, 1.0, 0.0)

    return at


def meet(peers):
    barrier = pltpu.get_barrier_semaphore()
    for peer in peers:
        pl.semaphore_signal(barrier, inc=1, device_id=peer, device_id_type=MESH)
    pl.semaphore_wait(barrier, len(peers))


def remote(src, dst, send, recv, device):
    return pltpu.make_async_remote_copy(
        src_ref=src, dst_ref=dst, send_sem=send, recv_sem=recv, device_id=device, device_id_type=MESH
    )


def pick(index, values):
    out = values[0]
    for k in range(1, len(values)):
        out = jnp.where(index == k, values[k], out)
    return out


def tail_flow(me, t, r1, w1, r2, w2, r3, out, send, recv):
    nq = me.nq
    last = me.q == nq - 1
    out[...] = jnp.zeros_like(out)
    copy1 = remote(t.at[:, 1 - me.c], r1, send.at[0], recv.at[0], me.core)
    copy1.start()
    yield
    copy1.wait()
    for i in range(2):
        w1[i] = (t[i, me.c].astype(F32) + r1[i].astype(F32)).astype(BF16)
    copy2 = remote(w1.at[1 - me.y], r2, send.at[1], recv.at[1], me.side)
    copy2.start()
    yield
    copy2.wait()
    w2[...] = (w1[me.y].astype(F32) + r2[...].astype(F32)).astype(BF16)
    top = (me.g, (nq - 1) * 4 + me.pos)
    end = (me.g, nq * 4 - 1)
    for k in range(nq - 1):
        @pl.when(me.q == k)
        def _():
            remote(w2, r3.at[k], send.at[2], recv.at[2 + k], top).start()
    yield

    @pl.when(last)
    def _():
        total = w2[...].astype(F32)
        for k in range(nq - 1):
            remote(r3.at[k], r3.at[k], send.at[2], recv.at[2 + k], me.core).wait_recv()
            total = total + r3[k].astype(F32)
        w2[...] = total.astype(BF16)

        @pl.when(jnp.logical_not(me.is_last))
        def _():
            for j in range(3):
                @pl.when(me.pos == j)
                def _():
                    remote(w2, out.at[j // 2, j % 2], send.at[2], recv.at[nq + 1 + j], end).start()

        @pl.when(me.is_last)
        def _():
            out[1, 1] = w2[...]
    yield

    @pl.when(me.is_last)
    def _():
        for j in range(3):
            dst = out.at[j // 2, j % 2]
            remote(dst, dst, send.at[2], recv.at[nq + 1 + j], me.core).wait_recv()

    @pl.when(jnp.logical_not(me.is_last))
    def _():
        remote(w2, w2, send.at[2], recv.at[2], me.core).wait_send()


def tail_scratch(nq, shape):
    vm = pltpu.VMEM
    return [vm((2, *shape), BF16), vm((2, *shape), BF16), vm(shape, BF16), vm(shape, BF16), vm((nq - 1, *shape), BF16)]


class Sender:
    def __init__(self, spare):
        self.spare, self.started = spare, []

    def send(self, src, dst, send, recv, device, when=None):
        copy = remote(src, dst, send, recv, device)
        if when is None:
            copy.start()
        else:
            pl.when(when)(copy.start)
        self.started.append((copy, when))

    def got(self, ref, recv):
        remote(ref, ref, self.spare, recv, self.device).wait_recv()

    def finish(self):
        for copy, when in self.started:
            if when is None:
                copy.wait_send()
            else:
                pl.when(when)(copy.wait_send)


def small_gather(me, out, post, ss, sr):
    for k in range(1, me.n):
        post.send(out.at[me.s], out.at[me.s], ss.at[k - 1], sr.at[k - 1], (me.g, (me.s + k) % me.n))


def small_arrive(me, out, post, sr):
    for k in range(1, me.n):
        post.got(out.at[(me.s + me.n - k) % me.n], sr.at[k - 1])


def gather_flow(me, post, mats, zs, zr, ys, yr, xs, xr, cs, cr):
    nq = me.nq
    mats = [(out, out.shape[-1] // 2) for out in mats]
    other = 1 - me.x

    def half(ref, width, which):
        return ref.at[:, pl.ds(pl.multiple_of(which * width, 128), width)]

    def pieces(k, pos, which):
        shard = me.quad(nq - k) * 4 + pos
        return [half(out.at[shard], width, which) for out, width in mats]

    for i, (out, width) in enumerate(mats):
        mine = out.at[me.s]
        piece = half(mine, width, me.x)
        for k in range(1, nq):
            post.send(piece, piece, zs.at[k - 1, i], zr.at[k - 1, i], me.at_quad(me.quad(k)))
        post.send(mine, mine, ys.at[0, i], yr.at[0, i], me.side)
    for i, (out, width) in enumerate(mats):
        post.send(out.at[me.s], out.at[me.s], cs.at[0, i], cr.at[0, i], me.core)
    yield
    side_pos = me.pos + 2 - 4 * me.y
    for k in range(1, nq):
        for i, piece in enumerate(pieces(k, me.pos, me.x)):
            post.got(piece, zr.at[k - 1, i])
            post.send(piece, piece, ys.at[k, i], yr.at[k, i], me.side)
            post.send(piece, piece, xs.at[k - 1, i], xr.at[k - 1, i], me.cross)
            post.send(piece, piece, cs.at[k, i], cr.at[k, i], me.core)
        yield
    for k in range(nq):
        blocks = pieces(k, side_pos, me.x) if k else [out.at[me.q * 4 + side_pos] for out, _ in mats]
        for i, piece in enumerate(blocks):
            post.got(piece, yr.at[k, i])
            if k:
                post.send(piece, piece, xs.at[nq - 2 + k, i], xr.at[nq - 2 + k, i], me.cross)
            post.send(piece, piece, cs.at[nq + k, i], cr.at[nq + k, i], me.core)
        if k:
            yield
    for group, pos in ((0, me.pos), (1, side_pos)):
        for k in range(1, nq):
            at = group * (nq - 1) + k - 1
            for i, piece in enumerate(pieces(k, pos, other)):
                post.got(piece, xr.at[at, i])
                post.send(piece, piece, cs.at[2 * nq + at, i], cr.at[2 * nq + at, i], me.core)
        yield
    flip = 1 - 2 * me.c
    for group, pos in ((0, me.pos + flip), (1, side_pos + flip)):
        for i, (out, _) in enumerate(mats):
            post.got(out.at[me.q * 4 + pos], cr.at[group * nq, i])
        for k in range(1, nq):
            for i, piece in enumerate(pieces(k, pos, me.x)):
                post.got(piece, cr.at[group * nq + k, i])
            for i, piece in enumerate(pieces(k, pos, other)):
                post.got(piece, cr.at[2 * nq + group * (nq - 1) + k - 1, i])


def tokens_flow(me, post, x_in, x_out, ts, tr, local_sem):
    nq = me.nq
    rows = x_out.shape[1] // 4

    def quarter(ref, pos):
        return ref.at[:, pl.ds(pl.multiple_of(pos * rows, rows), rows)]

    in_last = me.q == nq - 1
    side_pos, flip = me.pos + 2 - 4 * me.y, 1 - 2 * me.c
    keep = pltpu.make_async_copy(quarter(x_in, me.pos), quarter(x_out, me.pos), local_sem)
    pl.when(me.is_last)(keep.start)
    for j in range(3):
        post.send(quarter(x_in, j), quarter(x_out, j), ts.at[j], tr.at[0], (me.g, 4 * (nq - 1) + j), me.is_last)
    yield

    @pl.when(jnp.logical_and(in_last, jnp.logical_not(me.is_last)))
    def _():
        post.got(quarter(x_out, me.pos), tr.at[0])

    pl.when(me.is_last)(keep.wait)
    mine = quarter(x_out, me.pos)
    for k in range(1, nq):
        post.send(mine, mine, ts.at[2 + k], tr.at[1], me.at_quad(me.quad(k)), in_last)
    yield

    @pl.when(jnp.logical_not(in_last))
    def _():
        post.got(mine, tr.at[1])

    post.send(mine, mine, ts.at[nq + 2], tr.at[2], me.side)
    post.send(mine, mine, ts.at[nq + 3], tr.at[3], me.core)
    yield
    theirs = quarter(x_out, side_pos)
    post.got(theirs, tr.at[2])
    post.send(theirs, theirs, ts.at[nq + 4], tr.at[4], me.core)
    yield
    post.got(quarter(x_out, me.pos + flip), tr.at[3])
    post.got(quarter(x_out, side_pos + flip), tr.at[4])


def gather_sems(nq, mats):
    shapes = [(nq - 1, mats)] * 2 + [(nq, mats)] * 2 + [(2 * nq - 2, mats)] * 2 + [(4 * nq - 2, mats)] * 2
    return [pltpu.SemaphoreType.DMA(shape) for shape in shapes]


def state_flow(me, f_ref, tabs, sel, s_ref, m0, r0, m1, r1, m2, r2, ss, rs, zs, zr, ps, pr):
    nq = me.nq
    one, two, three, four = tabs[4], tabs[5], tabs[6], tabs[7]
    ab = tabs[13]
    mine = f_ref[0:384].reshape(3, 2, 64, 128)
    m0[...] = mine.astype(BF16)
    copy = remote(m0, r0, ss.at[0], rs.at[0], me.core)
    copy.start()
    yield
    copy.wait()
    upper_core, upper_side = me.c == 1, me.y == 1
    other = r0[...].astype(F32)
    lower = jnp.where(upper_core, other, mine)
    upper = jnp.where(upper_core, mine, other)
    pair = one * lower + upper
    before = jnp.where(upper_core, other, 0.0)
    m1[0] = pair.astype(BF16)
    m1[1, :, 0] = lower[:, 0].astype(BF16)
    m1[1, :, 1] = jnp.zeros((3, 64, 128), BF16)
    copy = remote(m1, r1, ss.at[1], rs.at[1], me.side)
    copy.start()
    yield
    copy.wait()
    far = r1[0].astype(F32)
    low_pair = jnp.where(upper_side, far, pair)
    high_pair = jnp.where(upper_side, pair, far)
    total = two * low_pair + high_pair
    before = jnp.where(upper_side, jnp.where(upper_core, one * far, far), 0.0) + before
    third = jnp.where(upper_side, lower[:, 0], r1[1, :, 0].astype(F32))
    last_in = one * low_pair[:, 0] + third
    m2[0] = total[:, 0].astype(BF16)
    m2[1] = last_in.astype(BF16)
    sends = []
    for k in range(1, nq):
        copy = remote(m2.at[0], r2.at[me.q], zs.at[k - 1], zr.at[k - 1], me.at_quad(me.quad(k)))
        copy.start()
        sends.append(copy)

    @pl.when(me.q == nq - 1)
    def _():
        for k in range(1, nq):
            remote(m2.at[1], r2.at[nq], ps.at[k - 1], pr.at[0], me.at_quad(me.quad(k))).start()
        r2[nq] = m2[1]

    r2[me.q] = m2[0]
    yield
    for k in range(1, nq):
        src = r2.at[me.quad(nq - k)]
        remote(src, src, zs.at[k - 1], zr.at[k - 1], me.core).wait_recv()

    @pl.when(me.q != nq - 1)
    def _():
        remote(r2.at[nq], r2.at[nq], ps.at[0], pr.at[0], me.core).wait_recv()

    run = jnp.zeros((3, 64, 128), F32)
    carry, tail_in = run, run
    for k in range(nq):
        carry = jnp.where(me.q == k, run, carry)
        if k == nq - 1:
            tail_in = three * run + r2[nq].astype(F32)
        run = four * run + r2[k].astype(F32)
    low = (ab * run).astype(BF16).astype(F32)
    safe = jnp.abs(ab) >= TINY
    begin = jnp.where(safe, low / jnp.where(safe, ab, 1.0), run)
    lead = pick(me.pos, [jnp.ones_like(one), one, two, three])
    for p in range(3):
        start = sel(p, 0) * begin[0] + sel(p, 1) * begin[1] + sel(p, 2) * begin[2]
        s_ref[128 * p : 128 * p + 64] = lead * carry[p] + before[p, 0]
        s_ref[128 * p + 64 : 128 * p + 128] = lead * start + before[p, 1]
        s_ref[384 + 64 * p : 448 + 64 * p] = tail_in[p]
    for copy in sends:
        copy.wait_send()

    @pl.when(me.q == nq - 1)
    def _():
        for k in range(1, nq):
            remote(m2.at[1], r2.at[nq], ps.at[k - 1], pr.at[0], me.at_quad(me.quad(k))).wait_send()


def silu_grad(pre_act):
    sigmoid_val = sigmoid(pre_act)
    return sigmoid_val * (1.0 + pre_act * (1.0 - sigmoid_val))


def norm_rows(row_data):
    centered = row_data - jnp.mean(row_data, axis=-1, keepdims=True)
    scale_inv = lax.rsqrt(jnp.mean(centered * centered, axis=-1, keepdims=True) + NORM_EPS)
    return (centered * scale_inv, scale_inv)


def norm_back(grad_rows, plain, scale_inv, gain_vec):
    grad_norm = grad_rows * gain_vec
    inner_term = (
        grad_norm
        - jnp.mean(grad_norm, axis=-1, keepdims=True)
        - plain * jnp.mean(grad_norm * plain, axis=-1, keepdims=True)
    )
    return inner_term * scale_inv


def nt(lhs, rhs):
    return lax.dot_general(lhs, rhs, (((1,), (1,)), ((), ())), preferred_element_type=F32)


def tn(lhs, rhs):
    return lax.dot_general(lhs, rhs, (((0,), (0,)), ((), ())), preferred_element_type=F32)


def nn(lhs, rhs):
    return lax.dot_general(lhs, rhs, (((1,), (0,)), ((), ())), preferred_element_type=F32)


def sigmoid(value):
    return 0.5 * jnp.tanh(0.5 * value) + 0.5


def silu_pair(pre):
    sig = sigmoid(pre)
    return pre * sig, sig * (1.0 + pre * (1.0 - sig))


CHUNK = 256


def big_flow(me, cross_first, grads, r1, r2, r3, r4, rx, out, send, recv):
    nq = me.nq
    rows, width = out.shape
    wide = width // 2
    ours = pl.ds(pl.multiple_of(me.x * wide, 128), wide)
    others = pl.ds(pl.multiple_of((1 - me.x) * wide, 128), wide)
    copy1 = remote(grads.at[:, :, 1 - me.c], r1, send.at[0], recv.at[0], me.core)
    copy1.start()
    yield
    copy1.wait()

    def add1(i, carry):
        r1[i // 2, i % 2] = (grads[i // 2, i % 2, me.c].astype(F32) + r1[i // 2, i % 2].astype(F32)).astype(BF16)
        return carry

    lax.fori_loop(0, 2 * nq, add1, 0)
    if cross_first:
        copy2 = remote(r1.at[:, :, :, others], r2, send.at[1], recv.at[1], me.cross)
    else:
        copy2 = remote(r1.at[:, 1 - me.y], r2, send.at[1], recv.at[1], me.side)
    copy2.start()
    yield
    copy2.wait()
    if cross_first:
        def add2(i, carry):
            r2[i // 2, i % 2] = (r1[i // 2, i % 2, :, ours].astype(F32) + r2[i // 2, i % 2].astype(F32)).astype(BF16)
            return carry

        lax.fori_loop(0, 2 * nq, add2, 0)
        copy3 = remote(r2.at[:, 1 - me.y], r3, send.at[2], recv.at[2], me.side)
    else:
        def add2(i, carry):
            r2[i] = (r1[i, me.y].astype(F32) + r2[i].astype(F32)).astype(BF16)
            return carry

        lax.fori_loop(0, nq, add2, 0)
        copy3 = remote(r2.at[:, :, others], r3, send.at[2], recv.at[2], me.cross)
    copy3.start()
    yield
    copy3.wait()

    def add3(i, carry):
        mine = r2[i, me.y] if cross_first else r2[i, :, ours]
        r3[i] = (mine.astype(F32) + r3[i].astype(F32)).astype(BF16)
        return carry

    lax.fori_loop(0, nq, add3, 0)
    copies = []
    for k in range(1, nq):
        copy = remote(r3.at[me.quad(k)], r4.at[k - 1], send.at[2 + k], recv.at[2 + k], me.at_quad(me.quad(k)))
        copy.start()
        copies.append(copy)
    yield
    total = r3[me.q].astype(F32)
    for k in range(1, nq):
        copies[k - 1].wait()
        total = total + r4[k - 1].astype(F32)
    out[:, ours] = total.astype(BF16)
    copy5 = remote(out.at[:, ours], out.at[:, ours], send.at[nq + 2], recv.at[nq + 2], me.cross)
    copy5.start()
    yield
    remote(out.at[:, others], out.at[:, others], send.at[nq + 2], recv.at[nq + 2], me.cross).wait_recv()
    copy5.wait_send()
    for at, bit in enumerate(me.cross_bits()[1:]):
        copy = remote(out, rx.at[at], send.at[nq + 3 + at], recv.at[nq + 3 + at], me.cross_bit(bit))
        copy.start()
        copy.wait()
        out[...] = (out[...].astype(F32) + rx[at].astype(F32)).astype(BF16)


def big_scratch(nq, groups, cross_first, rows, width):
    extra = max(groups.bit_length() - 2, 1)
    half = width // 2
    second = (nq, 2, rows, half) if cross_first else (nq, rows, width)
    spare = (extra, rows, width) if groups > 2 else (1, 16, 128)
    shapes = [(nq, 2, rows, width), second, (nq, rows, half), (nq - 1, rows, half), spare]
    return [pltpu.VMEM(shape, BF16) for shape in shapes]


def small_flow(me, grads, r1, w1, r2, w2, rx, out, send, recv):
    many = 2 * me.nq
    copy1 = remote(grads.at[:, 1 - me.c], r1, send.at[0], recv.at[0], me.core)
    copy1.start()
    yield
    copy1.wait()

    def add(i, carry):
        w1[i] = (grads[i, me.c].astype(F32) + r1[i].astype(F32)).astype(BF16)
        return carry

    lax.fori_loop(0, many, add, 0)
    mine = me.q * 2 + me.y
    copies = []
    for k in range(1, many):
        to = (mine + k) % many
        copy = remote(w1.at[to], r2.at[k - 1], send.at[k], recv.at[k], (me.g, to * 2 + me.c))
        copy.start()
        copies.append(copy)
    yield
    total = w1[mine].astype(F32)
    for k in range(1, many):
        copies[k - 1].wait()
        total = total + r2[k - 1].astype(F32)
    bits = me.cross_bits()
    for at, bit in enumerate(bits):
        w2[at] = total.astype(BF16)
        copy = remote(w2.at[at], rx.at[at], send.at[many + at], recv.at[many + at], me.cross_bit(bit))
        copy.start()
        if at == 0:
            yield
        copy.wait()
        total = total + rx[at].astype(F32)
    out[...] = total.astype(BF16)


def small_scratch(nq, groups, rows):
    bits = groups.bit_length() - 1
    return [
        pltpu.VMEM((2 * nq, rows, 128), BF16), pltpu.VMEM((2 * nq, rows, 128), BF16),
        pltpu.VMEM((2 * nq - 1, rows, 128), BF16), pltpu.VMEM((bits, rows, 128), BF16), pltpu.VMEM((bits, rows, 128), BF16),
    ]


def adjoint_flow(me, f_ref, tabs, sel, s_ref, m0, r0, m1, r1, m2, r2, ss, rs, zs, zr):
    nq = me.nq
    one, two, three, four = tabs[4], tabs[5], tabs[6], tabs[7]
    mine = f_ref[...].reshape(3, 2, 64, 128)
    m0[...] = mine.astype(BF16)
    copy = remote(m0, r0, ss.at[0], rs.at[0], me.core)
    copy.start()
    yield
    copy.wait()
    upper_core, upper_side = me.c == 1, me.y == 1
    other = r0[...].astype(F32)
    lower = jnp.where(upper_core, other, mine)
    upper = jnp.where(upper_core, mine, other)
    pair = lower + one * upper
    after = jnp.where(upper_core, 0.0, other)
    m1[...] = pair.astype(BF16)
    copy = remote(m1, r1, ss.at[1], rs.at[1], me.side)
    copy.start()
    yield
    copy.wait()
    far = r1[...].astype(F32)
    low_pair = jnp.where(upper_side, far, pair)
    high_pair = jnp.where(upper_side, pair, far)
    total = low_pair + two * high_pair
    after = jnp.where(upper_side, 0.0, jnp.where(upper_core, far, one * far)) + after
    m2[0] = total[:, 0].astype(BF16)
    for m in range(3):
        m2[1, m] = (sel(0, m) * total[0, 1] + sel(1, m) * total[1, 1] + sel(2, m) * total[2, 1]).astype(BF16)
    sends = []
    for k in range(1, nq):
        copy = remote(m2, r2.at[me.q], zs.at[k - 1], zr.at[k - 1], me.at_quad(me.quad(k)))
        copy.start()
        sends.append(copy)
    r2[me.q] = m2[...]
    yield
    for k in range(1, nq):
        src = r2.at[me.quad(nq - k)]
        remote(src, src, zs.at[k - 1], zr.at[k - 1], me.core).wait_recv()
    run = r2[0, 1].astype(F32)
    for k in range(1, nq):
        run = run + r2[k, 1].astype(F32)
    carry = run
    for k in range(nq - 1, -1, -1):
        carry = jnp.where(me.q == k, run, carry)
        run = four * run + r2[k, 0].astype(F32)
    lead = pick(me.pos, [three, two, one, jnp.ones_like(one)])
    for p in range(3):
        s_ref[2 * p * 64 : (2 * p + 1) * 64] = lead * carry[p] + after[p, 0]
        s_ref[(2 * p + 1) * 64 : (2 * p + 2) * 64] = after[p, 1]
    for copy in sends:
        copy.wait_send()


class Steps:
    def __init__(self, flows):
        self.flows, self.live = flows, [True] * len(flows)

    def __call__(self, *which):
        for i in which:
            if self.live[i]:
                try:
                    next(self.flows[i])
                except StopIteration:
                    self.live[i] = False

    def finish(self):
        while any(self.live):
            self(*range(len(self.flows)))


ORDERS = (True, True, True, True, True)
N_BIG = 5
TURNS = ((2,), (0, 3), (1, 4), (0, 2), (1, 3), (0, 2, 4))


def layer_kernel(n, groups, *refs):
    refs = list(refs)

    def take(count):
        got = refs[:count]
        del refs[:count]
        return got

    p_rates, p_vecs, (resumed,) = take(4), take(6), take(1)
    cot, h_tokens, i_value, i_reset, i_inner, i_hidden, i_outer, i_shared = take(8)
    o_result, o_input = take(2)
    sums, (out_early, out_late), (staged,) = take(N_BIG), take(2), take(1)
    tabs, power, power_rev, vec_wide, vec_head, starts, w_shared = take(7)
    g_middle, g_act, g_base, slope_s, shared_out = take(5)
    grads, (t_keys_sent, sum_wide, sum_head) = take(N_BIG), take(3)
    gathered, lift, tok, tail, x_lanes, ema, inner, finals = take(8)
    early_all, late_all = take(2)
    (
        values, slope_v, t_values, t_slope, t_keys, t_dv, t_dk, k_units, k_activ, k_gated, k_mid, k_inner, k_branch, k_gin,
        k_greset, k_gvalue,
    ) = take(16)
    g_lanes, b_inner, dx_lanes, k_gs, b_start, acc_in, acc_decay, acc_out, kept, omega_acc, gain_acc = take(11)
    b_flow = finals.at[0:384]
    t_sum, t_grad, t_out, g_early, g_late = take(5)
    big = [take(5) for _ in range(N_BIG)]
    small_early, small_late, keys_s, tail_s, back_exchange = take(5), take(5), take(5), take(5), take(6)
    exchange = take(6)
    load_sem, ss, sr, hs, hr, ts, tr = take(7)
    early_sem, late_sem = take(8), take(8)
    ess, ers, ezs, ezr, eps, epr = take(6)
    big_send, big_recv, fs, fr, small_send, small_recv, k_send, k_recv, t_send, t_recv, bss, brs, bzs, bzr = take(14)

    me = Place(n, groups)
    length = 128
    width = tok.shape[1]
    lanes = width // 128
    own = tok.shape[0]
    total = own + tail.shape[0] * length
    count = own // length
    chan = width // n
    heads = 128 // n
    rows_b = i_hidden.shape[0]
    sets = count // 2
    sel = chosen(resumed, me)

    def local_copy(src, dst, at):
        copy = pltpu.make_async_copy(src, dst, load_sem.at[at])
        copy.start()
        return copy

    x_in = h_tokens.at[:, 0]
    packing = [
        local_copy(i_value, early_all.at[me.s, 0:chan], 0),
        local_copy(i_reset, early_all.at[me.s, chan : 2 * chan], 1),
        local_copy(i_hidden, late_all.at[me.s, 0:rows_b], 2),
        local_copy(i_outer, late_all.at[me.s, rows_b : 2 * rows_b], 3),
        local_copy(i_inner.at[:, 0:width], late_all.at[me.s, 2 * rows_b : 2 * rows_b + chan], 4),
        local_copy(i_inner.at[:, width : 2 * width], late_all.at[me.s, 2 * rows_b + chan : 2 * rows_b + 2 * chan], 14),
        local_copy(i_shared, w_shared.at[me.s], 5),
    ]
    fetch = [local_copy(h_tokens.at[p, k], tok.at[(p * 2 + k) * length : (p * 2 + k + 1) * length], 6 + p * 2 + k) for p in range(sets) for k in range(2)]
    lift[...] = jnp.zeros_like(lift)
    block = jnp.zeros((16, 128), F32)
    for i, ref in enumerate(p_rates):
        lift[i, :, 0:chan] = ref[...].astype(F32)
        block = block + pltpu.roll(lift[i], 32 * i, 1)
    for i, ref in enumerate(p_vecs):
        lift[4, i : i + 1, 0 : ref.shape[1]] = ref[...].astype(F32)
    gathered[me.s, 0:16] = block.astype(BF16)
    gathered[me.s, 16:32] = lift[4].astype(BF16)
    meet(me.group_peers() + [me.cross_bit(bit) for bit in me.cross_bits()])
    post = Sender(load_sem.at[12])
    post.device = me.core
    small_gather(me, gathered, post, ss, sr)
    for copy in packing:
        copy.wait()
    early = gather_flow(me, post, [early_all], *early_sem)
    late = gather_flow(me, post, [late_all], *late_sem)
    words = tokens_flow(me, post, x_in, tail, ts, tr, load_sem.at[13])
    next(early)
    next(words)
    next(late)
    small_gather(me, w_shared, post, hs, hr)
    for copy in fetch:
        copy.wait()

    def norm_step(row, carry):
        here = pl.ds(pl.multiple_of(row * length, length), length)
        plain, _ = norm_rows(tok[here, :].astype(F32))
        for lane in range(lanes):
            x_lanes[pl.ds(lane * total + row * length, length), :] = plain[:, lane * 128 : (lane + 1) * 128]
        return carry

    lax.fori_loop(0, count, norm_step, 0)
    small_arrive(me, gathered, post, sr)
    per = 128 // chan
    column = lax.broadcasted_iota(jnp.int32, (16, 128), 1)
    head_sum = jnp.zeros((16, 128), F32)
    for lane in range(lanes):
        rates = [jnp.zeros((16, 128), F32)] * 4
        wide = jnp.zeros((16, 128), F32)
        for k in range(per):
            block = gathered[lane * per + k, 0:16].astype(F32)
            for i in range(4):
                mine = jnp.where((column >= 32 * i) & (column < 32 * i + chan), block, 0.0)
                rates[i] = rates[i] + pltpu.roll(mine, (chan * k - 32 * i) % 128, 1)
            rows = gathered[lane * per + k, 16:32].astype(F32)
            wide = wide + pltpu.roll(rows, chan * k, 1)
            head_sum = head_sum + pltpu.roll(rows, heads * (lane * per + k), 1)
        for i in range(4):
            tabs[9 + i, lane * 16 : lane * 16 + 16] = rates[i]
        vec_wide[:, lane * 128 : (lane + 1) * 128] = wide[0:8]
        vec_head[4 + lane : 5 + lane] = wide[2:3]
    vec_head[0:3] = head_sum[3:6]
    vec_head[3:4] = head_sum[3:4]
    alpha, delta, beta, eta = tabs[9], tabs[10], tabs[11], tabs[12]
    decay = 1.0 - alpha * delta
    chain = [decay]
    for _ in range(9):
        chain.append(chain[-1] * chain[-1])
    ab = alpha * beta
    tabs[10], tabs[11] = beta, delta
    tabs[0], tabs[1], tabs[2], tabs[3] = decay, chain[4], chain[5], chain[6]
    tabs[4], tabs[5], tabs[6], tabs[7] = chain[7], chain[8], chain[8] * chain[7], chain[9]
    tabs[8], tabs[13] = ab * eta, ab
    d16, d32, d64 = chain[4], chain[5], chain[6]
    steps = [jnp.ones_like(decay), d16, d32, d32 * d16, d64, d64 * d16, d64 * d32, d64 * d32 * d16]
    for k in range(8):
        power[pl.ds(k, 64, stride=8), :] = steps[k]
        power_rev[pl.ds(7 - k, 64, stride=8), :] = steps[k]
    for lane in range(lanes):
        x_lanes[lane * total : lane * total + own] = x_lanes[lane * total : lane * total + own] * vec_wide[0:1, lane * 128 : (lane + 1) * 128]

    def local_pass(first, many):
        ema_local_pass(
            total // length, (first, 1, many), x_lanes, tabs.at[0], tabs.at[1], tabs.at[2], tabs.at[3], inner, finals, False
        )

    def apply_pass(first, many):
        ema_apply_pass(total // length, (first, many), x_lanes, tabs.at[0], tabs.at[8], vec_head, power, inner, starts, ema)

    def step(*flows):
        for flow in flows:
            next(flow, None)

    step(words, early)
    local_pass(0, count // 2)
    step(early, early)
    local_pass(count // 2, count // 2)
    state = state_flow(me, finals, tabs, sel, starts, *exchange, ess, ers, ezs, ezr, eps, epr)
    step(state)
    step(state)
    step(words, early)
    step(state)
    step(late, early, early)
    step(state)
    step(words, late, late)
    for part in range(3):
        apply_pass(part * (count // 3), count // 3)
        step(early)
    for _ in words:
        pass

    def tail_norm(m, carry):
        plain, _ = norm_rows(tail[m].astype(F32))
        plain = plain * vec_wide[0:1]
        for lane in range(lanes):
            x_lanes[pl.ds(lane * total + own + m * length, length), :] = plain[:, lane * 128 : (lane + 1) * 128]
        return carry

    step(late)
    lax.fori_loop(0, sets, tail_norm, 0)
    local_pass(count, sets)
    step(late)
    apply_pass(count, sets)
    step(late)
    small_arrive(me, w_shared, post, hr)
    for _ in early:
        pass
    w_value, w_reset = early_all.at[:, 0:chan], early_all.at[:, chan : 2 * chan]
    w_hidden, w_outer = late_all.at[:, 0:rows_b], late_all.at[:, rows_b : 2 * rows_b]
    w_inner = [late_all.at[:, 2 * rows_b + i * chan : 2 * rows_b + (i + 1) * chan] for i in range(2)]
    hv = w_value.shape[2]
    parts = hv // CHUNK
    scale = 1.0 / math.sqrt(128.0)

    def ready(name):
        if name == "hidden":
            for _ in late:
                pass
        elif name == "tail":
            step(late)
        elif name == "reset":
            step(late, late)

    gain_one, gain_two = vec_wide[0:1], vec_wide[1:2]
    q_mul, q_add, k_mul = vec_head[0:1], vec_head[1:2], vec_head[2:3]
    t_dv[...] = jnp.zeros_like(t_dv)
    t_dk[...] = jnp.zeros_like(t_dk)
    sum_wide[...] = jnp.zeros_like(sum_wide)
    sum_head[...] = jnp.zeros_like(sum_head)

    def columns(ref, at):
        block = ref[:, :, at * CHUNK : (at + 1) * CHUNK]
        return block.reshape(block.shape[0] * block.shape[1], CHUNK)

    def rows(ref, at):
        per = CHUNK // rows_b
        return ref[at * per : (at + 1) * per].reshape(CHUNK, ref.shape[2])

    def ema_rows(start, count):
        return jnp.concatenate([ema[pl.ds(lane * total + start, count), :] for lane in range(4)], axis=1)

    def tail_step(m, carry):
        at = pl.multiple_of(m * length, length)
        plain, _ = norm_rows(tail[m].astype(F32))
        units = (plain * gain_one).astype(BF16)
        k_units[pl.ds(own + at, length), :] = units
        for part in range(parts):
            value, slope = silu_pair(nn(units, columns(w_value, part)))
            t_values[m, :, part * CHUNK : (part + 1) * CHUNK] = value.astype(BF16)
            t_slope[m, :, part * CHUNK : (part + 1) * CHUNK] = slope.astype(BF16)
        pre = ema_rows(own + at, length)
        activ = (pre * sigmoid(pre)).astype(BF16)
        shared = nn(activ, w_shared[...].reshape(width, 128))
        t_keys[m] = (shared * sigmoid(shared) * k_mul).astype(BF16)
        return carry

    lax.fori_loop(0, sets, tail_step, 0)
    ready("tail")
    causal = lax.broadcasted_iota(jnp.int32, (length, length), 0) >= lax.broadcasted_iota(jnp.int32, (length, length), 1)

    reset_pre, mixed, slope_i = g_lanes, b_inner, dx_lanes

    def put(ref, part, value):
        for i in range(CHUNK // 128):
            at = (part * (CHUNK // 128) + i) * 2 * length
            ref[at : at + 2 * length] = value[:, i * 128 : (i + 1) * 128]

    def get(ref, part):
        at = [(part * (CHUNK // 128) + i) * 2 * length for i in range(CHUNK // 128)]
        return jnp.concatenate([ref[start : start + 2 * length] for start in at], axis=1)

    def set_step(p, ready):
        here = pl.ds(pl.multiple_of(p * 2 * length, 2 * length), 2 * length)
        m = resumed[0, p * me.nq + me.q]
        x = tok[here, :].astype(F32)
        plain, _ = norm_rows(x)
        units = (plain * gain_one).astype(BF16)
        k_units[here, :] = units
        for part in range(parts):
            cut = slice(part * CHUNK, (part + 1) * CHUNK)
            value, slope = silu_pair(nn(units, columns(w_value, part)))
            values[:, cut] = value.astype(BF16)
            slope_v[:, cut] = slope.astype(BF16)
        ready("reset")
        pre = ema_rows(p * 2 * length, 2 * length)
        activ = (pre * sigmoid(pre)).astype(BF16)
        k_activ[here, :] = activ
        shared, slope = silu_pair(nn(activ, w_shared[...].reshape(width, 128)))
        slope_s[here, :] = slope
        shared_out[here, :] = shared
        queries = (shared * q_mul + q_add).astype(BF16)
        keys = (shared * k_mul).astype(BF16)
        for part in range(parts):
            put(reset_pre, part, nn(activ, columns(w_reset, part)))
        p_q, c_q, p_k, c_k = queries[:length], queries[length:], keys[:length], keys[length:]
        e_k = t_keys[m]

        def weights(scores):
            expo = jnp.exp(scores - jnp.max(scores, axis=-1, keepdims=True))
            return expo * (1.0 / jnp.sum(expo, axis=-1, keepdims=True))

        p_probs = weights(jnp.where(causal, nt(p_q, p_k) * scale, MASKED_SCORE))
        c_probs = weights(
            jnp.concatenate((nt(c_q, e_k) * scale, jnp.where(causal, nt(c_q, c_k) * scale, MASKED_SCORE)), axis=1)
        )
        p_low, c_low = p_probs.astype(BF16), c_probs.astype(BF16)
        for part in range(parts):
            cut = slice(part * CHUNK, (part + 1) * CHUNK)
            mix_p = nn(p_low, values[:length, cut])
            mix_c = nn(c_low, jnp.concatenate((t_values[m, :, cut], values[length:, cut]), axis=0))
            mix = jnp.concatenate((mix_p, mix_c), axis=0)
            put(mixed, part, mix)
            gate = get(reset_pre, part)
            k_gated[here, cut] = (gate * sigmoid(gate) * mix).astype(BF16)
        ready("hidden")
        middle = x + nn(k_gated[here, :], w_hidden[...].reshape(-1, width))
        plain_mid, inv_mid = norm_rows(middle)
        mid_low = (plain_mid * gain_two).astype(BF16)
        k_mid[here, :] = mid_low
        ready("inner")
        for part in range(parts):
            cut = slice(part * CHUNK, (part + 1) * CHUNK)
            inner, slope = silu_pair(nn(mid_low, columns(w_inner[part * CHUNK // width], part % (width // CHUNK))))
            k_inner[here, cut] = inner.astype(BF16)
            put(slope_i, part, slope)
        ready("outer")
        staged[here, :] = (middle + nn(k_inner[here, :], w_outer[...].reshape(-1, width))).astype(BF16)
        top = cot[here, :]
        for part in range(parts):
            cut = slice(part * CHUNK, (part + 1) * CHUNK)
            k_gin[here, cut] = (nt(top, rows(w_outer, part)) * get(slope_i, part)).astype(BF16)
        back = nt(k_gin[here, 0:width], w_inner[0][...].reshape(width, width))
        back = back + nt(k_gin[here, width : 2 * width], w_inner[1][...].reshape(width, width))
        sum_wide[0:1] += jnp.sum(back * plain_mid, axis=0, keepdims=True)
        g_mid = top.astype(F32) + norm_back(back, plain_mid, inv_mid, gain_two)
        g_middle[here, :] = g_mid
        branch = g_mid.astype(BF16)
        k_branch[here, :] = branch
        dp_p = jnp.zeros((length, length), F32)
        dp_c = jnp.zeros((length, 2 * length), F32)
        for part in range(parts):
            cut = slice(part * CHUNK, (part + 1) * CHUNK)
            gated_back = nt(branch, rows(w_hidden, part))
            gate, slope = silu_pair(get(reset_pre, part))
            g_mix = (gated_back * gate).astype(BF16)
            k_greset[here, cut] = (gated_back * get(mixed, part) * slope).astype(BF16)
            dp_p += nt(g_mix[:length], values[:length, cut])
            dp_c += nt(g_mix[length:], jnp.concatenate((t_values[m, :, cut], values[length:, cut]), axis=0))
            dv_p = tn(p_low, g_mix[:length])
            dv_c = tn(c_low, g_mix[length:])
            for to in range(sets):
                t_dv[to, :, cut] += sel(p, to) * dv_c[:length]
            dv = jnp.concatenate((dv_p, dv_c[length:]), axis=0)
            k_gvalue[here, cut] = (dv * slope_v[:, cut].astype(F32)).astype(BF16)
        g_act[here, :] = nt(k_greset[here, :], w_reset[...].reshape(width, -1))

        def score_back(probs, grads):
            return (probs * (grads - jnp.sum(grads * probs, axis=-1, keepdims=True))).astype(BF16)

        p_ds, c_ds = score_back(p_probs, dp_p), score_back(c_probs, dp_c)
        d_q = jnp.concatenate((nn(p_ds, p_k), nn(c_ds, jnp.concatenate((e_k, c_k), axis=0))), axis=0) * scale
        dk_c = tn(c_ds, c_q) * scale
        for to in range(sets):
            t_dk[to] += sel(p, to) * dk_c[:length]
        d_k = jnp.concatenate((tn(p_ds, p_q) * scale, dk_c[length:]), axis=0)
        sum_head[0:1] += jnp.sum(d_q * shared, axis=0, keepdims=True)
        sum_head[1:2] += jnp.sum(d_q, axis=0, keepdims=True)
        sum_head[2:3] += jnp.sum(d_k * shared, axis=0, keepdims=True)
        g_base[here, :] = d_q * q_mul + d_k * k_mul

    def quiet(name):
        return None

    def later_step(p, carry):
        set_step(p, quiet)
        return carry

    set_step(0, ready)
    lax.fori_loop(1, sets, later_step, 0)
    leave = local_copy(staged, o_result, 0)
    tail_rows = length // 4
    for part in range(4):
        t_keys_sent[part // 2, part % 2] = t_dk[:, part * tail_rows : (part + 1) * tail_rows].astype(BF16)
    keys = tail_flow(me, t_keys_sent, *keys_s, t_sum, k_send, k_recv)
    next(keys)
    for ref in (omega_acc, gain_acc, acc_in, acc_decay, acc_out):
        ref[...] = jnp.zeros_like(ref)

    def grad_rows(row, with_tail):
        at = pl.multiple_of(row * length, length)
        here = pl.ds(at, length)
        d_shared = g_base[here, :]
        if with_tail:
            extra = jnp.concatenate([t_sum[part // 2, part % 2, row // 2] for part in range(4)], axis=0).astype(F32)
            d_shared = d_shared + extra * k_mul
            gain_acc[1:2, 0:128] += jnp.sum(extra * shared_out[here, :], axis=0, keepdims=True)
        gs = (d_shared * slope_s[here, :]).astype(BF16)
        k_gs[here, :] = gs
        for lane in range(lanes):
            cut = slice(lane * 128, (lane + 1) * 128)
            pre = ema[pl.ds(lane * total + at, length), :]
            sig = sigmoid(pre)
            back = g_act[here, cut] + nt(gs, w_shared[lane * per : (lane + 1) * per].reshape(128, 128))
            back = back * (sig * (1.0 + pre * (1.0 - sig)))
            g_lanes[pl.ds(lane * own + at, length), :] = back
            x = x_lanes[pl.ds(lane * total + at, length), :]
            omega_acc[lane : lane + 1] += jnp.sum(back * x, axis=0, keepdims=True)

    def local_back(first):
        ema_local_pass(
            count, (first, 2, count // 2), g_lanes, tabs.at[0], tabs.at[1], tabs.at[2], tabs.at[3], b_inner, b_flow, True
        )

    def cont_rows(p, carry):
        grad_rows(2 * p + 1, False)
        return carry

    def prompt_rows(p, carry):
        grad_rows(2 * p, True)
        return carry

    def norm_rows_back(x, units):
        plain, inv = norm_rows(x.astype(F32))
        gain_acc[0:1] += jnp.sum(units * plain, axis=0, keepdims=True)
        return norm_back(units, plain, inv, gain_one)

    def weight_grad(lhs, rhs, out, many):
        quads = CHUNK // out.shape[3] // 4

        def step(i, carry):
            block = tn(lhs[0:many, pl.ds(pl.multiple_of(i * CHUNK, CHUNK), CHUNK)], rhs[0:many, :])
            out[pl.ds(i * quads, quads)] = block.astype(BF16).reshape(quads, *out.shape[1:])
            return carry

        lax.fori_loop(0, lhs.shape[1] // CHUNK, step, 0)

    steps = Steps(
        [big_flow(me, ORDERS[i], grads[i], *big[i], sums[i], big_send.at[i], big_recv.at[i]) for i in range(N_BIG)]
    )
    weight_grad(k_inner, cot, grads[0], own)
    steps(0)
    next(keys)
    weight_grad(k_mid, k_gin, grads[1], own)
    steps(1, 0)
    lax.fori_loop(0, count // 2, cont_rows, 0)
    next(keys)
    weight_grad(k_gated, k_branch, grads[2], own)
    steps(2, 1)
    local_back(1)
    next(keys)
    weight_grad(k_activ, k_greset, grads[3], own)
    steps(3, 2)
    for _ in keys:
        pass
    lax.fori_loop(0, count // 2, prompt_rows, 0)
    local_back(0)
    adjoint = adjoint_flow(me, b_flow, tabs, sel, b_start, *back_exchange, bss, brs, bzs, bzr)
    next(adjoint)
    steps(3)

    def tail_back(m, carry):
        at = pl.multiple_of(own + m * length, length)
        k_gvalue[pl.ds(at, length), :] = (t_dv[m] * t_slope[m].astype(F32)).astype(BF16)
        return carry

    lax.fori_loop(0, sets, tail_back, 0)
    block = tn(k_activ[...], k_gs[...]).astype(BF16)
    g_early[:, :, 0:chan] = block.reshape(n // 2, 2, chan, 128)
    tops = jnp.concatenate((sum_head[0:2], sum_head[2:3] + gain_acc[1:2, 0:128], jnp.zeros((13, 128), F32)), axis=0)
    tops = jnp.broadcast_to(tops.astype(BF16)[None, None], (n // 2, 2, 16, 128))
    g_early[:, :, chan:] = tops
    first = small_flow(me, g_early, *small_early, out_early, fs, fr)
    next(first)
    next(adjoint)
    weight_grad(k_units, k_gvalue, grads[4], total)
    steps(4)
    next(adjoint)
    steps(0, 1)

    def units_step(i, carry):
        at = pl.multiple_of(i * CHUNK, CHUNK)
        block = nt(k_gvalue[pl.ds(at, CHUNK), :], w_value[...].reshape(width, -1))
        for lane in range(lanes):
            dx_lanes[pl.ds(lane * own + at, CHUNK), :] = block[:, lane * 128 : (lane + 1) * 128]
        return carry

    lax.fori_loop(0, own // CHUNK, units_step, 0)

    def tail_grad_step(m, carry):
        at = pl.multiple_of(own + m * length, length)
        units = nt(k_gvalue[pl.ds(at, length), :], w_value[...].reshape(width, -1))
        block = norm_rows_back(tail[m], units).astype(BF16)
        for part in range(4):
            t_grad[part // 2, part % 2, m] = block[part * tail_rows : (part + 1) * tail_rows]
        return carry

    lax.fori_loop(0, sets, tail_grad_step, 0)
    ends = tail_flow(me, t_grad, *tail_s, t_out, t_send, t_recv)
    next(ends)
    steps(2, 4)
    for _ in adjoint:
        pass
    for row in range(count):
        ema_back_pass(
            count, total // length, row, x_lanes, g_lanes, tabs.at[0], tabs.at[8], vec_head, power, inner, starts,
            power_rev, b_inner, b_start, dx_lanes, acc_in, acc_decay, acc_out, kept,
        )
        if row < 3:
            next(ends)
        next(first, None)
        steps(*TURNS[row])

    def own_rows(row, carry):
        here = pl.ds(pl.multiple_of(row * length, length), length)
        units = jnp.concatenate(
            [dx_lanes[pl.ds(lane * own + row * length, length), :] for lane in range(lanes)], axis=1
        )
        g_middle[here, :] = g_middle[here, :] + norm_rows_back(tok[here, :], units)
        return carry

    lax.fori_loop(0, count, own_rows, 0)
    alpha, beta, delta, eta, ab = (tabs[9 + i] for i in range(5))
    m_sum, q_sum = eta * acc_in[...], eta * ab * acc_decay[...]
    parts = (beta * m_sum - delta * q_sum, -alpha * q_sum, alpha * m_sum, ab * acc_out[...])
    per = 128 // chan // 2
    for lane in range(lanes):
        cut = slice(lane * 128, (lane + 1) * 128)
        block = [part[lane * 16 : lane * 16 + 16] for part in parts]
        block += [omega_acc[lane : lane + 1], gain_acc[0:1, cut], sum_wide[0:1, cut], jnp.zeros((61, 128), F32)]
        block = jnp.concatenate(block, axis=0).T.astype(BF16)
        g_late[lane * per : (lane + 1) * per] = block.reshape(per, 2, chan, 128)
    little = small_flow(me, g_late, *small_late, out_late, small_send, small_recv)
    next(little)
    for _ in ends:
        pass
    next(little)
    steps(*range(N_BIG))
    for part in range(4):
        for m in range(sets):
            at = 2 * m * length + part * tail_rows
            here = slice(at, at + tail_rows)
            g_middle[here] = g_middle[here] + t_out[part // 2, part % 2, m].astype(F32)

    def cast_rows(row, carry):
        here = pl.ds(pl.multiple_of(row * length, length), length)
        staged[here, :] = g_middle[here, :].astype(BF16)
        return carry

    leave.wait()
    lax.fori_loop(0, count, cast_rows, 0)
    leave = local_copy(staged, o_input, 1)
    next(little)
    steps(*range(N_BIG))
    for _ in little:
        pass
    steps.finish()
    post.finish()
    leave.wait()


def layer_call(n, groups, rates, vectors, resumed, cot, tokens, weights):
    nq = n // 4
    dma = pltpu.SemaphoreType.DMA
    vm = pltpu.VMEM
    shape = jax.ShapeDtypeStruct
    sets, kinds, length, width = tokens.shape
    own = sets * kinds * length
    total = own + sets * length
    chan, hv = weights[0].shape
    rows_b = weights[3].shape[0]
    early_rows = chan + 16
    wide, tall = (nq, 2, 2, chan, hv), (nq, 2, 2, rows_b, width)
    shapes = [tall, wide, tall, wide, wide]
    piece = (sets, length // 4)
    outs = [shape((own, width), BF16)] * 2 + [shape(part[3:], BF16) for part in shapes] + [shape((early_rows, 128), BF16), shape((chan, 128), BF16)]
    scratch = [
        vm((own, width), BF16), vm((14, 64, 128), F32), vm((512, 128), F32), vm((512, 128), F32), vm((8, width), F32), vm((8, 128), F32),
        vm((total // 2, 128), F32), vm((n, chan, 128), BF16),
        vm((own, width), F32), vm((own, width), F32), vm((own, 128), F32), vm((own, 128), F32), vm((own, 128), F32),
    ]
    scratch += [vm(part, BF16) for part in shapes]
    scratch += [vm((2, 2, *piece, 128), BF16), vm((8, width), F32), vm((8, 128), F32)]
    scratch += [
        vm((n, 32, 128), BF16), vm((5, 16, 128), F32), vm((own, width), BF16), vm((sets, length, width), BF16),
        vm((total * 4, 128), F32), vm((total * 4, 128), F32), vm((total * 4, 128), F32), vm((total // 2, 128), F32),
        vm((n, 2 * chan, hv), BF16), vm((n, 2 * rows_b + 2 * chan, width), BF16),
        vm((2 * length, hv), BF16), vm((2 * length, hv), BF16),
        vm((sets, length, hv), BF16), vm((sets, length, hv), BF16), vm((sets, length, 128), BF16),
        vm((sets, length, hv), F32), vm((sets, length, 128), F32),
        vm((total, width), BF16), vm((own, width), BF16), vm((own, hv), BF16), vm((own, width), BF16),
        vm((own, hv), BF16), vm((own, width), BF16), vm((own, hv), BF16), vm((own, hv), BF16), vm((total, hv), BF16),
    ]
    scratch += [vm((own * 4, 128), F32)] * 3 + [vm((own, 128), BF16), vm((own // 2, 128), F32)]
    scratch += [vm((64, 128), F32)] * 3 + [vm((SUB * 11, 8, 128), F32), vm((8, 128), F32), vm((8, width), F32)]
    scratch += [
        vm((2, 2, *piece, 128), BF16), vm((2, 2, *piece, width), BF16),
        vm((2, 2, *piece, width), BF16), vm((n // 2, 2, early_rows, 128), BF16), vm((n // 2, 2, chan, 128), BF16),
    ]
    for i, part in enumerate(shapes):
        scratch += big_scratch(nq, groups, ORDERS[i], *part[3:])
    scratch += small_scratch(nq, groups, early_rows) + small_scratch(nq, groups, chan)
    scratch += tail_scratch(nq, (*piece, 128)) + tail_scratch(nq, (*piece, width))
    scratch += [vm((3, 2, 64, 128), BF16)] * 4 + [vm((2, 3, 64, 128), BF16), vm((nq, 2, 3, 64, 128), BF16)]
    scratch += [vm((3, 2, 64, 128), BF16)] * 2 + [vm((2, 3, 2, 64, 128), BF16)] * 2
    scratch += [vm((2, 3, 64, 128), BF16), vm((nq + 1, 3, 64, 128), BF16)]
    scratch += [dma((18,)), dma((n - 1,)), dma((n - 1,)), dma((n - 1,)), dma((n - 1,)), dma((nq + 5,)), dma((5,))]
    scratch += gather_sems(nq, 1) + gather_sems(nq, 1)
    scratch += [dma((2,)), dma((2,)), dma((nq - 1,)), dma((nq - 1,)), dma((nq - 1,)), dma((1,))]
    sems = nq + 3 + max(groups.bit_length() - 2, 1)
    small_sems = 2 * nq + groups.bit_length() - 1
    scratch += [
        dma((N_BIG, sems)), dma((N_BIG, sems)), dma((small_sems,)), dma((small_sems,)), dma((small_sems,)), dma((small_sems,)), dma((3,)), dma((nq + 4,)),
        dma((3,)), dma((nq + 4,)), dma((2,)), dma((2,)), dma((nq - 1,)), dma((nq - 1,)),
    ]
    return pl.pallas_call(
        functools.partial(layer_kernel, n, groups),
        out_shape=outs,
        in_specs=[VMEM] * 10 + [SMEM, VMEM] + [HBM] * 7,
        out_specs=[HBM] * 2 + [VMEM] * (len(outs) - 2),
        scratch_shapes=scratch,
        compiler_params=pltpu.CompilerParams(collective_id=0, has_side_effects=True, vmem_limit_bytes=63 << 20),
        name="layer",
    )(*rates, *vectors, resumed, cot, tokens, *weights)


def finish_kernel(heads, result_in, grad_in, *refs):
    sums, early, late, result_out, grad_out = refs[:N_BIG], *refs[N_BIG : N_BIG + 4]
    refs = refs[2:]
    outs = refs[N_BIG + 2 : 2 * N_BIG + 2]
    shared, rates, vecs = refs[2 * N_BIG + 2], refs[2 * N_BIG + 3 : 2 * N_BIG + 7], refs[2 * N_BIG + 7 : 2 * N_BIG + 13]
    result_out[...] = result_in[...]
    grad_out[...] = grad_in[...]
    for src, dst in zip(sums, outs):
        dst[...] = src[...].astype(F32)
    chan = shared.shape[0]
    shared[...] = early[0:chan].astype(F32)
    block = late[...].astype(F32).T
    for i, ref in enumerate(rates):
        ref[...] = block[16 * i : 16 * i + 16]
    for i in range(3):
        vecs[i][...] = block[64 + i : 65 + i]
    mine = lax.axis_index("seq") * heads
    rows = pltpu.roll(early[chan : chan + 16].astype(F32), (128 - mine) % 128, 1)
    for i in range(3):
        vecs[3 + i][...] = rows[i : i + 1, 0:heads]


def finish_call(n, heads, result, input_grad, sums, early, late):
    shape = jax.ShapeDtypeStruct
    chan = late.shape[0]
    outs = [shape(input_grad.shape, BF16)] * 2 + [shape(part.shape, F32) for part in sums] + [shape((chan, 128), F32)]
    outs += [shape((16, chan), F32)] * 4 + [shape((1, chan), F32)] * 3 + [shape((1, heads), F32)] * 3
    return pl.pallas_call(
        functools.partial(finish_kernel, heads),
        out_shape=outs,
        in_specs=[VMEM] * (N_BIG + 4),
        out_specs=[VMEM] * len(outs),
        compiler_params=pltpu.CompilerParams(vmem_limit_bytes=60 << 20),
        name="finish",
    )(result, input_grad, *sums, early, late)


def local(
    hidden_in, cotangent, cont_prompt, value_proj, shared_proj, reset_proj, hidden_proj, inner_proj,
    outer_proj, ema_alpha, ema_delta, ema_beta, ema_eta, ema_omega, norm_gain, ffn_gain, query_scale,
    query_shift, key_scale,
):
    n, groups = lax.axis_size("seq"), lax.axis_size("grp")
    sets, kinds, length, width = hidden_in.shape[1:]
    heads = query_scale.shape[0]
    own_rows = sets * kinds * length
    vectors = (norm_gain, ffn_gain, ema_omega, query_scale, query_shift, key_scale)
    result, input_grad, *sums, early, late = layer_call(
        n, groups, [part.T for part in (ema_alpha, ema_delta, ema_beta, ema_eta)], [part[None] for part in vectors],
        cont_prompt, cotangent[0].reshape(own_rows, width), hidden_in[0],
        (value_proj, reset_proj, inner_proj, hidden_proj, outer_proj, shared_proj),
    )
    result, *wide = finish_call(n, heads, result, input_grad, sums, early, late)
    input_grad, d_outer, d_inner, d_hidden, d_reset, d_value, d_shared = wide[:7]
    rates = [part.T for part in wide[7:11]]
    vecs = [part.reshape(part.shape[1]) for part in wide[11:17]]
    return (
        result.reshape(hidden_in.shape), input_grad.reshape(hidden_in.shape), d_value, d_shared, d_reset, d_hidden, d_inner,
        d_outer, *rates, *vecs,
    )


def solution(mesh):
    mat, vec = P("seq", None), P("seq")
    tok = P("grp", None, None, "seq", None)
    in_specs = (tok, tok, P("grp", None)) + (mat,) * 10 + (vec,) * 6
    out_specs = (tok, tok) + (mat,) * 10 + (vec,) * 6
    return jax.shard_map(local, mesh=mesh, in_specs=in_specs, out_specs=out_specs, check_vma=False)
```
